32 devices in a mesh: dp: 32 (over z, y, x, core).
Axes of the slice: x: 2, y: 2, z: 4, core: 2. Of those that a mesh axis runs over, the one named last changes fastest.
Arguments:
- tokens: bfloat16 [16384, 1024], P('dp')
- cot_hidden: bfloat16 [16384, 1024], P('dp'), may hold values from -6 to 6
- cot_embed: bfloat16 [16384, 128], P('dp'), may hold values from -6 to 6
- lengths: int32 [32], replicated, may hold values from 128 to 512, as said below
- offsets: int32 [32], replicated, may hold values from 0 to 384, as said below
- pack_order: int32 [32], replicated, may hold values from 0 to 31, each once
- w_query: bfloat16 [1024, 1024], P('dp'), may hold values from -0.1875 to 0.1875
- b_query: bfloat16 [1024], P('dp'), may hold values from -1.75 to 1.75
- w_key: bfloat16 [1024, 1024], P('dp'), may hold values from -0.1875 to 0.1875
- b_key: bfloat16 [1024], P('dp'), may hold values from -1.75 to 1.75
- w_value: bfloat16 [1024, 1024], P('dp'), may hold values from -0.1875 to 0.1875
- b_value: bfloat16 [1024], P('dp'), may hold values from -1.75 to 1.75
- w_out: bfloat16 [1024, 1024], P('dp'), may hold values from -3 to 3
- b_out: bfloat16 [1024], P('dp'), may hold values from -1.75 to 1.75
- gain_attn: bfloat16 [1024], P('dp'), may hold values from 0.5 to 1.5
- shift_attn: bfloat16 [1024], P('dp'), may hold values from -1.75 to 1.75
- w_up: bfloat16 [1024, 4096], P('dp'), may hold values from -0.1875 to 0.1875
- b_up: bfloat16 [4096], P('dp'), may hold values from -1.75 to 1.75
- w_down: bfloat16 [4096, 1024], P('dp'), may hold values from -0.09375 to 0.09375
- b_down: bfloat16 [1024], P('dp'), may hold values from -1.75 to 1.75
- gain_ffn: bfloat16 [1024], P('dp'), may hold values from 0.5 to 1.5
- shift_ffn: bfloat16 [1024], P('dp'), may hold values from -1.75 to 1.75
- w_proj: bfloat16 [1024, 128], P('dp'), may hold values from -0.1875 to 0.1875
Outputs:
- hidden: bfloat16 [16384, 1024], P('dp')
- embedding: bfloat16 [16384, 128], P('dp')
- grad_tokens: float32 [16384, 1024], P('dp')
- grad_w_query: float32 [1024, 1024], P('dp')
- grad_b_query: float32 [1024], P('dp')
- grad_w_key: float32 [1024, 1024], P('dp')
- grad_b_key: float32 [1024], P('dp')
- grad_w_value: float32 [1024, 1024], P('dp')
- grad_b_value: float32 [1024], P('dp')
- grad_w_out: float32 [1024, 1024], P('dp')
- grad_b_out: float32 [1024], P('dp')
- grad_gain_attn: float32 [1024], P('dp')
- grad_shift_attn: float32 [1024], P('dp')
- grad_w_up: float32 [1024, 4096], P('dp')
- grad_b_up: float32 [4096], P('dp')
- grad_w_down: float32 [4096, 1024], P('dp')
- grad_b_down: float32 [1024], P('dp')
- grad_gain_ffn: float32 [1024], P('dp')
- grad_shift_ffn: float32 [1024], P('dp')
- grad_w_proj: float32 [1024, 128], P('dp')
- rms_stats: float32 [3], replicated
The draws below stay inside these ranges and needn't reach their ends.
Inputs may be any that keep to these rules, and one draw needn't show every extreme that they name: The sequence of pack i fills slots offsets[i] to offsets[i] + lengths[i] - 1 of that pack's 512 slots; the rest is padding. offsets[i] + lengths[i] <= 512.
All inputs are finite; a program needn't handle non-finite values.
Results may differ from the reference program's by a relative error of at most 0.018.
Values may be sent and summed in bfloat16 or wider, within the bound.
A program may use at most 192 MiB of HBM per device.

```python
import math
import jax
import jax.numpy as jnp
from jax import lax

D = 1024
H = 16
FF = 4096
PROJ = 128
TOK_DEV = 512
TOKENS = 16384
PACKS = 32
MINLEN = 128


def pack_layout(key):
    key_len, key_long, key_apart, key_start = jax.random.split(jax.random.fold_in(key, 7), 4)
    slots = jnp.arange(PACKS, dtype=jnp.int32)
    seq_lengths = jax.random.randint(key_len, (PACKS,), MINLEN, TOK_DEV + 1)
    longest = jax.random.randint(key_long, (), 0, PACKS)
    step_away = jax.random.randint(key_apart, (), 1, PACKS)
    shortest = (longest + step_away) % PACKS
    seq_lengths = jnp.where(slots == longest, TOK_DEV, seq_lengths)
    seq_lengths = jnp.where(slots == shortest, MINLEN, seq_lengths)
    spare_slots = TOK_DEV - seq_lengths
    seq_starts = jax.random.randint(key_start, (PACKS,), 0, spare_slots + 1)
    seq_starts = jnp.where(slots == shortest, TOK_DEV - MINLEN, seq_starts)
    return (seq_lengths.astype(jnp.int32), seq_starts.astype(jnp.int32))


def draw_lengths(key, part):
    return pack_layout(key)[0]


def draw_offsets(key, part):
    return pack_layout(key)[1]


def draw_tokens(key, part):
    key_val, key_row = jax.random.split(jax.random.fold_in(key, 11))
    row_place = jnp.arange(TOKENS, dtype=jnp.float32) / (TOKENS - 1)
    values = jnp.clip(jax.random.normal(key_val, (TOKENS, D), jnp.float32), -6.0, 6.0)
    row_scale = 0.7 * jnp.exp(row_place * 0.6931472)
    jitter = jax.random.uniform(key_row, (TOKENS,), jnp.float32, 0.85, 1.15)
    return (values * (row_scale * jitter)[:, None]).astype(jnp.bfloat16)


def levels(key, extent, cuts, low, high):
    def one(axis_at, shards_of):
        heights = jax.random.uniform(jax.random.fold_in(jax.random.fold_in(key, 6), axis_at), (shards_of,), jnp.float32, low / len(cuts), high / len(cuts))
        return jnp.repeat(jnp.exp(heights), extent[axis_at] // shards_of).reshape((-1,) + (1,) * (len(extent) - axis_at - 1))

    level = one(*cuts[0])
    for cut in cuts[1:]:
        level = level * one(*cut)
    return level


def bell_draw(rng, extent, width, bound, pieces=(), held_as=jnp.bfloat16):
    level = levels(rng, extent, pieces, -0.22, 0.18) if pieces else 1.0
    values = jax.random.normal(rng, extent, jnp.float32) * width * level
    return jnp.minimum(jnp.maximum(values, -bound), bound).astype(held_as)


def setup_inputs(seed: int = 0) -> dict:
    seeds = jax.random.split(jax.random.key(seed), 24)
    return {
        "tokens": draw_tokens(jax.random.fold_in(seeds[23], 71), 0),
        "cot_hidden": bell_draw(seeds[1], (TOKENS, D), 1.0, 6.0, ((0, 32),)),
        "cot_embed": bell_draw(seeds[2], (TOKENS, PROJ), 1.0, 6.0, ((0, 32),)),
        "lengths": draw_lengths(jax.random.fold_in(seeds[23], 71), 0),
        "offsets": draw_offsets(jax.random.fold_in(seeds[23], 71), 0),
        "pack_order": jax.random.permutation(seeds[5], PACKS).astype(jnp.int32),
        "w_query": bell_draw(seeds[6], (D, D), D ** -0.5, 0.1875, ((0, 32),)),
        "b_query": bell_draw(seeds[7], (D,), 0.3, 1.75, ((0, 32),)),
        "w_key": bell_draw(seeds[8], (D, D), D ** -0.5, 0.1875, ((0, 32),)),
        "b_key": bell_draw(seeds[9], (D,), 0.3, 1.75, ((0, 32),)),
        "w_value": bell_draw(seeds[10], (D, D), D ** -0.5, 0.1875, ((0, 32),)),
        "b_value": bell_draw(seeds[11], (D,), 0.3, 1.75, ((0, 32),)),
        "w_out": bell_draw(seeds[12], (D, D), (max(2 * D // TOK_DEV, 1)) ** -0.5, 3.0, ((0, 32),)),
        "b_out": bell_draw(seeds[13], (D,), 0.3, 1.75, ((0, 32),)),
        "gain_attn": jnp.clip(1.0 + 0.1 * jax.random.normal(seeds[14], (D,), jnp.float32), 0.5, 1.5).astype(jnp.bfloat16),
        "shift_attn": bell_draw(seeds[15], (D,), 0.3, 1.75, ((0, 32),)),
        "w_up": bell_draw(seeds[16], (D, FF), D ** -0.5, 0.1875, ((0, 32),)),
        "b_up": bell_draw(seeds[17], (FF,), 0.3, 1.75, ((0, 32),)),
        "w_down": bell_draw(seeds[18], (FF, D), FF ** -0.5, 0.09375, ((0, 32),)),
        "b_down": bell_draw(seeds[19], (D,), 0.3, 1.75, ((0, 32),)),
        "gain_ffn": jnp.clip(1.0 + 0.1 * jax.random.normal(seeds[20], (D,), jnp.float32), 0.5, 1.5).astype(jnp.bfloat16),
        "shift_ffn": bell_draw(seeds[21], (D,), 0.3, 1.75, ((0, 32),)),
        "w_proj": bell_draw(seeds[22], (D, PROJ), D ** -0.5, 0.1875, ((0, 32),)),
    }


@jax.custom_vjp
def low(v):
    return lax.optimization_barrier(v.astype(jnp.bfloat16)).astype(jnp.float32)

@jax.custom_vjp
def low_back(v):
    return v

def low_keep(v):
    return (low(v), None)

def low_pass(kept, grad):
    return (grad,)

def back_keep(v):
    return (v, None)

def back_low(kept, grad):
    return (low(grad),)
low.defvjp(low_keep, low_pass)
low_back.defvjp(back_keep, back_low)
highest = lax.Precision.HIGHEST
eps_norm = 1e-05
neg_large = -1e+30

def matmul(left, right):
    return jnp.dot(left, right, precision=highest, preferred_element_type=jnp.float32)

def layer_norm(values, gain, shift):
    row_mean = lax.optimization_barrier(jnp.mean(values, axis=-1, keepdims=True))
    centred = values - row_mean
    variance = lax.optimization_barrier(jnp.mean(centred * centred, axis=-1, keepdims=True))
    return centred * lax.rsqrt(variance + eps_norm) * gain + shift

def rope_tables(position, head_dim):
    half_dim = head_dim // 2
    freq_index = jnp.arange(half_dim, dtype=jnp.float32)
    frequency = jnp.exp(-math.log(10000.0) * 2.0 * freq_index / head_dim)
    angles = position[:, None] * frequency[None, :]
    return (jnp.cos(angles)[:, None, :], jnp.sin(angles)[:, None, :])

def rotate(values, cosine, sine_part):
    half_dim = values.shape[-1] // 2
    first_half = values[..., :half_dim]
    second = values[..., half_dim:]
    return jnp.concatenate([first_half * cosine - second * sine_part, second * cosine + first_half * sine_part], axis=-1)

def one_pack(params, rows_in, length, offset):
    wt_query, bias_query, wt_key, bias_key, wt_value, bias_value, wt_out, bias_out, gain_a, shift_a, wt_up, bias_up, wt_down, bias_down, gain_f, shift_f, wt_proj = params
    row_count = rows_in.shape[0]
    head_dim = D // H
    row_index = jnp.arange(row_count, dtype=jnp.int32)
    is_valid = (row_index >= offset) & (row_index < offset + length)
    keep_rows = is_valid.astype(jnp.float32)[:, None]
    cosine, sine_part = rope_tables((row_index - offset).astype(jnp.float32), head_dim)
    query_pre = low_back(matmul(rows_in, wt_query) + bias_query)
    key_pre = low_back(matmul(rows_in, wt_key) + bias_key)
    value_low = low(low_back(matmul(rows_in, wt_value) + bias_value)).reshape(row_count, H, head_dim)
    query_rot = low(rotate(query_pre.reshape(row_count, H, head_dim), cosine, sine_part))
    key_rot = low(rotate(key_pre.reshape(row_count, H, head_dim), cosine, sine_part))
    raw_scores = jnp.einsum('qhd,khd->hqk', query_rot, key_rot, precision=highest)
    scores = low_back(raw_scores * (1.0 / math.sqrt(head_dim)))
    allowed = (is_valid[:, None] & is_valid[None, :])[None]
    masked = jnp.where(allowed, scores, neg_large)
    row_top = lax.optimization_barrier(jnp.max(masked, axis=-1, keepdims=True))
    exponent = jnp.exp(masked - row_top)
    prob_low = low(exponent / lax.optimization_barrier(jnp.sum(exponent, axis=-1, keepdims=True)))
    context = low(low_back(jnp.einsum('hqk,khd->qhd', prob_low, value_low, precision=highest))).reshape(row_count, D)
    attn_branch = low_back(matmul(context, wt_out) + bias_out)
    first = layer_norm(rows_in + attn_branch, gain_a, shift_a)
    up_pre = low_back(matmul(low(first), wt_up) + bias_up)
    act_low = low(jax.nn.gelu(up_pre, approximate=False))
    down_branch = low_back(matmul(act_low, wt_down) + bias_down)
    out = layer_norm(first + down_branch, gain_f, shift_f)
    hidden = out * keep_rows
    embedding = matmul(low(out), wt_proj) * keep_rows
    pack_sums = jnp.stack([jnp.sum(keep_rows * rows_in * rows_in), jnp.sum(keep_rows * attn_branch * attn_branch), jnp.sum(keep_rows * down_branch * down_branch), jnp.sum(keep_rows)])
    return (hidden, embedding, pack_sums)

def reference(tokens, cot_hidden, cot_embed, lengths, offsets, pack_order, w_query, b_query, w_key, b_key, w_value, b_value, w_out, b_out, gain_attn, shift_attn, w_up, b_up, w_down, b_down, gain_ffn, shift_ffn, w_proj):
    params = tuple((weight.astype(jnp.float32) for weight in (w_query, b_query, w_key, b_key, w_value, b_value, w_out, b_out, gain_attn, shift_attn, w_up, b_up, w_down, b_down, gain_ffn, shift_ffn, w_proj)))
    blocks = tokens.astype(jnp.float32).reshape(PACKS, TOK_DEV, D)
    pack_lengths = lengths[pack_order].astype(jnp.int32)
    pack_offsets = offsets[pack_order].astype(jnp.int32)

    def forward(block_in, weights):

        def one_step(pack_item):
            return one_pack(weights, pack_item[0], pack_item[1], pack_item[2])
        hidden, embedding, pack_sums = lax.map(jax.checkpoint(one_step), (block_in, pack_lengths, pack_offsets))
        return ((hidden, embedding), pack_sums)
    (hidden, embedding), pullback, pack_sums = jax.vjp(forward, blocks, params, has_aux=True)
    cotangents = (cot_hidden.astype(jnp.float32).reshape(PACKS, TOK_DEV, D), cot_embed.astype(jnp.float32).reshape(PACKS, TOK_DEV, PROJ))
    grad_blocks, grads = pullback(cotangents)
    totals = lax.optimization_barrier(jnp.sum(pack_sums, axis=0))
    rms_stats = jnp.sqrt(totals[:3] / (totals[3] * D))
    return (hidden.reshape(TOKENS, D).astype(jnp.bfloat16), embedding.reshape(TOKENS, PROJ).astype(jnp.bfloat16), grad_blocks.reshape(TOKENS, D), grads[0], grads[1], grads[2], grads[3], grads[4], grads[5], grads[6], grads[7], grads[8], grads[9], grads[10], grads[11], grads[12], grads[13], grads[14], grads[15], grads[16], rms_stats)
```

```python
import functools
import math

import jax
import jax.numpy as jnp
from jax import lax
from jax.experimental import pallas as pl
from jax.experimental.pallas import tpu as pltpu
from jax.sharding import PartitionSpec as P

MESH = pl.DeviceIdType.MESH

H = 16


eps_norm = 1e-05
neg_large = -1e30


def matmul(left, right):
    return jnp.dot(left, right, preferred_element_type=jnp.float32)


def matmul_nt(left, right):
    return lax.dot_general(
        left, right, (((1,), (1,)), ((), ())), preferred_element_type=jnp.float32
    )


def matmul_tn(left, right):
    return lax.dot_general(
        left, right, (((0,), (0,)), ((), ())), preferred_element_type=jnp.float32
    )


def exact_gelu(values):
    return jax.nn.gelu(values, approximate=False)


def norm_forward(values, gain, shift):
    row_mean = jnp.mean(values, axis=-1, keepdims=True)
    centred = values - row_mean
    inverse = lax.rsqrt(jnp.mean(centred * centred, axis=-1, keepdims=True) + eps_norm)
    normed = centred * inverse
    return (normed * gain + shift, normed, inverse)


def norm_backward(grad_in, normed, inverse, gain):
    scaled = grad_in * gain
    adjusted = (
        scaled
        - jnp.mean(scaled, axis=-1, keepdims=True)
        - normed * jnp.mean(scaled * normed, axis=-1, keepdims=True)
    )
    return (adjusted * inverse, jnp.sum(grad_in * normed, axis=0), jnp.sum(grad_in, axis=0))


def rope_tables(position, head_dim):
    half_dim = head_dim // 2
    freq_index = jnp.arange(half_dim, dtype=jnp.float32)
    frequency = jnp.exp(-math.log(10000.0) * 2.0 * freq_index / head_dim)
    angles = position[:, None] * frequency[None, :]
    return (jnp.cos(angles)[:, None, :], jnp.sin(angles)[:, None, :])


def rotate(values, cosine, sine_part):
    half_dim = values.shape[-1] // 2
    first_half = values[..., :half_dim]
    second = values[..., half_dim:]
    return jnp.concatenate(
        [first_half * cosine - second * sine_part, second * cosine + first_half * sine_part],
        axis=-1,
    )


def unrotate(grad_in, cosine, sine_part):
    half_dim = grad_in.shape[-1] // 2
    first_half = grad_in[..., :half_dim]
    second = grad_in[..., half_dim:]
    return jnp.concatenate(
        [first_half * cosine + second * sine_part, second * cosine - first_half * sine_part],
        axis=-1,
    )


def masked_scores(query_block, key_rot, allowed, score_scale):
    raw_scores = jnp.einsum(
        "qhd,khd->hqk", query_block, key_rot, preferred_element_type=jnp.float32
    )
    return jnp.where(allowed, raw_scores * score_scale, neg_large)

GATHER = (
    (16, 128, jnp.float32),
    (32, 1024, jnp.bfloat16),
    (32, 1024, jnp.bfloat16),
    (32, 1024, jnp.bfloat16),
    (32, 1024, jnp.bfloat16),
    (32, 4096, jnp.bfloat16),
    (32, 128, jnp.bfloat16),
    (128, 1024, jnp.bfloat16),
)


def device_at(z, y, x, c):
    return ((z * 2 + y) * 2 + x) * 2 + c


def wait_bytes(ref, sem):
    pltpu.make_async_copy(ref, ref, sem).wait()


def send(src, dst, sem_out, sem_in, target):
    pltpu.make_async_remote_copy(
        src_ref=src,
        dst_ref=dst,
        send_sem=sem_out,
        recv_sem=sem_in,
        device_id=(target,),
        device_id_type=MESH,
    ).start()


def gather_kernel(*refs):
    count = len(GATHER)
    src = refs[:count]
    full = refs[count : 2 * count]
    ss, rs, ls = refs[2 * count :]
    me = lax.axis_index("dp")
    z, y, x, c = me // 8, (me // 4) % 2, (me // 2) % 2, me % 2
    near_x = device_at(z, y, 1 - x, c)
    near_y = device_at(z, 1 - y, x, c)
    sibling = device_at(z, y, x, 1 - c)
    others = [(z + k) % 4 for k in (1, 2, 3)]
    barrier = pltpu.get_barrier_semaphore()
    peers = [near_x, near_y, sibling] + [device_at(zz, y, x, c) for zz in others]
    for peer in peers:
        pl.semaphore_signal(barrier, inc=1, device_id=(peer,), device_id_type=MESH)
    pl.semaphore_wait(barrier, len(peers))
    for t in range(count):
        mine = full[t].at[z, y, x, c]
        for zz in others:
            send(src[t], mine, ss.at[t, 0], rs.at[t, 0], device_at(zz, y, x, c))
        send(src[t], mine, ss.at[t, 1], rs.at[t, 1], near_x)
        send(src[t], mine, ss.at[t, 2], rs.at[t, 2], near_y)
        pltpu.make_async_copy(src[t], mine, ls.at[t]).start()

    def column(t):
        wait_bytes(full[t].at[pl.ds(0, 3), 0, 0, 0], rs.at[t, 0])
        for zz in others:
            block = full[t].at[zz, y, x, c]
            send(block, block, ss.at[t, 3], rs.at[t, 3], near_x)
            send(block, block, ss.at[t, 4], rs.at[t, 4], near_y)

    def plane(t):
        half = GATHER[t][0] // 2
        wait_bytes(full[t].at[0, 0, 0, 0], rs.at[t, 1])
        wait_bytes(full[t].at[pl.ds(0, 3), 0, 0, 0], rs.at[t, 3])
        block = full[t].at[:, y, 1 - x, c, pl.ds(0, half)]
        send(block, block, ss.at[t, 5], rs.at[t, 5], near_y)
        wait_bytes(full[t].at[0, 0, 0, 0], rs.at[t, 2])
        wait_bytes(full[t].at[pl.ds(0, 3), 0, 0, 0], rs.at[t, 4])
        block = full[t].at[:, 1 - y, x, c, pl.ds(half, half)]
        send(block, block, ss.at[t, 6], rs.at[t, 6], near_x)

    def pair(t):
        half = GATHER[t][0] // 2
        wait_bytes(full[t].at[:, 0, 0, 0, pl.ds(0, half)], rs.at[t, 5])
        wait_bytes(full[t].at[:, 0, 0, 0, pl.ds(0, half)], rs.at[t, 6])
        wait_bytes(full[t].at[0, 0, 0, 0], ls.at[t])
        block = full[t].at[:, :, :, c]
        send(block, block, ss.at[t, 7], rs.at[t, 7], sibling)

    for step in range(count + 3):
        if step < count:
            column(step)
        if 0 <= step - 1 < count:
            plane(step - 1)
        if 0 <= step - 2 < count:
            pair(step - 2)
        if 0 <= step - 3 < count:
            wait_bytes(full[step - 3].at[:, :, :, 0], rs.at[step - 3, 7])
    for t in range(count):
        half = GATHER[t][0] // 2
        one = full[t].at[0, 0, 0, 0]
        three = full[t].at[pl.ds(0, 3), 0, 0, 0]
        halves = full[t].at[:, 0, 0, 0, pl.ds(0, half)]
        for kind, ref in enumerate(
            (three, one, one, three, three, halves, halves, full[t].at[:, :, :, 0])
        ):
            wait_bytes(ref, ss.at[t, kind])


def gather_weights(pieces):
    count = len(GATHER)
    return pl.pallas_call(
        gather_kernel,
        out_shape=[jax.ShapeDtypeStruct((4, 2, 2, 2, r, k), dt) for r, k, dt in GATHER],
        in_specs=[pl.BlockSpec(memory_space=pl.ANY)] * count,
        out_specs=[pl.BlockSpec(memory_space=pl.ANY)] * count,
        scratch_shapes=[
            pltpu.SemaphoreType.DMA((count, 8)),
            pltpu.SemaphoreType.DMA((count, 8)),
            pltpu.SemaphoreType.DMA((count,)),
        ],
        compiler_params=pltpu.CompilerParams(collective_id=0, has_side_effects=True),
        name="gather_weights",
    )(*pieces)


def gather_all(weights, vectors):
    device = lax.axis_index("dp")
    lanes = jnp.arange(128, dtype=jnp.int32)[None, :] // 32 == device % 4
    rows = [jnp.where(lanes, jnp.tile(v.astype(jnp.float32), 4)[None, :], 0.0) for v in vectors[:9]]
    rows.append(vectors[9].astype(jnp.float32)[None, :])
    rows.append(jnp.zeros((6, 128), jnp.float32))
    packed = jnp.concatenate(rows, axis=0)
    out = gather_weights([packed] + list(weights))
    table = out[0].reshape(32, 16, 128)
    full_vectors = [table[:, i].reshape(8, 4, 128).sum(1).reshape(1024) for i in range(9)]
    full_vectors.append(table[:, 9].reshape(4096))
    full = [
        o.reshape(-1, o.shape[-1]) for o in out[1:]
    ]
    return full, full_vectors


def shards(
    tokens,
    cot_hidden,
    cot_embed,
    lengths,
    offsets,
    pack_order,
    w_query,
    b_query,
    w_key,
    b_key,
    w_value,
    b_value,
    w_out,
    b_out,
    gain_attn,
    shift_attn,
    w_up,
    b_up,
    w_down,
    b_down,
    gain_ffn,
    shift_ffn,
    w_proj,
):
    full, vectors = gather_all(
        (w_query, w_key, w_value, w_out, w_up, w_proj, w_down),
        (b_query, b_key, b_value, b_out, gain_attn, shift_attn, b_down, gain_ffn, shift_ffn, b_up),
    )
    wt_query, wt_key, wt_value, wt_out, wt_up, wt_proj, wt_down = full
    (
        bias_query,
        bias_key,
        bias_value,
        bias_out,
        norm_gain_a,
        norm_shift_a,
        bias_down,
        norm_gain_f,
        norm_shift_f,
        bias_up,
    ) = vectors
    row_count = tokens.shape[0]
    model_width = tokens.shape[1]
    head_count = H
    head_dim = model_width // head_count
    device = lax.axis_index("dp")
    slots = jnp.arange(pack_order.shape[0], dtype=jnp.int32)
    pack_id = jnp.sum(jnp.where(slots == device, pack_order, 0))
    length = jnp.sum(jnp.where(slots == pack_id, lengths, 0))
    offset = jnp.sum(jnp.where(slots == pack_id, offsets, 0))
    row_index = jnp.arange(row_count, dtype=jnp.int32)
    is_valid = (row_index >= offset) & (row_index < offset + length)
    keep_rows = is_valid.astype(jnp.float32)[:, None]
    cosine, sine_part = rope_tables((row_index - offset).astype(jnp.float32), head_dim)
    query_pre = matmul(tokens, wt_query) + bias_query
    key_pre = matmul(tokens, wt_key) + bias_key
    value_low = (
        (matmul(tokens, wt_value) + bias_value)
        .astype(jnp.bfloat16)
        .reshape(row_count, head_count, head_dim)
    )
    query_rot = rotate(
        query_pre.reshape(row_count, head_count, head_dim), cosine, sine_part
    ).astype(jnp.bfloat16)
    key_rot = rotate(key_pre.reshape(row_count, head_count, head_dim), cosine, sine_part).astype(
        jnp.bfloat16
    )
    score_scale = 1.0 / math.sqrt(head_dim)
    key_valid = is_valid[None, None, :]
    allowed = is_valid[None, :, None] & key_valid
    masked = masked_scores(query_rot, key_rot, allowed, score_scale)
    row_top = jnp.max(masked, axis=-1, keepdims=True)
    exponent = jnp.exp(masked - row_top)
    row_total = jnp.sum(exponent, axis=-1, keepdims=True)
    prob_low = (exponent / row_total).astype(jnp.bfloat16)
    contexts = jnp.einsum("hqk,khd->qhd", prob_low, value_low, preferred_element_type=jnp.float32)
    log_totals = row_top + jnp.log(row_total)
    context = contexts.astype(jnp.bfloat16).reshape(row_count, model_width)
    tokens_wide = tokens.astype(jnp.float32)
    attn_branch = matmul(context, wt_out) + bias_out
    first, normed_one, inverse_one = norm_forward(
        tokens_wide + attn_branch, norm_gain_a, norm_shift_a
    )
    first_low = first.astype(jnp.bfloat16)
    up_pre = matmul(first_low, wt_up) + bias_up
    act_full, gelu_pull = jax.vjp(exact_gelu, up_pre)
    act_low = act_full.astype(jnp.bfloat16)
    down_branch = matmul(act_low, wt_down) + bias_down
    out, normed_two, inverse_two = norm_forward(first + down_branch, norm_gain_f, norm_shift_f)
    out_low = out.astype(jnp.bfloat16)
    hidden = (out * keep_rows).astype(jnp.bfloat16)
    embedding = (matmul(out_low, wt_proj) * keep_rows).astype(jnp.bfloat16)
    stat_sums = lax.psum(
        (
            jnp.sum(keep_rows * tokens_wide * tokens_wide),
            jnp.sum(keep_rows * attn_branch * attn_branch),
            jnp.sum(keep_rows * down_branch * down_branch),
            jnp.sum(keep_rows),
        ),
        "dp",
    )
    rms_stats = jnp.sqrt(
        jnp.stack([stat_sums[0], stat_sums[1], stat_sums[2]]) / (stat_sums[3] * model_width)
    )
    back_query, back_key, back_value, back_out, back_up, back_down, back_proj = (
        wt_query, wt_key, wt_value, wt_out, wt_up, wt_down, wt_proj
    )
    back_gain_a = norm_gain_a
    back_gain_f = norm_gain_f
    cot_low = jnp.where(is_valid[:, None], cot_embed, jnp.zeros_like(cot_embed))
    grad_w_proj = matmul_tn(out_low, cot_low)
    grad_out = keep_rows * cot_hidden.astype(jnp.float32) + matmul_nt(cot_low, back_proj)
    grad_resid_two, grad_gain_f, grad_shift_f = norm_backward(
        grad_out, normed_two, inverse_two, back_gain_f
    )
    down_grad = grad_resid_two.astype(jnp.bfloat16)
    grad_w_down = matmul_tn(act_low, down_grad)
    grad_b_down = jnp.sum(down_grad.astype(jnp.float32), axis=0)
    up_grad = gelu_pull(matmul_nt(down_grad, back_down))[0].astype(jnp.bfloat16)
    grad_w_up = matmul_tn(first_low, up_grad)
    grad_b_up = jnp.sum(up_grad.astype(jnp.float32), axis=0)
    grad_first = grad_resid_two + matmul_nt(up_grad, back_up)
    grad_resid_one, grad_gain_a, grad_shift_a = norm_backward(
        grad_first, normed_one, inverse_one, back_gain_a
    )
    attn_grad = grad_resid_one.astype(jnp.bfloat16)
    grad_w_out = matmul_tn(context, attn_grad)
    grad_b_out = jnp.sum(attn_grad.astype(jnp.float32), axis=0)
    ctx_grad = (
        matmul_nt(attn_grad, back_out).astype(jnp.bfloat16).reshape(row_count, head_count, head_dim)
    )
    allowed = is_valid[None, :, None] & key_valid
    masked = masked_scores(query_rot, key_rot, allowed, score_scale)
    prob_full = jnp.exp(masked - log_totals)
    prob_low = prob_full.astype(jnp.bfloat16)
    prob_grad = jnp.einsum("qhd,khd->hqk", ctx_grad, value_low, preferred_element_type=jnp.float32)
    value_sum = jnp.einsum("hqk,qhd->khd", prob_low, ctx_grad, preferred_element_type=jnp.float32)
    row_dot = jnp.sum(prob_full * prob_grad, axis=-1, keepdims=True)
    score_grad = jnp.where(allowed, prob_full * (prob_grad - row_dot), 0.0).astype(jnp.bfloat16)
    query_parts = (
        jnp.einsum("hqk,khd->qhd", score_grad, key_rot, preferred_element_type=jnp.float32)
        * score_scale
    )
    key_sum = (
        jnp.einsum("hqk,qhd->khd", score_grad, query_rot, preferred_element_type=jnp.float32)
        * score_scale
    )
    query_grad = (
        unrotate(query_parts, cosine, sine_part)
        .reshape(row_count, model_width)
        .astype(jnp.bfloat16)
    )
    key_grad = (
        unrotate(key_sum, cosine, sine_part).reshape(row_count, model_width).astype(jnp.bfloat16)
    )
    value_grad = value_sum.reshape(row_count, model_width).astype(jnp.bfloat16)
    grad_w_query = matmul_tn(tokens, query_grad)
    grad_b_query = jnp.sum(query_grad.astype(jnp.float32), axis=0)
    grad_w_key = matmul_tn(tokens, key_grad)
    grad_b_key = jnp.sum(key_grad.astype(jnp.float32), axis=0)
    grad_w_value = matmul_tn(tokens, value_grad)
    grad_b_value = jnp.sum(value_grad.astype(jnp.float32), axis=0)
    grad_tokens = (
        grad_resid_one
        + matmul_nt(query_grad, back_query)
        + matmul_nt(key_grad, back_key)
        + matmul_nt(value_grad, back_value)
    )
    all_parts = (
        lax.psum_scatter(grad_w_query, "dp", scatter_dimension=0, tiled=True),
        lax.psum_scatter(grad_w_key, "dp", scatter_dimension=0, tiled=True),
        lax.psum_scatter(grad_w_value, "dp", scatter_dimension=0, tiled=True),
        lax.psum_scatter(grad_w_out, "dp", scatter_dimension=0, tiled=True),
        lax.psum_scatter(grad_b_query, "dp", scatter_dimension=0, tiled=True),
        lax.psum_scatter(grad_b_key, "dp", scatter_dimension=0, tiled=True),
        lax.psum_scatter(grad_b_value, "dp", scatter_dimension=0, tiled=True),
        lax.psum_scatter(grad_b_out, "dp", scatter_dimension=0, tiled=True),
        lax.psum_scatter(grad_gain_a, "dp", scatter_dimension=0, tiled=True),
        lax.psum_scatter(grad_shift_a, "dp", scatter_dimension=0, tiled=True),
        lax.psum_scatter(grad_w_up, "dp", scatter_dimension=0, tiled=True),
        lax.psum_scatter(grad_w_down, "dp", scatter_dimension=0, tiled=True),
        lax.psum_scatter(grad_w_proj, "dp", scatter_dimension=0, tiled=True),
        lax.psum_scatter(grad_b_up, "dp", scatter_dimension=0, tiled=True),
        lax.psum_scatter(grad_b_down, "dp", scatter_dimension=0, tiled=True),
        lax.psum_scatter(grad_gain_f, "dp", scatter_dimension=0, tiled=True),
        lax.psum_scatter(grad_shift_f, "dp", scatter_dimension=0, tiled=True),
    )
    attn_parts = all_parts[:10]
    ffn_parts = all_parts[10:]
    return (
        hidden,
        embedding,
        grad_tokens,
        attn_parts[0],
        attn_parts[4],
        attn_parts[1],
        attn_parts[5],
        attn_parts[2],
        attn_parts[6],
        attn_parts[3],
        attn_parts[7],
        attn_parts[8],
        attn_parts[9],
        ffn_parts[0],
        ffn_parts[3],
        ffn_parts[1],
        ffn_parts[4],
        ffn_parts[5],
        ffn_parts[6],
        ffn_parts[2],
        rms_stats,
    )


def shards_any(
    tokens,
    cot_hidden,
    cot_embed,
    lengths,
    offsets,
    pack_order,
    w_query,
    b_query,
    w_key,
    b_key,
    w_value,
    b_value,
    w_out,
    b_out,
    gain_attn,
    shift_attn,
    w_up,
    b_up,
    w_down,
    b_down,
    gain_ffn,
    shift_ffn,
    w_proj,
):
    gathered = (
        lax.all_gather(w_query, "dp", axis=0, tiled=True),
        lax.all_gather(w_key, "dp", axis=0, tiled=True),
        lax.all_gather(w_value, "dp", axis=0, tiled=True),
        lax.all_gather(w_out, "dp", axis=0, tiled=True),
        lax.all_gather(w_up, "dp", axis=0, tiled=True),
        lax.all_gather(w_down, "dp", axis=0, tiled=True),
        lax.all_gather(w_proj, "dp", axis=0, tiled=True),
        lax.all_gather(b_query, "dp", axis=0, tiled=True),
        lax.all_gather(b_key, "dp", axis=0, tiled=True),
        lax.all_gather(b_value, "dp", axis=0, tiled=True),
        lax.all_gather(b_out, "dp", axis=0, tiled=True),
        lax.all_gather(gain_attn, "dp", axis=0, tiled=True),
        lax.all_gather(shift_attn, "dp", axis=0, tiled=True),
        lax.all_gather(b_up, "dp", axis=0, tiled=True),
        lax.all_gather(b_down, "dp", axis=0, tiled=True),
        lax.all_gather(gain_ffn, "dp", axis=0, tiled=True),
        lax.all_gather(shift_ffn, "dp", axis=0, tiled=True),
    )
    wt_query, wt_key, wt_value, wt_out, wt_up, wt_down, wt_proj = gathered[:7]
    vectors = [piece.astype(jnp.float32) for piece in gathered[7:]]
    (
        bias_query,
        bias_key,
        bias_value,
        bias_out,
        norm_gain_a,
        norm_shift_a,
        bias_up,
        bias_down,
        norm_gain_f,
        norm_shift_f,
    ) = vectors
    row_count = tokens.shape[0]
    model_width = tokens.shape[1]
    head_count = H
    head_dim = model_width // head_count
    device = lax.axis_index("dp")
    slots = jnp.arange(pack_order.shape[0], dtype=jnp.int32)
    pack_id = jnp.sum(jnp.where(slots == device, pack_order, 0))
    length = jnp.sum(jnp.where(slots == pack_id, lengths, 0))
    offset = jnp.sum(jnp.where(slots == pack_id, offsets, 0))
    row_index = jnp.arange(row_count, dtype=jnp.int32)
    is_valid = (row_index >= offset) & (row_index < offset + length)
    keep_rows = is_valid.astype(jnp.float32)[:, None]
    cosine, sine_part = rope_tables((row_index - offset).astype(jnp.float32), head_dim)
    query_pre = matmul(tokens, wt_query) + bias_query
    key_pre = matmul(tokens, wt_key) + bias_key
    value_low = (
        (matmul(tokens, wt_value) + bias_value)
        .astype(jnp.bfloat16)
        .reshape(row_count, head_count, head_dim)
    )
    query_rot = rotate(
        query_pre.reshape(row_count, head_count, head_dim), cosine, sine_part
    ).astype(jnp.bfloat16)
    key_rot = rotate(key_pre.reshape(row_count, head_count, head_dim), cosine, sine_part).astype(
        jnp.bfloat16
    )
    score_scale = 1.0 / math.sqrt(head_dim)
    key_valid = is_valid[None, None, :]
    allowed = is_valid[None, :, None] & key_valid
    masked = masked_scores(query_rot, key_rot, allowed, score_scale)
    row_top = jnp.max(masked, axis=-1, keepdims=True)
    exponent = jnp.exp(masked - row_top)
    row_total = jnp.sum(exponent, axis=-1, keepdims=True)
    prob_low = (exponent / row_total).astype(jnp.bfloat16)
    contexts = jnp.einsum("hqk,khd->qhd", prob_low, value_low, preferred_element_type=jnp.float32)
    log_totals = row_top + jnp.log(row_total)
    context = contexts.astype(jnp.bfloat16).reshape(row_count, model_width)
    tokens_wide = tokens.astype(jnp.float32)
    attn_branch = matmul(context, wt_out) + bias_out
    first, normed_one, inverse_one = norm_forward(
        tokens_wide + attn_branch, norm_gain_a, norm_shift_a
    )
    first_low = first.astype(jnp.bfloat16)
    up_pre = matmul(first_low, wt_up) + bias_up
    act_full, gelu_pull = jax.vjp(exact_gelu, up_pre)
    act_low = act_full.astype(jnp.bfloat16)
    down_branch = matmul(act_low, wt_down) + bias_down
    out, normed_two, inverse_two = norm_forward(first + down_branch, norm_gain_f, norm_shift_f)
    out_low = out.astype(jnp.bfloat16)
    hidden = (out * keep_rows).astype(jnp.bfloat16)
    embedding = (matmul(out_low, wt_proj) * keep_rows).astype(jnp.bfloat16)
    stat_sums = lax.psum(
        (
            jnp.sum(keep_rows * tokens_wide * tokens_wide),
            jnp.sum(keep_rows * attn_branch * attn_branch),
            jnp.sum(keep_rows * down_branch * down_branch),
            jnp.sum(keep_rows),
        ),
        "dp",
    )
    rms_stats = jnp.sqrt(
        jnp.stack([stat_sums[0], stat_sums[1], stat_sums[2]]) / (stat_sums[3] * model_width)
    )
    backward_set = (
        lax.all_gather(w_query, "dp", axis=0, tiled=True),
        lax.all_gather(w_key, "dp", axis=0, tiled=True),
        lax.all_gather(w_value, "dp", axis=0, tiled=True),
        lax.all_gather(w_out, "dp", axis=0, tiled=True),
        lax.all_gather(w_up, "dp", axis=0, tiled=True),
        lax.all_gather(w_down, "dp", axis=0, tiled=True),
        lax.all_gather(w_proj, "dp", axis=0, tiled=True),
        lax.all_gather(b_query, "dp", axis=0, tiled=True),
        lax.all_gather(b_key, "dp", axis=0, tiled=True),
        lax.all_gather(b_value, "dp", axis=0, tiled=True),
        lax.all_gather(b_out, "dp", axis=0, tiled=True),
        lax.all_gather(gain_attn, "dp", axis=0, tiled=True),
        lax.all_gather(shift_attn, "dp", axis=0, tiled=True),
        lax.all_gather(b_up, "dp", axis=0, tiled=True),
        lax.all_gather(b_down, "dp", axis=0, tiled=True),
        lax.all_gather(gain_ffn, "dp", axis=0, tiled=True),
        lax.all_gather(shift_ffn, "dp", axis=0, tiled=True),
    )
    back_query, back_key, back_value, back_out, back_up, back_down, back_proj = backward_set[:7]
    back_gain_a = backward_set[11].astype(jnp.float32)
    back_gain_f = backward_set[15].astype(jnp.float32)
    cot_low = jnp.where(is_valid[:, None], cot_embed, jnp.zeros_like(cot_embed))
    grad_w_proj = matmul_tn(out_low, cot_low)
    grad_out = keep_rows * cot_hidden.astype(jnp.float32) + matmul_nt(cot_low, back_proj)
    grad_resid_two, grad_gain_f, grad_shift_f = norm_backward(
        grad_out, normed_two, inverse_two, back_gain_f
    )
    down_grad = grad_resid_two.astype(jnp.bfloat16)
    grad_w_down = matmul_tn(act_low, down_grad)
    grad_b_down = jnp.sum(down_grad.astype(jnp.float32), axis=0)
    up_grad = gelu_pull(matmul_nt(down_grad, back_down))[0].astype(jnp.bfloat16)
    grad_w_up = matmul_tn(first_low, up_grad)
    grad_b_up = jnp.sum(up_grad.astype(jnp.float32), axis=0)
    grad_first = grad_resid_two + matmul_nt(up_grad, back_up)
    grad_resid_one, grad_gain_a, grad_shift_a = norm_backward(
        grad_first, normed_one, inverse_one, back_gain_a
    )
    attn_grad = grad_resid_one.astype(jnp.bfloat16)
    grad_w_out = matmul_tn(context, attn_grad)
    grad_b_out = jnp.sum(attn_grad.astype(jnp.float32), axis=0)
    ctx_grad = (
        matmul_nt(attn_grad, back_out).astype(jnp.bfloat16).reshape(row_count, head_count, head_dim)
    )
    allowed = is_valid[None, :, None] & key_valid
    masked = masked_scores(query_rot, key_rot, allowed, score_scale)
    prob_full = jnp.exp(masked - log_totals)
    prob_low = prob_full.astype(jnp.bfloat16)
    prob_grad = jnp.einsum("qhd,khd->hqk", ctx_grad, value_low, preferred_element_type=jnp.float32)
    value_sum = jnp.einsum("hqk,qhd->khd", prob_low, ctx_grad, preferred_element_type=jnp.float32)
    row_dot = jnp.sum(prob_full * prob_grad, axis=-1, keepdims=True)
    score_grad = jnp.where(allowed, prob_full * (prob_grad - row_dot), 0.0).astype(jnp.bfloat16)
    query_parts = (
        jnp.einsum("hqk,khd->qhd", score_grad, key_rot, preferred_element_type=jnp.float32)
        * score_scale
    )
    key_sum = (
        jnp.einsum("hqk,qhd->khd", score_grad, query_rot, preferred_element_type=jnp.float32)
        * score_scale
    )
    query_grad = (
        unrotate(query_parts, cosine, sine_part)
        .reshape(row_count, model_width)
        .astype(jnp.bfloat16)
    )
    key_grad = (
        unrotate(key_sum, cosine, sine_part).reshape(row_count, model_width).astype(jnp.bfloat16)
    )
    value_grad = value_sum.reshape(row_count, model_width).astype(jnp.bfloat16)
    grad_w_query = matmul_tn(tokens, query_grad)
    grad_b_query = jnp.sum(query_grad.astype(jnp.float32), axis=0)
    grad_w_key = matmul_tn(tokens, key_grad)
    grad_b_key = jnp.sum(key_grad.astype(jnp.float32), axis=0)
    grad_w_value = matmul_tn(tokens, value_grad)
    grad_b_value = jnp.sum(value_grad.astype(jnp.float32), axis=0)
    grad_tokens = (
        grad_resid_one
        + matmul_nt(query_grad, back_query)
        + matmul_nt(key_grad, back_key)
        + matmul_nt(value_grad, back_value)
    )
    all_parts = (
        lax.psum_scatter(grad_w_query, "dp", scatter_dimension=0, tiled=True),
        lax.psum_scatter(grad_w_key, "dp", scatter_dimension=0, tiled=True),
        lax.psum_scatter(grad_w_value, "dp", scatter_dimension=0, tiled=True),
        lax.psum_scatter(grad_w_out, "dp", scatter_dimension=0, tiled=True),
        lax.psum_scatter(grad_b_query, "dp", scatter_dimension=0, tiled=True),
        lax.psum_scatter(grad_b_key, "dp", scatter_dimension=0, tiled=True),
        lax.psum_scatter(grad_b_value, "dp", scatter_dimension=0, tiled=True),
        lax.psum_scatter(grad_b_out, "dp", scatter_dimension=0, tiled=True),
        lax.psum_scatter(grad_gain_a, "dp", scatter_dimension=0, tiled=True),
        lax.psum_scatter(grad_shift_a, "dp", scatter_dimension=0, tiled=True),
        lax.psum_scatter(grad_w_up, "dp", scatter_dimension=0, tiled=True),
        lax.psum_scatter(grad_w_down, "dp", scatter_dimension=0, tiled=True),
        lax.psum_scatter(grad_w_proj, "dp", scatter_dimension=0, tiled=True),
        lax.psum_scatter(grad_b_up, "dp", scatter_dimension=0, tiled=True),
        lax.psum_scatter(grad_b_down, "dp", scatter_dimension=0, tiled=True),
        lax.psum_scatter(grad_gain_f, "dp", scatter_dimension=0, tiled=True),
        lax.psum_scatter(grad_shift_f, "dp", scatter_dimension=0, tiled=True),
    )
    attn_parts = all_parts[:10]
    ffn_parts = all_parts[10:]
    return (
        hidden,
        embedding,
        grad_tokens,
        attn_parts[0],
        attn_parts[4],
        attn_parts[1],
        attn_parts[5],
        attn_parts[2],
        attn_parts[6],
        attn_parts[3],
        attn_parts[7],
        attn_parts[8],
        attn_parts[9],
        ffn_parts[0],
        ffn_parts[3],
        ffn_parts[1],
        ffn_parts[4],
        ffn_parts[5],
        ffn_parts[6],
        ffn_parts[2],
        rms_stats,
    )


def solution(mesh):
    fast = mesh.shape["dp"] == 32
    placed = (
        P("dp", None),
        P("dp", None),
        P("dp", None),
        P(),
        P(),
        P(),
        P("dp", None),
        P("dp"),
        P("dp", None),
        P("dp"),
        P("dp", None),
        P("dp"),
        P("dp", None),
        P("dp"),
        P("dp"),
        P("dp"),
        P("dp", None),
        P("dp"),
        P("dp", None),
        P("dp"),
        P("dp"),
        P("dp"),
        P("dp", None),
    )
    return jax.shard_map(
        shards if fast else shards_any,
        mesh=mesh,
        in_specs=placed,
        out_specs=(
            P("dp", None),
            P("dp", None),
            P("dp", None),
            P("dp", None),
            P("dp"),
            P("dp", None),
            P("dp"),
            P("dp", None),
            P("dp"),
            P("dp", None),
            P("dp"),
            P("dp"),
            P("dp"),
            P("dp", None),
            P("dp"),
            P("dp", None),
            P("dp"),
            P("dp"),
            P("dp"),
            P("dp", None),
            P(),
        ),
        check_vma=False,
    )
```

```python
import functools
import math

import jax
import jax.numpy as jnp
from jax import lax
from jax.experimental import pallas as pl
from jax.experimental.pallas import tpu as pltpu
from jax.sharding import PartitionSpec as P

MESH = pl.DeviceIdType.MESH

H = 16


eps_norm = 1e-05
neg_large = -1e30


def matmul(left, right):
    return jnp.dot(left, right, preferred_element_type=jnp.float32)


def matmul_nt(left, right):
    return lax.dot_general(
        left, right, (((1,), (1,)), ((), ())), preferred_element_type=jnp.float32
    )


def matmul_tn(left, right):
    return lax.dot_general(
        left, right, (((0,), (0,)), ((), ())), preferred_element_type=jnp.float32
    )


def exact_gelu(values):
    return jax.nn.gelu(values, approximate=False)


def norm_forward(values, gain, shift):
    row_mean = jnp.mean(values, axis=-1, keepdims=True)
    centred = values - row_mean
    inverse = lax.rsqrt(jnp.mean(centred * centred, axis=-1, keepdims=True) + eps_norm)
    normed = centred * inverse
    return (normed * gain + shift, normed, inverse)


def norm_backward(grad_in, normed, inverse, gain):
    scaled = grad_in * gain
    adjusted = (
        scaled
        - jnp.mean(scaled, axis=-1, keepdims=True)
        - normed * jnp.mean(scaled * normed, axis=-1, keepdims=True)
    )
    return (adjusted * inverse, jnp.sum(grad_in * normed, axis=0), jnp.sum(grad_in, axis=0))


def rope_tables(position, head_dim):
    half_dim = head_dim // 2
    freq_index = jnp.arange(half_dim, dtype=jnp.float32)
    frequency = jnp.exp(-math.log(10000.0) * 2.0 * freq_index / head_dim)
    angles = position[:, None] * frequency[None, :]
    return (jnp.cos(angles)[:, None, :], jnp.sin(angles)[:, None, :])


def rotate(values, cosine, sine_part):
    half_dim = values.shape[-1] // 2
    first_half = values[..., :half_dim]
    second = values[..., half_dim:]
    return jnp.concatenate(
        [first_half * cosine - second * sine_part, second * cosine + first_half * sine_part],
        axis=-1,
    )


def unrotate(grad_in, cosine, sine_part):
    half_dim = grad_in.shape[-1] // 2
    first_half = grad_in[..., :half_dim]
    second = grad_in[..., half_dim:]
    return jnp.concatenate(
        [first_half * cosine + second * sine_part, second * cosine - first_half * sine_part],
        axis=-1,
    )


def masked_scores(query_block, key_rot, allowed, score_scale):
    raw_scores = jnp.einsum(
        "qhd,khd->hqk", query_block, key_rot, preferred_element_type=jnp.float32
    )
    return jnp.where(allowed, raw_scores * score_scale, neg_large)

GATHER = (
    (16, 128, jnp.float32),
    (32, 1024, jnp.bfloat16),
    (32, 1024, jnp.bfloat16),
    (32, 1024, jnp.bfloat16),
    (32, 1024, jnp.bfloat16),
    (32, 4096, jnp.bfloat16),
    (32, 128, jnp.bfloat16),
    (128, 1024, jnp.bfloat16),
)


def device_at(z, y, x, c):
    return ((z * 2 + y) * 2 + x) * 2 + c


def wait_bytes(ref, sem):
    pltpu.make_async_copy(ref, ref, sem).wait()


def send(src, dst, sem_out, sem_in, target):
    pltpu.make_async_remote_copy(
        src_ref=src,
        dst_ref=dst,
        send_sem=sem_out,
        recv_sem=sem_in,
        device_id=(target,),
        device_id_type=MESH,
    ).start()


def gather_kernel(*refs):
    count = len(GATHER)
    src = refs[:count]
    full = refs[count : 2 * count]
    ss, rs, ls = refs[2 * count :]
    me = lax.axis_index("dp")
    z, y, x, c = me // 8, (me // 4) % 2, (me // 2) % 2, me % 2
    near_x = device_at(z, y, 1 - x, c)
    near_y = device_at(z, 1 - y, x, c)
    sibling = device_at(z, y, x, 1 - c)
    others = [(z + k) % 4 for k in (1, 2, 3)]
    barrier = pltpu.get_barrier_semaphore()
    peers = [near_x, near_y, sibling] + [device_at(zz, y, x, c) for zz in others]
    for peer in peers:
        pl.semaphore_signal(barrier, inc=1, device_id=(peer,), device_id_type=MESH)
    pl.semaphore_wait(barrier, len(peers))
    for t in range(count):
        mine = full[t].at[z, y, x, c]
        for zz in others:
            send(src[t], mine, ss.at[t, 0], rs.at[t, 0], device_at(zz, y, x, c))
        send(src[t], mine, ss.at[t, 1], rs.at[t, 1], near_x)
        send(src[t], mine, ss.at[t, 2], rs.at[t, 2], near_y)
        pltpu.make_async_copy(src[t], mine, ls.at[t]).start()

    def column(t):
        wait_bytes(full[t].at[pl.ds(0, 3), 0, 0, 0], rs.at[t, 0])
        for zz in others:
            block = full[t].at[zz, y, x, c]
            send(block, block, ss.at[t, 3], rs.at[t, 3], near_x)
            send(block, block, ss.at[t, 4], rs.at[t, 4], near_y)

    def plane(t):
        half = GATHER[t][0] // 2
        wait_bytes(full[t].at[0, 0, 0, 0], rs.at[t, 1])
        wait_bytes(full[t].at[pl.ds(0, 3), 0, 0, 0], rs.at[t, 3])
        block = full[t].at[:, y, 1 - x, c, pl.ds(0, half)]
        send(block, block, ss.at[t, 5], rs.at[t, 5], near_y)
        wait_bytes(full[t].at[0, 0, 0, 0], rs.at[t, 2])
        wait_bytes(full[t].at[pl.ds(0, 3), 0, 0, 0], rs.at[t, 4])
        block = full[t].at[:, 1 - y, x, c, pl.ds(half, half)]
        send(block, block, ss.at[t, 6], rs.at[t, 6], near_x)

    def pair(t):
        half = GATHER[t][0] // 2
        wait_bytes(full[t].at[:, 0, 0, 0, pl.ds(0, half)], rs.at[t, 5])
        wait_bytes(full[t].at[:, 0, 0, 0, pl.ds(0, half)], rs.at[t, 6])
        wait_bytes(full[t].at[0, 0, 0, 0], ls.at[t])
        block = full[t].at[:, :, :, c]
        send(block, block, ss.at[t, 7], rs.at[t, 7], sibling)

    for step in range(count + 3):
        if step < count:
            column(step)
        if 0 <= step - 1 < count:
            plane(step - 1)
        if 0 <= step - 2 < count:
            pair(step - 2)
        if 0 <= step - 3 < count:
            wait_bytes(full[step - 3].at[:, :, :, 0], rs.at[step - 3, 7])
    for t in range(count):
        half = GATHER[t][0] // 2
        one = full[t].at[0, 0, 0, 0]
        three = full[t].at[pl.ds(0, 3), 0, 0, 0]
        halves = full[t].at[:, 0, 0, 0, pl.ds(0, half)]
        for kind, ref in enumerate(
            (three, one, one, three, three, halves, halves, full[t].at[:, :, :, 0])
        ):
            wait_bytes(ref, ss.at[t, kind])


def gather_weights(pieces):
    count = len(GATHER)
    return pl.pallas_call(
        gather_kernel,
        out_shape=[jax.ShapeDtypeStruct((4, 2, 2, 2, r, k), dt) for r, k, dt in GATHER],
        in_specs=[pl.BlockSpec(memory_space=pl.ANY)] * count,
        out_specs=[pl.BlockSpec(memory_space=pl.ANY)] * count,
        scratch_shapes=[
            pltpu.SemaphoreType.DMA((count, 8)),
            pltpu.SemaphoreType.DMA((count, 8)),
            pltpu.SemaphoreType.DMA((count,)),
        ],
        compiler_params=pltpu.CompilerParams(collective_id=0, has_side_effects=True),
        name="gather_weights",
    )(*pieces)


def gather_all(weights, vectors):
    device = lax.axis_index("dp")
    lanes = jnp.arange(128, dtype=jnp.int32)[None, :] // 32 == device % 4
    rows = [jnp.where(lanes, jnp.tile(v.astype(jnp.float32), 4)[None, :], 0.0) for v in vectors[:9]]
    rows.append(vectors[9].astype(jnp.float32)[None, :])
    rows.append(jnp.zeros((6, 128), jnp.float32))
    packed = jnp.concatenate(rows, axis=0)
    out = gather_weights([packed] + list(weights))
    table = out[0].reshape(32, 16, 128)
    full_vectors = [table[:, i].reshape(8, 4, 128).sum(1).reshape(1024) for i in range(9)]
    full_vectors.append(table[:, 9].reshape(4096))
    full = [
        o.reshape(-1, o.shape[-1]) for o in out[1:]
    ]
    return full, full_vectors


REDUCE = (
    (32, 128, jnp.bfloat16),
    (128, 1024, jnp.bfloat16),
    (32, 4096, jnp.bfloat16),
    (32, 1024, jnp.bfloat16),
    (32, 1024, jnp.bfloat16),
    (32, 1024, jnp.bfloat16),
    (32, 1024, jnp.bfloat16),
    (16, 128, jnp.float32),
)
PIECES = (
    ((0, 0, 128),)
    + tuple((1, 256 * k, 256) for k in range(4))
    + tuple((2, 1024 * k, 1024) for k in range(4))
    + ((3, 0, 1024), (4, 0, 1024), (5, 0, 1024), (6, 0, 1024), (7, 0, 128))
)


def piece_shape(t):
    tensor, _, width = PIECES[t]
    rows, _, dtype = REDUCE[tensor]
    return rows, width, dtype


def reduce_kernel(*refs):
    tensors, count = len(REDUCE), len(PIECES)
    terms = refs[:tensors]
    outs = refs[tensors : 2 * tensors]
    rest = refs[2 * tensors :]
    held, pair, diag, from_x, from_y = (rest[k * count : (k + 1) * count] for k in range(5))
    ss, rs, ls = rest[5 * count :]
    me = lax.axis_index("dp")
    z, y, x, c = me // 8, (me // 4) % 2, (me // 2) % 2, me % 2
    near_x = device_at(z, y, 1 - x, c)
    near_y = device_at(z, 1 - y, x, c)
    sibling = device_at(z, y, x, 1 - c)
    others = [(z + k) % 4 for k in (1, 2, 3)]
    barrier = pltpu.get_barrier_semaphore()
    peers = [near_x, near_y, sibling] + [device_at(zz, y, x, c) for zz in others]
    for peer in peers:
        pl.semaphore_signal(barrier, inc=1, device_id=(peer,), device_id_type=MESH)
    pl.semaphore_wait(barrier, len(peers))

    def view(t, parity):
        tensor, first, width = PIECES[t]
        return terms[tensor].at[:, :, :, parity, :, pl.ds(first, width)]

    for t in range(count):
        send(view(t, 1 - c), pair[t], ss.at[t, 0], rs.at[t, 0], sibling)
        pltpu.make_async_copy(view(t, c), held[t], ls.at[t, 0]).start()

    def add_pair(t):
        rows = piece_shape(t)[0]
        half = rows // 2
        h = held[t]
        wait_bytes(h, ls.at[t, 0])
        wait_bytes(pair[t], rs.at[t, 0])

        @pl.loop(0, 16)
        def _(i):
            zz, yy, xx = i // 4, (i // 2) % 2, i % 2
            for r in range(0, rows, min(rows, 32)):
                part = slice(r, r + min(rows, 32))
                h[zz, yy, xx, part, :] = h[zz, yy, xx, part, :] + pair[t][zz, yy, xx, part, :]

        low, high = pl.ds(0, half), pl.ds(half, half)
        send(h.at[:, 1 - y, 1 - x, low], diag[t].at[0], ss.at[t, 1], rs.at[t, 1], near_x)
        send(h.at[:, 1 - y, 1 - x, high], diag[t].at[1], ss.at[t, 2], rs.at[t, 2], near_y)
        send(h.at[:, y, 1 - x, low], from_x[t].at[:, low], ss.at[t, 3], rs.at[t, 3], near_x)
        send(h.at[:, 1 - y, x, high], from_y[t].at[:, high], ss.at[t, 4], rs.at[t, 4], near_y)

    def add_diagonal(t):
        rows = piece_shape(t)[0]
        half = rows // 2
        h = held[t]
        low, high = pl.ds(0, half), pl.ds(half, half)
        wait_bytes(diag[t].at[0], rs.at[t, 1])

        @pl.loop(0, 4)
        def _(i):
            h[i, 1 - y, x, 0:half, :] = h[i, 1 - y, x, 0:half, :] + diag[t][0, i]

        send(h.at[:, 1 - y, x, low], from_y[t].at[:, low], ss.at[t, 6], rs.at[t, 6], near_y)
        wait_bytes(diag[t].at[1], rs.at[t, 2])

        @pl.loop(0, 4)
        def _(i):
            h[i, y, 1 - x, half:rows, :] = h[i, y, 1 - x, half:rows, :] + diag[t][1, i]

        send(h.at[:, y, 1 - x, high], from_x[t].at[:, high], ss.at[t, 5], rs.at[t, 5], near_x)

    def add_plane(t):
        tensor, first, width = PIECES[t]
        rows = piece_shape(t)[0]
        half = rows // 2
        h = held[t]
        low, high = pl.ds(0, half), pl.ds(half, half)
        wait_bytes(from_x[t].at[:, low], rs.at[t, 3])
        wait_bytes(from_x[t].at[:, high], rs.at[t, 5])
        wait_bytes(from_y[t].at[:, high], rs.at[t, 4])
        wait_bytes(from_y[t].at[:, low], rs.at[t, 6])

        @pl.loop(0, 4)
        def _(i):
            for r in range(0, rows, min(rows, 32)):
                part = slice(r, r + min(rows, 32))
                h[i, y, x, part, :] = h[i, y, x, part, :] + from_x[t][i, part, :] + from_y[t][i, part, :]

        slot = outs[tensor].at[z, :, pl.ds(first, width)]
        for zz in others:
            send(h.at[zz, y, x], slot, ss.at[t, 7], rs.at[t, 7], device_at(zz, y, x, c))
        pltpu.make_async_copy(h.at[z, y, x], slot, ls.at[t, 1]).start()

    def finish(t):
        tensor, first, width = PIECES[t]
        half = piece_shape(t)[0] // 2
        three = outs[tensor].at[pl.ds(0, 3), :, pl.ds(first, width)]
        wait_bytes(three, rs.at[t, 7])
        wait_bytes(outs[tensor].at[0, :, pl.ds(first, width)], ls.at[t, 1])
        wait_bytes(pair[t], ss.at[t, 0])
        wait_bytes(diag[t].at[0], ss.at[t, 1])
        wait_bytes(diag[t].at[1], ss.at[t, 2])
        for kind in (3, 4, 5, 6):
            wait_bytes(from_x[t].at[:, pl.ds(0, half)], ss.at[t, kind])
        wait_bytes(three, ss.at[t, 7])

    for step in range(count + 3):
        if step < count:
            add_pair(step)
        if 0 <= step - 1 < count:
            add_diagonal(step - 1)
        if 0 <= step - 2 < count:
            add_plane(step - 2)
        if 0 <= step - 3 < count:
            finish(step - 3)


def reduce_terms(terms):
    tensors, count = len(REDUCE), len(PIECES)
    scratch = []
    for lead in ((4, 2, 2), (4, 2, 2), (2, 4), (4,), (4,)):
        for t in range(count):
            rows, width, dtype = piece_shape(t)
            scratch.append(pltpu.VMEM(lead + (rows // 2 if lead == (2, 4) else rows, width), dtype))
    return pl.pallas_call(
        reduce_kernel,
        out_shape=[jax.ShapeDtypeStruct((4, r, k), dt) for r, k, dt in REDUCE],
        in_specs=[pl.BlockSpec(memory_space=pl.ANY)] * tensors,
        out_specs=[pl.BlockSpec(memory_space=pl.ANY)] * tensors,
        scratch_shapes=scratch
        + [
            pltpu.SemaphoreType.DMA((count, 8)),
            pltpu.SemaphoreType.DMA((count, 8)),
            pltpu.SemaphoreType.DMA((count, 2)),
        ],
        compiler_params=pltpu.CompilerParams(
            collective_id=1, has_side_effects=True, vmem_limit_bytes=56 * 2**20
        ),
        name="reduce_terms",
    )(*terms)


def reduce_all(weights, vectors, stats):
    device = lax.axis_index("dp")
    terms = [
        w.astype(jnp.bfloat16).reshape(4, 2, 2, 2, w.shape[0] // 32, w.shape[1]) for w in weights
    ]
    rows = [
        jnp.broadcast_to(v.reshape(8, 1, 128), (8, 4, 128)).reshape(32, 128) for v in vectors[:9]
    ]
    rows.append(vectors[9].reshape(32, 128))
    rows.append(jnp.broadcast_to(jnp.pad(jnp.stack(stats), (0, 124))[None, :], (32, 128)))
    table = jnp.pad(jnp.stack(rows, axis=1), ((0, 0), (0, 5), (0, 0)))
    terms.append(table.reshape(4, 2, 2, 2, 16, 128))
    outs = [jnp.sum(o.astype(jnp.float32), axis=0) for o in reduce_terms(terms)]
    table = outs[7]
    lanes = (device % 4) * 32
    own = lax.dynamic_slice(table, (0, lanes), (9, 32))
    return outs[:7], [own[i] for i in range(9)] + [table[9]], table[10, :4]


def shards(
    tokens,
    cot_hidden,
    cot_embed,
    lengths,
    offsets,
    pack_order,
    w_query,
    b_query,
    w_key,
    b_key,
    w_value,
    b_value,
    w_out,
    b_out,
    gain_attn,
    shift_attn,
    w_up,
    b_up,
    w_down,
    b_down,
    gain_ffn,
    shift_ffn,
    w_proj,
):
    full, vectors = gather_all(
        (w_query, w_key, w_value, w_out, w_up, w_proj, w_down),
        (b_query, b_key, b_value, b_out, gain_attn, shift_attn, b_down, gain_ffn, shift_ffn, b_up),
    )
    wt_query, wt_key, wt_value, wt_out, wt_up, wt_proj, wt_down = full
    (
        bias_query,
        bias_key,
        bias_value,
        bias_out,
        norm_gain_a,
        norm_shift_a,
        bias_down,
        norm_gain_f,
        norm_shift_f,
        bias_up,
    ) = vectors
    row_count = tokens.shape[0]
    model_width = tokens.shape[1]
    head_count = H
    head_dim = model_width // head_count
    device = lax.axis_index("dp")
    slots = jnp.arange(pack_order.shape[0], dtype=jnp.int32)
    pack_id = jnp.sum(jnp.where(slots == device, pack_order, 0))
    length = jnp.sum(jnp.where(slots == pack_id, lengths, 0))
    offset = jnp.sum(jnp.where(slots == pack_id, offsets, 0))
    row_index = jnp.arange(row_count, dtype=jnp.int32)
    is_valid = (row_index >= offset) & (row_index < offset + length)
    keep_rows = is_valid.astype(jnp.float32)[:, None]
    cosine, sine_part = rope_tables((row_index - offset).astype(jnp.float32), head_dim)
    query_pre = matmul(tokens, wt_query) + bias_query
    key_pre = matmul(tokens, wt_key) + bias_key
    value_low = (
        (matmul(tokens, wt_value) + bias_value)
        .astype(jnp.bfloat16)
        .reshape(row_count, head_count, head_dim)
    )
    query_rot = rotate(
        query_pre.reshape(row_count, head_count, head_dim), cosine, sine_part
    ).astype(jnp.bfloat16)
    key_rot = rotate(key_pre.reshape(row_count, head_count, head_dim), cosine, sine_part).astype(
        jnp.bfloat16
    )
    score_scale = 1.0 / math.sqrt(head_dim)
    key_valid = is_valid[None, None, :]
    allowed = is_valid[None, :, None] & key_valid
    masked = masked_scores(query_rot, key_rot, allowed, score_scale)
    row_top = jnp.max(masked, axis=-1, keepdims=True)
    exponent = jnp.exp(masked - row_top)
    row_total = jnp.sum(exponent, axis=-1, keepdims=True)
    prob_low = (exponent / row_total).astype(jnp.bfloat16)
    contexts = jnp.einsum("hqk,khd->qhd", prob_low, value_low, preferred_element_type=jnp.float32)
    log_totals = row_top + jnp.log(row_total)
    context = contexts.astype(jnp.bfloat16).reshape(row_count, model_width)
    tokens_wide = tokens.astype(jnp.float32)
    attn_branch = matmul(context, wt_out) + bias_out
    first, normed_one, inverse_one = norm_forward(
        tokens_wide + attn_branch, norm_gain_a, norm_shift_a
    )
    first_low = first.astype(jnp.bfloat16)
    up_pre = matmul(first_low, wt_up) + bias_up
    act_full, gelu_pull = jax.vjp(exact_gelu, up_pre)
    act_low = act_full.astype(jnp.bfloat16)
    down_branch = matmul(act_low, wt_down) + bias_down
    out, normed_two, inverse_two = norm_forward(first + down_branch, norm_gain_f, norm_shift_f)
    out_low = out.astype(jnp.bfloat16)
    hidden = (out * keep_rows).astype(jnp.bfloat16)
    embedding = (matmul(out_low, wt_proj) * keep_rows).astype(jnp.bfloat16)
    back_query, back_key, back_value, back_out, back_up, back_down, back_proj = (
        wt_query, wt_key, wt_value, wt_out, wt_up, wt_down, wt_proj
    )
    back_gain_a = norm_gain_a
    back_gain_f = norm_gain_f
    cot_low = jnp.where(is_valid[:, None], cot_embed, jnp.zeros_like(cot_embed))
    grad_w_proj = matmul_tn(out_low, cot_low)
    grad_out = keep_rows * cot_hidden.astype(jnp.float32) + matmul_nt(cot_low, back_proj)
    grad_resid_two, grad_gain_f, grad_shift_f = norm_backward(
        grad_out, normed_two, inverse_two, back_gain_f
    )
    down_grad = grad_resid_two.astype(jnp.bfloat16)
    grad_w_down = matmul_tn(act_low, down_grad)
    grad_b_down = jnp.sum(down_grad.astype(jnp.float32), axis=0)
    up_grad = gelu_pull(matmul_nt(down_grad, back_down))[0].astype(jnp.bfloat16)
    grad_w_up = matmul_tn(first_low, up_grad)
    grad_b_up = jnp.sum(up_grad.astype(jnp.float32), axis=0)
    grad_first = grad_resid_two + matmul_nt(up_grad, back_up)
    grad_resid_one, grad_gain_a, grad_shift_a = norm_backward(
        grad_first, normed_one, inverse_one, back_gain_a
    )
    attn_grad = grad_resid_one.astype(jnp.bfloat16)
    grad_w_out = matmul_tn(context, attn_grad)
    grad_b_out = jnp.sum(attn_grad.astype(jnp.float32), axis=0)
    ctx_grad = (
        matmul_nt(attn_grad, back_out).astype(jnp.bfloat16).reshape(row_count, head_count, head_dim)
    )
    allowed = is_valid[None, :, None] & key_valid
    masked = masked_scores(query_rot, key_rot, allowed, score_scale)
    prob_full = jnp.exp(masked - log_totals)
    prob_low = prob_full.astype(jnp.bfloat16)
    prob_grad = jnp.einsum("qhd,khd->hqk", ctx_grad, value_low, preferred_element_type=jnp.float32)
    value_sum = jnp.einsum("hqk,qhd->khd", prob_low, ctx_grad, preferred_element_type=jnp.float32)
    row_dot = jnp.sum(prob_full * prob_grad, axis=-1, keepdims=True)
    score_grad = jnp.where(allowed, prob_full * (prob_grad - row_dot), 0.0).astype(jnp.bfloat16)
    query_parts = (
        jnp.einsum("hqk,khd->qhd", score_grad, key_rot, preferred_element_type=jnp.float32)
        * score_scale
    )
    key_sum = (
        jnp.einsum("hqk,qhd->khd", score_grad, query_rot, preferred_element_type=jnp.float32)
        * score_scale
    )
    query_grad = (
        unrotate(query_parts, cosine, sine_part)
        .reshape(row_count, model_width)
        .astype(jnp.bfloat16)
    )
    key_grad = (
        unrotate(key_sum, cosine, sine_part).reshape(row_count, model_width).astype(jnp.bfloat16)
    )
    value_grad = value_sum.reshape(row_count, model_width).astype(jnp.bfloat16)
    grad_w_query = matmul_tn(tokens, query_grad)
    grad_b_query = jnp.sum(query_grad.astype(jnp.float32), axis=0)
    grad_w_key = matmul_tn(tokens, key_grad)
    grad_b_key = jnp.sum(key_grad.astype(jnp.float32), axis=0)
    grad_w_value = matmul_tn(tokens, value_grad)
    grad_b_value = jnp.sum(value_grad.astype(jnp.float32), axis=0)
    grad_tokens = (
        grad_resid_one
        + matmul_nt(query_grad, back_query)
        + matmul_nt(key_grad, back_key)
        + matmul_nt(value_grad, back_value)
    )
    weight_parts, vector_parts, stat_sums = reduce_all(
        (grad_w_proj, grad_w_down, grad_w_up, grad_w_out, grad_w_query, grad_w_key, grad_w_value),
        (
            grad_b_query,
            grad_b_key,
            grad_b_value,
            grad_b_out,
            grad_gain_a,
            grad_shift_a,
            grad_b_down,
            grad_gain_f,
            grad_shift_f,
            grad_b_up,
        ),
        (
            jnp.sum(keep_rows * tokens_wide * tokens_wide),
            jnp.sum(keep_rows * attn_branch * attn_branch),
            jnp.sum(keep_rows * down_branch * down_branch),
            jnp.sum(keep_rows),
        ),
    )
    rms_stats = jnp.sqrt(stat_sums[:3] / (stat_sums[3] * model_width))
    return (
        hidden,
        embedding,
        grad_tokens,
        weight_parts[4],
        vector_parts[0],
        weight_parts[5],
        vector_parts[1],
        weight_parts[6],
        vector_parts[2],
        weight_parts[3],
        vector_parts[3],
        vector_parts[4],
        vector_parts[5],
        weight_parts[2],
        vector_parts[9],
        weight_parts[1],
        vector_parts[6],
        vector_parts[7],
        vector_parts[8],
        weight_parts[0],
        rms_stats,
    )


def shards_any(
    tokens,
    cot_hidden,
    cot_embed,
    lengths,
    offsets,
    pack_order,
    w_query,
    b_query,
    w_key,
    b_key,
    w_value,
    b_value,
    w_out,
    b_out,
    gain_attn,
    shift_attn,
    w_up,
    b_up,
    w_down,
    b_down,
    gain_ffn,
    shift_ffn,
    w_proj,
):
    gathered = (
        lax.all_gather(w_query, "dp", axis=0, tiled=True),
        lax.all_gather(w_key, "dp", axis=0, tiled=True),
        lax.all_gather(w_value, "dp", axis=0, tiled=True),
        lax.all_gather(w_out, "dp", axis=0, tiled=True),
        lax.all_gather(w_up, "dp", axis=0, tiled=True),
        lax.all_gather(w_down, "dp", axis=0, tiled=True),
        lax.all_gather(w_proj, "dp", axis=0, tiled=True),
        lax.all_gather(b_query, "dp", axis=0, tiled=True),
        lax.all_gather(b_key, "dp", axis=0, tiled=True),
        lax.all_gather(b_value, "dp", axis=0, tiled=True),
        lax.all_gather(b_out, "dp", axis=0, tiled=True),
        lax.all_gather(gain_attn, "dp", axis=0, tiled=True),
        lax.all_gather(shift_attn, "dp", axis=0, tiled=True),
        lax.all_gather(b_up, "dp", axis=0, tiled=True),
        lax.all_gather(b_down, "dp", axis=0, tiled=True),
        lax.all_gather(gain_ffn, "dp", axis=0, tiled=True),
        lax.all_gather(shift_ffn, "dp", axis=0, tiled=True),
    )
    wt_query, wt_key, wt_value, wt_out, wt_up, wt_down, wt_proj = gathered[:7]
    vectors = [piece.astype(jnp.float32) for piece in gathered[7:]]
    (
        bias_query,
        bias_key,
        bias_value,
        bias_out,
        norm_gain_a,
        norm_shift_a,
        bias_up,
        bias_down,
        norm_gain_f,
        norm_shift_f,
    ) = vectors
    row_count = tokens.shape[0]
    model_width = tokens.shape[1]
    head_count = H
    head_dim = model_width // head_count
    device = lax.axis_index("dp")
    slots = jnp.arange(pack_order.shape[0], dtype=jnp.int32)
    pack_id = jnp.sum(jnp.where(slots == device, pack_order, 0))
    length = jnp.sum(jnp.where(slots == pack_id, lengths, 0))
    offset = jnp.sum(jnp.where(slots == pack_id, offsets, 0))
    row_index = jnp.arange(row_count, dtype=jnp.int32)
    is_valid = (row_index >= offset) & (row_index < offset + length)
    keep_rows = is_valid.astype(jnp.float32)[:, None]
    cosine, sine_part = rope_tables((row_index - offset).astype(jnp.float32), head_dim)
    query_pre = matmul(tokens, wt_query) + bias_query
    key_pre = matmul(tokens, wt_key) + bias_key
    value_low = (
        (matmul(tokens, wt_value) + bias_value)
        .astype(jnp.bfloat16)
        .reshape(row_count, head_count, head_dim)
    )
    query_rot = rotate(
        query_pre.reshape(row_count, head_count, head_dim), cosine, sine_part
    ).astype(jnp.bfloat16)
    key_rot = rotate(key_pre.reshape(row_count, head_count, head_dim), cosine, sine_part).astype(
        jnp.bfloat16
    )
    score_scale = 1.0 / math.sqrt(head_dim)
    key_valid = is_valid[None, None, :]
    allowed = is_valid[None, :, None] & key_valid
    masked = masked_scores(query_rot, key_rot, allowed, score_scale)
    row_top = jnp.max(masked, axis=-1, keepdims=True)
    exponent = jnp.exp(masked - row_top)
    row_total = jnp.sum(exponent, axis=-1, keepdims=True)
    prob_low = (exponent / row_total).astype(jnp.bfloat16)
    contexts = jnp.einsum("hqk,khd->qhd", prob_low, value_low, preferred_element_type=jnp.float32)
    log_totals = row_top + jnp.log(row_total)
    context = contexts.astype(jnp.bfloat16).reshape(row_count, model_width)
    tokens_wide = tokens.astype(jnp.float32)
    attn_branch = matmul(context, wt_out) + bias_out
    first, normed_one, inverse_one = norm_forward(
        tokens_wide + attn_branch, norm_gain_a, norm_shift_a
    )
    first_low = first.astype(jnp.bfloat16)
    up_pre = matmul(first_low, wt_up) + bias_up
    act_full, gelu_pull = jax.vjp(exact_gelu, up_pre)
    act_low = act_full.astype(jnp.bfloat16)
    down_branch = matmul(act_low, wt_down) + bias_down
    out, normed_two, inverse_two = norm_forward(first + down_branch, norm_gain_f, norm_shift_f)
    out_low = out.astype(jnp.bfloat16)
    hidden = (out * keep_rows).astype(jnp.bfloat16)
    embedding = (matmul(out_low, wt_proj) * keep_rows).astype(jnp.bfloat16)
    stat_sums = lax.psum(
        (
            jnp.sum(keep_rows * tokens_wide * tokens_wide),
            jnp.sum(keep_rows * attn_branch * attn_branch),
            jnp.sum(keep_rows * down_branch * down_branch),
            jnp.sum(keep_rows),
        ),
        "dp",
    )
    rms_stats = jnp.sqrt(
        jnp.stack([stat_sums[0], stat_sums[1], stat_sums[2]]) / (stat_sums[3] * model_width)
    )
    backward_set = (
        lax.all_gather(w_query, "dp", axis=0, tiled=True),
        lax.all_gather(w_key, "dp", axis=0, tiled=True),
        lax.all_gather(w_value, "dp", axis=0, tiled=True),
        lax.all_gather(w_out, "dp", axis=0, tiled=True),
        lax.all_gather(w_up, "dp", axis=0, tiled=True),
        lax.all_gather(w_down, "dp", axis=0, tiled=True),
        lax.all_gather(w_proj, "dp", axis=0, tiled=True),
        lax.all_gather(b_query, "dp", axis=0, tiled=True),
        lax.all_gather(b_key, "dp", axis=0, tiled=True),
        lax.all_gather(b_value, "dp", axis=0, tiled=True),
        lax.all_gather(b_out, "dp", axis=0, tiled=True),
        lax.all_gather(gain_attn, "dp", axis=0, tiled=True),
        lax.all_gather(shift_attn, "dp", axis=0, tiled=True),
        lax.all_gather(b_up, "dp", axis=0, tiled=True),
        lax.all_gather(b_down, "dp", axis=0, tiled=True),
        lax.all_gather(gain_ffn, "dp", axis=0, tiled=True),
        lax.all_gather(shift_ffn, "dp", axis=0, tiled=True),
    )
    back_query, back_key, back_value, back_out, back_up, back_down, back_proj = backward_set[:7]
    back_gain_a = backward_set[11].astype(jnp.float32)
    back_gain_f = backward_set[15].astype(jnp.float32)
    cot_low = jnp.where(is_valid[:, None], cot_embed, jnp.zeros_like(cot_embed))
    grad_w_proj = matmul_tn(out_low, cot_low)
    grad_out = keep_rows * cot_hidden.astype(jnp.float32) + matmul_nt(cot_low, back_proj)
    grad_resid_two, grad_gain_f, grad_shift_f = norm_backward(
        grad_out, normed_two, inverse_two, back_gain_f
    )
    down_grad = grad_resid_two.astype(jnp.bfloat16)
    grad_w_down = matmul_tn(act_low, down_grad)
    grad_b_down = jnp.sum(down_grad.astype(jnp.float32), axis=0)
    up_grad = gelu_pull(matmul_nt(down_grad, back_down))[0].astype(jnp.bfloat16)
    grad_w_up = matmul_tn(first_low, up_grad)
    grad_b_up = jnp.sum(up_grad.astype(jnp.float32), axis=0)
    grad_first = grad_resid_two + matmul_nt(up_grad, back_up)
    grad_resid_one, grad_gain_a, grad_shift_a = norm_backward(
        grad_first, normed_one, inverse_one, back_gain_a
    )
    attn_grad = grad_resid_one.astype(jnp.bfloat16)
    grad_w_out = matmul_tn(context, attn_grad)
    grad_b_out = jnp.sum(attn_grad.astype(jnp.float32), axis=0)
    ctx_grad = (
        matmul_nt(attn_grad, back_out).astype(jnp.bfloat16).reshape(row_count, head_count, head_dim)
    )
    allowed = is_valid[None, :, None] & key_valid
    masked = masked_scores(query_rot, key_rot, allowed, score_scale)
    prob_full = jnp.exp(masked - log_totals)
    prob_low = prob_full.astype(jnp.bfloat16)
    prob_grad = jnp.einsum("qhd,khd->hqk", ctx_grad, value_low, preferred_element_type=jnp.float32)
    value_sum = jnp.einsum("hqk,qhd->khd", prob_low, ctx_grad, preferred_element_type=jnp.float32)
    row_dot = jnp.sum(prob_full * prob_grad, axis=-1, keepdims=True)
    score_grad = jnp.where(allowed, prob_full * (prob_grad - row_dot), 0.0).astype(jnp.bfloat16)
    query_parts = (
        jnp.einsum("hqk,khd->qhd", score_grad, key_rot, preferred_element_type=jnp.float32)
        * score_scale
    )
    key_sum = (
        jnp.einsum("hqk,qhd->khd", score_grad, query_rot, preferred_element_type=jnp.float32)
        * score_scale
    )
    query_grad = (
        unrotate(query_parts, cosine, sine_part)
        .reshape(row_count, model_width)
        .astype(jnp.bfloat16)
    )
    key_grad = (
        unrotate(key_sum, cosine, sine_part).reshape(row_count, model_width).astype(jnp.bfloat16)
    )
    value_grad = value_sum.reshape(row_count, model_width).astype(jnp.bfloat16)
    grad_w_query = matmul_tn(tokens, query_grad)
    grad_b_query = jnp.sum(query_grad.astype(jnp.float32), axis=0)
    grad_w_key = matmul_tn(tokens, key_grad)
    grad_b_key = jnp.sum(key_grad.astype(jnp.float32), axis=0)
    grad_w_value = matmul_tn(tokens, value_grad)
    grad_b_value = jnp.sum(value_grad.astype(jnp.float32), axis=0)
    grad_tokens = (
        grad_resid_one
        + matmul_nt(query_grad, back_query)
        + matmul_nt(key_grad, back_key)
        + matmul_nt(value_grad, back_value)
    )
    all_parts = (
        lax.psum_scatter(grad_w_query, "dp", scatter_dimension=0, tiled=True),
        lax.psum_scatter(grad_w_key, "dp", scatter_dimension=0, tiled=True),
        lax.psum_scatter(grad_w_value, "dp", scatter_dimension=0, tiled=True),
        lax.psum_scatter(grad_w_out, "dp", scatter_dimension=0, tiled=True),
        lax.psum_scatter(grad_b_query, "dp", scatter_dimension=0, tiled=True),
        lax.psum_scatter(grad_b_key, "dp", scatter_dimension=0, tiled=True),
        lax.psum_scatter(grad_b_value, "dp", scatter_dimension=0, tiled=True),
        lax.psum_scatter(grad_b_out, "dp", scatter_dimension=0, tiled=True),
        lax.psum_scatter(grad_gain_a, "dp", scatter_dimension=0, tiled=True),
        lax.psum_scatter(grad_shift_a, "dp", scatter_dimension=0, tiled=True),
        lax.psum_scatter(grad_w_up, "dp", scatter_dimension=0, tiled=True),
        lax.psum_scatter(grad_w_down, "dp", scatter_dimension=0, tiled=True),
        lax.psum_scatter(grad_w_proj, "dp", scatter_dimension=0, tiled=True),
        lax.psum_scatter(grad_b_up, "dp", scatter_dimension=0, tiled=True),
        lax.psum_scatter(grad_b_down, "dp", scatter_dimension=0, tiled=True),
        lax.psum_scatter(grad_gain_f, "dp", scatter_dimension=0, tiled=True),
        lax.psum_scatter(grad_shift_f, "dp", scatter_dimension=0, tiled=True),
    )
    attn_parts = all_parts[:10]
    ffn_parts = all_parts[10:]
    return (
        hidden,
        embedding,
        grad_tokens,
        attn_parts[0],
        attn_parts[4],
        attn_parts[1],
        attn_parts[5],
        attn_parts[2],
        attn_parts[6],
        attn_parts[3],
        attn_parts[7],
        attn_parts[8],
        attn_parts[9],
        ffn_parts[0],
        ffn_parts[3],
        ffn_parts[1],
        ffn_parts[4],
        ffn_parts[5],
        ffn_parts[6],
        ffn_parts[2],
        rms_stats,
    )


def solution(mesh):
    fast = mesh.shape["dp"] == 32
    placed = (
        P("dp", None),
        P("dp", None),
        P("dp", None),
        P(),
        P(),
        P(),
        P("dp", None),
        P("dp"),
        P("dp", None),
        P("dp"),
        P("dp", None),
        P("dp"),
        P("dp", None),
        P("dp"),
        P("dp"),
        P("dp"),
        P("dp", None),
        P("dp"),
        P("dp", None),
        P("dp"),
        P("dp"),
        P("dp"),
        P("dp", None),
    )
    return jax.shard_map(
        shards if fast else shards_any,
        mesh=mesh,
        in_specs=placed,
        out_specs=(
            P("dp", None),
            P("dp", None),
            P("dp", None),
            P("dp", None),
            P("dp"),
            P("dp", None),
            P("dp"),
            P("dp", None),
            P("dp"),
            P("dp", None),
            P("dp"),
            P("dp"),
            P("dp"),
            P("dp", None),
            P("dp"),
            P("dp", None),
            P("dp"),
            P("dp"),
            P("dp"),
            P("dp", None),
            P(),
        ),
        check_vma=False,
    )
```

```python
import functools
import math

import jax
import jax.numpy as jnp
from jax import lax
from jax.experimental import pallas as pl
from jax.experimental.pallas import tpu as pltpu
from jax.sharding import PartitionSpec as P

MESH = pl.DeviceIdType.MESH

H = 16


eps_norm = 1e-05
neg_large = -1e30


def matmul(left, right):
    return jnp.dot(left, right, preferred_element_type=jnp.float32)


def matmul_nt(left, right):
    return lax.dot_general(
        left, right, (((1,), (1,)), ((), ())), preferred_element_type=jnp.float32
    )


def matmul_tn(left, right):
    return lax.dot_general(
        left, right, (((0,), (0,)), ((), ())), preferred_element_type=jnp.float32
    )


def exact_gelu(values):
    return jax.nn.gelu(values, approximate=False)


def norm_forward(values, gain, shift):
    row_mean = jnp.mean(values, axis=-1, keepdims=True)
    centred = values - row_mean
    inverse = lax.rsqrt(jnp.mean(centred * centred, axis=-1, keepdims=True) + eps_norm)
    normed = centred * inverse
    return (normed * gain + shift, normed, inverse)


def norm_backward(grad_in, normed, inverse, gain):
    scaled = grad_in * gain
    adjusted = (
        scaled
        - jnp.mean(scaled, axis=-1, keepdims=True)
        - normed * jnp.mean(scaled * normed, axis=-1, keepdims=True)
    )
    return (adjusted * inverse, jnp.sum(grad_in * normed, axis=0), jnp.sum(grad_in, axis=0))


def rope_tables(position, head_dim):
    half_dim = head_dim // 2
    freq_index = jnp.arange(half_dim, dtype=jnp.float32)
    frequency = jnp.exp(-math.log(10000.0) * 2.0 * freq_index / head_dim)
    angles = position[:, None] * frequency[None, :]
    return (jnp.cos(angles)[:, None, :], jnp.sin(angles)[:, None, :])


def rotate(values, cosine, sine_part):
    half_dim = values.shape[-1] // 2
    first_half = values[..., :half_dim]
    second = values[..., half_dim:]
    return jnp.concatenate(
        [first_half * cosine - second * sine_part, second * cosine + first_half * sine_part],
        axis=-1,
    )


def unrotate(grad_in, cosine, sine_part):
    half_dim = grad_in.shape[-1] // 2
    first_half = grad_in[..., :half_dim]
    second = grad_in[..., half_dim:]
    return jnp.concatenate(
        [first_half * cosine + second * sine_part, second * cosine - first_half * sine_part],
        axis=-1,
    )


def masked_scores(query_block, key_rot, allowed, score_scale):
    raw_scores = jnp.einsum(
        "qhd,khd->hqk", query_block, key_rot, preferred_element_type=jnp.float32
    )
    return jnp.where(allowed, raw_scores * score_scale, neg_large)


def device_at(z, y, x, c):
    return ((z * 2 + y) * 2 + x) * 2 + c


def wait_bytes(ref, sem):
    pltpu.make_async_copy(ref, ref, sem).wait()


def send(src, dst, sem_out, sem_in, target):
    pltpu.make_async_remote_copy(
        src_ref=src,
        dst_ref=dst,
        send_sem=sem_out,
        recv_sem=sem_in,
        device_id=(target,),
        device_id_type=MESH,
    ).start()


F32, BF16 = jnp.float32, jnp.bfloat16
ANY = pl.BlockSpec(memory_space=pl.ANY)
FWD_TENSORS = (
    (16, 128, F32),
    (32, 1024, BF16),
    (32, 1024, BF16),
    (32, 1024, BF16),
    (32, 1024, BF16),
    (32, 4096, BF16),
    (32, 128, BF16),
    (128, 1024, BF16),
)
FWD_PIECES = (
    ((0, 0, 128), (1, 0, 1024), (2, 0, 1024), (3, 0, 1024), (4, 0, 1024))
    + tuple((5, 1024 * k, 1024) for k in range(4))
    + ((6, 0, 128),)
    + tuple((7, 256 * k, 256) for k in range(4))
)
P_VEC, P_Q, P_K, P_V, P_O, P_UP, P_PROJ, P_DOWN = 0, 1, 2, 3, 4, 5, 9, 10
V_BQ, V_BK, V_BV, V_BO, V_GA, V_SA, V_BD, V_GF, V_SF = range(9)


def dot(left, right):
    return jnp.dot(left, right, preferred_element_type=F32)


def dot_nt(left, right):
    return lax.dot_general(left, right, (((1,), (1,)), ((), ())), preferred_element_type=F32)


def local_copy(src, dst, sem):
    pltpu.make_async_copy(src, dst, sem).start()


def lanes_at(start, size):
    return pl.ds(pl.multiple_of(start, 128), size)


def rows_at(start, size):
    return pl.ds(pl.multiple_of(start, size), size)


def place():
    me = lax.axis_index("dp")
    return me // 8, (me // 4) % 2, (me // 2) % 2, me % 2


def greet(z, y, x, c):
    others = [(z + k) % 4 for k in (1, 2, 3)]
    peers = [device_at(z, y, 1 - x, c), device_at(z, 1 - y, x, c), device_at(z, y, x, 1 - c)]
    peers += [device_at(zz, y, x, c) for zz in others]
    barrier = pltpu.get_barrier_semaphore()
    for peer in peers:
        pl.semaphore_signal(barrier, inc=1, device_id=(peer,), device_id_type=MESH)
    pl.semaphore_wait(barrier, len(peers))


def transpose_blocks(src, dst):
    @pl.loop(0, src.shape[1] // 128)
    def _(j):
        block = src[:, lanes_at(j * 128, 128)].T
        for b in range(4):
            dst[b % 2, rows_at((2 * j + b // 2) * 32, 32), :] = block[32 * b : 32 * b + 32]


def forward_kernel(
    tokens_h, vec_h, lengths_s, offsets_s, order_s, *refs
):
    src = (None,) + refs[:7]
    refs = refs[7:]
    full = (None,) + refs[:7]
    (
        q_h, kt_h, v_h, prob_h, ctxp_h, n1_h, inv1_h, firstp_h, tokp_h, act_h, slope_h,
        n2_h, inv2_h, outp_h, hidden_h, embed_h, vecs_h, stats_h, cos_h, sin_h,
    ) = refs[7:27]
    refs = refs[27:]
    (
        tok, veclocal, packed, table, vecs, bias_up, cosine, sine, mask, stats,
        q, k, v, kt, vt, prob, ctx, ctxp, tokp, resid, n1, inv1, low, lowp, act, slope, n2, inv2,
        hidden, embed, outp,
    ) = refs[:31]
    refs = refs[31:]
    wbuf = (None,) + refs[: len(FWD_PIECES) - 1]
    ss, rs, ls, ld, os, ps, ins = refs[len(FWD_PIECES) - 1 :]
    count = len(FWD_PIECES)
    z, y, x, c = place()
    me = device_at(z, y, x, c)
    near_x, near_y = device_at(z, y, 1 - x, c), device_at(z, 1 - y, x, c)
    sibling = device_at(z, y, x, 1 - c)
    others = [(z + kk) % 4 for kk in (1, 2, 3)]

    local_copy(vec_h, veclocal, ins.at[0])
    local_copy(tokens_h, tok, ins.at[1])
    greet(z, y, x, c)

    def home(t, *lead):
        tensor, first, width = FWD_PIECES[t]
        if t == P_VEC:
            return table.at[lead]
        return full[tensor].at[lead + (slice(None), pl.ds(first, width))]

    def part(t, lead, rows):
        tensor, first, width = FWD_PIECES[t]
        if t == P_VEC:
            return table.at[lead + (rows,)]
        return full[tensor].at[lead + (rows, pl.ds(first, width))]

    def own(t):
        tensor, first, width = FWD_PIECES[t]
        piece = packed if t == P_VEC else src[tensor].at[:, pl.ds(first, width)]
        mine = home(t, z, y, x, c)
        for zz in others:
            send(piece, mine, ss.at[t, 0], rs.at[t, 0], device_at(zz, y, x, c))
        send(piece, mine, ss.at[t, 1], rs.at[t, 1], near_x)
        send(piece, mine, ss.at[t, 2], rs.at[t, 2], near_y)
        local_copy(piece, mine, ls.at[t])

    def column(t):
        wait_bytes(home(t, pl.ds(0, 3), 0, 0, 0), rs.at[t, 0])
        for zz in others:
            block = home(t, zz, y, x, c)
            send(block, block, ss.at[t, 3], rs.at[t, 3], near_x)
            send(block, block, ss.at[t, 4], rs.at[t, 4], near_y)

    def plane(t):
        half = FWD_TENSORS[FWD_PIECES[t][0]][0] // 2
        wait_bytes(home(t, 0, 0, 0, 0), rs.at[t, 1])
        wait_bytes(home(t, pl.ds(0, 3), 0, 0, 0), rs.at[t, 3])
        block = part(t, (slice(None), y, 1 - x, c), pl.ds(0, half))
        send(block, block, ss.at[t, 5], rs.at[t, 5], near_y)
        wait_bytes(home(t, 0, 0, 0, 0), rs.at[t, 2])
        wait_bytes(home(t, pl.ds(0, 3), 0, 0, 0), rs.at[t, 4])
        block = part(t, (slice(None), 1 - y, x, c), pl.ds(half, half))
        send(block, block, ss.at[t, 6], rs.at[t, 6], near_x)

    def pair(t):
        half = FWD_TENSORS[FWD_PIECES[t][0]][0] // 2
        for kind in (5, 6):
            wait_bytes(part(t, (slice(None), 0, 0, 0), pl.ds(0, half)), rs.at[t, kind])
        wait_bytes(home(t, 0, 0, 0, 0), ls.at[t])
        block = home(t, slice(None), slice(None), slice(None), c)
        send(block, block, ss.at[t, 7], rs.at[t, 7], sibling)

    def arrive(t):
        everything = home(t, slice(None), slice(None), slice(None), 0)
        wait_bytes(everything, rs.at[t, 7])
        if t != P_VEC:
            tensor, first, width = FWD_PIECES[t]
            local_copy(
                full[tensor].at[:, :, :, :, :, pl.ds(first, width)], wbuf[t], ld.at[t]
            )

    def loaded(t):
        wait_bytes(wbuf[t], ld.at[t])

    def sent(t):
        half = FWD_TENSORS[FWD_PIECES[t][0]][0] // 2
        one = home(t, 0, 0, 0, 0)
        three = home(t, pl.ds(0, 3), 0, 0, 0)
        halves = part(t, (slice(None), 0, 0, 0), pl.ds(0, half))
        everything = home(t, slice(None), slice(None), slice(None), 0)
        for kind, ref in enumerate((three, one, one, three, three, halves, halves, everything)):
            wait_bytes(ref, ss.at[t, kind])

    pack = order_s[me]
    length, offset = lengths_s[pack], offsets_s[pack]
    saved = []

    def save(value, out):
        n = len(saved)
        local_copy(value, out, os.at[n])
        saved.append((out, os.at[n]))

    def row_valid(rows, start):
        r = lax.broadcasted_iota(jnp.int32, (rows, 1), 0) + start
        return ((r >= offset) & (r < offset + length)).astype(F32)

    def pack_vectors():
        wait_bytes(veclocal, ins.at[0])
        val = veclocal[...]
        wide = jnp.concatenate([val] * 4, axis=1)
        lane = lax.broadcasted_iota(jnp.int32, (16, 128), 1)
        row = lax.broadcasted_iota(jnp.int32, (16, 128), 0)
        bias = jnp.concatenate([val[9 + i : 10 + i] for i in range(4)], axis=1)
        spread = jnp.where((lane // 32 == me % 4) & (row < 9), wide, 0.0)
        packed[...] = jnp.where(row == 9, jnp.broadcast_to(bias, (16, 128)), spread)

    def prepare():
        lane = lax.broadcasted_iota(jnp.int32, (1, 128), 1)
        freq = jnp.exp((lane % 32).astype(F32) * (-math.log(10000.0) * 2.0 / 64))

        @pl.loop(0, 8)
        def _(i):
            r = lax.broadcasted_iota(jnp.int32, (64, 1), 0) + i * 64
            angle = (r - offset).astype(F32) * freq
            cosine[rows_at(i * 64, 64), :] = jnp.cos(angle)
            sine[rows_at(i * 64, 64), :] = jnp.where(lane % 64 < 32, -1.0, 1.0) * jnp.sin(angle)

        s = lax.broadcasted_iota(jnp.int32, (1, 512), 1)
        col_valid = ((s >= offset) & (s < offset + length)).astype(F32)
        stats[...] = jnp.zeros_like(stats)

        @pl.loop(0, 8)
        def _(i):
            mask[rows_at(i * 64, 64), :] = row_valid(64, i * 64) * col_valid

        stats[3:4, :] = jnp.broadcast_to(
            jnp.sum(col_valid, axis=1, keepdims=True), (1, 128)
        )
        wait_bytes(tok, ins.at[1])

        @pl.loop(0, 8)
        def _(i):
            t32 = tok[rows_at(i * 64, 64), :].astype(F32)
            add_stat(0, jnp.sum(row_valid(64, i * 64) * t32 * t32, axis=0, keepdims=True))

        transpose_blocks(tok, tokp)
        save(tokp, tokp_h)
        save(cosine, cos_h)
        save(sine, sin_h)

    def add_stat(row, wide):
        total = wide[:, 0:128]
        for i in range(1, wide.shape[1] // 128):
            total = total + wide[:, 128 * i : 128 * i + 128]
        stats[row : row + 1, :] = stats[row : row + 1, :] + total

    def unpack_vectors():
        grouped = table[...].reshape(8, 4, 16, 128).sum(axis=1)
        for b in range(8):
            vecs[:, 128 * b : 128 * b + 128] = grouped[b]
        for d in range(32):
            bias_up[0:1, 128 * d : 128 * d + 128] = table[
                d // 8, (d // 4) % 2, (d // 2) % 2, d % 2, 9:10, :
            ]
        save(vecs, vecs_h)

    def weight(t, first, width):
        w = wbuf[t]
        return w[:, :, :, :, :, lanes_at(first, width)].reshape(-1, width)

    lane128 = lambda: lax.broadcasted_iota(jnp.int32, (1, 128), 1)

    def rotary(t, bias, dst, scale, transposed, j0, j1):
        @pl.loop(j0, j1)
        def _(j):
            pre = dot(tok[...], weight(t, j * 256, 256)) + vecs[bias : bias + 1, lanes_at(j * 256, 256)]
            for b in range(2):
                part_in = pre[:, 128 * b : 128 * b + 128]
                swapped = jnp.where(
                    lane128() % 64 < 32, pltpu.roll(part_in, 96, 1), pltpu.roll(part_in, 32, 1)
                )
                turned = (part_in * cosine[...] + swapped * sine[...]).astype(BF16)
                if transposed is not None:
                    transposed[rows_at(j * 256 + 128 * b, 128), :] = turned.T
                dst[:, lanes_at(j * 256 + 128 * b, 128)] = turned * jnp.asarray(scale, BF16)

    def value(j0, j1):
        @pl.loop(j0, j1)
        def _(j):
            pre = dot(tok[...], weight(P_V, j * 256, 256)) + vecs[V_BV : V_BV + 1, lanes_at(j * 256, 256)]
            val = pre.astype(BF16)
            v[:, lanes_at(j * 256, 256)] = val
            vt[rows_at(j * 256, 256), :] = val.T

    def attend(p0, p1):
        @pl.loop(p0, p1)
        def _(p):
            cols = lanes_at(p * 128, 128)
            qp, kp = q[:, cols], k[:, cols]
            pieces = []
            for j in range(2):
                keep = lane128() < 64 if j == 0 else lane128() >= 64
                scores = dot_nt(jnp.where(keep, kp, jnp.zeros((), BF16)), qp)
                scores = jnp.where(mask[...] > 0.0, scores, -1e30)
                top = jnp.max(scores, axis=0, keepdims=True)
                expo = jnp.exp(scores - top)
                total = jnp.sum(expo, axis=0, keepdims=True)
                weights = (expo * (1.0 / total)).astype(BF16)

                @pl.when(p > 0)
                def _():
                    wait_bytes(prob.at[j], ps.at[j])

                prob[j] = weights
                local_copy(prob.at[j], prob_h.at[p, j], ps.at[j])
                mixed = dot(vt[rows_at(p * 128 + 64 * j, 64), :], weights).astype(BF16)
                for b in range(2):
                    ctxp[b, rows_at((2 * p + j) * 32, 32), :] = mixed[32 * b : 32 * b + 32]
                pieces.append(mixed)
            ctx[:, cols] = jnp.concatenate(pieces, axis=0).T

    def attended():
        for j in range(2):
            wait_bytes(prob.at[j], ps.at[j])
        save(ctxp, ctxp_h)

    def project():
        loaded(P_O)

        @pl.loop(0, 4)
        def _(j):
            cols = lanes_at(j * 256, 256)
            branch = dot(ctx[...], weight(P_O, j * 256, 256)) + vecs[V_BO : V_BO + 1, cols]
            add_stat(1, jnp.sum(row_valid(512, 0) * branch * branch, axis=0, keepdims=True))
            resid[:, cols] = branch + tok[:, cols].astype(F32)

    def normalise(dst, inv):
        def at(i, finish):
            rows = rows_at(i * 32, 32)
            val = resid[rows, :]
            mean = jnp.sum(val, axis=1, keepdims=True) * (1.0 / 1024)
            centred = val - mean
            scale = lax.rsqrt(jnp.sum(centred * centred, axis=1, keepdims=True) * (1.0 / 1024) + eps_norm)
            normed = centred * scale
            dst[rows, :] = normed
            inv[rows, :] = jnp.broadcast_to(scale, (32, 128))
            finish(i, rows, normed)

        return at

    def norm_first():
        at = normalise(n1, inv1)

        def finish(i, rows, normed):
            low[rows, :] = (normed * vecs[V_GA : V_GA + 1, :] + vecs[V_SA : V_SA + 1, :]).astype(BF16)

        @pl.loop(0, 16)
        def _(i):
            at(i, finish)

        save(n1, n1_h)
        save(inv1, inv1_h)
        transpose_blocks(low, lowp)
        save(lowp, firstp_h)

    def expand(k0, j0, j1):
        @pl.loop(j0, j1)
        def _(j):
            cols = lanes_at(k0 * 1024 + j * 256, 256)
            pre = dot(low[...], weight(P_UP + k0, j * 256, 256)) + bias_up[0:1, cols]
            cdf = 0.5 * (1.0 + lax.erf(pre * math.sqrt(0.5)))
            val = (pre * cdf).astype(BF16)
            pdf = jnp.exp(pre * pre * -0.5) * (1.0 / math.sqrt(2 * math.pi))
            slope[:, cols] = (cdf + pre * pdf).astype(BF16)
            half = lanes_at(k0 * 512 + j * 128, 128)
            act[0, :, half] = val[:, :128]
            act[1, :, half] = val[:, 128:]

    def contract(k0):
        cols = pl.ds(256 * k0, 256)
        w = wbuf[P_DOWN + k0]
        branch = dot(act[0], w[:, :, :, 0].reshape(2048, 256))
        branch = branch + dot(act[1], w[:, :, :, 1].reshape(2048, 256)) + vecs[V_BD : V_BD + 1, cols]
        add_stat(2, jnp.sum(row_valid(512, 0) * branch * branch, axis=0, keepdims=True))
        first = n1[:, cols] * vecs[V_GA : V_GA + 1, cols] + vecs[V_SA : V_SA + 1, cols]
        resid[:, cols] = first + branch

    def norm_second():
        at = normalise(n2, inv2)

        def finish(i, rows, normed):
            out = normed * vecs[V_GF : V_GF + 1, :] + vecs[V_SF : V_SF + 1, :]
            low[rows, :] = out.astype(BF16)
            hidden[rows, :] = (out * row_valid(32, i * 32)).astype(BF16)

        @pl.loop(0, 16)
        def _(i):
            at(i, finish)

        save(n2, n2_h)
        save(inv2, inv2_h)
        save(hidden, hidden_h)
        embed[...] = (dot(low[...], weight(P_PROJ, 0, 128)) * row_valid(512, 0)).astype(BF16)
        save(embed, embed_h)
        transpose_blocks(low, outp)
        save(outp, outp_h)
        save(stats, stats_h)

    pack_vectors()
    for t in range(4):
        own(t)
    prepare()
    work = {
        4: [unpack_vectors],
        5: [lambda: (loaded(P_Q), rotary(P_Q, V_BQ, q, 0.125, None, 0, 4), save(q, q_h))],
        6: [lambda: (loaded(P_K), rotary(P_K, V_BK, k, 1.0, kt, 0, 4), save(kt, kt_h))],
        7: [lambda: (loaded(P_V), value(0, 4), save(v, v_h)), lambda: attend(0, 2)],
        8: [lambda: attend(2, 4), lambda: attend(4, 6)],
        9: [lambda: (attend(6, 8), attended()), project, norm_first],
        10: [lambda: (loaded(P_UP), expand(0, 0, 2)), lambda: expand(0, 2, 4)],
        11: [lambda: (loaded(P_UP + 1), expand(1, 0, 2)), lambda: expand(1, 2, 4)],
        12: [lambda: (loaded(P_UP + 2), expand(2, 0, 2)), lambda: expand(2, 2, 4)],
        13: [lambda: (loaded(P_UP + 3), expand(3, 0, 2)), lambda: expand(3, 2, 4)],
        14: [lambda: (save(act, act_h), save(slope, slope_h)), lambda: (loaded(P_PROJ), loaded(P_DOWN), contract(0))],
        15: [lambda: (loaded(P_DOWN + 1), contract(1))],
        16: [lambda: (loaded(P_DOWN + 2), contract(2))],
        17: [lambda: (loaded(P_DOWN + 3), contract(3))],
    }
    for step in range(count + 4):
        todo = list(work.get(step, []))
        moves = []
        if step + 4 < count:
            moves.append(lambda: own(step + 4))
        if step < count:
            moves.append(lambda: column(step))
        if 0 <= step - 1 < count:
            moves.append(lambda: plane(step - 1))
        if 0 <= step - 2 < count:
            moves.append(lambda: pair(step - 2))
        if 0 <= step - 3 < count:
            moves.append(lambda: arrive(step - 3))
        while moves or todo:
            if moves:
                moves.pop(0)()
            if todo and len(moves) <= 3:
                todo.pop(0)()
    norm_second()
    for t in range(count):
        sent(t)
    for out, sem in saved:
        wait_bytes(out, sem)


FWD_SAVED = (
    ((512, 1024), BF16),
    ((1024, 512), BF16),
    ((512, 1024), BF16),
    ((8, 2, 512, 512), BF16),
    ((2, 512, 512), BF16),
    ((512, 1024), F32),
    ((512, 128), F32),
    ((2, 512, 512), BF16),
    ((2, 512, 512), BF16),
    ((2, 512, 2048), BF16),
    ((512, 4096), BF16),
    ((512, 1024), F32),
    ((512, 128), F32),
    ((2, 512, 512), BF16),
    ((512, 1024), BF16),
    ((512, 128), BF16),
    ((16, 1024), F32),
    ((8, 128), F32),
    ((512, 128), F32),
    ((512, 128), F32),
)


def forward_pass(tokens, vec, lengths, offsets, order, weights):
    count = len(FWD_PIECES)
    shape = jax.ShapeDtypeStruct
    outs = [shape((4, 2, 2, 2, r, k), dt) for r, k, dt in FWD_TENSORS[1:]]
    outs += [shape(s, dt) for s, dt in FWD_SAVED]
    big = lambda *s: pltpu.VMEM(s, BF16)
    scratch = [
        big(512, 1024),
        pltpu.VMEM((16, 32), F32),
        pltpu.VMEM((16, 128), F32),
        pltpu.VMEM((4, 2, 2, 2, 16, 128), F32),
        pltpu.VMEM((16, 1024), F32),
        pltpu.VMEM((1, 4096), F32),
        pltpu.VMEM((512, 128), F32),
        pltpu.VMEM((512, 128), F32),
        pltpu.VMEM((512, 512), F32),
        pltpu.VMEM((8, 128), F32),
        big(512, 1024),
        big(512, 1024),
        big(512, 1024),
        big(1024, 512),
        big(1024, 512),
        big(2, 512, 512),
        big(512, 1024),
        big(2, 512, 512),
        big(2, 512, 512),
        pltpu.VMEM((512, 1024), F32),
        pltpu.VMEM((512, 1024), F32),
        pltpu.VMEM((512, 128), F32),
        big(512, 1024),
        big(2, 512, 512),
        big(2, 512, 2048),
        big(512, 4096),
        pltpu.VMEM((512, 1024), F32),
        pltpu.VMEM((512, 128), F32),
        big(512, 1024),
        big(512, 128),
        big(2, 512, 512),
    ]
    for tensor, _, width in FWD_PIECES[1:]:
        scratch.append(big(4, 2, 2, 2, FWD_TENSORS[tensor][0], width))
    dma = pltpu.SemaphoreType.DMA
    scratch += [dma((count, 8)), dma((count, 8)), dma((count,)), dma((count,)), dma((24,)), dma((2,)), dma((2,))]
    smem = pl.BlockSpec(memory_space=pltpu.SMEM)
    return pl.pallas_call(
        forward_kernel,
        out_shape=outs,
        in_specs=[ANY, ANY, smem, smem, smem] + [ANY] * 7,
        out_specs=[ANY] * len(outs),
        scratch_shapes=scratch,
        compiler_params=pltpu.CompilerParams(
            collective_id=0, has_side_effects=True, vmem_limit_bytes=62 * 2**20
        ),
        name="forward_pass",
    )(tokens, vec, lengths, offsets, order, *weights)


R_PROJ, R_DOWN, R_UP, R_OUT, R_Q, R_K, R_VEC, R_V = 0, 1, 5, 9, 10, 11, 12, 13
BWD_OUTS = (
    (32, 128, BF16),
    (1024, 128, BF16),
    (32, 4096, BF16),
    (32, 1024, BF16),
    (32, 1024, BF16),
    (32, 1024, BF16),
    (16, 128, F32),
    (32, 1024, BF16),
)
BWD_PIECES = (
    ((0, 0, 32, 128, BF16),)
    + tuple((1, 256 * k, 256, 128, BF16) for k in range(4))
    + tuple((2, 1024 * k, 32, 1024, BF16) for k in range(4))
    + (
        (3, 0, 32, 1024, BF16),
        (4, 0, 32, 1024, BF16),
        (5, 0, 32, 1024, BF16),
        (6, 0, 16, 128, F32),
        (7, 0, 32, 1024, BF16),
    )
)


def backward_kernel(cot_h, cote_h, lengths_s, offsets_s, order_s, *refs):
    wq_h, wk_h, wv_h, wo_h, wup_h, wproj_h, wdown_h = refs[:7]
    (
        q_h, kt_h, v_h, prob_h, ctxp_h, n1_h, inv1_h, firstp_h, tokp_h, act_h, slope_h,
        n2_h, inv2_h, outp_h, vecs_h, stats_h, cos_h, sin_h,
    ) = refs[7:25]
    refs = refs[25:]
    grad_h = refs[0]
    outs = refs[1:9]
    refs = refs[9:]
    (
        ring, wproj, resid, nbuf, inv2, inv1, dg, dgt, upg, four, slopes, blocks, kt, mask,
        cosine, sine, cot, vecs, stats, sums, sum_up, table, stage_d, stage_u, stage_p,
    ) = refs[:25]
    refs = refs[25:]
    count = len(BWD_PIECES)
    acc, diag, from_x, from_y = (refs[i * count : (i + 1) * count] for i in range(4))
    ss, rs, ls, ins, rsem, psem, gsem = refs[4 * count :]
    z, y, x, c = place()
    me = device_at(z, y, x, c)
    near_x, near_y = device_at(z, y, 1 - x, c), device_at(z, 1 - y, x, c)
    sibling = device_at(z, y, x, 1 - c)
    others = [(z + kk) % 4 for kk in (1, 2, 3)]
    pack = order_s[me]
    length, offset = lengths_s[pack], offsets_s[pack]

    ring_src = []
    for j in range(4):
        ring_src.append(wdown_h.at[pl.ds(1024 * j, 1024), :])
        ring_src.append(wup_h.at[:, pl.ds(1024 * j, 1024)])
    ring_src += [wo_h, wq_h, wk_h, wv_h]

    def ring_start(n):
        local_copy(ring_src[n], ring.at[n % 3], rsem.at[n])

    def ring_wait(n):
        wait_bytes(ring.at[n % 3], rsem.at[n])
        return ring.at[n % 3]

    def ring_next(n):
        if n + 3 < len(ring_src):
            ring_start(n + 3)

    loads = {}

    def load(name, src, dst):
        n = len(loads)
        loads[name] = (dst, ins.at[n])
        local_copy(src, dst, ins.at[n])

    def ready(name):
        dst, sem = loads[name]
        wait_bytes(dst, sem)

    load("cote", cote_h, cot)
    load("wproj", wproj_h, wproj)
    load("cot", cot_h, slopes.at[1])
    load("n2", n2_h, nbuf)
    load("inv2", inv2_h, inv2)
    load("vecs", vecs_h, vecs)
    load("outp", outp_h, blocks.at[0])
    for p in range(2):
        for h in range(2):
            load("act%d%d" % (p, h), act_h.at[p, :, pl.ds(1024 * h, 1024)], four.at[2 * p + h])
    ring_start(0)
    load("slope0", slope_h.at[:, pl.ds(0, 1024)], slopes.at[0])
    load("firstp", firstp_h, blocks.at[1])
    ring_start(1)
    load("inv1", inv1_h, inv1)
    load("stats", stats_h, stats)
    load("cos", cos_h, cosine)
    load("sin", sin_h, sine)
    load("kt", kt_h, kt)
    ring_start(2)
    greet(z, y, x, c)

    def out_view(t, *lead):
        out, first, rows, width, _ = BWD_PIECES[t]
        if R_DOWN <= t < R_UP:
            return outs[out].at[lead + (pl.ds(first, rows), slice(None))]
        return outs[out].at[lead + (slice(None), pl.ds(first, width))]

    def give(t, stage):
        send(stage, acc[t], ss.at[t, 0], rs.at[t, 0], sibling)

    def net(t):
        half = BWD_PIECES[t][2] // 2
        h = acc[t]
        first, second = pl.ds(0, half), pl.ds(half, half)
        send(h.at[:, 1 - y, 1 - x, first], diag[t].at[0], ss.at[t, 1], rs.at[t, 1], near_x)
        send(h.at[:, 1 - y, 1 - x, second], diag[t].at[1], ss.at[t, 2], rs.at[t, 2], near_y)
        send(h.at[:, y, 1 - x, first], from_x[t].at[:, first], ss.at[t, 3], rs.at[t, 3], near_x)
        send(h.at[:, 1 - y, x, second], from_y[t].at[:, second], ss.at[t, 4], rs.at[t, 4], near_y)

    def add_diagonal(t):
        rows = BWD_PIECES[t][2]
        half = rows // 2
        h = acc[t]
        first, second = pl.ds(0, half), pl.ds(half, half)
        wait_bytes(diag[t].at[0], rs.at[t, 1])

        @pl.loop(0, 4)
        def _(i):
            h[i, 1 - y, x, 0:half, :] = h[i, 1 - y, x, 0:half, :] + diag[t][0, i]

        send(h.at[:, 1 - y, x, first], from_y[t].at[:, first], ss.at[t, 6], rs.at[t, 6], near_y)
        wait_bytes(diag[t].at[1], rs.at[t, 2])

        @pl.loop(0, 4)
        def _(i):
            h[i, y, 1 - x, half:rows, :] = h[i, y, 1 - x, half:rows, :] + diag[t][1, i]

        send(h.at[:, y, 1 - x, second], from_x[t].at[:, second], ss.at[t, 5], rs.at[t, 5], near_x)

    def add_plane(t):
        rows = BWD_PIECES[t][2]
        half = rows // 2
        h = acc[t]
        first, second = pl.ds(0, half), pl.ds(half, half)
        wait_bytes(from_x[t].at[:, first], rs.at[t, 3])
        wait_bytes(from_x[t].at[:, second], rs.at[t, 5])
        wait_bytes(from_y[t].at[:, second], rs.at[t, 4])
        wait_bytes(from_y[t].at[:, first], rs.at[t, 6])

        @pl.loop(0, 4)
        def _(i):
            h[i, y, x] = h[i, y, x] + from_x[t][i] + from_y[t][i]

        slot = out_view(t, z)
        for zz in others:
            send(h.at[zz, y, x], slot, ss.at[t, 7], rs.at[t, 7], device_at(zz, y, x, c))
        local_copy(h.at[z, y, x], slot, ls.at[t])

    def finish(t):
        half = BWD_PIECES[t][2] // 2
        three = out_view(t, pl.ds(0, 3))
        wait_bytes(three, rs.at[t, 7])
        wait_bytes(out_view(t, 0), ls.at[t])
        wait_bytes(diag[t].at[0], ss.at[t, 1])
        wait_bytes(diag[t].at[1], ss.at[t, 2])
        for kind in (3, 4, 5, 6):
            wait_bytes(from_x[t].at[:, pl.ds(0, half)], ss.at[t, kind])
        wait_bytes(three, ss.at[t, 7])

    given = {}

    def take_stage(key, t):
        if key in given:
            wait_bytes(acc[given[key]], ss.at[given[key], 0])
        given[key] = t

    def rows_sib(t, lhs, rhs, stage, key):
        take_stage(key, t)
        width = BWD_PIECES[t][3]
        tile = min(width, 256)

        @pl.loop(0, width // tile)
        def _(j):
            cols = lanes_at(j * tile, tile)
            val = dot(lhs[1 - c], rhs[:, cols]).astype(BF16)
            stage[:, :, :, :, cols] = val.reshape(4, 2, 2, 32, tile)

        give(t, stage)

    def rows_own(t, lhs, rhs):
        width = BWD_PIECES[t][3]
        tile = min(width, 256)
        wait_bytes(acc[t], rs.at[t, 0])

        @pl.loop(0, width // tile)
        def _(j):
            cols = lanes_at(j * tile, tile)
            val = dot(lhs[c], rhs[:, cols]) + acc[t][:, :, :, :, cols].reshape(512, tile).astype(F32)
            acc[t][:, :, :, :, cols] = val.astype(BF16).reshape(4, 2, 2, 32, tile)

    def down_sib(k0):
        t = R_DOWN + k0
        stage = stage_d.at[k0 % 2]
        take_stage("d%d" % (k0 % 2), t)

        @pl.loop(0, 8)
        def _(j):
            rhs = four[2 * (1 - c) + j // 4, :, lanes_at((j % 4) * 256, 256)]
            val = dot(dgt[256 * k0 : 256 * k0 + 256, :], rhs).astype(BF16)
            stage[j // 2, j % 2, 0] = val[:, :128]
            stage[j // 2, j % 2, 1] = val[:, 128:]

        give(t, stage)

    def down_own(k0):
        t = R_DOWN + k0
        wait_bytes(acc[t], rs.at[t, 0])

        @pl.loop(0, 8)
        def _(j):
            rhs = four[2 * c + j // 4, :, lanes_at((j % 4) * 256, 256)]
            val = dot(dgt[256 * k0 : 256 * k0 + 256, :], rhs)
            for b in range(2):
                a = acc[t][j // 2, j % 2, b].astype(F32)
                acc[t][j // 2, j % 2, b] = (val[:, 128 * b : 128 * b + 128] + a).astype(BF16)

    def column_sum(ref):
        return dot(jnp.ones((16, 512), BF16), ref)[0:1]

    def row_valid(rows, start):
        r = lax.broadcasted_iota(jnp.int32, (rows, 1), 0) + start
        return ((r >= offset) & (r < offset + length)).astype(F32)

    def norm_back(inv, gain, to_gain, to_shift):
        sums[to_gain : to_gain + 1, :] = jnp.zeros((1, 1024), F32)
        sums[to_shift : to_shift + 1, :] = jnp.zeros((1, 1024), F32)

        @pl.loop(0, 16)
        def _(i):
            rows = rows_at(i * 32, 32)
            grad, normed = resid[rows, :], nbuf[rows, :]
            scaled = grad * vecs[gain : gain + 1, :]
            mean = jnp.sum(scaled, axis=1, keepdims=True) * (1.0 / 1024)
            cross = jnp.sum(scaled * normed, axis=1, keepdims=True) * (1.0 / 1024)
            out = (scaled - mean - normed * cross) * inv[rows, 0:1]
            resid[rows, :] = out
            dg[rows, :] = out.astype(BF16)
            sums[to_gain : to_gain + 1, :] = sums[to_gain : to_gain + 1, :] + jnp.sum(
                grad * normed, axis=0, keepdims=True
            )
            sums[to_shift : to_shift + 1, :] = sums[to_shift : to_shift + 1, :] + jnp.sum(
                grad, axis=0, keepdims=True
            )

    def begin():
        ready("cote")
        cot[...] = jnp.where(row_valid(512, 0) > 0.0, cot[...].astype(F32), 0.0).astype(BF16)
        ready("wproj")
        ready("cot")
        ready("vecs")

        @pl.loop(0, 4)
        def _(j):
            cols = lanes_at(j * 256, 256)
            resid[:, cols] = row_valid(512, 0) * slopes[1, :, cols].astype(F32) + dot_nt(
                cot[...], wproj[rows_at(j * 256, 256), :]
            )

        ready("n2")
        ready("inv2")
        norm_back(inv2, V_GF, V_GF, V_SF)
        load("n1", n1_h, nbuf)
        sums[V_BD : V_BD + 1, :] = column_sum(dg[...])
        load("slope1", slope_h.at[:, pl.ds(1024, 1024)], slopes.at[1])

    def turn():
        @pl.loop(0, 8)
        def _(j):
            dgt[rows_at(j * 128, 128), :] = dg[:, lanes_at(j * 128, 128)].T

    def acts():
        for p in range(2):
            for h in range(2):
                ready("act%d%d" % (p, h))

    def up_grad(k0):
        w = ring_wait(2 * k0)
        ready("slope%d" % k0)

        @pl.loop(0, 4)
        def _(j):
            cols = lanes_at(j * 256, 256)
            back = dot_nt(dg[...], w[rows_at(j * 256, 256), :]) * slopes[k0 % 2, :, cols].astype(F32)
            upg[k0, :, cols] = back.astype(BF16)

        ring_next(2 * k0)
        if k0 + 2 < 4:
            load("slope%d" % (k0 + 2), slope_h.at[:, pl.ds(1024 * (k0 + 2), 1024)], slopes.at[k0 % 2])
        sum_up[0:1, 1024 * k0 : 1024 * k0 + 1024] = column_sum(upg[k0])

    def first_grad(k0):
        w = ring_wait(2 * k0 + 1)

        @pl.loop(0, 4)
        def _(j):
            cols = lanes_at(j * 256, 256)
            resid[:, cols] = resid[:, cols] + dot_nt(upg[k0], w[rows_at(j * 256, 256), :])

        ring_next(2 * k0 + 1)

    def up_sib(k0):
        if k0 == 0:
            ready("firstp")
        rows_sib(R_UP + k0, blocks.at[1], upg.at[k0], stage_u.at[k0 % 2], "u%d" % (k0 % 2))

    def up_own(k0):
        rows_own(R_UP + k0, blocks.at[1], upg.at[k0])

    def norm_one():
        ready("n1")
        ready("inv1")
        norm_back(inv1, V_GA, V_GA, V_SA)
        sums[V_BO : V_BO + 1, :] = column_sum(dg[...])
        load("ctxp", ctxp_h, blocks.at[0])

    def start_attention():
        load("q", q_h, upg.at[0])
        load("v", v_h, upg.at[1])
        load("tokp", tokp_h, blocks.at[1])
        prob_start(0)

    def prob_start(p):
        for j in range(2):
            local_copy(
                prob_h.at[p, j],
                upg.at[2 + p % 2, :, pl.ds(512 * j, 512)],
                psem.at[p % 2, j],
            )

    def ctx_back():
        w = ring_wait(8)

        @pl.loop(0, 4)
        def _(j):
            four[3, :, lanes_at(j * 256, 256)] = dot_nt(dg[...], w[rows_at(j * 256, 256), :]).astype(BF16)

        ring_next(8)

    def make_mask():
        s = lax.broadcasted_iota(jnp.int32, (1, 512), 1)
        col_valid = ((s >= offset) & (s < offset + length)).astype(F32)

        @pl.loop(0, 8)
        def _(i):
            mask[rows_at(i * 64, 64), :] = row_valid(64, i * 64) * col_valid

    def lane128():
        return lax.broadcasted_iota(jnp.int32, (1, 128), 1)

    def unturn(val):
        swapped = jnp.where(lane128() % 64 < 32, pltpu.roll(val, 96, 1), pltpu.roll(val, 32, 1))
        return (val * cosine[...] - swapped * sine[...]).astype(BF16)

    def attend_back(p0, p1):
        @pl.loop(p0, p1)
        def _(p):
            cols = lanes_at(p * 128, 128)
            for j in range(2):
                wait_bytes(upg.at[2 + p % 2, :, pl.ds(512 * j, 512)], psem.at[p % 2, j])

            @pl.when(p + 1 < 8)
            def _():
                prob_start(p + 1)

            qp, vp, grad = upg[0, :, cols], upg[1, :, cols], four[3, :, cols]
            dv, dk, dqt = [], [], []
            for j in range(2):
                keep = lane128() < 64 if j == 0 else lane128() >= 64
                low = upg[2 + p % 2, :, 512 * j : 512 * j + 512]
                wide = low.astype(F32)
                back = dot_nt(jnp.where(keep, vp, jnp.zeros((), BF16)), grad)
                row_dot = jnp.sum(wide * back, axis=0, keepdims=True)
                sgrad = jnp.where(mask[...] > 0.0, wide * (back - row_dot), 0.0).astype(BF16)
                dv.append(dot(low, grad))
                dk.append(dot(sgrad, qp))
                dqt.append(dot(kt[rows_at(p * 128 + 64 * j, 64), :], sgrad))
            four[2, :, cols] = jnp.where(lane128() < 64, dv[0], dv[1]).astype(BF16)
            four[1, :, cols] = unturn(jnp.where(lane128() < 64, dk[0], dk[1]))
            four[0, :, cols] = unturn(jnp.concatenate(dqt, axis=0).T * 0.125)

    def bias_sums():
        sums[V_BQ : V_BQ + 1, :] = column_sum(four[0])
        sums[V_BK : V_BK + 1, :] = column_sum(four[1])
        sums[V_BV : V_BV + 1, :] = column_sum(four[2])

    def vector_table():
        ready("stats")
        for b in range(8):
            val = jnp.concatenate(
                [sums[0:9, 128 * b : 128 * b + 128], jnp.zeros((1, 128), F32), stats[0:4, :], jnp.zeros((2, 128), F32)],
                axis=0,
            )
            for i in range(4):
                table[b // 2, b % 2, i // 2, i % 2] = val
        for d in range(32):
            table[d // 8, (d // 4) % 2, (d // 2) % 2, d % 2, 9:10, :] = sum_up[
                0:1, 128 * d : 128 * d + 128
            ]
        give(R_VEC, table.at[:, :, :, 1 - c])

    def vector_own():
        wait_bytes(acc[R_VEC], rs.at[R_VEC, 0])
        acc[R_VEC][...] = acc[R_VEC][...] + table[:, :, :, c]

    def token_grad(i):
        w = ring_wait(9 + i)

        @pl.loop(0, 4)
        def _(j):
            cols = lanes_at(j * 256, 256)
            resid[:, cols] = resid[:, cols] + dot_nt(four[i], w[rows_at(j * 256, 256), :])

    def token_out():
        local_copy(resid, grad_h, gsem)

    begin()
    ready("outp")
    rows_sib(R_PROJ, blocks.at[0], cot, stage_p, "p")
    turn()
    acts()
    down_sib(0)
    down_sib(1)
    rows_own(R_PROJ, blocks.at[0], cot)
    down_own(0)
    work = {
        1: [lambda: down_sib(2), lambda: down_sib(3), lambda: up_grad(0), lambda: down_own(1)],
        2: [lambda: up_sib(0), lambda: first_grad(0), lambda: down_own(2), lambda: up_grad(1), lambda: up_sib(1)],
        3: [lambda: down_own(3), lambda: first_grad(1), lambda: up_own(0), lambda: up_grad(2)],
        4: [lambda: up_sib(2), lambda: up_own(1), lambda: first_grad(2), lambda: up_grad(3)],
        5: [lambda: up_sib(3), lambda: first_grad(3), lambda: up_own(2), norm_one, make_mask],
        6: [
            lambda: up_own(3),
            start_attention,
            ctx_back,
            lambda: (ready("ctxp"), rows_sib(R_OUT, blocks.at[0], dg, stage_u.at[0], "u0")),
            lambda: (ready("kt"), ready("q"), ready("v"), ready("cos"), ready("sin"), attend_back(0, 1)),
        ],
        7: [lambda: attend_back(1, 2), lambda: attend_back(2, 3), lambda: rows_own(R_OUT, blocks.at[0], dg)],
        8: [lambda: attend_back(3, 4), lambda: attend_back(4, 6)],
        9: [
            lambda: attend_back(6, 8),
            bias_sums,
            lambda: (ready("tokp"), rows_sib(R_Q, blocks.at[1], four.at[0], stage_u.at[1], "u1")),
            lambda: rows_sib(R_K, blocks.at[1], four.at[1], stage_u.at[0], "u0"),
            lambda: rows_own(R_Q, blocks.at[1], four.at[0]),
        ],
        10: [
            lambda: rows_sib(R_V, blocks.at[1], four.at[2], stage_u.at[1], "u1"),
            vector_table,
            lambda: rows_own(R_K, blocks.at[1], four.at[1]),
            lambda: token_grad(0),
        ],
        11: [vector_own, lambda: rows_own(R_V, blocks.at[1], four.at[2]), lambda: token_grad(1)],
        12: [lambda: token_grad(2), token_out],
    }
    for step in range(count + 2):
        todo = list(work.get(step, []))
        moves = []
        if step < count:
            moves.append(lambda: net(step))
        if 0 <= step - 1 < count:
            moves.append(lambda: add_diagonal(step - 1))
        if 0 <= step - 2 < count:
            moves.append(lambda: add_plane(step - 2))
        while moves or todo:
            if moves:
                moves.pop(0)()
            if todo:
                todo.pop(0)()
            if todo and len(moves) < 2:
                todo.pop(0)()
    for t in range(count):
        finish(t)
    for t in given.values():
        wait_bytes(acc[t], ss.at[t, 0])
    wait_bytes(acc[R_VEC], ss.at[R_VEC, 0])
    wait_bytes(resid, gsem)


def backward_pass(cot_hidden, cot_embed, lengths, offsets, order, weights, kept):
    count = len(BWD_PIECES)
    outs = [jax.ShapeDtypeStruct((512, 1024), F32)]
    outs += [jax.ShapeDtypeStruct((4, r, k), dt) for r, k, dt in BWD_OUTS]
    big = lambda *s: pltpu.VMEM(s, BF16)
    wide = lambda *s: pltpu.VMEM(s, F32)
    scratch = [
        big(3, 1024, 1024),
        big(1024, 128),
        wide(512, 1024),
        wide(512, 1024),
        wide(512, 128),
        wide(512, 128),
        big(512, 1024),
        big(1024, 512),
        big(4, 512, 1024),
        big(4, 512, 1024),
        big(2, 512, 1024),
        big(2, 2, 512, 512),
        big(1024, 512),
        wide(512, 512),
        wide(512, 128),
        wide(512, 128),
        big(512, 128),
        wide(16, 1024),
        wide(8, 128),
        wide(16, 1024),
        wide(1, 4096),
        wide(4, 2, 2, 2, 16, 128),
        big(2, 4, 2, 2, 256, 128),
        big(2, 4, 2, 2, 32, 1024),
        big(4, 2, 2, 32, 128),
    ]
    for lead in ((4, 2, 2), (2, 4), (4,), (4,)):
        for _, _, rows, width, dtype in BWD_PIECES:
            scratch.append(pltpu.VMEM(lead + (rows // 2 if lead == (2, 4) else rows, width), dtype))
    dma = pltpu.SemaphoreType.DMA
    scratch += [dma((count, 8)), dma((count, 8)), dma((count,)), dma((32,)), dma((12,)), dma((2, 2)), dma]
    smem = pl.BlockSpec(memory_space=pltpu.SMEM)
    return pl.pallas_call(
        backward_kernel,
        out_shape=outs,
        in_specs=[ANY, ANY, smem, smem, smem] + [ANY] * (7 + 18),
        out_specs=[ANY] * len(outs),
        scratch_shapes=scratch,
        compiler_params=pltpu.CompilerParams(
            collective_id=1, has_side_effects=True, vmem_limit_bytes=62 * 2**20
        ),
        name="backward_pass",
    )(cot_hidden, cot_embed, lengths, offsets, order, *weights, *kept)


def shards(
    tokens, cot_hidden, cot_embed, lengths, offsets, pack_order,
    w_query, b_query, w_key, b_key, w_value, b_value, w_out, b_out, gain_attn, shift_attn,
    w_up, b_up, w_down, b_down, gain_ffn, shift_ffn, w_proj,
):
    device = lax.axis_index("dp")
    parts = (b_query, b_key, b_value, b_out, gain_attn, shift_attn, b_down, gain_ffn, shift_ffn, b_up)
    vec = jnp.concatenate(parts + (jnp.zeros((96,), BF16),)).astype(F32).reshape(16, 32)
    done = forward_pass(
        tokens, vec, lengths, offsets, pack_order,
        (w_query, w_key, w_value, w_out, w_up, w_proj, w_down),
    )
    weights = [w.reshape(-1, w.shape[-1]) for w in done[:7]]
    hidden, embed = done[7 + 14], done[7 + 15]
    kept = list(done[7 : 7 + 14]) + list(done[7 + 16 :])
    back = backward_pass(cot_hidden, cot_embed, lengths, offsets, pack_order, weights, kept)
    proj, down, up, out, query, key, vec, val = (
        jnp.sum(part.astype(F32), axis=0) for part in back[1:]
    )
    own = lax.dynamic_slice(vec, (0, (device % 4) * 32), (9, 32))
    stats = jnp.sum(vec[10:14], axis=1)
    rms_stats = jnp.sqrt(stats[:3] / (stats[3] * (1024 / 128)))
    return (
        hidden, embed, back[0],
        query, own[V_BQ], key, own[V_BK], val, own[V_BV], out, own[V_BO],
        own[V_GA], own[V_SA], up, vec[9], down.T, own[V_BD], own[V_GF], own[V_SF],
        proj, rms_stats,
    )


def shards_any(
    tokens,
    cot_hidden,
    cot_embed,
    lengths,
    offsets,
    pack_order,
    w_query,
    b_query,
    w_key,
    b_key,
    w_value,
    b_value,
    w_out,
    b_out,
    gain_attn,
    shift_attn,
    w_up,
    b_up,
    w_down,
    b_down,
    gain_ffn,
    shift_ffn,
    w_proj,
):
    gathered = (
        lax.all_gather(w_query, "dp", axis=0, tiled=True),
        lax.all_gather(w_key, "dp", axis=0, tiled=True),
        lax.all_gather(w_value, "dp", axis=0, tiled=True),
        lax.all_gather(w_out, "dp", axis=0, tiled=True),
        lax.all_gather(w_up, "dp", axis=0, tiled=True),
        lax.all_gather(w_down, "dp", axis=0, tiled=True),
        lax.all_gather(w_proj, "dp", axis=0, tiled=True),
        lax.all_gather(b_query, "dp", axis=0, tiled=True),
        lax.all_gather(b_key, "dp", axis=0, tiled=True),
        lax.all_gather(b_value, "dp", axis=0, tiled=True),
        lax.all_gather(b_out, "dp", axis=0, tiled=True),
        lax.all_gather(gain_attn, "dp", axis=0, tiled=True),
        lax.all_gather(shift_attn, "dp", axis=0, tiled=True),
        lax.all_gather(b_up, "dp", axis=0, tiled=True),
        lax.all_gather(b_down, "dp", axis=0, tiled=True),
        lax.all_gather(gain_ffn, "dp", axis=0, tiled=True),
        lax.all_gather(shift_ffn, "dp", axis=0, tiled=True),
    )
    wt_query, wt_key, wt_value, wt_out, wt_up, wt_down, wt_proj = gathered[:7]
    vectors = [piece.astype(jnp.float32) for piece in gathered[7:]]
    (
        bias_query,
        bias_key,
        bias_value,
        bias_out,
        norm_gain_a,
        norm_shift_a,
        bias_up,
        bias_down,
        norm_gain_f,
        norm_shift_f,
    ) = vectors
    row_count = tokens.shape[0]
    model_width = tokens.shape[1]
    head_count = H
    head_dim = model_width // head_count
    device = lax.axis_index("dp")
    slots = jnp.arange(pack_order.shape[0], dtype=jnp.int32)
    pack_id = jnp.sum(jnp.where(slots == device, pack_order, 0))
    length = jnp.sum(jnp.where(slots == pack_id, lengths, 0))
    offset = jnp.sum(jnp.where(slots == pack_id, offsets, 0))
    row_index = jnp.arange(row_count, dtype=jnp.int32)
    is_valid = (row_index >= offset) & (row_index < offset + length)
    keep_rows = is_valid.astype(jnp.float32)[:, None]
    cosine, sine_part = rope_tables((row_index - offset).astype(jnp.float32), head_dim)
    query_pre = matmul(tokens, wt_query) + bias_query
    key_pre = matmul(tokens, wt_key) + bias_key
    value_low = (
        (matmul(tokens, wt_value) + bias_value)
        .astype(jnp.bfloat16)
        .reshape(row_count, head_count, head_dim)
    )
    query_rot = rotate(
        query_pre.reshape(row_count, head_count, head_dim), cosine, sine_part
    ).astype(jnp.bfloat16)
    key_rot = rotate(key_pre.reshape(row_count, head_count, head_dim), cosine, sine_part).astype(
        jnp.bfloat16
    )
    score_scale = 1.0 / math.sqrt(head_dim)
    key_valid = is_valid[None, None, :]
    allowed = is_valid[None, :, None] & key_valid
    masked = masked_scores(query_rot, key_rot, allowed, score_scale)
    row_top = jnp.max(masked, axis=-1, keepdims=True)
    exponent = jnp.exp(masked - row_top)
    row_total = jnp.sum(exponent, axis=-1, keepdims=True)
    prob_low = (exponent / row_total).astype(jnp.bfloat16)
    contexts = jnp.einsum("hqk,khd->qhd", prob_low, value_low, preferred_element_type=jnp.float32)
    log_totals = row_top + jnp.log(row_total)
    context = contexts.astype(jnp.bfloat16).reshape(row_count, model_width)
    tokens_wide = tokens.astype(jnp.float32)
    attn_branch = matmul(context, wt_out) + bias_out
    first, normed_one, inverse_one = norm_forward(
        tokens_wide + attn_branch, norm_gain_a, norm_shift_a
    )
    first_low = first.astype(jnp.bfloat16)
    up_pre = matmul(first_low, wt_up) + bias_up
    act_full, gelu_pull = jax.vjp(exact_gelu, up_pre)
    act_low = act_full.astype(jnp.bfloat16)
    down_branch = matmul(act_low, wt_down) + bias_down
    out, normed_two, inverse_two = norm_forward(first + down_branch, norm_gain_f, norm_shift_f)
    out_low = out.astype(jnp.bfloat16)
    hidden = (out * keep_rows).astype(jnp.bfloat16)
    embedding = (matmul(out_low, wt_proj) * keep_rows).astype(jnp.bfloat16)
    stat_sums = lax.psum(
        (
            jnp.sum(keep_rows * tokens_wide * tokens_wide),
            jnp.sum(keep_rows * attn_branch * attn_branch),
            jnp.sum(keep_rows * down_branch * down_branch),
            jnp.sum(keep_rows),
        ),
        "dp",
    )
    rms_stats = jnp.sqrt(
        jnp.stack([stat_sums[0], stat_sums[1], stat_sums[2]]) / (stat_sums[3] * model_width)
    )
    backward_set = (
        lax.all_gather(w_query, "dp", axis=0, tiled=True),
        lax.all_gather(w_key, "dp", axis=0, tiled=True),
        lax.all_gather(w_value, "dp", axis=0, tiled=True),
        lax.all_gather(w_out, "dp", axis=0, tiled=True),
        lax.all_gather(w_up, "dp", axis=0, tiled=True),
        lax.all_gather(w_down, "dp", axis=0, tiled=True),
        lax.all_gather(w_proj, "dp", axis=0, tiled=True),
        lax.all_gather(b_query, "dp", axis=0, tiled=True),
        lax.all_gather(b_key, "dp", axis=0, tiled=True),
        lax.all_gather(b_value, "dp", axis=0, tiled=True),
        lax.all_gather(b_out, "dp", axis=0, tiled=True),
        lax.all_gather(gain_attn, "dp", axis=0, tiled=True),
        lax.all_gather(shift_attn, "dp", axis=0, tiled=True),
        lax.all_gather(b_up, "dp", axis=0, tiled=True),
        lax.all_gather(b_down, "dp", axis=0, tiled=True),
        lax.all_gather(gain_ffn, "dp", axis=0, tiled=True),
        lax.all_gather(shift_ffn, "dp", axis=0, tiled=True),
    )
    back_query, back_key, back_value, back_out, back_up, back_down, back_proj = backward_set[:7]
    back_gain_a = backward_set[11].astype(jnp.float32)
    back_gain_f = backward_set[15].astype(jnp.float32)
    cot_low = jnp.where(is_valid[:, None], cot_embed, jnp.zeros_like(cot_embed))
    grad_w_proj = matmul_tn(out_low, cot_low)
    grad_out = keep_rows * cot_hidden.astype(jnp.float32) + matmul_nt(cot_low, back_proj)
    grad_resid_two, grad_gain_f, grad_shift_f = norm_backward(
        grad_out, normed_two, inverse_two, back_gain_f
    )
    down_grad = grad_resid_two.astype(jnp.bfloat16)
    grad_w_down = matmul_tn(act_low, down_grad)
    grad_b_down = jnp.sum(down_grad.astype(jnp.float32), axis=0)
    up_grad = gelu_pull(matmul_nt(down_grad, back_down))[0].astype(jnp.bfloat16)
    grad_w_up = matmul_tn(first_low, up_grad)
    grad_b_up = jnp.sum(up_grad.astype(jnp.float32), axis=0)
    grad_first = grad_resid_two + matmul_nt(up_grad, back_up)
    grad_resid_one, grad_gain_a, grad_shift_a = norm_backward(
        grad_first, normed_one, inverse_one, back_gain_a
    )
    attn_grad = grad_resid_one.astype(jnp.bfloat16)
    grad_w_out = matmul_tn(context, attn_grad)
    grad_b_out = jnp.sum(attn_grad.astype(jnp.float32), axis=0)
    ctx_grad = (
        matmul_nt(attn_grad, back_out).astype(jnp.bfloat16).reshape(row_count, head_count, head_dim)
    )
    allowed = is_valid[None, :, None] & key_valid
    masked = masked_scores(query_rot, key_rot, allowed, score_scale)
    prob_full = jnp.exp(masked - log_totals)
    prob_low = prob_full.astype(jnp.bfloat16)
    prob_grad = jnp.einsum("qhd,khd->hqk", ctx_grad, value_low, preferred_element_type=jnp.float32)
    value_sum = jnp.einsum("hqk,qhd->khd", prob_low, ctx_grad, preferred_element_type=jnp.float32)
    row_dot = jnp.sum(prob_full * prob_grad, axis=-1, keepdims=True)
    score_grad = jnp.where(allowed, prob_full * (prob_grad - row_dot), 0.0).astype(jnp.bfloat16)
    query_parts = (
        jnp.einsum("hqk,khd->qhd", score_grad, key_rot, preferred_element_type=jnp.float32)
        * score_scale
    )
    key_sum = (
        jnp.einsum("hqk,qhd->khd", score_grad, query_rot, preferred_element_type=jnp.float32)
        * score_scale
    )
    query_grad = (
        unrotate(query_parts, cosine, sine_part)
        .reshape(row_count, model_width)
        .astype(jnp.bfloat16)
    )
    key_grad = (
        unrotate(key_sum, cosine, sine_part).reshape(row_count, model_width).astype(jnp.bfloat16)
    )
    value_grad = value_sum.reshape(row_count, model_width).astype(jnp.bfloat16)
    grad_w_query = matmul_tn(tokens, query_grad)
    grad_b_query = jnp.sum(query_grad.astype(jnp.float32), axis=0)
    grad_w_key = matmul_tn(tokens, key_grad)
    grad_b_key = jnp.sum(key_grad.astype(jnp.float32), axis=0)
    grad_w_value = matmul_tn(tokens, value_grad)
    grad_b_value = jnp.sum(value_grad.astype(jnp.float32), axis=0)
    grad_tokens = (
        grad_resid_one
        + matmul_nt(query_grad, back_query)
        + matmul_nt(key_grad, back_key)
        + matmul_nt(value_grad, back_value)
    )
    all_parts = (
        lax.psum_scatter(grad_w_query, "dp", scatter_dimension=0, tiled=True),
        lax.psum_scatter(grad_w_key, "dp", scatter_dimension=0, tiled=True),
        lax.psum_scatter(grad_w_value, "dp", scatter_dimension=0, tiled=True),
        lax.psum_scatter(grad_w_out, "dp", scatter_dimension=0, tiled=True),
        lax.psum_scatter(grad_b_query, "dp", scatter_dimension=0, tiled=True),
        lax.psum_scatter(grad_b_key, "dp", scatter_dimension=0, tiled=True),
        lax.psum_scatter(grad_b_value, "dp", scatter_dimension=0, tiled=True),
        lax.psum_scatter(grad_b_out, "dp", scatter_dimension=0, tiled=True),
        lax.psum_scatter(grad_gain_a, "dp", scatter_dimension=0, tiled=True),
        lax.psum_scatter(grad_shift_a, "dp", scatter_dimension=0, tiled=True),
        lax.psum_scatter(grad_w_up, "dp", scatter_dimension=0, tiled=True),
        lax.psum_scatter(grad_w_down, "dp", scatter_dimension=0, tiled=True),
        lax.psum_scatter(grad_w_proj, "dp", scatter_dimension=0, tiled=True),
        lax.psum_scatter(grad_b_up, "dp", scatter_dimension=0, tiled=True),
        lax.psum_scatter(grad_b_down, "dp", scatter_dimension=0, tiled=True),
        lax.psum_scatter(grad_gain_f, "dp", scatter_dimension=0, tiled=True),
        lax.psum_scatter(grad_shift_f, "dp", scatter_dimension=0, tiled=True),
    )
    attn_parts = all_parts[:10]
    ffn_parts = all_parts[10:]
    return (
        hidden,
        embedding,
        grad_tokens,
        attn_parts[0],
        attn_parts[4],
        attn_parts[1],
        attn_parts[5],
        attn_parts[2],
        attn_parts[6],
        attn_parts[3],
        attn_parts[7],
        attn_parts[8],
        attn_parts[9],
        ffn_parts[0],
        ffn_parts[3],
        ffn_parts[1],
        ffn_parts[4],
        ffn_parts[5],
        ffn_parts[6],
        ffn_parts[2],
        rms_stats,
    )


def solution(mesh):
    fast = mesh.shape["dp"] == 32
    placed = (
        P("dp", None),
        P("dp", None),
        P("dp", None),
        P(),
        P(),
        P(),
        P("dp", None),
        P("dp"),
        P("dp", None),
        P("dp"),
        P("dp", None),
        P("dp"),
        P("dp", None),
        P("dp"),
        P("dp"),
        P("dp"),
        P("dp", None),
        P("dp"),
        P("dp", None),
        P("dp"),
        P("dp"),
        P("dp"),
        P("dp", None),
    )
    return jax.shard_map(
        shards if fast else shards_any,
        mesh=mesh,
        in_specs=placed,
        out_specs=(
            P("dp", None),
            P("dp", None),
            P("dp", None),
            P("dp", None),
            P("dp"),
            P("dp", None),
            P("dp"),
            P("dp", None),
            P("dp"),
            P("dp", None),
            P("dp"),
            P("dp"),
            P("dp"),
            P("dp", None),
            P("dp"),
            P("dp", None),
            P("dp"),
            P("dp"),
            P("dp"),
            P("dp", None),
            P(),
        ),
        check_vma=False,
    )
```

```python
import functools
import math

import jax
import jax.numpy as jnp
from jax import lax
from jax.experimental import pallas as pl
from jax.experimental.pallas import tpu as pltpu
from jax.sharding import PartitionSpec as P

MESH = pl.DeviceIdType.MESH

H = 16


eps_norm = 1e-05
neg_large = -1e30


def matmul(left, right):
    return jnp.dot(left, right, preferred_element_type=jnp.float32)


def matmul_nt(left, right):
    return lax.dot_general(
        left, right, (((1,), (1,)), ((), ())), preferred_element_type=jnp.float32
    )


def matmul_tn(left, right):
    return lax.dot_general(
        left, right, (((0,), (0,)), ((), ())), preferred_element_type=jnp.float32
    )


def exact_gelu(values):
    return jax.nn.gelu(values, approximate=False)


def norm_forward(values, gain, shift):
    row_mean = jnp.mean(values, axis=-1, keepdims=True)
    centred = values - row_mean
    inverse = lax.rsqrt(jnp.mean(centred * centred, axis=-1, keepdims=True) + eps_norm)
    normed = centred * inverse
    return (normed * gain + shift, normed, inverse)


def norm_backward(grad_in, normed, inverse, gain):
    scaled = grad_in * gain
    adjusted = (
        scaled
        - jnp.mean(scaled, axis=-1, keepdims=True)
        - normed * jnp.mean(scaled * normed, axis=-1, keepdims=True)
    )
    return (adjusted * inverse, jnp.sum(grad_in * normed, axis=0), jnp.sum(grad_in, axis=0))


def rope_tables(position, head_dim):
    half_dim = head_dim // 2
    freq_index = jnp.arange(half_dim, dtype=jnp.float32)
    frequency = jnp.exp(-math.log(10000.0) * 2.0 * freq_index / head_dim)
    angles = position[:, None] * frequency[None, :]
    return (jnp.cos(angles)[:, None, :], jnp.sin(angles)[:, None, :])


def rotate(values, cosine, sine_part):
    half_dim = values.shape[-1] // 2
    first_half = values[..., :half_dim]
    second = values[..., half_dim:]
    return jnp.concatenate(
        [first_half * cosine - second * sine_part, second * cosine + first_half * sine_part],
        axis=-1,
    )


def unrotate(grad_in, cosine, sine_part):
    half_dim = grad_in.shape[-1] // 2
    first_half = grad_in[..., :half_dim]
    second = grad_in[..., half_dim:]
    return jnp.concatenate(
        [first_half * cosine + second * sine_part, second * cosine - first_half * sine_part],
        axis=-1,
    )


def masked_scores(query_block, key_rot, allowed, score_scale):
    raw_scores = jnp.einsum(
        "qhd,khd->hqk", query_block, key_rot, preferred_element_type=jnp.float32
    )
    return jnp.where(allowed, raw_scores * score_scale, neg_large)


def device_at(z, y, x, c):
    return ((z * 2 + y) * 2 + x) * 2 + c


def wait_bytes(ref, sem):
    pltpu.make_async_copy(ref, ref, sem).wait()


def send(src, dst, sem_out, sem_in, target):
    pltpu.make_async_remote_copy(
        src_ref=src,
        dst_ref=dst,
        send_sem=sem_out,
        recv_sem=sem_in,
        device_id=(target,),
        device_id_type=MESH,
    ).start()


F32, BF16 = jnp.float32, jnp.bfloat16
ANY = pl.BlockSpec(memory_space=pl.ANY)
FWD_TENSORS = (
    (16, 128, F32),
    (32, 1024, BF16),
    (32, 1024, BF16),
    (32, 1024, BF16),
    (32, 1024, BF16),
    (32, 4096, BF16),
    (32, 128, BF16),
    (128, 1024, BF16),
)
FWD_PIECES = (
    ((0, 0, 128), (1, 0, 1024), (2, 0, 1024), (3, 0, 1024), (4, 0, 1024))
    + tuple((5, 1024 * k, 1024) for k in range(4))
    + ((6, 0, 128),)
    + tuple((7, 256 * k, 256) for k in range(4))
)
P_VEC, P_Q, P_K, P_V, P_O, P_UP, P_PROJ, P_DOWN = 0, 1, 2, 3, 4, 5, 9, 10
V_BQ, V_BK, V_BV, V_BO, V_GA, V_SA, V_BD, V_GF, V_SF = range(9)


def dot(left, right):
    return jnp.dot(left, right, preferred_element_type=F32)


def dot_nt(left, right):
    return lax.dot_general(left, right, (((1,), (1,)), ((), ())), preferred_element_type=F32)


def local_copy(src, dst, sem):
    pltpu.make_async_copy(src, dst, sem).start()


def lanes_at(start, size):
    return pl.ds(pl.multiple_of(start, 128), size)


def rows_at(start, size):
    return pl.ds(pl.multiple_of(start, size), size)


def place():
    me = lax.axis_index("dp")
    return me // 8, (me // 4) % 2, (me // 2) % 2, me % 2


def greet_start(z, y, x, c):
    others = [(z + k) % 4 for k in (1, 2, 3)]
    peers = [device_at(z, y, 1 - x, c), device_at(z, 1 - y, x, c), device_at(z, y, x, 1 - c)]
    peers += [device_at(zz, y, x, c) for zz in others]
    barrier = pltpu.get_barrier_semaphore()
    for peer in peers:
        pl.semaphore_signal(barrier, inc=1, device_id=(peer,), device_id_type=MESH)


def greet_end():
    pl.semaphore_wait(pltpu.get_barrier_semaphore(), 6)


def transpose_blocks(src, dst):
    @pl.loop(0, src.shape[1] // 128)
    def _(j):
        block = src[:, lanes_at(j * 128, 128)].T
        for b in range(4):
            dst[b % 2, rows_at((2 * j + b // 2) * 32, 32), :] = block[32 * b : 32 * b + 32]


def forward_kernel(
    tokens_h, cot_h, cote_h, lengths_s, offsets_s, order_s, *refs
):
    vectors = refs[:10]
    refs = refs[10:]
    src = (None,) + refs[:7]
    refs = refs[7:]
    full = (None,) + refs[:7]
    (
        q_h, kt_h, v_h, prob_h, ctxp_h, n1_h, inv1_h, firstp_h, tokp_h, act_h, slope_h,
        back_h, dg_h, outp_h, hidden_h, embed_h, vecs_h, stats_h, cos_h, sin_h, sums_h,
    ) = refs[7:28]
    refs = refs[28:]
    (
        tok, packed, table, vecs, bias_up, cosine, sine, mask, stats,
        q, k, v, kt, vt, prob, ctx, ctxp, tokp, resid, n1, inv1, low, lowp, act, slope, back, sums,
        hidden, embed, outp,
    ) = refs[:30]
    refs = refs[30:]
    count = len(FWD_PIECES)
    wbuf = (None,) + refs[: count - 1]
    mybuf = (None,) + refs[count - 1 : 2 * count - 2]
    ss, rs, ls, ld, os, ps, ins, ms = refs[2 * count - 2 :]
    z, y, x, c = place()
    me = device_at(z, y, x, c)
    near_x, near_y = device_at(z, y, 1 - x, c), device_at(z, 1 - y, x, c)
    sibling = device_at(z, y, x, 1 - c)
    others = [(z + kk) % 4 for kk in (1, 2, 3)]

    greet_start(z, y, x, c)
    for t in range(1, count):
        tensor, first, width = FWD_PIECES[t]
        local_copy(src[tensor].at[:, pl.ds(first, width)], mybuf[t], ms.at[t])
    local_copy(tokens_h, tok, ins.at[1])
    local_copy(cot_h, hidden, ins.at[0])
    local_copy(cote_h, embed, ins.at[2])

    def home(t, *lead):
        tensor, first, width = FWD_PIECES[t]
        if t == P_VEC:
            return table.at[lead]
        return full[tensor].at[lead + (slice(None), pl.ds(first, width))]

    def part(t, lead, rows):
        tensor, first, width = FWD_PIECES[t]
        if t == P_VEC:
            return table.at[lead + (rows,)]
        return full[tensor].at[lead + (rows, pl.ds(first, width))]

    def own(t):
        tensor, first, width = FWD_PIECES[t]
        piece = packed if t == P_VEC else src[tensor].at[:, pl.ds(first, width)]
        mine = home(t, z, y, x, c)
        for zz in others:
            send(piece, mine, ss.at[t, 0], rs.at[t, 0], device_at(zz, y, x, c))
        send(piece, mine, ss.at[t, 1], rs.at[t, 1], near_x)
        send(piece, mine, ss.at[t, 2], rs.at[t, 2], near_y)
        if t == P_VEC:
            local_copy(packed, mine, ls.at[t])
        else:
            wait_bytes(mybuf[t], ms.at[t])
            local_copy(mybuf[t], mine, ls.at[t])

    def column(t):
        wait_bytes(home(t, pl.ds(0, 3), 0, 0, 0), rs.at[t, 0])
        for zz in others:
            block = home(t, zz, y, x, c)
            send(block, block, ss.at[t, 3], rs.at[t, 3], near_x)
            send(block, block, ss.at[t, 4], rs.at[t, 4], near_y)

    def plane(t):
        half = FWD_TENSORS[FWD_PIECES[t][0]][0] // 2
        wait_bytes(home(t, 0, 0, 0, 0), rs.at[t, 1])
        wait_bytes(home(t, pl.ds(0, 3), 0, 0, 0), rs.at[t, 3])
        block = part(t, (slice(None), y, 1 - x, c), pl.ds(0, half))
        send(block, block, ss.at[t, 5], rs.at[t, 5], near_y)
        wait_bytes(home(t, 0, 0, 0, 0), rs.at[t, 2])
        wait_bytes(home(t, pl.ds(0, 3), 0, 0, 0), rs.at[t, 4])
        block = part(t, (slice(None), 1 - y, x, c), pl.ds(half, half))
        send(block, block, ss.at[t, 6], rs.at[t, 6], near_x)

    def pair(t):
        half = FWD_TENSORS[FWD_PIECES[t][0]][0] // 2
        for kind in (5, 6):
            wait_bytes(part(t, (slice(None), 0, 0, 0), pl.ds(0, half)), rs.at[t, kind])
        wait_bytes(home(t, 0, 0, 0, 0), ls.at[t])
        block = home(t, slice(None), slice(None), slice(None), c)
        send(block, block, ss.at[t, 7], rs.at[t, 7], sibling)

    def arrive(t):
        everything = home(t, slice(None), slice(None), slice(None), 0)
        wait_bytes(everything, rs.at[t, 7])
        if t != P_VEC:
            tensor, first, width = FWD_PIECES[t]
            local_copy(
                full[tensor].at[:, :, :, :, :, pl.ds(first, width)], wbuf[t], ld.at[t]
            )

    def loaded(t):
        wait_bytes(wbuf[t], ld.at[t])

    def sent(t):
        half = FWD_TENSORS[FWD_PIECES[t][0]][0] // 2
        one = home(t, 0, 0, 0, 0)
        three = home(t, pl.ds(0, 3), 0, 0, 0)
        halves = part(t, (slice(None), 0, 0, 0), pl.ds(0, half))
        everything = home(t, slice(None), slice(None), slice(None), 0)
        for kind, ref in enumerate((three, one, one, three, three, halves, halves, everything)):
            wait_bytes(ref, ss.at[t, kind])

    pack = order_s[me]
    length, offset = lengths_s[pack], offsets_s[pack]
    saved = []

    def save(value, out):
        n = len(saved)
        local_copy(value, out, os.at[n])
        saved.append((out, os.at[n]))

    def row_valid(rows, start):
        r = lax.broadcasted_iota(jnp.int32, (rows, 1), 0) + start
        return ((r >= offset) & (r < offset + length)).astype(F32)

    def pack_vectors():
        lane = lax.broadcasted_iota(jnp.int32, (1, 128), 1)
        for i in range(9):
            val = vectors[i][...].astype(F32).reshape(1, 32)
            wide = jnp.concatenate([val] * 4, axis=1)
            packed[i : i + 1, :] = jnp.where(lane // 32 == me % 4, wide, 0.0)
        packed[9:10, :] = vectors[9][...].astype(F32).reshape(1, 128)
        packed[10:16, :] = jnp.zeros((6, 128), F32)

    def prepare():
        lane = lax.broadcasted_iota(jnp.int32, (1, 128), 1)
        freq = jnp.exp((lane % 32).astype(F32) * (-math.log(10000.0) * 2.0 / 64))

        @pl.loop(0, 8)
        def _(i):
            r = lax.broadcasted_iota(jnp.int32, (64, 1), 0) + i * 64
            angle = (r - offset).astype(F32) * freq
            cosine[rows_at(i * 64, 64), :] = jnp.cos(angle)
            sine[rows_at(i * 64, 64), :] = jnp.where(lane % 64 < 32, -1.0, 1.0) * jnp.sin(angle)

        s = lax.broadcasted_iota(jnp.int32, (1, 512), 1)
        col_valid = ((s >= offset) & (s < offset + length)).astype(F32)
        stats[...] = jnp.zeros_like(stats)

        @pl.loop(0, 8)
        def _(i):
            mask[rows_at(i * 64, 64), :] = row_valid(64, i * 64) * col_valid

        stats[3:4, :] = jnp.broadcast_to(
            jnp.sum(col_valid, axis=1, keepdims=True), (1, 128)
        )
        wait_bytes(tok, ins.at[1])

        @pl.loop(0, 8)
        def _(i):
            t32 = tok[rows_at(i * 64, 64), :].astype(F32)
            add_stat(0, jnp.sum(row_valid(64, i * 64) * t32 * t32, axis=0, keepdims=True))

        transpose_blocks(tok, tokp)
        save(tokp, tokp_h)
        save(cosine, cos_h)
        save(sine, sin_h)

    def add_stat(row, wide):
        total = wide[:, 0:128]
        for i in range(1, wide.shape[1] // 128):
            total = total + wide[:, 128 * i : 128 * i + 128]
        stats[row : row + 1, :] = stats[row : row + 1, :] + total

    def unpack_vectors():
        grouped = table[...].reshape(8, 4, 16, 128).sum(axis=1)
        for b in range(8):
            vecs[:, 128 * b : 128 * b + 128] = grouped[b]
        for d in range(32):
            bias_up[0:1, 128 * d : 128 * d + 128] = table[
                d // 8, (d // 4) % 2, (d // 2) % 2, d % 2, 9:10, :
            ]
        save(vecs, vecs_h)

    def weight(t, first, width):
        w = wbuf[t]
        return w[:, :, :, :, :, lanes_at(first, width)].reshape(-1, width)

    lane128 = lambda: lax.broadcasted_iota(jnp.int32, (1, 128), 1)

    def rotary(t, bias, dst, scale, transposed, j0, j1):
        @pl.loop(j0, j1)
        def _(j):
            pre = dot(tok[...], weight(t, j * 256, 256)) + vecs[bias : bias + 1, lanes_at(j * 256, 256)]
            for b in range(2):
                part_in = pre[:, 128 * b : 128 * b + 128]
                swapped = jnp.where(
                    lane128() % 64 < 32, pltpu.roll(part_in, 96, 1), pltpu.roll(part_in, 32, 1)
                )
                turned = (part_in * cosine[...] + swapped * sine[...]).astype(BF16)
                if transposed is not None:
                    transposed[rows_at(j * 256 + 128 * b, 128), :] = turned.T
                dst[:, lanes_at(j * 256 + 128 * b, 128)] = turned * jnp.asarray(scale, BF16)

    def value(j0, j1):
        @pl.loop(j0, j1)
        def _(j):
            pre = dot(tok[...], weight(P_V, j * 256, 256)) + vecs[V_BV : V_BV + 1, lanes_at(j * 256, 256)]
            val = pre.astype(BF16)
            v[:, lanes_at(j * 256, 256)] = val
            vt[rows_at(j * 256, 256), :] = val.T

    def attend(p0, p1):
        @pl.loop(p0, p1)
        def _(p):
            cols = lanes_at(p * 128, 128)
            qp, kp = q[:, cols], k[:, cols]
            pieces = []
            for j in range(2):
                keep = lane128() < 64 if j == 0 else lane128() >= 64
                scores = dot_nt(jnp.where(keep, kp, jnp.zeros((), BF16)), qp)
                scores = jnp.where(mask[...] > 0.0, scores, -1e30)
                top = jnp.max(scores, axis=0, keepdims=True)
                expo = jnp.exp(scores - top)
                total = jnp.sum(expo, axis=0, keepdims=True)
                weights = (expo * (1.0 / total)).astype(BF16)

                @pl.when(p > 0)
                def _():
                    wait_bytes(prob.at[j], ps.at[j])

                prob[j] = weights
                local_copy(prob.at[j], prob_h.at[p, j], ps.at[j])
                mixed = dot(vt[rows_at(p * 128 + 64 * j, 64), :], weights).astype(BF16)
                for b in range(2):
                    ctxp[b, rows_at((2 * p + j) * 32, 32), :] = mixed[32 * b : 32 * b + 32]
                pieces.append(mixed)
            ctx[:, cols] = jnp.concatenate(pieces, axis=0).T

    def attended():
        for j in range(2):
            wait_bytes(prob.at[j], ps.at[j])
        save(ctxp, ctxp_h)

    def project():
        loaded(P_O)

        @pl.loop(0, 4)
        def _(j):
            cols = lanes_at(j * 256, 256)
            branch = dot(ctx[...], weight(P_O, j * 256, 256)) + vecs[V_BO : V_BO + 1, cols]
            add_stat(1, jnp.sum(row_valid(512, 0) * branch * branch, axis=0, keepdims=True))
            resid[:, cols] = branch + tok[:, cols].astype(F32)

    def normalise(i):
        rows = rows_at(i * 32, 32)
        val = resid[rows, :]
        mean = jnp.sum(val, axis=1, keepdims=True) * (1.0 / 1024)
        centred = val - mean
        scale = lax.rsqrt(jnp.sum(centred * centred, axis=1, keepdims=True) * (1.0 / 1024) + eps_norm)
        return rows, centred * scale, scale

    def norm_first():
        @pl.loop(0, 16)
        def _(i):
            rows, normed, scale = normalise(i)
            n1[rows, :] = normed
            inv1[rows, :] = jnp.broadcast_to(scale, (32, 128))
            low[rows, :] = (normed * vecs[V_GA : V_GA + 1, :] + vecs[V_SA : V_SA + 1, :]).astype(BF16)

        save(n1, n1_h)
        save(inv1, inv1_h)
        transpose_blocks(low, lowp)
        save(lowp, firstp_h)

    def incoming():
        loaded(P_PROJ)
        wait_bytes(hidden, ins.at[0])
        wait_bytes(embed, ins.at[2])
        cot = jnp.where(row_valid(512, 0) > 0.0, embed[...].astype(F32), 0.0).astype(BF16)
        w = weight(P_PROJ, 0, 128)
        for j in range(4):
            cols = pl.ds(256 * j, 256)
            back[:, cols] = row_valid(512, 0) * hidden[:, cols].astype(F32) + dot_nt(
                cot, w[256 * j : 256 * j + 256]
            )
        sums[...] = jnp.zeros_like(sums)

    def expand(k0, j0, j1):
        @pl.loop(j0, j1)
        def _(j):
            cols = lanes_at(k0 * 1024 + j * 256, 256)
            pre = dot(low[...], weight(P_UP + k0, j * 256, 256)) + bias_up[0:1, cols]
            cdf = 0.5 * (1.0 + lax.erf(pre * math.sqrt(0.5)))
            val = (pre * cdf).astype(BF16)
            pdf = jnp.exp(pre * pre * -0.5) * (1.0 / math.sqrt(2 * math.pi))
            slope[:, cols] = (cdf + pre * pdf).astype(BF16)
            half = lanes_at(k0 * 512 + j * 128, 128)
            act[0, :, half] = val[:, :128]
            act[1, :, half] = val[:, 128:]

    def contract(k0):
        cols = pl.ds(256 * k0, 256)
        w = wbuf[P_DOWN + k0]
        branch = dot(act[0], w[:, :, :, 0].reshape(2048, 256))
        branch = branch + dot(act[1], w[:, :, :, 1].reshape(2048, 256)) + vecs[V_BD : V_BD + 1, cols]
        add_stat(2, jnp.sum(row_valid(512, 0) * branch * branch, axis=0, keepdims=True))
        first = n1[:, cols] * vecs[V_GA : V_GA + 1, cols] + vecs[V_SA : V_SA + 1, cols]
        resid[:, cols] = first + branch

    def norm_second():
        @pl.loop(0, 16)
        def _(i):
            rows, normed, scale = normalise(i)
            gain = vecs[V_GF : V_GF + 1, :]
            out = normed * gain + vecs[V_SF : V_SF + 1, :]
            low[rows, :] = out.astype(BF16)
            hidden[rows, :] = (out * row_valid(32, i * 32)).astype(BF16)
            grad = back[rows, :]
            scaled = grad * gain
            mean = jnp.sum(scaled, axis=1, keepdims=True) * (1.0 / 1024)
            cross = jnp.sum(scaled * normed, axis=1, keepdims=True) * (1.0 / 1024)
            res = (scaled - mean - normed * cross) * scale
            back[rows, :] = res
            ctx[rows, :] = res.astype(BF16)
            sums[0:1, :] = sums[0:1, :] + jnp.sum(grad * normed, axis=0, keepdims=True)
            sums[1:2, :] = sums[1:2, :] + jnp.sum(grad, axis=0, keepdims=True)

        save(ctx, dg_h)
        save(back, back_h)
        save(hidden, hidden_h)
        save(sums, sums_h)
        embed[...] = (dot(low[...], weight(P_PROJ, 0, 128)) * row_valid(512, 0)).astype(BF16)
        save(embed, embed_h)
        transpose_blocks(low, outp)
        save(outp, outp_h)
        save(stats, stats_h)

    pack_vectors()
    greet_end()
    for t in range(4):
        own(t)
    prepare()
    work = {
        4: [unpack_vectors],
        5: [lambda: (loaded(P_Q), rotary(P_Q, V_BQ, q, 0.125, None, 0, 4), save(q, q_h))],
        6: [lambda: (loaded(P_K), rotary(P_K, V_BK, k, 1.0, kt, 0, 4), save(kt, kt_h))],
        7: [lambda: (loaded(P_V), value(0, 4), save(v, v_h)), lambda: attend(0, 2)],
        8: [lambda: attend(2, 4), lambda: attend(4, 6)],
        9: [lambda: (attend(6, 8), attended()), project, norm_first],
        10: [lambda: (loaded(P_UP), expand(0, 0, 2)), lambda: expand(0, 2, 4)],
        11: [lambda: (loaded(P_UP + 1), expand(1, 0, 2)), lambda: expand(1, 2, 4)],
        12: [lambda: (loaded(P_UP + 2), expand(2, 0, 2)), lambda: expand(2, 2, 4)],
        13: [lambda: (loaded(P_UP + 3), expand(3, 0, 2)), lambda: expand(3, 2, 4)],
        14: [lambda: (save(act, act_h), save(slope, slope_h)), incoming, lambda: (loaded(P_DOWN), contract(0))],
        15: [lambda: (loaded(P_DOWN + 1), contract(1))],
        16: [lambda: (loaded(P_DOWN + 2), contract(2))],
        17: [lambda: (loaded(P_DOWN + 3), contract(3))],
    }
    for step in range(count + 4):
        todo = list(work.get(step, []))
        moves = []
        if step + 4 < count:
            moves.append(lambda: own(step + 4))
        if step < count:
            moves.append(lambda: column(step))
        if 0 <= step - 1 < count:
            moves.append(lambda: plane(step - 1))
        if 0 <= step - 2 < count:
            moves.append(lambda: pair(step - 2))
        if 0 <= step - 3 < count:
            moves.append(lambda: arrive(step - 3))
        while moves or todo:
            if moves:
                moves.pop(0)()
            if todo and len(moves) <= 3:
                todo.pop(0)()
    norm_second()
    for t in range(count):
        sent(t)
    for out, sem in saved:
        wait_bytes(out, sem)


FWD_SAVED = (
    ((512, 1024), BF16),
    ((1024, 512), BF16),
    ((512, 1024), BF16),
    ((8, 2, 512, 512), BF16),
    ((2, 512, 512), BF16),
    ((512, 1024), F32),
    ((512, 128), F32),
    ((2, 512, 512), BF16),
    ((2, 512, 512), BF16),
    ((2, 512, 2048), BF16),
    ((512, 4096), BF16),
    ((512, 1024), F32),
    ((512, 1024), BF16),
    ((2, 512, 512), BF16),
    ((512, 1024), BF16),
    ((512, 128), BF16),
    ((16, 1024), F32),
    ((8, 128), F32),
    ((512, 128), F32),
    ((512, 128), F32),
    ((8, 1024), F32),
)


def forward_pass(tokens, cot_hidden, cot_embed, vectors, lengths, offsets, order, weights):
    count = len(FWD_PIECES)
    shape = jax.ShapeDtypeStruct
    outs = [shape((4, 2, 2, 2, r, k), dt) for r, k, dt in FWD_TENSORS[1:]]
    outs += [shape(s, dt) for s, dt in FWD_SAVED]
    big = lambda *s: pltpu.VMEM(s, BF16)
    scratch = [
        big(512, 1024),
        pltpu.VMEM((16, 128), F32),
        pltpu.VMEM((4, 2, 2, 2, 16, 128), F32),
        pltpu.VMEM((16, 1024), F32),
        pltpu.VMEM((1, 4096), F32),
        pltpu.VMEM((512, 128), F32),
        pltpu.VMEM((512, 128), F32),
        pltpu.VMEM((512, 512), F32),
        pltpu.VMEM((8, 128), F32),
        big(512, 1024),
        big(512, 1024),
        big(512, 1024),
        big(1024, 512),
        big(1024, 512),
        big(2, 512, 512),
        big(512, 1024),
        big(2, 512, 512),
        big(2, 512, 512),
        pltpu.VMEM((512, 1024), F32),
        pltpu.VMEM((512, 1024), F32),
        pltpu.VMEM((512, 128), F32),
        big(512, 1024),
        big(2, 512, 512),
        big(2, 512, 2048),
        big(512, 4096),
        pltpu.VMEM((512, 1024), F32),
        pltpu.VMEM((8, 1024), F32),
        big(512, 1024),
        big(512, 128),
        big(2, 512, 512),
    ]
    for tensor, _, width in FWD_PIECES[1:]:
        scratch.append(big(4, 2, 2, 2, FWD_TENSORS[tensor][0], width))
    for tensor, _, width in FWD_PIECES[1:]:
        scratch.append(big(FWD_TENSORS[tensor][0], width))
    dma = pltpu.SemaphoreType.DMA
    scratch += [
        dma((count, 8)), dma((count, 8)), dma((count,)), dma((count,)), dma((24,)), dma((2,)), dma((3,)),
        dma((count,)),
    ]
    smem = pl.BlockSpec(memory_space=pltpu.SMEM)
    return pl.pallas_call(
        forward_kernel,
        out_shape=outs,
        in_specs=[ANY, ANY, ANY, smem, smem, smem]
        + [pl.BlockSpec(memory_space=pltpu.VMEM)] * 10
        + [ANY] * 7,
        out_specs=[ANY] * len(outs),
        scratch_shapes=scratch,
        compiler_params=pltpu.CompilerParams(
            collective_id=0, has_side_effects=True, vmem_limit_bytes=62 * 2**20
        ),
        name="forward_pass",
    )(tokens, cot_hidden, cot_embed, lengths, offsets, order, *vectors, *weights)


DOWN_TILE = 1024
R_PROJ, R_DOWN, R_UP, R_OUT, R_Q, R_K, R_VEC, R_V = 0, 1, 5, 9, 10, 11, 12, 13
BWD_OUTS = (
    (32, 128, BF16),
    (1024, 128, BF16),
    (32, 4096, BF16),
    (32, 1024, BF16),
    (32, 1024, BF16),
    (32, 1024, BF16),
    (16, 128, F32),
    (32, 1024, BF16),
)
BWD_PIECES = (
    ((0, 0, 32, 128, BF16),)
    + tuple((1, 256 * k, 256, 128, BF16) for k in range(4))
    + tuple((2, 1024 * k, 32, 1024, BF16) for k in range(4))
    + (
        (3, 0, 32, 1024, BF16),
        (4, 0, 32, 1024, BF16),
        (5, 0, 32, 1024, BF16),
        (6, 0, 16, 128, F32),
        (7, 0, 32, 1024, BF16),
    )
)


def backward_kernel(cote_h, lengths_s, offsets_s, order_s, *refs):
    wq_h, wk_h, wv_h, wo_h, wup_h, wdown_h = refs[:6]
    (
        q_h, kt_h, v_h, prob_h, ctxp_h, n1_h, inv1_h, firstp_h, tokp_h, act_h, slope_h,
        back_h, dg_h, outp_h, vecs_h, stats_h, cos_h, sin_h, sumf_h,
    ) = refs[6:25]
    refs = refs[25:]
    grad_h = refs[0]
    outs = refs[1:9]
    refs = refs[9:]
    (
        ring, resid, nbuf, sumf, inv1, dg, dgt, upg, four, slopes, blocks, kt, mask,
        cosine, sine, cot, vecs, stats, sums, sum_up, table, stage_d, stage_u, stage_p,
    ) = refs[:24]
    refs = refs[24:]
    count = len(BWD_PIECES)
    acc, diag, from_x, from_y = (refs[i * count : (i + 1) * count] for i in range(4))
    ss, rs, ls, ins, rsem, psem, gsem = refs[4 * count :]
    z, y, x, c = place()
    me = device_at(z, y, x, c)
    near_x, near_y = device_at(z, y, 1 - x, c), device_at(z, 1 - y, x, c)
    sibling = device_at(z, y, x, 1 - c)
    others = [(z + kk) % 4 for kk in (1, 2, 3)]
    pack = order_s[me]
    length, offset = lengths_s[pack], offsets_s[pack]

    ring_src = []
    for j in range(4):
        ring_src.append(wdown_h.at[pl.ds(1024 * j, 1024), :])
        ring_src.append(wup_h.at[:, pl.ds(1024 * j, 1024)])
    ring_src += [wo_h, wq_h, wk_h, wv_h]

    def ring_start(n):
        local_copy(ring_src[n], ring.at[n % 3], rsem.at[n])

    def ring_wait(n):
        wait_bytes(ring.at[n % 3], rsem.at[n])
        return ring.at[n % 3]

    def ring_next(n):
        if n + 3 < len(ring_src):
            ring_start(n + 3)

    loads = {}

    def load(name, src, dst):
        n = len(loads)
        loads[name] = (dst, ins.at[n])
        local_copy(src, dst, ins.at[n])

    def ready(name):
        dst, sem = loads[name]
        wait_bytes(dst, sem)

    load("dg", dg_h, dg)
    for p in range(2):
        for h in range(2):
            load("act%d%d" % (p, h), act_h.at[p, :, pl.ds(1024 * h, 1024)], four.at[2 * p + h])
    load("cote", cote_h, cot)
    load("outp", outp_h, blocks.at[0])
    ring_start(0)
    load("slope0", slope_h.at[:, pl.ds(0, 1024)], slopes.at[0])
    load("firstp", firstp_h, blocks.at[1])
    load("back", back_h, resid)
    ring_start(1)
    load("slope1", slope_h.at[:, pl.ds(1024, 1024)], slopes.at[1])
    ring_start(2)
    load("n1", n1_h, nbuf)
    load("inv1", inv1_h, inv1)
    load("vecs", vecs_h, vecs)
    load("sumf", sumf_h, sumf)
    load("stats", stats_h, stats)
    load("cos", cos_h, cosine)
    load("sin", sin_h, sine)
    load("kt", kt_h, kt)
    greet_start(z, y, x, c)

    def out_view(t, *lead):
        out, first, rows, width, _ = BWD_PIECES[t]
        if R_DOWN <= t < R_UP:
            return outs[out].at[lead + (pl.ds(first, rows), slice(None))]
        return outs[out].at[lead + (slice(None), pl.ds(first, width))]

    def give(t, stage):
        send(stage, acc[t], ss.at[t, 0], rs.at[t, 0], sibling)

    def net(t):
        half = BWD_PIECES[t][2] // 2
        h = acc[t]
        first, second = pl.ds(0, half), pl.ds(half, half)
        send(h.at[:, 1 - y, 1 - x, first], diag[t].at[0], ss.at[t, 1], rs.at[t, 1], near_x)
        send(h.at[:, 1 - y, 1 - x, second], diag[t].at[1], ss.at[t, 2], rs.at[t, 2], near_y)
        send(h.at[:, y, 1 - x, first], from_x[t].at[:, first], ss.at[t, 3], rs.at[t, 3], near_x)
        send(h.at[:, 1 - y, x, second], from_y[t].at[:, second], ss.at[t, 4], rs.at[t, 4], near_y)

    def add_diagonal(t):
        rows = BWD_PIECES[t][2]
        half = rows // 2
        h = acc[t]
        first, second = pl.ds(0, half), pl.ds(half, half)
        wait_bytes(diag[t].at[0], rs.at[t, 1])

        @pl.loop(0, 4)
        def _(i):
            h[i, 1 - y, x, 0:half, :] = h[i, 1 - y, x, 0:half, :] + diag[t][0, i]

        send(h.at[:, 1 - y, x, first], from_y[t].at[:, first], ss.at[t, 6], rs.at[t, 6], near_y)
        wait_bytes(diag[t].at[1], rs.at[t, 2])

        @pl.loop(0, 4)
        def _(i):
            h[i, y, 1 - x, half:rows, :] = h[i, y, 1 - x, half:rows, :] + diag[t][1, i]

        send(h.at[:, y, 1 - x, second], from_x[t].at[:, second], ss.at[t, 5], rs.at[t, 5], near_x)

    def add_plane(t):
        rows = BWD_PIECES[t][2]
        half = rows // 2
        h = acc[t]
        first, second = pl.ds(0, half), pl.ds(half, half)
        wait_bytes(from_x[t].at[:, first], rs.at[t, 3])
        wait_bytes(from_x[t].at[:, second], rs.at[t, 5])
        wait_bytes(from_y[t].at[:, second], rs.at[t, 4])
        wait_bytes(from_y[t].at[:, first], rs.at[t, 6])

        @pl.loop(0, 4)
        def _(i):
            h[i, y, x] = h[i, y, x] + from_x[t][i] + from_y[t][i]

        slot = out_view(t, z)
        for zz in others:
            send(h.at[zz, y, x], slot, ss.at[t, 7], rs.at[t, 7], device_at(zz, y, x, c))
        local_copy(h.at[z, y, x], slot, ls.at[t])

    def finish(t):
        half = BWD_PIECES[t][2] // 2
        three = out_view(t, pl.ds(0, 3))
        wait_bytes(three, rs.at[t, 7])
        wait_bytes(out_view(t, 0), ls.at[t])
        wait_bytes(diag[t].at[0], ss.at[t, 1])
        wait_bytes(diag[t].at[1], ss.at[t, 2])
        for kind in (3, 4, 5, 6):
            wait_bytes(from_x[t].at[:, pl.ds(0, half)], ss.at[t, kind])
        wait_bytes(three, ss.at[t, 7])

    given = {}

    def take_stage(key, t):
        if key in given:
            wait_bytes(acc[given[key]], ss.at[given[key], 0])
        given[key] = t

    def rows_sib(t, lhs, rhs, stage, key):
        take_stage(key, t)
        width = BWD_PIECES[t][3]
        tile = min(width, 1024)

        @pl.loop(0, width // tile)
        def _(j):
            cols = lanes_at(j * tile, tile)
            val = dot(lhs[1 - c], rhs[:, cols]).astype(BF16)
            stage[:, :, :, :, cols] = val.reshape(4, 2, 2, 32, tile)

        give(t, stage)

    def rows_own(t, lhs, rhs):
        width = BWD_PIECES[t][3]
        tile = min(width, 1024)
        wait_bytes(acc[t], rs.at[t, 0])

        @pl.loop(0, width // tile)
        def _(j):
            cols = lanes_at(j * tile, tile)
            val = dot(lhs[c], rhs[:, cols]) + acc[t][:, :, :, :, cols].reshape(512, tile).astype(F32)
            acc[t][:, :, :, :, cols] = val.astype(BF16).reshape(4, 2, 2, 32, tile)

    def down_tile(h, parity, j):
        per = 1024 // DOWN_TILE
        rhs = four[2 * parity + j // per, :, lanes_at((j % per) * DOWN_TILE, DOWN_TILE)]
        return dot(dgt[512 * h : 512 * h + 512, :], rhs)

    def down_blocks(j):
        for b in range(DOWN_TILE // 128):
            s = j * (DOWN_TILE // 128) + b
            yield b, s // 4, (s // 2) % 2, s % 2

    def down_sib(h):
        for k0 in (2 * h, 2 * h + 1):
            take_stage("d%d" % (k0 % 2), R_DOWN + k0)

        @pl.loop(0, 2048 // DOWN_TILE)
        def _(j):
            val = down_tile(h, 1 - c, j).astype(BF16)
            for b, sz, sy, sx in down_blocks(j):
                for i in range(2):
                    stage_d[i, sz, sy, sx] = val[256 * i : 256 * i + 256, 128 * b : 128 * b + 128]

        for k0 in (2 * h, 2 * h + 1):
            give(R_DOWN + k0, stage_d.at[k0 % 2])

    def down_own(h):
        for k0 in (2 * h, 2 * h + 1):
            wait_bytes(acc[R_DOWN + k0], rs.at[R_DOWN + k0, 0])

        @pl.loop(0, 2048 // DOWN_TILE)
        def _(j):
            val = down_tile(h, c, j)
            for b, sz, sy, sx in down_blocks(j):
                for i in range(2):
                    t = R_DOWN + 2 * h + i
                    old = acc[t][sz, sy, sx].astype(F32)
                    acc[t][sz, sy, sx] = (
                        val[256 * i : 256 * i + 256, 128 * b : 128 * b + 128] + old
                    ).astype(BF16)

    def column_sum(ref):
        return dot(jnp.ones((16, 512), BF16), ref)[0:1]

    def row_valid(rows, start):
        r = lax.broadcasted_iota(jnp.int32, (rows, 1), 0) + start
        return ((r >= offset) & (r < offset + length)).astype(F32)

    def norm_back(inv, gain, to_gain, to_shift):
        sums[to_gain : to_gain + 1, :] = jnp.zeros((1, 1024), F32)
        sums[to_shift : to_shift + 1, :] = jnp.zeros((1, 1024), F32)

        @pl.loop(0, 16)
        def _(i):
            rows = rows_at(i * 32, 32)
            grad, normed = resid[rows, :], nbuf[rows, :]
            scaled = grad * vecs[gain : gain + 1, :]
            mean = jnp.sum(scaled, axis=1, keepdims=True) * (1.0 / 1024)
            cross = jnp.sum(scaled * normed, axis=1, keepdims=True) * (1.0 / 1024)
            out = (scaled - mean - normed * cross) * inv[rows, 0:1]
            resid[rows, :] = out
            dg[rows, :] = out.astype(BF16)
            sums[to_gain : to_gain + 1, :] = sums[to_gain : to_gain + 1, :] + jnp.sum(
                grad * normed, axis=0, keepdims=True
            )
            sums[to_shift : to_shift + 1, :] = sums[to_shift : to_shift + 1, :] + jnp.sum(
                grad, axis=0, keepdims=True
            )

    def begin():
        ready("cote")
        cot[...] = jnp.where(row_valid(512, 0) > 0.0, cot[...].astype(F32), 0.0).astype(BF16)
        sums[V_BD : V_BD + 1, :] = column_sum(dg[...])

    def turn():
        @pl.loop(0, 8)
        def _(j):
            dgt[rows_at(j * 128, 128), :] = dg[:, lanes_at(j * 128, 128)].T

    def acts():
        for p in range(2):
            for h in range(2):
                ready("act%d%d" % (p, h))

    def up_grad(k0):
        w = ring_wait(2 * k0)
        ready("slope%d" % k0)

        @pl.loop(0, 1)
        def _(j):
            cols = lanes_at(j * 1024, 1024)
            back = dot_nt(dg[...], w[rows_at(j * 1024, 1024), :]) * slopes[k0 % 2, :, cols].astype(F32)
            upg[k0, :, cols] = back.astype(BF16)

        ring_next(2 * k0)
        if k0 + 2 < 4:
            load("slope%d" % (k0 + 2), slope_h.at[:, pl.ds(1024 * (k0 + 2), 1024)], slopes.at[k0 % 2])
        sum_up[0:1, 1024 * k0 : 1024 * k0 + 1024] = column_sum(upg[k0])

    def first_grad(k0):
        if k0 == 0:
            ready("back")
        w = ring_wait(2 * k0 + 1)

        @pl.loop(0, 1)
        def _(j):
            cols = lanes_at(j * 1024, 1024)
            resid[:, cols] = resid[:, cols] + dot_nt(upg[k0], w[rows_at(j * 1024, 1024), :])

        ring_next(2 * k0 + 1)

    def up_sib(k0):
        if k0 == 0:
            ready("firstp")
        rows_sib(R_UP + k0, blocks.at[1], upg.at[k0], stage_u.at[k0 % 2], "u%d" % (k0 % 2))

    def up_own(k0):
        rows_own(R_UP + k0, blocks.at[1], upg.at[k0])

    def norm_one():
        ready("n1")
        ready("inv1")
        ready("vecs")
        norm_back(inv1, V_GA, V_GA, V_SA)
        sums[V_BO : V_BO + 1, :] = column_sum(dg[...])
        load("ctxp", ctxp_h, blocks.at[0])

    def start_attention():
        load("q", q_h, upg.at[0])
        load("v", v_h, upg.at[1])
        load("tokp", tokp_h, blocks.at[1])
        prob_start(0)

    def prob_start(p):
        for j in range(2):
            local_copy(
                prob_h.at[p, j],
                upg.at[2 + p % 2, :, pl.ds(512 * j, 512)],
                psem.at[p % 2, j],
            )

    def ctx_back():
        w = ring_wait(8)

        @pl.loop(0, 1)
        def _(j):
            four[3, :, lanes_at(j * 1024, 1024)] = dot_nt(dg[...], w[rows_at(j * 1024, 1024), :]).astype(BF16)

        ring_next(8)

    def make_mask():
        s = lax.broadcasted_iota(jnp.int32, (1, 512), 1)
        col_valid = ((s >= offset) & (s < offset + length)).astype(F32)

        @pl.loop(0, 8)
        def _(i):
            mask[rows_at(i * 64, 64), :] = row_valid(64, i * 64) * col_valid

    def lane128():
        return lax.broadcasted_iota(jnp.int32, (1, 128), 1)

    def unturn(val):
        swapped = jnp.where(lane128() % 64 < 32, pltpu.roll(val, 96, 1), pltpu.roll(val, 32, 1))
        return (val * cosine[...] - swapped * sine[...]).astype(BF16)

    def attend_back(p0, p1):
        @pl.loop(p0, p1)
        def _(p):
            cols = lanes_at(p * 128, 128)
            for j in range(2):
                wait_bytes(upg.at[2 + p % 2, :, pl.ds(512 * j, 512)], psem.at[p % 2, j])

            @pl.when(p + 1 < 8)
            def _():
                prob_start(p + 1)

            qp, vp, grad = upg[0, :, cols], upg[1, :, cols], four[3, :, cols]
            dv, dk, dqt = [], [], []
            for j in range(2):
                keep = lane128() < 64 if j == 0 else lane128() >= 64
                low = upg[2 + p % 2, :, 512 * j : 512 * j + 512]
                wide = low.astype(F32)
                back = dot_nt(jnp.where(keep, vp, jnp.zeros((), BF16)), grad)
                row_dot = jnp.sum(wide * back, axis=0, keepdims=True)
                sgrad = jnp.where(mask[...] > 0.0, wide * (back - row_dot), 0.0).astype(BF16)
                dv.append(dot(low, grad))
                dk.append(dot(sgrad, qp))
                dqt.append(dot(kt[rows_at(p * 128 + 64 * j, 64), :], sgrad))
            four[2, :, cols] = jnp.where(lane128() < 64, dv[0], dv[1]).astype(BF16)
            four[1, :, cols] = unturn(jnp.where(lane128() < 64, dk[0], dk[1]))
            four[0, :, cols] = unturn(jnp.concatenate(dqt, axis=0).T * 0.125)

    def bias_sums():
        sums[V_BQ : V_BQ + 1, :] = column_sum(four[0])
        sums[V_BK : V_BK + 1, :] = column_sum(four[1])
        sums[V_BV : V_BV + 1, :] = column_sum(four[2])

    def vector_table():
        ready("stats")
        ready("sumf")
        for b in range(8):
            val = jnp.concatenate(
                [sums[0:7, 128 * b : 128 * b + 128], sumf[0:2, 128 * b : 128 * b + 128], jnp.zeros((1, 128), F32), stats[0:4, :], jnp.zeros((2, 128), F32)],
                axis=0,
            )
            for i in range(4):
                table[b // 2, b % 2, i // 2, i % 2] = val
        for d in range(32):
            table[d // 8, (d // 4) % 2, (d // 2) % 2, d % 2, 9:10, :] = sum_up[
                0:1, 128 * d : 128 * d + 128
            ]
        give(R_VEC, table.at[:, :, :, 1 - c])

    def vector_own():
        wait_bytes(acc[R_VEC], rs.at[R_VEC, 0])
        acc[R_VEC][...] = acc[R_VEC][...] + table[:, :, :, c]

    def token_grad(i):
        w = ring_wait(9 + i)

        @pl.loop(0, 1)
        def _(j):
            cols = lanes_at(j * 1024, 1024)
            resid[:, cols] = resid[:, cols] + dot_nt(four[i], w[rows_at(j * 1024, 1024), :])

    def token_out():
        local_copy(resid, grad_h, gsem)

    ready("dg")
    turn()
    acts()
    greet_end()
    down_sib(0)
    begin()
    ready("outp")
    rows_sib(R_PROJ, blocks.at[0], cot, stage_p, "p")
    down_own(0)
    rows_own(R_PROJ, blocks.at[0], cot)
    work = {
        1: [lambda: down_sib(1), lambda: up_grad(0), lambda: up_sib(0), lambda: first_grad(0)],
        2: [lambda: down_own(1), lambda: up_grad(1), lambda: up_sib(1)],
        3: [lambda: first_grad(1), lambda: up_own(0), lambda: up_grad(2)],
        4: [lambda: up_sib(2), lambda: up_own(1), lambda: first_grad(2), lambda: up_grad(3)],
        5: [lambda: up_sib(3), lambda: first_grad(3), lambda: up_own(2), norm_one, make_mask],
        6: [
            lambda: up_own(3),
            start_attention,
            ctx_back,
            lambda: (ready("ctxp"), rows_sib(R_OUT, blocks.at[0], dg, stage_u.at[0], "u0")),
            lambda: (ready("kt"), ready("q"), ready("v"), ready("cos"), ready("sin"), attend_back(0, 1)),
        ],
        7: [lambda: attend_back(1, 2), lambda: attend_back(2, 3), lambda: rows_own(R_OUT, blocks.at[0], dg)],
        8: [lambda: attend_back(3, 4), lambda: attend_back(4, 6)],
        9: [
            lambda: attend_back(6, 8),
            bias_sums,
            lambda: (ready("tokp"), rows_sib(R_Q, blocks.at[1], four.at[0], stage_u.at[1], "u1")),
            lambda: rows_sib(R_K, blocks.at[1], four.at[1], stage_u.at[0], "u0"),
            lambda: rows_own(R_Q, blocks.at[1], four.at[0]),
        ],
        10: [
            lambda: rows_sib(R_V, blocks.at[1], four.at[2], stage_u.at[1], "u1"),
            vector_table,
            lambda: rows_own(R_K, blocks.at[1], four.at[1]),
            lambda: token_grad(0),
        ],
        11: [vector_own, lambda: rows_own(R_V, blocks.at[1], four.at[2]), lambda: token_grad(1)],
        12: [lambda: token_grad(2), token_out],
    }
    for step in range(count + 2):
        todo = list(work.get(step, []))
        moves = []
        if step < count:
            moves.append(lambda: net(step))
        if 0 <= step - 1 < count:
            moves.append(lambda: add_diagonal(step - 1))
        if 0 <= step - 2 < count:
            moves.append(lambda: add_plane(step - 2))
        while moves or todo:
            if moves:
                moves.pop(0)()
            if todo:
                todo.pop(0)()
            if todo and len(moves) < 2:
                todo.pop(0)()
    for t in range(count):
        finish(t)
    for t in given.values():
        wait_bytes(acc[t], ss.at[t, 0])
    wait_bytes(acc[R_VEC], ss.at[R_VEC, 0])
    wait_bytes(resid, gsem)


def backward_pass(cot_embed, lengths, offsets, order, weights, kept):
    count = len(BWD_PIECES)
    outs = [jax.ShapeDtypeStruct((512, 1024), F32)]
    outs += [jax.ShapeDtypeStruct((4, r, k), dt) for r, k, dt in BWD_OUTS]
    big = lambda *s: pltpu.VMEM(s, BF16)
    wide = lambda *s: pltpu.VMEM(s, F32)
    scratch = [
        big(3, 1024, 1024),
        wide(512, 1024),
        wide(512, 1024),
        wide(8, 1024),
        wide(512, 128),
        big(512, 1024),
        big(1024, 512),
        big(4, 512, 1024),
        big(4, 512, 1024),
        big(2, 512, 1024),
        big(2, 2, 512, 512),
        big(1024, 512),
        wide(512, 512),
        wide(512, 128),
        wide(512, 128),
        big(512, 128),
        wide(16, 1024),
        wide(8, 128),
        wide(16, 1024),
        wide(1, 4096),
        wide(4, 2, 2, 2, 16, 128),
        big(2, 4, 2, 2, 256, 128),
        big(2, 4, 2, 2, 32, 1024),
        big(4, 2, 2, 32, 128),
    ]
    for lead in ((4, 2, 2), (2, 4), (4,), (4,)):
        for _, _, rows, width, dtype in BWD_PIECES:
            scratch.append(pltpu.VMEM(lead + (rows // 2 if lead == (2, 4) else rows, width), dtype))
    dma = pltpu.SemaphoreType.DMA
    scratch += [dma((count, 8)), dma((count, 8)), dma((count,)), dma((32,)), dma((12,)), dma((2, 2)), dma]
    smem = pl.BlockSpec(memory_space=pltpu.SMEM)
    return pl.pallas_call(
        backward_kernel,
        out_shape=outs,
        in_specs=[ANY, smem, smem, smem] + [ANY] * (6 + 19),
        out_specs=[ANY] * len(outs),
        scratch_shapes=scratch,
        compiler_params=pltpu.CompilerParams(
            collective_id=1, has_side_effects=True, vmem_limit_bytes=62 * 2**20
        ),
        name="backward_pass",
    )(cot_embed, lengths, offsets, order, *weights, *kept)


def finish_kernel(*refs):
    parts, (hidden_h, embed_h, tokens_h) = refs[:8], refs[8:11]
    outs, hidden_o, embed_o, tokens_o = refs[11:19], *refs[19:22]
    bufs, results, carry, ins, done, moved = refs[22:30], refs[30:38], refs[38:41], *refs[41:44]
    order = (6, 1, 2, 3, 4, 5, 7, 0)
    for i in order:
        local_copy(parts[i], bufs[i], ins.at[i])
    moves = ((hidden_h, hidden_o), (embed_h, embed_o), (tokens_h, tokens_o))
    for i, (src, _) in enumerate(moves):
        local_copy(src, carry[i], moved.at[i, 0])
    me = lax.axis_index("dp")
    for i in order:
        wait_bytes(bufs[i], ins.at[i])
        buf = bufs[i]
        total = buf[0].astype(F32) + buf[1].astype(F32) + buf[2].astype(F32) + buf[3].astype(F32)
        if i == 1:
            total = total.T
        if i == 6:
            own = jnp.where(me % 4 == 0, total[:, 0:32], 0.0)
            for j in range(1, 4):
                own = own + jnp.where(me % 4 == j, total[:, 32 * j : 32 * j + 32], 0.0)
            stat = jnp.sum(total, axis=1, keepdims=True)
            root = jnp.sqrt(stat[10:13] / (stat[13:14] * (1024 / 128)))
            results[6][...] = jnp.zeros((16, 256), F32)
            results[6][:, 0:32] = own
            results[6][:, 128:256] = total
            results[6][10:13, 0:1] = root
        else:
            results[i][...] = total
        local_copy(results[i], outs[i], done.at[i])
        if i == 2:
            for k, (src, dst) in enumerate(moves):
                wait_bytes(carry[k], moved.at[k, 0])
                local_copy(carry[k], dst, moved.at[k, 1])
    for i in order:
        wait_bytes(results[i], done.at[i])
    for i in range(3):
        wait_bytes(carry[i], moved.at[i, 1])


def finish(parts, hidden, embed, grad):
    shape = jax.ShapeDtypeStruct
    sums = [shape(p.shape[1:], F32) for p in parts]
    sums[1] = shape((128, 1024), F32)
    sums[6] = shape((16, 256), F32)
    moved = [shape(a.shape, a.dtype) for a in (hidden, embed, grad)]
    dma = pltpu.SemaphoreType.DMA
    return pl.pallas_call(
        finish_kernel,
        out_shape=sums + moved,
        in_specs=[pl.BlockSpec(memory_space=pltpu.HBM)] * 11,
        out_specs=[pl.BlockSpec(memory_space=pltpu.HBM)] * 11,
        scratch_shapes=[pltpu.VMEM(p.shape, p.dtype) for p in parts]
        + [pltpu.VMEM(s.shape, F32) for s in sums]
        + [pltpu.VMEM(a.shape, a.dtype) for a in moved]
        + [dma((8,)), dma((8,)), dma((3, 2))],
        compiler_params=pltpu.CompilerParams(vmem_limit_bytes=60 * 2**20),
        name="finish",
    )(*parts, hidden, embed, grad)


def shards(
    tokens, cot_hidden, cot_embed, lengths, offsets, pack_order,
    w_query, b_query, w_key, b_key, w_value, b_value, w_out, b_out, gain_attn, shift_attn,
    w_up, b_up, w_down, b_down, gain_ffn, shift_ffn, w_proj,
):
    done = forward_pass(
        tokens, cot_hidden, cot_embed,
        (b_query, b_key, b_value, b_out, gain_attn, shift_attn, b_down, gain_ffn, shift_ffn, b_up),
        lengths, offsets, pack_order,
        (w_query, w_key, w_value, w_out, w_up, w_proj, w_down),
    )
    weights = [w.reshape(-1, w.shape[-1]) for w in list(done[:5]) + list(done[6:7])]
    kept = list(done[7 : 7 + 14]) + list(done[7 + 16 :])
    back = backward_pass(cot_embed, lengths, offsets, pack_order, weights, kept)
    *totals, hidden, embed, grad = finish(back[1:], done[7 + 14], done[7 + 15], back[0])
    proj, down, up, out, query, key, vec, val = totals
    own = vec[:9, :32]
    return (
        hidden, embed, grad,
        query, own[V_BQ], key, own[V_BK], val, own[V_BV], out, own[V_BO],
        own[V_GA], own[V_SA], up, vec[9, 128:], down, own[V_BD], own[V_GF], own[V_SF],
        proj, vec[10:13, 0],
    )


def shards_any(
    tokens,
    cot_hidden,
    cot_embed,
    lengths,
    offsets,
    pack_order,
    w_query,
    b_query,
    w_key,
    b_key,
    w_value,
    b_value,
    w_out,
    b_out,
    gain_attn,
    shift_attn,
    w_up,
    b_up,
    w_down,
    b_down,
    gain_ffn,
    shift_ffn,
    w_proj,
):
    gathered = (
        lax.all_gather(w_query, "dp", axis=0, tiled=True),
        lax.all_gather(w_key, "dp", axis=0, tiled=True),
        lax.all_gather(w_value, "dp", axis=0, tiled=True),
        lax.all_gather(w_out, "dp", axis=0, tiled=True),
        lax.all_gather(w_up, "dp", axis=0, tiled=True),
        lax.all_gather(w_down, "dp", axis=0, tiled=True),
        lax.all_gather(w_proj, "dp", axis=0, tiled=True),
        lax.all_gather(b_query, "dp", axis=0, tiled=True),
        lax.all_gather(b_key, "dp", axis=0, tiled=True),
        lax.all_gather(b_value, "dp", axis=0, tiled=True),
        lax.all_gather(b_out, "dp", axis=0, tiled=True),
        lax.all_gather(gain_attn, "dp", axis=0, tiled=True),
        lax.all_gather(shift_attn, "dp", axis=0, tiled=True),
        lax.all_gather(b_up, "dp", axis=0, tiled=True),
        lax.all_gather(b_down, "dp", axis=0, tiled=True),
        lax.all_gather(gain_ffn, "dp", axis=0, tiled=True),
        lax.all_gather(shift_ffn, "dp", axis=0, tiled=True),
    )
    wt_query, wt_key, wt_value, wt_out, wt_up, wt_down, wt_proj = gathered[:7]
    vectors = [piece.astype(jnp.float32) for piece in gathered[7:]]
    (
        bias_query,
        bias_key,
        bias_value,
        bias_out,
        norm_gain_a,
        norm_shift_a,
        bias_up,
        bias_down,
        norm_gain_f,
        norm_shift_f,
    ) = vectors
    row_count = tokens.shape[0]
    model_width = tokens.shape[1]
    head_count = H
    head_dim = model_width // head_count
    device = lax.axis_index("dp")
    slots = jnp.arange(pack_order.shape[0], dtype=jnp.int32)
    pack_id = jnp.sum(jnp.where(slots == device, pack_order, 0))
    length = jnp.sum(jnp.where(slots == pack_id, lengths, 0))
    offset = jnp.sum(jnp.where(slots == pack_id, offsets, 0))
    row_index = jnp.arange(row_count, dtype=jnp.int32)
    is_valid = (row_index >= offset) & (row_index < offset + length)
    keep_rows = is_valid.astype(jnp.float32)[:, None]
    cosine, sine_part = rope_tables((row_index - offset).astype(jnp.float32), head_dim)
    query_pre = matmul(tokens, wt_query) + bias_query
    key_pre = matmul(tokens, wt_key) + bias_key
    value_low = (
        (matmul(tokens, wt_value) + bias_value)
        .astype(jnp.bfloat16)
        .reshape(row_count, head_count, head_dim)
    )
    query_rot = rotate(
        query_pre.reshape(row_count, head_count, head_dim), cosine, sine_part
    ).astype(jnp.bfloat16)
    key_rot = rotate(key_pre.reshape(row_count, head_count, head_dim), cosine, sine_part).astype(
        jnp.bfloat16
    )
    score_scale = 1.0 / math.sqrt(head_dim)
    key_valid = is_valid[None, None, :]
    allowed = is_valid[None, :, None] & key_valid
    masked = masked_scores(query_rot, key_rot, allowed, score_scale)
    row_top = jnp.max(masked, axis=-1, keepdims=True)
    exponent = jnp.exp(masked - row_top)
    row_total = jnp.sum(exponent, axis=-1, keepdims=True)
    prob_low = (exponent / row_total).astype(jnp.bfloat16)
    contexts = jnp.einsum("hqk,khd->qhd", prob_low, value_low, preferred_element_type=jnp.float32)
    log_totals = row_top + jnp.log(row_total)
    context = contexts.astype(jnp.bfloat16).reshape(row_count, model_width)
    tokens_wide = tokens.astype(jnp.float32)
    attn_branch = matmul(context, wt_out) + bias_out
    first, normed_one, inverse_one = norm_forward(
        tokens_wide + attn_branch, norm_gain_a, norm_shift_a
    )
    first_low = first.astype(jnp.bfloat16)
    up_pre = matmul(first_low, wt_up) + bias_up
    act_full, gelu_pull = jax.vjp(exact_gelu, up_pre)
    act_low = act_full.astype(jnp.bfloat16)
    down_branch = matmul(act_low, wt_down) + bias_down
    out, normed_two, inverse_two = norm_forward(first + down_branch, norm_gain_f, norm_shift_f)
    out_low = out.astype(jnp.bfloat16)
    hidden = (out * keep_rows).astype(jnp.bfloat16)
    embedding = (matmul(out_low, wt_proj) * keep_rows).astype(jnp.bfloat16)
    stat_sums = lax.psum(
        (
            jnp.sum(keep_rows * tokens_wide * tokens_wide),
            jnp.sum(keep_rows * attn_branch * attn_branch),
            jnp.sum(keep_rows * down_branch * down_branch),
            jnp.sum(keep_rows),
        ),
        "dp",
    )
    rms_stats = jnp.sqrt(
        jnp.stack([stat_sums[0], stat_sums[1], stat_sums[2]]) / (stat_sums[3] * model_width)
    )
    backward_set = (
        lax.all_gather(w_query, "dp", axis=0, tiled=True),
        lax.all_gather(w_key, "dp", axis=0, tiled=True),
        lax.all_gather(w_value, "dp", axis=0, tiled=True),
        lax.all_gather(w_out, "dp", axis=0, tiled=True),
        lax.all_gather(w_up, "dp", axis=0, tiled=True),
        lax.all_gather(w_down, "dp", axis=0, tiled=True),
        lax.all_gather(w_proj, "dp", axis=0, tiled=True),
        lax.all_gather(b_query, "dp", axis=0, tiled=True),
        lax.all_gather(b_key, "dp", axis=0, tiled=True),
        lax.all_gather(b_value, "dp", axis=0, tiled=True),
        lax.all_gather(b_out, "dp", axis=0, tiled=True),
        lax.all_gather(gain_attn, "dp", axis=0, tiled=True),
        lax.all_gather(shift_attn, "dp", axis=0, tiled=True),
        lax.all_gather(b_up, "dp", axis=0, tiled=True),
        lax.all_gather(b_down, "dp", axis=0, tiled=True),
        lax.all_gather(gain_ffn, "dp", axis=0, tiled=True),
        lax.all_gather(shift_ffn, "dp", axis=0, tiled=True),
    )
    back_query, back_key, back_value, back_out, back_up, back_down, back_proj = backward_set[:7]
    back_gain_a = backward_set[11].astype(jnp.float32)
    back_gain_f = backward_set[15].astype(jnp.float32)
    cot_low = jnp.where(is_valid[:, None], cot_embed, jnp.zeros_like(cot_embed))
    grad_w_proj = matmul_tn(out_low, cot_low)
    grad_out = keep_rows * cot_hidden.astype(jnp.float32) + matmul_nt(cot_low, back_proj)
    grad_resid_two, grad_gain_f, grad_shift_f = norm_backward(
        grad_out, normed_two, inverse_two, back_gain_f
    )
    down_grad = grad_resid_two.astype(jnp.bfloat16)
    grad_w_down = matmul_tn(act_low, down_grad)
    grad_b_down = jnp.sum(down_grad.astype(jnp.float32), axis=0)
    up_grad = gelu_pull(matmul_nt(down_grad, back_down))[0].astype(jnp.bfloat16)
    grad_w_up = matmul_tn(first_low, up_grad)
    grad_b_up = jnp.sum(up_grad.astype(jnp.float32), axis=0)
    grad_first = grad_resid_two + matmul_nt(up_grad, back_up)
    grad_resid_one, grad_gain_a, grad_shift_a = norm_backward(
        grad_first, normed_one, inverse_one, back_gain_a
    )
    attn_grad = grad_resid_one.astype(jnp.bfloat16)
    grad_w_out = matmul_tn(context, attn_grad)
    grad_b_out = jnp.sum(attn_grad.astype(jnp.float32), axis=0)
    ctx_grad = (
        matmul_nt(attn_grad, back_out).astype(jnp.bfloat16).reshape(row_count, head_count, head_dim)
    )
    allowed = is_valid[None, :, None] & key_valid
    masked = masked_scores(query_rot, key_rot, allowed, score_scale)
    prob_full = jnp.exp(masked - log_totals)
    prob_low = prob_full.astype(jnp.bfloat16)
    prob_grad = jnp.einsum("qhd,khd->hqk", ctx_grad, value_low, preferred_element_type=jnp.float32)
    value_sum = jnp.einsum("hqk,qhd->khd", prob_low, ctx_grad, preferred_element_type=jnp.float32)
    row_dot = jnp.sum(prob_full * prob_grad, axis=-1, keepdims=True)
    score_grad = jnp.where(allowed, prob_full * (prob_grad - row_dot), 0.0).astype(jnp.bfloat16)
    query_parts = (
        jnp.einsum("hqk,khd->qhd", score_grad, key_rot, preferred_element_type=jnp.float32)
        * score_scale
    )
    key_sum = (
        jnp.einsum("hqk,qhd->khd", score_grad, query_rot, preferred_element_type=jnp.float32)
        * score_scale
    )
    query_grad = (
        unrotate(query_parts, cosine, sine_part)
        .reshape(row_count, model_width)
        .astype(jnp.bfloat16)
    )
    key_grad = (
        unrotate(key_sum, cosine, sine_part).reshape(row_count, model_width).astype(jnp.bfloat16)
    )
    value_grad = value_sum.reshape(row_count, model_width).astype(jnp.bfloat16)
    grad_w_query = matmul_tn(tokens, query_grad)
    grad_b_query = jnp.sum(query_grad.astype(jnp.float32), axis=0)
    grad_w_key = matmul_tn(tokens, key_grad)
    grad_b_key = jnp.sum(key_grad.astype(jnp.float32), axis=0)
    grad_w_value = matmul_tn(tokens, value_grad)
    grad_b_value = jnp.sum(value_grad.astype(jnp.float32), axis=0)
    grad_tokens = (
        grad_resid_one
        + matmul_nt(query_grad, back_query)
        + matmul_nt(key_grad, back_key)
        + matmul_nt(value_grad, back_value)
    )
    all_parts = (
        lax.psum_scatter(grad_w_query, "dp", scatter_dimension=0, tiled=True),
        lax.psum_scatter(grad_w_key, "dp", scatter_dimension=0, tiled=True),
        lax.psum_scatter(grad_w_value, "dp", scatter_dimension=0, tiled=True),
        lax.psum_scatter(grad_w_out, "dp", scatter_dimension=0, tiled=True),
        lax.psum_scatter(grad_b_query, "dp", scatter_dimension=0, tiled=True),
        lax.psum_scatter(grad_b_key, "dp", scatter_dimension=0, tiled=True),
        lax.psum_scatter(grad_b_value, "dp", scatter_dimension=0, tiled=True),
        lax.psum_scatter(grad_b_out, "dp", scatter_dimension=0, tiled=True),
        lax.psum_scatter(grad_gain_a, "dp", scatter_dimension=0, tiled=True),
        lax.psum_scatter(grad_shift_a, "dp", scatter_dimension=0, tiled=True),
        lax.psum_scatter(grad_w_up, "dp", scatter_dimension=0, tiled=True),
        lax.psum_scatter(grad_w_down, "dp", scatter_dimension=0, tiled=True),
        lax.psum_scatter(grad_w_proj, "dp", scatter_dimension=0, tiled=True),
        lax.psum_scatter(grad_b_up, "dp", scatter_dimension=0, tiled=True),
        lax.psum_scatter(grad_b_down, "dp", scatter_dimension=0, tiled=True),
        lax.psum_scatter(grad_gain_f, "dp", scatter_dimension=0, tiled=True),
        lax.psum_scatter(grad_shift_f, "dp", scatter_dimension=0, tiled=True),
    )
    attn_parts = all_parts[:10]
    ffn_parts = all_parts[10:]
    return (
        hidden,
        embedding,
        grad_tokens,
        attn_parts[0],
        attn_parts[4],
        attn_parts[1],
        attn_parts[5],
        attn_parts[2],
        attn_parts[6],
        attn_parts[3],
        attn_parts[7],
        attn_parts[8],
        attn_parts[9],
        ffn_parts[0],
        ffn_parts[3],
        ffn_parts[1],
        ffn_parts[4],
        ffn_parts[5],
        ffn_parts[6],
        ffn_parts[2],
        rms_stats,
    )


def solution(mesh):
    fast = mesh.shape["dp"] == 32
    placed = (
        P("dp", None),
        P("dp", None),
        P("dp", None),
        P(),
        P(),
        P(),
        P("dp", None),
        P("dp"),
        P("dp", None),
        P("dp"),
        P("dp", None),
        P("dp"),
        P("dp", None),
        P("dp"),
        P("dp"),
        P("dp"),
        P("dp", None),
        P("dp"),
        P("dp", None),
        P("dp"),
        P("dp"),
        P("dp"),
        P("dp", None),
    )
    return jax.shard_map(
        shards if fast else shards_any,
        mesh=mesh,
        in_specs=placed,
        out_specs=(
            P("dp", None),
            P("dp", None),
            P("dp", None),
            P("dp", None),
            P("dp"),
            P("dp", None),
            P("dp"),
            P("dp", None),
            P("dp"),
            P("dp", None),
            P("dp"),
            P("dp"),
            P("dp"),
            P("dp", None),
            P("dp"),
            P("dp", None),
            P("dp"),
            P("dp"),
            P("dp"),
            P("dp", None),
            P(),
        ),
        check_vma=False,
    )
```

```python
import functools
import math

import jax
import jax.numpy as jnp
from jax import lax
from jax.experimental import pallas as pl
from jax.experimental.pallas import tpu as pltpu
from jax.sharding import PartitionSpec as P

MESH = pl.DeviceIdType.MESH

H = 16


eps_norm = 1e-05
neg_large = -1e30


def matmul(left, right):
    return jnp.dot(left, right, preferred_element_type=jnp.float32)


def matmul_nt(left, right):
    return lax.dot_general(
        left, right, (((1,), (1,)), ((), ())), preferred_element_type=jnp.float32
    )


def matmul_tn(left, right):
    return lax.dot_general(
        left, right, (((0,), (0,)), ((), ())), preferred_element_type=jnp.float32
    )


def exact_gelu(values):
    return jax.nn.gelu(values, approximate=False)


def norm_forward(values, gain, shift):
    row_mean = jnp.mean(values, axis=-1, keepdims=True)
    centred = values - row_mean
    inverse = lax.rsqrt(jnp.mean(centred * centred, axis=-1, keepdims=True) + eps_norm)
    normed = centred * inverse
    return (normed * gain + shift, normed, inverse)


def norm_backward(grad_in, normed, inverse, gain):
    scaled = grad_in * gain
    adjusted = (
        scaled
        - jnp.mean(scaled, axis=-1, keepdims=True)
        - normed * jnp.mean(scaled * normed, axis=-1, keepdims=True)
    )
    return (adjusted * inverse, jnp.sum(grad_in * normed, axis=0), jnp.sum(grad_in, axis=0))


def rope_tables(position, head_dim):
    half_dim = head_dim // 2
    freq_index = jnp.arange(half_dim, dtype=jnp.float32)
    frequency = jnp.exp(-math.log(10000.0) * 2.0 * freq_index / head_dim)
    angles = position[:, None] * frequency[None, :]
    return (jnp.cos(angles)[:, None, :], jnp.sin(angles)[:, None, :])


def rotate(values, cosine, sine_part):
    half_dim = values.shape[-1] // 2
    first_half = values[..., :half_dim]
    second = values[..., half_dim:]
    return jnp.concatenate(
        [first_half * cosine - second * sine_part, second * cosine + first_half * sine_part],
        axis=-1,
    )


def unrotate(grad_in, cosine, sine_part):
    half_dim = grad_in.shape[-1] // 2
    first_half = grad_in[..., :half_dim]
    second = grad_in[..., half_dim:]
    return jnp.concatenate(
        [first_half * cosine + second * sine_part, second * cosine - first_half * sine_part],
        axis=-1,
    )


def masked_scores(query_block, key_rot, allowed, score_scale):
    raw_scores = jnp.einsum(
        "qhd,khd->hqk", query_block, key_rot, preferred_element_type=jnp.float32
    )
    return jnp.where(allowed, raw_scores * score_scale, neg_large)


def device_at(z, y, x, c):
    return ((z * 2 + y) * 2 + x) * 2 + c


def wait_bytes(ref, sem):
    pltpu.make_async_copy(ref, ref, sem).wait()


def send(src, dst, sem_out, sem_in, target):
    pltpu.make_async_remote_copy(
        src_ref=src,
        dst_ref=dst,
        send_sem=sem_out,
        recv_sem=sem_in,
        device_id=(target,),
        device_id_type=MESH,
    ).start()


F32, BF16 = jnp.float32, jnp.bfloat16
ANY = pl.BlockSpec(memory_space=pl.ANY)
FWD_TENSORS = (
    (16, 128, F32),
    (32, 1024, BF16),
    (32, 1024, BF16),
    (32, 1024, BF16),
    (32, 1024, BF16),
    (32, 4096, BF16),
    (32, 128, BF16),
    (128, 1024, BF16),
)
FWD_PIECES = (
    ((0, 0, 128), (1, 0, 1024), (2, 0, 1024), (3, 0, 1024), (4, 0, 1024))
    + tuple((5, 1024 * k, 1024) for k in range(4))
    + ((6, 0, 128),)
    + ((7, 0, 256), (7, 256, 256), (7, 512, 256), (7, 768, 128), (7, 896, 128))
)
P_VEC, P_Q, P_K, P_V, P_O, P_UP, P_PROJ, P_DOWN, P_REST = 0, 1, 2, 3, 4, 5, 9, 10, 15
PLANE_FIRST = ()
V_BQ, V_BK, V_BV, V_BO, V_GA, V_SA, V_BD, V_GF, V_SF = range(9)


FWD_ORDER = (
    ("own", 0),
    ("own", 1),
    ("own", 2),
    ("own", 3),
    ("own", 4),
    ("own", 5),
    ("prepare", 0),
    ("own", 6),
    ("column", 0),
    ("own", 7),
    ("column", 1),
    ("plane", 0),
    ("own", 8),
    ("column", 2),
    ("plane", 1),
    ("pair", 0),
    ("own", 9),
    ("column", 3),
    ("plane", 2),
    ("pair", 1),
    ("arrive", 0),
    ("own", 10),
    ("column", 4),
    ("unpack", 0),
    ("plane", 3),
    ("pair", 2),
    ("arrive", 1),
    ("own", 11),
    ("column", 5),
    ("q", 0),
    ("plane", 4),
    ("pair", 3),
    ("arrive", 2),
    ("own", 12),
    ("column", 6),
    ("k", 0),
    ("plane", 5),
    ("pair", 4),
    ("arrive", 3),
    ("own", 13),
    ("column", 7),
    ("v", 0),
    ("plane", 6),
    ("attend", 0),
    ("pair", 5),
    ("arrive", 4),
    ("own", 14),
    ("column", 8),
    ("attend", 1),
    ("plane", 7),
    ("attend", 2),
    ("pair", 6),
    ("arrive", 5),
    ("column", 9),
    ("attend", 3),
    ("plane", 8),
    ("project", 0),
    ("pair", 7),
    ("norm", 0),
    ("arrive", 6),
    ("column", 10),
    ("up", 0),
    ("plane", 9),
    ("pair", 8),
    ("arrive", 7),
    ("column", 11),
    ("up", 1),
    ("plane", 10),
    ("pair", 9),
    ("arrive", 8),
    ("column", 12),
    ("up", 2),
    ("plane", 11),
    ("pair", 10),
    ("arrive", 9),
    ("column", 13),
    ("up", 3),
    ("plane", 12),
    ("pair", 11),
    ("arrive", 10),
    ("column", 14),
    ("incoming", 0),
    ("plane", 13),
    ("down", 0),
    ("pair", 12),
    ("arrive", 11),
    ("plane", 14),
    ("down", 1),
    ("pair", 13),
    ("arrive", 12),
    ("pair", 14),
    ("down", 2),
    ("arrive", 13),
    ("arrive", 14),
    ("down", 3),
    ("down", 4),
    ("tail", 0),
)


def dot(left, right):
    return jnp.dot(left, right, preferred_element_type=F32)


def dot_nt(left, right):
    return lax.dot_general(left, right, (((1,), (1,)), ((), ())), preferred_element_type=F32)


def local_copy(src, dst, sem):
    pltpu.make_async_copy(src, dst, sem).start()


def lanes_at(start, size):
    return pl.ds(pl.multiple_of(start, 128), size)


def rows_at(start, size):
    return pl.ds(pl.multiple_of(start, size), size)


def place():
    me = lax.axis_index("dp")
    return me // 8, (me // 4) % 2, (me // 2) % 2, me % 2


def greet_start(z, y, x, c):
    others = [(z + k) % 4 for k in (1, 2, 3)]
    peers = [device_at(z, y, 1 - x, c), device_at(z, 1 - y, x, c), device_at(z, y, x, 1 - c)]
    peers += [device_at(zz, y, x, c) for zz in others]
    barrier = pltpu.get_barrier_semaphore()
    for peer in peers:
        pl.semaphore_signal(barrier, inc=1, device_id=(peer,), device_id_type=MESH)


def greet_end():
    pl.semaphore_wait(pltpu.get_barrier_semaphore(), 6)


def transpose_blocks(src, dst):
    @pl.loop(0, src.shape[1] // 128)
    def _(j):
        block = src[:, lanes_at(j * 128, 128)].T
        for b in range(4):
            dst[b % 2, rows_at((2 * j + b // 2) * 32, 32), :] = block[32 * b : 32 * b + 32]


def forward_kernel(
    tokens_h, cot_h, cote_h, lengths_s, offsets_s, order_s, *refs
):
    vectors = refs[:10]
    refs = refs[10:]
    src = (None,) + refs[:7]
    refs = refs[7:]
    full = (None,) + refs[:7]
    (
        q_h, kt_h, v_h, prob_h, ctxp_h, n1_h, inv1_h, firstp_h, tokp_h, act_h, slope_h,
        back_h, dg_h, outp_h, hidden_h, embed_h, vecs_h, stats_h, cos_h, sin_h, sums_h,
    ) = refs[7:28]
    refs = refs[28:]
    (
        tok, packed, table, vecs, bias_up, cosine, sine, mask, stats,
        q, k, v, kt, vt, prob, ctx, ctxp, tokp, resid, n1, inv1, low, lowp, act, slope, back, sums,
        hidden, embed, outp,
    ) = refs[:30]
    refs = refs[30:]
    count = len(FWD_PIECES)
    wbuf = (None,) + refs[: count - 1]
    mybuf = (None,) + refs[count - 1 : 2 * count - 2]
    ss, rs, ls, ld, os, ps, ins, ms = refs[2 * count - 2 :]
    z, y, x, c = place()
    me = device_at(z, y, x, c)
    near_x, near_y = device_at(z, y, 1 - x, c), device_at(z, 1 - y, x, c)
    sibling = device_at(z, y, x, 1 - c)
    others = [(z + kk) % 4 for kk in (1, 2, 3)]

    greet_start(z, y, x, c)
    for t in range(1, count):
        tensor, first, width = FWD_PIECES[t]
        local_copy(src[tensor].at[:, pl.ds(first, width)], mybuf[t], ms.at[t])
    local_copy(tokens_h, tok, ins.at[1])
    local_copy(cot_h, hidden, ins.at[0])
    local_copy(cote_h, embed, ins.at[2])

    def home(t, *lead):
        tensor, first, width = FWD_PIECES[t]
        if t == P_VEC:
            return table.at[lead]
        return full[tensor].at[lead + (slice(None), pl.ds(first, width))]

    def part(t, lead, rows):
        tensor, first, width = FWD_PIECES[t]
        if t == P_VEC:
            return table.at[lead + (rows,)]
        return full[tensor].at[lead + (rows, pl.ds(first, width))]

    every = slice(None)

    def cast(t, block, mine):
        for zz in others:
            send(block, mine, ss.at[t, 0], rs.at[t, 0], device_at(zz, y, x, c))

    def wait_cast(t, sem):
        lead = (every, every, 0) if t in PLANE_FIRST else (0, 0, 0)
        wait_bytes(home(t, pl.ds(0, 3), *lead), sem)

    def own(t):
        tensor, first, width = FWD_PIECES[t]
        piece = packed if t == P_VEC else src[tensor].at[:, pl.ds(first, width)]
        mine = home(t, z, y, x, c)
        if t not in PLANE_FIRST:
            cast(t, piece, mine)
        send(piece, mine, ss.at[t, 1], rs.at[t, 1], near_x)
        send(piece, mine, ss.at[t, 2], rs.at[t, 2], near_y)
        if t == P_VEC:
            local_copy(packed, mine, ls.at[t])
        else:
            wait_bytes(mybuf[t], ms.at[t])
            local_copy(mybuf[t], mine, ls.at[t])

    def column(t):
        wait_cast(t, rs.at[t, 0])
        for zz in others:
            block = home(t, zz, y, x, c)
            send(block, block, ss.at[t, 3], rs.at[t, 3], near_x)
            send(block, block, ss.at[t, 4], rs.at[t, 4], near_y)

    def plane(t):
        half = FWD_TENSORS[FWD_PIECES[t][0]][0] // 2
        flat = t in PLANE_FIRST
        layers = z if flat else every
        wait_bytes(home(t, 0, 0, 0, 0), rs.at[t, 1])
        if not flat:
            wait_bytes(home(t, pl.ds(0, 3), 0, 0, 0), rs.at[t, 3])
        block = part(t, (layers, y, 1 - x, c), pl.ds(0, half))
        send(block, block, ss.at[t, 5], rs.at[t, 5], near_y)
        wait_bytes(home(t, 0, 0, 0, 0), rs.at[t, 2])
        if not flat:
            wait_bytes(home(t, pl.ds(0, 3), 0, 0, 0), rs.at[t, 4])
        block = part(t, (layers, 1 - y, x, c), pl.ds(half, half))
        send(block, block, ss.at[t, 6], rs.at[t, 6], near_x)
        wait_bytes(home(t, 0, 0, 0, 0), ls.at[t])
        if not flat:
            for block in (home(t, every, y, every, c), home(t, every, 1 - y, x, c)):
                send(block, block, ss.at[t, 8], rs.at[t, 8], sibling)

    def gathered(t):
        half = FWD_TENSORS[FWD_PIECES[t][0]][0] // 2
        layers = 0 if t in PLANE_FIRST else every
        for kind in (5, 6):
            wait_bytes(part(t, (layers, 0, 0, 0), pl.ds(0, half)), rs.at[t, kind])

    def plane_cast(t):
        gathered(t)
        cast(t, home(t, z, every, every, c), home(t, z, every, every, c))

    def load(t, parity):
        if t != P_VEC:
            tensor, first, width = FWD_PIECES[t]
            local_copy(
                full[tensor].at[:, :, :, parity, :, pl.ds(first, width)],
                wbuf[t].at[:, :, :, parity],
                ld.at[t],
            )

    def pair(t):
        if t in PLANE_FIRST:
            wait_cast(t, rs.at[t, 0])
            block = home(t, every, every, every, c)
        else:
            gathered(t)
            block = home(t, every, 1 - y, 1 - x, c)
        send(block, block, ss.at[t, 7], rs.at[t, 7], sibling)
        load(t, c)

    def last_part(t):
        if t in PLANE_FIRST:
            return home(t, every, every, every, 0)
        return home(t, every, 0, 0, 0)

    def arrive(t):
        wait_bytes(last_part(t), rs.at[t, 7])
        if t not in PLANE_FIRST:
            wait_bytes(home(t, pl.ds(0, 3), every, every, 0), rs.at[t, 8])
        load(t, 1 - c)

    def loaded(t):
        wait_bytes(wbuf[t], ld.at[t])

    def sent(t):
        half = FWD_TENSORS[FWD_PIECES[t][0]][0] // 2
        flat = t in PLANE_FIRST
        wait_cast(t, ss.at[t, 0])
        for kind in (1, 2):
            wait_bytes(home(t, 0, 0, 0, 0), ss.at[t, kind])
        if not flat:
            for kind in (3, 4):
                wait_bytes(home(t, pl.ds(0, 3), 0, 0, 0), ss.at[t, kind])
            wait_bytes(home(t, pl.ds(0, 3), every, every, 0), ss.at[t, 8])
        for kind in (5, 6):
            wait_bytes(part(t, (0 if flat else every, 0, 0, 0), pl.ds(0, half)), ss.at[t, kind])
        wait_bytes(last_part(t), ss.at[t, 7])

    pack = order_s[me]
    length, offset = lengths_s[pack], offsets_s[pack]
    saved = []

    def save(value, out):
        n = len(saved)
        local_copy(value, out, os.at[n])
        saved.append((out, os.at[n]))

    def row_valid(rows, start):
        r = lax.broadcasted_iota(jnp.int32, (rows, 1), 0) + start
        return ((r >= offset) & (r < offset + length)).astype(F32)

    def pack_vectors():
        lane = lax.broadcasted_iota(jnp.int32, (1, 128), 1)
        for i in range(9):
            val = vectors[i][...].astype(F32).reshape(1, 32)
            wide = jnp.concatenate([val] * 4, axis=1)
            packed[i : i + 1, :] = jnp.where(lane // 32 == me % 4, wide, 0.0)
        packed[9:10, :] = vectors[9][...].astype(F32).reshape(1, 128)
        packed[10:16, :] = jnp.zeros((6, 128), F32)

    def prepare():
        lane = lax.broadcasted_iota(jnp.int32, (1, 128), 1)
        freq = jnp.exp((lane % 32).astype(F32) * (-math.log(10000.0) * 2.0 / 64))

        @pl.loop(0, 8)
        def _(i):
            r = lax.broadcasted_iota(jnp.int32, (64, 1), 0) + i * 64
            angle = (r - offset).astype(F32) * freq
            cosine[rows_at(i * 64, 64), :] = jnp.cos(angle)
            sine[rows_at(i * 64, 64), :] = jnp.where(lane % 64 < 32, -1.0, 1.0) * jnp.sin(angle)

        s = lax.broadcasted_iota(jnp.int32, (1, 512), 1)
        col_valid = ((s >= offset) & (s < offset + length)).astype(F32)
        stats[...] = jnp.zeros_like(stats)

        @pl.loop(0, 8)
        def _(i):
            mask[rows_at(i * 64, 64), :] = row_valid(64, i * 64) * col_valid

        stats[3:4, :] = jnp.broadcast_to(
            jnp.sum(col_valid, axis=1, keepdims=True), (1, 128)
        )
        wait_bytes(tok, ins.at[1])

        @pl.loop(0, 8)
        def _(i):
            t32 = tok[rows_at(i * 64, 64), :].astype(F32)
            add_stat(0, jnp.sum(row_valid(64, i * 64) * t32 * t32, axis=0, keepdims=True))

        transpose_blocks(tok, tokp)
        save(tokp, tokp_h)
        save(cosine, cos_h)
        save(sine, sin_h)

    def add_stat(row, wide):
        total = wide[:, 0:128]
        for i in range(1, wide.shape[1] // 128):
            total = total + wide[:, 128 * i : 128 * i + 128]
        stats[row : row + 1, :] = stats[row : row + 1, :] + total

    def unpack_vectors():
        grouped = table[...].reshape(8, 4, 16, 128).sum(axis=1)
        for b in range(8):
            vecs[:, 128 * b : 128 * b + 128] = grouped[b]
        for d in range(32):
            bias_up[0:1, 128 * d : 128 * d + 128] = table[
                d // 8, (d // 4) % 2, (d // 2) % 2, d % 2, 9:10, :
            ]
        save(vecs, vecs_h)

    def weight(t, first, width):
        w = wbuf[t]
        return w[:, :, :, :, :, lanes_at(first, width)].reshape(-1, width)

    lane128 = lambda: lax.broadcasted_iota(jnp.int32, (1, 128), 1)

    def rotary(t, bias, dst, scale, transposed, j0, j1):
        @pl.loop(j0, j1)
        def _(j):
            pre = dot(tok[...], weight(t, j * 256, 256)) + vecs[bias : bias + 1, lanes_at(j * 256, 256)]
            for b in range(2):
                part_in = pre[:, 128 * b : 128 * b + 128]
                swapped = jnp.where(
                    lane128() % 64 < 32, pltpu.roll(part_in, 96, 1), pltpu.roll(part_in, 32, 1)
                )
                turned = (part_in * cosine[...] + swapped * sine[...]).astype(BF16)
                if transposed is not None:
                    transposed[rows_at(j * 256 + 128 * b, 128), :] = turned.T
                dst[:, lanes_at(j * 256 + 128 * b, 128)] = turned * jnp.asarray(scale, BF16)

    def value(j0, j1):
        @pl.loop(j0, j1)
        def _(j):
            pre = dot(tok[...], weight(P_V, j * 256, 256)) + vecs[V_BV : V_BV + 1, lanes_at(j * 256, 256)]
            val = pre.astype(BF16)
            v[:, lanes_at(j * 256, 256)] = val
            vt[rows_at(j * 256, 256), :] = val.T

    def attend(p0, p1):
        @pl.loop(p0, p1)
        def _(p):
            cols = lanes_at(p * 128, 128)
            qp, kp = q[:, cols], k[:, cols]
            pieces = []
            for j in range(2):
                keep = lane128() < 64 if j == 0 else lane128() >= 64
                scores = dot_nt(jnp.where(keep, kp, jnp.zeros((), BF16)), qp)
                scores = jnp.where(mask[...] > 0.0, scores, -1e30)
                top = jnp.max(scores, axis=0, keepdims=True)
                expo = jnp.exp(scores - top)
                total = jnp.sum(expo, axis=0, keepdims=True)
                weights = (expo * (1.0 / total)).astype(BF16)

                @pl.when(p > 0)
                def _():
                    wait_bytes(prob.at[j], ps.at[j])

                prob[j] = weights
                local_copy(prob.at[j], prob_h.at[p, j], ps.at[j])
                mixed = dot(vt[rows_at(p * 128 + 64 * j, 64), :], weights).astype(BF16)
                for b in range(2):
                    ctxp[b, rows_at((2 * p + j) * 32, 32), :] = mixed[32 * b : 32 * b + 32]
                pieces.append(mixed)
            ctx[:, cols] = jnp.concatenate(pieces, axis=0).T

    def attended():
        for j in range(2):
            wait_bytes(prob.at[j], ps.at[j])
        save(ctxp, ctxp_h)

    def project():
        loaded(P_O)

        @pl.loop(0, 4)
        def _(j):
            cols = lanes_at(j * 256, 256)
            branch = dot(ctx[...], weight(P_O, j * 256, 256)) + vecs[V_BO : V_BO + 1, cols]
            add_stat(1, jnp.sum(row_valid(512, 0) * branch * branch, axis=0, keepdims=True))
            resid[:, cols] = branch + tok[:, cols].astype(F32)

    def normalise(i):
        rows = rows_at(i * 32, 32)
        val = resid[rows, :]
        mean = jnp.sum(val, axis=1, keepdims=True) * (1.0 / 1024)
        centred = val - mean
        scale = lax.rsqrt(jnp.sum(centred * centred, axis=1, keepdims=True) * (1.0 / 1024) + eps_norm)
        return rows, centred * scale, scale

    def norm_first():
        @pl.loop(0, 16, unroll=4)
        def _(i):
            rows, normed, scale = normalise(i)
            n1[rows, :] = normed
            inv1[rows, :] = jnp.broadcast_to(scale, (32, 128))
            low[rows, :] = (normed * vecs[V_GA : V_GA + 1, :] + vecs[V_SA : V_SA + 1, :]).astype(BF16)

        save(n1, n1_h)
        save(inv1, inv1_h)
        transpose_blocks(low, lowp)
        save(lowp, firstp_h)

    def incoming():
        loaded(P_PROJ)
        wait_bytes(hidden, ins.at[0])
        wait_bytes(embed, ins.at[2])
        cot = jnp.where(row_valid(512, 0) > 0.0, embed[...].astype(F32), 0.0).astype(BF16)
        w = weight(P_PROJ, 0, 128)
        for j in range(4):
            cols = pl.ds(256 * j, 256)
            back[:, cols] = row_valid(512, 0) * hidden[:, cols].astype(F32) + dot_nt(
                cot, w[256 * j : 256 * j + 256]
            )
        sums[...] = jnp.zeros_like(sums)

    def expand(k0):
        def tile(j, w):
            cols = lanes_at(k0 * 1024 + j * 256, 256)
            pre = dot(low[...], w) + bias_up[0:1, cols]
            cdf = 0.5 * (1.0 + lax.erf(pre * math.sqrt(0.5)))
            val = (pre * cdf).astype(BF16)
            pdf = jnp.exp(pre * pre * -0.5) * (1.0 / math.sqrt(2 * math.pi))
            slope[:, cols] = (cdf + pre * pdf).astype(BF16)
            half = lanes_at(k0 * 512 + j * 128, 128)
            act[0, :, half] = val[:, :128]
            act[1, :, half] = val[:, 128:]

        wide = FWD_PIECES[P_UP + k0][2] // 256

        @pl.loop(0, wide)
        def _(j):
            tile(j, weight(P_UP + k0, j * 256, 256))

        if wide < 4:
            tile(3, weight(P_REST + k0, 0, 256))

    def contract(k0):
        _, first_col, width = FWD_PIECES[P_DOWN + k0]
        cols = pl.ds(first_col, width)
        w = wbuf[P_DOWN + k0]
        branch = dot(act[0], w[:, :, :, 0].reshape(2048, width))
        branch = branch + dot(act[1], w[:, :, :, 1].reshape(2048, width)) + vecs[V_BD : V_BD + 1, cols]
        add_stat(2, jnp.sum(row_valid(512, 0) * branch * branch, axis=0, keepdims=True))
        first = n1[:, cols] * vecs[V_GA : V_GA + 1, cols] + vecs[V_SA : V_SA + 1, cols]
        resid[:, cols] = first + branch

    def norm_second():
        @pl.loop(0, 16, unroll=4)
        def _(i):
            rows, normed, scale = normalise(i)
            gain = vecs[V_GF : V_GF + 1, :]
            out = normed * gain + vecs[V_SF : V_SF + 1, :]
            low[rows, :] = out.astype(BF16)
            hidden[rows, :] = (out * row_valid(32, i * 32)).astype(BF16)
            grad = back[rows, :]
            scaled = grad * gain
            mean = jnp.sum(scaled, axis=1, keepdims=True) * (1.0 / 1024)
            cross = jnp.sum(scaled * normed, axis=1, keepdims=True) * (1.0 / 1024)
            res = (scaled - mean - normed * cross) * scale
            back[rows, :] = res
            ctx[rows, :] = res.astype(BF16)
            sums[0:1, :] = sums[0:1, :] + jnp.sum(grad * normed, axis=0, keepdims=True)
            sums[1:2, :] = sums[1:2, :] + jnp.sum(grad, axis=0, keepdims=True)

        save(ctx, dg_h)
        save(back, back_h)
        save(hidden, hidden_h)
        save(sums, sums_h)
        embed[...] = (dot(low[...], weight(P_PROJ, 0, 128)) * row_valid(512, 0)).astype(BF16)
        save(embed, embed_h)
        transpose_blocks(low, outp)
        save(outp, outp_h)
        save(stats, stats_h)

    pack_vectors()
    greet_end()
    moves = {
        "own": own, "column": column, "plane": plane, "cast": plane_cast, "pair": pair, "arrive": arrive,
    }
    work = {
        "prepare": prepare,
        "unpack": unpack_vectors,
        "q": lambda: (loaded(P_Q), rotary(P_Q, V_BQ, q, 0.125, None, 0, 4), save(q, q_h)),
        "k": lambda: (loaded(P_K), rotary(P_K, V_BK, k, 1.0, kt, 0, 4), save(kt, kt_h)),
        "v": lambda: (loaded(P_V), value(0, 4), save(v, v_h)),
        "project": project,
        "norm": norm_first,
        "incoming": incoming,
        "tail": norm_second,
    }
    for name, t in FWD_ORDER:
        if name in moves:
            moves[name](t)
        elif name == "attend":
            attend(2 * t, 2 * t + 2)
            if t == 3:
                attended()
        elif name == "up":
            loaded(P_UP + t)
            if P_REST + t < count:
                loaded(P_REST + t)
            expand(t)
            if t == 3:
                save(act, act_h)
                save(slope, slope_h)
        elif name == "down":
            loaded(P_DOWN + t)
            contract(t)
        else:
            work[name]()
    for t in range(count):
        sent(t)
    for out, sem in saved:
        wait_bytes(out, sem)


FWD_SAVED = (
    ((512, 1024), BF16),
    ((1024, 512), BF16),
    ((512, 1024), BF16),
    ((8, 2, 512, 512), BF16),
    ((2, 512, 512), BF16),
    ((512, 1024), F32),
    ((512, 128), F32),
    ((2, 512, 512), BF16),
    ((2, 512, 512), BF16),
    ((2, 512, 2048), BF16),
    ((512, 4096), BF16),
    ((512, 1024), F32),
    ((512, 1024), BF16),
    ((2, 512, 512), BF16),
    ((512, 1024), BF16),
    ((512, 128), BF16),
    ((16, 1024), F32),
    ((8, 128), F32),
    ((512, 128), F32),
    ((512, 128), F32),
    ((8, 1024), F32),
)


def forward_pass(tokens, cot_hidden, cot_embed, vectors, lengths, offsets, order, weights):
    count = len(FWD_PIECES)
    shape = jax.ShapeDtypeStruct
    outs = [shape((4, 2, 2, 2, r, k), dt) for r, k, dt in FWD_TENSORS[1:]]
    outs += [shape(s, dt) for s, dt in FWD_SAVED]
    big = lambda *s: pltpu.VMEM(s, BF16)
    scratch = [
        big(512, 1024),
        pltpu.VMEM((16, 128), F32),
        pltpu.VMEM((4, 2, 2, 2, 16, 128), F32),
        pltpu.VMEM((16, 1024), F32),
        pltpu.VMEM((1, 4096), F32),
        pltpu.VMEM((512, 128), F32),
        pltpu.VMEM((512, 128), F32),
        pltpu.VMEM((512, 512), F32),
        pltpu.VMEM((8, 128), F32),
        big(512, 1024),
        big(512, 1024),
        big(512, 1024),
        big(1024, 512),
        big(1024, 512),
        big(2, 512, 512),
        big(512, 1024),
        big(2, 512, 512),
        big(2, 512, 512),
        pltpu.VMEM((512, 1024), F32),
        pltpu.VMEM((512, 1024), F32),
        pltpu.VMEM((512, 128), F32),
        big(512, 1024),
        big(2, 512, 512),
        big(2, 512, 2048),
        big(512, 4096),
        pltpu.VMEM((512, 1024), F32),
        pltpu.VMEM((8, 1024), F32),
        big(512, 1024),
        big(512, 128),
        big(2, 512, 512),
    ]
    for tensor, _, width in FWD_PIECES[1:]:
        scratch.append(big(4, 2, 2, 2, FWD_TENSORS[tensor][0], width))
    for tensor, _, width in FWD_PIECES[1:]:
        scratch.append(big(FWD_TENSORS[tensor][0], width))
    dma = pltpu.SemaphoreType.DMA
    scratch += [
        dma((count, 9)), dma((count, 9)), dma((count,)), dma((count,)), dma((24,)), dma((2,)), dma((3,)),
        dma((count,)),
    ]
    smem = pl.BlockSpec(memory_space=pltpu.SMEM)
    return pl.pallas_call(
        forward_kernel,
        out_shape=outs,
        in_specs=[ANY, ANY, ANY, smem, smem, smem]
        + [pl.BlockSpec(memory_space=pltpu.VMEM)] * 10
        + [ANY] * 7,
        out_specs=[ANY] * len(outs),
        scratch_shapes=scratch,
        compiler_params=pltpu.CompilerParams(
            collective_id=0, has_side_effects=True, vmem_limit_bytes=62 * 2**20
        ),
        name="forward_pass",
    )(tokens, cot_hidden, cot_embed, lengths, offsets, order, *vectors, *weights)


DOWN_TILE = 1024
R_PROJ, R_DOWN, R_UP, R_OUT, R_Q, R_K, R_VEC, R_V = 0, 1, 5, 9, 10, 11, 12, 13
BWD_OUTS = (
    (32, 128, BF16),
    (1024, 128, BF16),
    (32, 4096, BF16),
    (32, 1024, BF16),
    (32, 1024, BF16),
    (32, 1024, BF16),
    (16, 128, F32),
    (32, 1024, BF16),
)
BWD_PIECES = (
    ((0, 0, 32, 128, BF16),)
    + tuple((1, 256 * k, 256, 128, BF16) for k in range(4))
    + tuple((2, 1024 * k, 32, 1024, BF16) for k in range(4))
    + (
        (3, 0, 32, 1024, BF16),
        (4, 0, 32, 1024, BF16),
        (5, 0, 32, 1024, BF16),
        (6, 0, 16, 128, F32),
        (7, 0, 32, 1024, BF16),
    )
)


BWD_ORDER = (
    ("turn", 0),
    ("acts", 0),
    ("downsib", 0),
    ("begin", 0),
    ("sib", 0),
    ("downown", 0),
    ("net", 1),
    ("net", 2),
    ("downsib", 1),
    ("up", 0),
    ("own", 0),
    ("diagonal", 1),
    ("sib", 5),
    ("first", 0),
    ("downown", 1),
    ("net", 0),
    ("net", 3),
    ("up", 1),
    ("diagonal", 2),
    ("sib", 6),
    ("first", 1),
    ("own", 5),
    ("net", 5),
    ("up", 2),
    ("diagonal", 0),
    ("plane", 1),
    ("sib", 7),
    ("net", 4),
    ("diagonal", 3),
    ("own", 6),
    ("first", 2),
    ("up", 3),
    ("sib", 8),
    ("first", 3),
    ("plane", 0),
    ("plane", 2),
    ("net", 6),
    ("own", 7),
    ("diagonal", 4),
    ("norm", 0),
    ("own", 8),
    ("back", 0),
    ("sib", 9),
    ("plane", 3),
    ("net", 7),
    ("attend", 0),
    ("diagonal", 6),
    ("own", 9),
    ("attend", 1),
    ("plane", 4),
    ("attend", 2),
    ("diagonal", 7),
    ("net", 8),
    ("attend", 3),
    ("bias", 0),
    ("sib", 10),
    ("plane", 6),
    ("column", 5),
    ("sib", 11),
    ("sib", 13),
    ("plane", 7),
    ("net", 9),
    ("own", 10),
    ("sib", 12),
    ("diagonal", 8),
    ("own", 11),
    ("tokens", 0),
    ("own", 13),
    ("diagonal", 5),
    ("own", 12),
    ("tokens", 1),
    ("tokens", 2),
    ("diagonal", 9),
    ("plane", 8),
    ("plane", 5),
    ("net", 10),
    ("plane", 9),
    ("net", 11),
    ("diagonal", 10),
    ("diagonal", 11),
    ("plane", 10),
    ("net", 12),
    ("net", 13),
    ("plane", 11),
    ("diagonal", 12),
    ("diagonal", 13),
    ("plane", 12),
    ("plane", 13),
)
Z_FIRST = (R_UP,)


def backward_kernel(cote_h, lengths_s, offsets_s, order_s, *refs):
    wq_h, wk_h, wv_h, wo_h, wup_h, wdown_h = refs[:6]
    (
        q_h, kt_h, v_h, prob_h, ctxp_h, n1_h, inv1_h, firstp_h, tokp_h, act_h, slope_h,
        back_h, dg_h, outp_h, vecs_h, stats_h, cos_h, sin_h, sumf_h,
    ) = refs[6:25]
    refs = refs[25:]
    grad_h = refs[0]
    outs = refs[1:9]
    refs = refs[9:]
    (
        ring, resid, nbuf, sumf, inv1, dg, dgt, upg, four, slopes, blocks, kt, mask,
        cosine, sine, cot, vecs, stats, sums, sum_up, table, stage_d, stage_u, stage_p,
    ) = refs[:24]
    refs = refs[24:]
    count = len(BWD_PIECES)
    acc, diag, from_x, from_y = (refs[i * count : (i + 1) * count] for i in range(4))
    refs = refs[4 * count :]
    from_z = dict(zip(Z_FIRST, refs))
    ss, rs, ls, ins, rsem, psem, gsem = refs[len(Z_FIRST) :]
    z, y, x, c = place()
    me = device_at(z, y, x, c)
    near_x, near_y = device_at(z, y, 1 - x, c), device_at(z, 1 - y, x, c)
    sibling = device_at(z, y, x, 1 - c)
    others = [(z + kk) % 4 for kk in (1, 2, 3)]
    pack = order_s[me]
    length, offset = lengths_s[pack], offsets_s[pack]

    ring_src = []
    for j in range(4):
        ring_src.append(wdown_h.at[pl.ds(1024 * j, 1024), :])
        ring_src.append(wup_h.at[:, pl.ds(1024 * j, 1024)])
    ring_src += [wo_h, wq_h, wk_h, wv_h]

    def ring_start(n):
        local_copy(ring_src[n], ring.at[n % 3], rsem.at[n])

    def ring_wait(n):
        wait_bytes(ring.at[n % 3], rsem.at[n])
        return ring.at[n % 3]

    def ring_next(n):
        if n + 3 < len(ring_src):
            ring_start(n + 3)

    loads = {}

    def load(name, src, dst):
        n = len(loads)
        loads[name] = (dst, ins.at[n])
        local_copy(src, dst, ins.at[n])

    def ready(name):
        dst, sem = loads[name]
        wait_bytes(dst, sem)

    load("dg", dg_h, dg)
    for p in range(2):
        for h in range(2):
            load("act%d%d" % (p, h), act_h.at[p, :, pl.ds(1024 * h, 1024)], four.at[2 * p + h])
    load("cote", cote_h, cot)
    load("outp", outp_h, blocks.at[0])
    ring_start(0)
    load("slope0", slope_h.at[:, pl.ds(0, 1024)], slopes.at[0])
    load("firstp", firstp_h, blocks.at[1])
    load("back", back_h, resid)
    ring_start(1)
    load("slope1", slope_h.at[:, pl.ds(1024, 1024)], slopes.at[1])
    ring_start(2)
    load("n1", n1_h, nbuf)
    load("inv1", inv1_h, inv1)
    load("vecs", vecs_h, vecs)
    load("sumf", sumf_h, sumf)
    load("stats", stats_h, stats)
    load("cos", cos_h, cosine)
    load("sin", sin_h, sine)
    load("kt", kt_h, kt)
    greet_start(z, y, x, c)

    def out_view(t, *lead):
        out, first, rows, width, _ = BWD_PIECES[t]
        if R_DOWN <= t < R_UP:
            return outs[out].at[lead + (pl.ds(first, rows), slice(None))]
        return outs[out].at[lead + (slice(None), pl.ds(first, width))]

    def give(t, stage):
        send(stage, acc[t], ss.at[t, 0], rs.at[t, 0], sibling)

    def layers(t):
        return z if t in Z_FIRST else slice(None)

    def side(ref, t, rows):
        return ref.at[rows] if t in Z_FIRST else ref.at[:, rows]

    def net(t):
        if t in Z_FIRST:
            for kk, zz in zip((1, 2, 3), others):
                send(acc[t].at[zz], from_z[t].at[3 - kk], ss.at[t, 7], rs.at[t, 7], device_at(zz, y, x, c))
        else:
            spread(t)

    def add_column(t):
        h = acc[t]
        wait_bytes(from_z[t], rs.at[t, 7])

        @pl.loop(0, 4)
        def _(i):
            total = h[z, i // 2, i % 2].astype(F32)
            for k in range(3):
                total = total + from_z[t][k, i // 2, i % 2].astype(F32)
            h[z, i // 2, i % 2] = total.astype(BF16)

        spread(t)

    def spread(t):
        half = BWD_PIECES[t][2] // 2
        h, a = acc[t], layers(t)
        first, second = pl.ds(0, half), pl.ds(half, half)
        send(h.at[a, 1 - y, 1 - x, first], diag[t].at[0], ss.at[t, 1], rs.at[t, 1], near_x)
        send(h.at[a, 1 - y, 1 - x, second], diag[t].at[1], ss.at[t, 2], rs.at[t, 2], near_y)
        send(h.at[a, y, 1 - x, first], side(from_x[t], t, first), ss.at[t, 3], rs.at[t, 3], near_x)
        send(h.at[a, 1 - y, x, second], side(from_y[t], t, second), ss.at[t, 4], rs.at[t, 4], near_y)

    def add_diagonal(t):
        rows = BWD_PIECES[t][2]
        half = rows // 2
        h, a = acc[t], layers(t)
        first, second = pl.ds(0, half), pl.ds(half, half)

        def add(k, yy, xx, lo):
            wait_bytes(diag[t].at[k], rs.at[t, 1 + k])
            if t in Z_FIRST:
                h[z, yy, xx, lo : lo + half, :] = h[z, yy, xx, lo : lo + half, :] + diag[t][k]
                return

            @pl.loop(0, 4)
            def _(i):
                h[i, yy, xx, lo : lo + half, :] = h[i, yy, xx, lo : lo + half, :] + diag[t][k, i]

        add(0, 1 - y, x, 0)
        send(h.at[a, 1 - y, x, first], side(from_y[t], t, first), ss.at[t, 6], rs.at[t, 6], near_y)
        add(1, y, 1 - x, half)
        send(h.at[a, y, 1 - x, second], side(from_x[t], t, second), ss.at[t, 5], rs.at[t, 5], near_x)

    def add_plane(t):
        half = BWD_PIECES[t][2] // 2
        h = acc[t]
        first, second = pl.ds(0, half), pl.ds(half, half)
        wait_bytes(side(from_x[t], t, first), rs.at[t, 3])
        wait_bytes(side(from_x[t], t, second), rs.at[t, 5])
        wait_bytes(side(from_y[t], t, second), rs.at[t, 4])
        wait_bytes(side(from_y[t], t, first), rs.at[t, 6])
        slot = out_view(t, z)
        if t in Z_FIRST:
            h[z, y, x] = h[z, y, x] + from_x[t][...] + from_y[t][...]
        else:

            @pl.loop(0, 4)
            def _(i):
                h[i, y, x] = h[i, y, x] + from_x[t][i] + from_y[t][i]

            for zz in others:
                send(h.at[zz, y, x], slot, ss.at[t, 7], rs.at[t, 7], device_at(zz, y, x, c))
        local_copy(h.at[z, y, x], slot, ls.at[t])

    def finish(t):
        half = BWD_PIECES[t][2] // 2
        three = out_view(t, pl.ds(0, 3))
        if t in Z_FIRST:
            wait_bytes(from_z[t], ss.at[t, 7])
        else:
            wait_bytes(three, rs.at[t, 7])
            wait_bytes(three, ss.at[t, 7])
        wait_bytes(out_view(t, 0), ls.at[t])
        wait_bytes(diag[t].at[0], ss.at[t, 1])
        wait_bytes(diag[t].at[1], ss.at[t, 2])
        for kind in (3, 4, 5, 6):
            wait_bytes(side(from_x[t], t, pl.ds(0, half)), ss.at[t, kind])

    given = {}

    def take_stage(key, t):
        if key in given:
            wait_bytes(acc[given[key]], ss.at[given[key], 0])
        given[key] = t

    def rows_sib(t, lhs, rhs, stage, key):
        take_stage(key, t)
        width = BWD_PIECES[t][3]
        tile = min(width, 1024)

        @pl.loop(0, width // tile)
        def _(j):
            cols = lanes_at(j * tile, tile)
            val = dot(lhs[1 - c], rhs[:, cols]).astype(BF16)
            stage[:, :, :, :, cols] = val.reshape(4, 2, 2, 32, tile)

        give(t, stage)

    def rows_own(t, lhs, rhs):
        width = BWD_PIECES[t][3]
        tile = min(width, 1024)
        wait_bytes(acc[t], rs.at[t, 0])

        @pl.loop(0, width // tile)
        def _(j):
            cols = lanes_at(j * tile, tile)
            val = dot(lhs[c], rhs[:, cols]) + acc[t][:, :, :, :, cols].reshape(512, tile).astype(F32)
            acc[t][:, :, :, :, cols] = val.astype(BF16).reshape(4, 2, 2, 32, tile)

    def down_tile(h, parity, j):
        per = 1024 // DOWN_TILE
        rhs = four[2 * parity + j // per, :, lanes_at((j % per) * DOWN_TILE, DOWN_TILE)]
        return dot(dgt[512 * h : 512 * h + 512, :], rhs)

    def down_blocks(j):
        for b in range(DOWN_TILE // 128):
            s = j * (DOWN_TILE // 128) + b
            yield b, s // 4, (s // 2) % 2, s % 2

    def down_sib(h):
        for k0 in (2 * h, 2 * h + 1):
            take_stage("d%d" % (k0 % 2), R_DOWN + k0)

        @pl.loop(0, 2048 // DOWN_TILE)
        def _(j):
            val = down_tile(h, 1 - c, j).astype(BF16)
            for b, sz, sy, sx in down_blocks(j):
                for i in range(2):
                    stage_d[i, sz, sy, sx] = val[256 * i : 256 * i + 256, 128 * b : 128 * b + 128]

        for k0 in (2 * h, 2 * h + 1):
            give(R_DOWN + k0, stage_d.at[k0 % 2])

    def down_own(h):
        for k0 in (2 * h, 2 * h + 1):
            wait_bytes(acc[R_DOWN + k0], rs.at[R_DOWN + k0, 0])

        @pl.loop(0, 2048 // DOWN_TILE)
        def _(j):
            val = down_tile(h, c, j)
            for b, sz, sy, sx in down_blocks(j):
                for i in range(2):
                    t = R_DOWN + 2 * h + i
                    old = acc[t][sz, sy, sx].astype(F32)
                    acc[t][sz, sy, sx] = (
                        val[256 * i : 256 * i + 256, 128 * b : 128 * b + 128] + old
                    ).astype(BF16)

    def column_sum(ref):
        return dot(jnp.ones((16, 512), BF16), ref)[0:1]

    def row_valid(rows, start):
        r = lax.broadcasted_iota(jnp.int32, (rows, 1), 0) + start
        return ((r >= offset) & (r < offset + length)).astype(F32)

    def norm_back(inv, gain, to_gain, to_shift):
        sums[to_gain : to_gain + 1, :] = jnp.zeros((1, 1024), F32)
        sums[to_shift : to_shift + 1, :] = jnp.zeros((1, 1024), F32)

        @pl.loop(0, 16, unroll=4)
        def _(i):
            rows = rows_at(i * 32, 32)
            grad, normed = resid[rows, :], nbuf[rows, :]
            scaled = grad * vecs[gain : gain + 1, :]
            mean = jnp.sum(scaled, axis=1, keepdims=True) * (1.0 / 1024)
            cross = jnp.sum(scaled * normed, axis=1, keepdims=True) * (1.0 / 1024)
            out = (scaled - mean - normed * cross) * inv[rows, 0:1]
            resid[rows, :] = out
            dg[rows, :] = out.astype(BF16)
            sums[to_gain : to_gain + 1, :] = sums[to_gain : to_gain + 1, :] + jnp.sum(
                grad * normed, axis=0, keepdims=True
            )
            sums[to_shift : to_shift + 1, :] = sums[to_shift : to_shift + 1, :] + jnp.sum(
                grad, axis=0, keepdims=True
            )

    def begin():
        ready("cote")
        cot[...] = jnp.where(row_valid(512, 0) > 0.0, cot[...].astype(F32), 0.0).astype(BF16)
        sums[V_BD : V_BD + 1, :] = column_sum(dg[...])

    def turn():
        @pl.loop(0, 8)
        def _(j):
            dgt[rows_at(j * 128, 128), :] = dg[:, lanes_at(j * 128, 128)].T

    def acts():
        for p in range(2):
            for h in range(2):
                ready("act%d%d" % (p, h))

    def up_grad(k0):
        w = ring_wait(2 * k0)
        ready("slope%d" % k0)

        @pl.loop(0, 1)
        def _(j):
            cols = lanes_at(j * 1024, 1024)
            back = dot_nt(dg[...], w[rows_at(j * 1024, 1024), :]) * slopes[k0 % 2, :, cols].astype(F32)
            upg[k0, :, cols] = back.astype(BF16)

        ring_next(2 * k0)
        if k0 + 2 < 4:
            load("slope%d" % (k0 + 2), slope_h.at[:, pl.ds(1024 * (k0 + 2), 1024)], slopes.at[k0 % 2])
        sum_up[0:1, 1024 * k0 : 1024 * k0 + 1024] = column_sum(upg[k0])

    def first_grad(k0):
        if k0 == 0:
            ready("back")
        w = ring_wait(2 * k0 + 1)

        @pl.loop(0, 1)
        def _(j):
            cols = lanes_at(j * 1024, 1024)
            resid[:, cols] = resid[:, cols] + dot_nt(upg[k0], w[rows_at(j * 1024, 1024), :])

        ring_next(2 * k0 + 1)

    def up_sib(k0):
        if k0 == 0:
            ready("firstp")
        rows_sib(R_UP + k0, blocks.at[1], upg.at[k0], stage_u.at[k0 % 2], "u%d" % (k0 % 2))

    def up_own(k0):
        rows_own(R_UP + k0, blocks.at[1], upg.at[k0])

    def norm_one():
        ready("n1")
        ready("inv1")
        ready("vecs")
        norm_back(inv1, V_GA, V_GA, V_SA)
        sums[V_BO : V_BO + 1, :] = column_sum(dg[...])
        load("ctxp", ctxp_h, blocks.at[0])

    def start_attention():
        load("q", q_h, upg.at[0])
        load("v", v_h, upg.at[1])
        load("tokp", tokp_h, blocks.at[1])
        prob_start(0)

    def prob_start(p):
        for j in range(2):
            local_copy(
                prob_h.at[p, j],
                upg.at[2 + p % 2, :, pl.ds(512 * j, 512)],
                psem.at[p % 2, j],
            )

    def ctx_back():
        w = ring_wait(8)

        @pl.loop(0, 1)
        def _(j):
            four[3, :, lanes_at(j * 1024, 1024)] = dot_nt(dg[...], w[rows_at(j * 1024, 1024), :]).astype(BF16)

        ring_next(8)

    def make_mask():
        s = lax.broadcasted_iota(jnp.int32, (1, 512), 1)
        col_valid = ((s >= offset) & (s < offset + length)).astype(F32)

        @pl.loop(0, 8)
        def _(i):
            mask[rows_at(i * 64, 64), :] = row_valid(64, i * 64) * col_valid

    def lane128():
        return lax.broadcasted_iota(jnp.int32, (1, 128), 1)

    def unturn(val):
        swapped = jnp.where(lane128() % 64 < 32, pltpu.roll(val, 96, 1), pltpu.roll(val, 32, 1))
        return (val * cosine[...] - swapped * sine[...]).astype(BF16)

    def attend_back(p0, p1):
        @pl.loop(p0, p1)
        def _(p):
            cols = lanes_at(p * 128, 128)
            for j in range(2):
                wait_bytes(upg.at[2 + p % 2, :, pl.ds(512 * j, 512)], psem.at[p % 2, j])

            @pl.when(p + 1 < 8)
            def _():
                prob_start(p + 1)

            qp, vp, grad = upg[0, :, cols], upg[1, :, cols], four[3, :, cols]
            dv, dk, dqt = [], [], []
            for j in range(2):
                keep = lane128() < 64 if j == 0 else lane128() >= 64
                low = upg[2 + p % 2, :, 512 * j : 512 * j + 512]
                wide = low.astype(F32)
                back = dot_nt(jnp.where(keep, vp, jnp.zeros((), BF16)), grad)
                row_dot = jnp.sum(wide * back, axis=0, keepdims=True)
                sgrad = jnp.where(mask[...] > 0.0, wide * (back - row_dot), 0.0).astype(BF16)
                dv.append(dot(low, grad))
                dk.append(dot(sgrad, qp))
                dqt.append(dot(kt[rows_at(p * 128 + 64 * j, 64), :], sgrad))
            four[2, :, cols] = jnp.where(lane128() < 64, dv[0], dv[1]).astype(BF16)
            four[1, :, cols] = unturn(jnp.where(lane128() < 64, dk[0], dk[1]))
            four[0, :, cols] = unturn(jnp.concatenate(dqt, axis=0).T * 0.125)

    def bias_sums():
        sums[V_BQ : V_BQ + 1, :] = column_sum(four[0])
        sums[V_BK : V_BK + 1, :] = column_sum(four[1])
        sums[V_BV : V_BV + 1, :] = column_sum(four[2])

    def vector_table():
        ready("stats")
        ready("sumf")
        for b in range(8):
            val = jnp.concatenate(
                [sums[0:7, 128 * b : 128 * b + 128], sumf[0:2, 128 * b : 128 * b + 128], jnp.zeros((1, 128), F32), stats[0:4, :], jnp.zeros((2, 128), F32)],
                axis=0,
            )
            for i in range(4):
                table[b // 2, b % 2, i // 2, i % 2] = val
        for d in range(32):
            table[d // 8, (d // 4) % 2, (d // 2) % 2, d % 2, 9:10, :] = sum_up[
                0:1, 128 * d : 128 * d + 128
            ]
        give(R_VEC, table.at[:, :, :, 1 - c])

    def vector_own():
        wait_bytes(acc[R_VEC], rs.at[R_VEC, 0])
        acc[R_VEC][...] = acc[R_VEC][...] + table[:, :, :, c]

    def token_grad(i):
        w = ring_wait(9 + i)

        @pl.loop(0, 1)
        def _(j):
            cols = lanes_at(j * 1024, 1024)
            resid[:, cols] = resid[:, cols] + dot_nt(four[i], w[rows_at(j * 1024, 1024), :])

    def token_out():
        local_copy(resid, grad_h, gsem)

    moves = {"net": net, "column": add_column, "diagonal": add_diagonal, "plane": add_plane}
    pieces = {
        "turn": turn,
        "acts": lambda: (acts(), greet_end()),
        "begin": begin,
        "norm": lambda: (norm_one(), make_mask()),
        "back": lambda: (start_attention(), ctx_back()),
        "bias": bias_sums,
    }

    def sib(t):
        if t == R_PROJ:
            ready("outp")
            rows_sib(t, blocks.at[0], cot, stage_p, "p")
        elif t < R_OUT:
            up_sib(t - R_UP)
        elif t == R_OUT:
            ready("ctxp")
            rows_sib(t, blocks.at[0], dg, stage_u.at[0], "u0")
        elif t == R_VEC:
            vector_table()
        else:
            if t == R_Q:
                ready("tokp")
            n, stage = {R_Q: (0, 1), R_K: (1, 0), R_V: (2, 1)}[t]
            rows_sib(t, blocks.at[1], four.at[n], stage_u.at[stage], "u%d" % stage)

    def mine(t):
        if t == R_PROJ:
            rows_own(t, blocks.at[0], cot)
        elif t < R_OUT:
            up_own(t - R_UP)
        elif t == R_OUT:
            rows_own(t, blocks.at[0], dg)
        elif t == R_VEC:
            vector_own()
        else:
            rows_own(t, blocks.at[1], four.at[{R_Q: 0, R_K: 1, R_V: 2}[t]])

    def attend_pairs(n):
        if n == 0:
            for name in ("kt", "q", "v", "cos", "sin"):
                ready(name)
        attend_back(2 * n, 2 * n + 2)

    def tokens(n):
        token_grad(n)
        if n == 2:
            token_out()

    moves.update(
        sib=sib, own=mine, attend=attend_pairs, tokens=tokens, up=up_grad, first=first_grad,
        downsib=down_sib, downown=down_own,
    )
    ready("dg")
    for name, t in BWD_ORDER:
        if name in moves:
            moves[name](t)
        else:
            pieces[name]()
    for t in range(count):
        finish(t)
    for t in given.values():
        wait_bytes(acc[t], ss.at[t, 0])
    wait_bytes(acc[R_VEC], ss.at[R_VEC, 0])
    wait_bytes(resid, gsem)


def backward_pass(cot_embed, lengths, offsets, order, weights, kept):
    count = len(BWD_PIECES)
    outs = [jax.ShapeDtypeStruct((512, 1024), F32)]
    outs += [jax.ShapeDtypeStruct((4, r, k), dt) for r, k, dt in BWD_OUTS]
    big = lambda *s: pltpu.VMEM(s, BF16)
    wide = lambda *s: pltpu.VMEM(s, F32)
    scratch = [
        big(3, 1024, 1024),
        wide(512, 1024),
        wide(512, 1024),
        wide(8, 1024),
        wide(512, 128),
        big(512, 1024),
        big(1024, 512),
        big(4, 512, 1024),
        big(4, 512, 1024),
        big(2, 512, 1024),
        big(2, 2, 512, 512),
        big(1024, 512),
        wide(512, 512),
        wide(512, 128),
        wide(512, 128),
        big(512, 128),
        wide(16, 1024),
        wide(8, 128),
        wide(16, 1024),
        wide(1, 4096),
        wide(4, 2, 2, 2, 16, 128),
        big(2, 4, 2, 2, 256, 128),
        big(2, 4, 2, 2, 32, 1024),
        big(4, 2, 2, 32, 128),
    ]
    for lead, flat in (((4, 2, 2), (4, 2, 2)), ((2, 4), (2,)), ((4,), ()), ((4,), ())):
        for t, (_, _, rows, width, dtype) in enumerate(BWD_PIECES):
            shape = flat if t in Z_FIRST else lead
            scratch.append(pltpu.VMEM(shape + (rows // 2 if lead == (2, 4) else rows, width), dtype))
    for t in Z_FIRST:
        scratch.append(big(3, 2, 2, *BWD_PIECES[t][2:4]))
    dma = pltpu.SemaphoreType.DMA
    scratch += [dma((count, 8)), dma((count, 8)), dma((count,)), dma((32,)), dma((12,)), dma((2, 2)), dma]
    smem = pl.BlockSpec(memory_space=pltpu.SMEM)
    return pl.pallas_call(
        backward_kernel,
        out_shape=outs,
        in_specs=[ANY, smem, smem, smem] + [ANY] * (6 + 19),
        out_specs=[ANY] * len(outs),
        scratch_shapes=scratch,
        compiler_params=pltpu.CompilerParams(
            collective_id=1, has_side_effects=True, vmem_limit_bytes=62 * 2**20
        ),
        name="backward_pass",
    )(cot_embed, lengths, offsets, order, *weights, *kept)


def finish_kernel(*refs):
    parts, (hidden_h, embed_h, tokens_h) = refs[:8], refs[8:11]
    outs, hidden_o, embed_o, tokens_o = refs[11:19], *refs[19:22]
    bufs, results, carry, ins, done, moved = refs[22:30], refs[30:38], refs[38:41], *refs[41:44]
    order = (6, 1, 2, 3, 4, 5, 7, 0)
    for i in order:
        local_copy(parts[i], bufs[i], ins.at[i])
    moves = ((hidden_h, hidden_o), (embed_h, embed_o), (tokens_h, tokens_o))
    for i, (src, _) in enumerate(moves):
        local_copy(src, carry[i], moved.at[i, 0])
    me = lax.axis_index("dp")
    z = me // 8
    for i in order:
        wait_bytes(bufs[i], ins.at[i])
        buf = bufs[i]
        total = buf[0].astype(F32) + buf[1].astype(F32) + buf[2].astype(F32) + buf[3].astype(F32)
        if i == 1:
            total = total.T
        if i == 6:
            own = jnp.where(me % 4 == 0, total[:, 0:32], 0.0)
            for j in range(1, 4):
                own = own + jnp.where(me % 4 == j, total[:, 32 * j : 32 * j + 32], 0.0)
            stat = jnp.sum(total, axis=1, keepdims=True)
            root = jnp.sqrt(stat[10:13] / (stat[13:14] * (1024 / 128)))
            results[6][...] = jnp.zeros((16, 256), F32)
            results[6][:, 0:32] = own
            results[6][:, 128:256] = total
            results[6][10:13, 0:1] = root
        else:
            results[i][...] = total
            for t in Z_FIRST:
                if BWD_PIECES[t][0] == i:
                    cols = slice(BWD_PIECES[t][1], BWD_PIECES[t][1] + BWD_PIECES[t][3])
                    results[i][:, cols] = buf[z, :, cols].astype(F32)
        local_copy(results[i], outs[i], done.at[i])
        if i == 2:
            for k, (src, dst) in enumerate(moves):
                wait_bytes(carry[k], moved.at[k, 0])
                local_copy(carry[k], dst, moved.at[k, 1])
    for i in order:
        wait_bytes(results[i], done.at[i])
    for i in range(3):
        wait_bytes(carry[i], moved.at[i, 1])


def finish(parts, hidden, embed, grad):
    shape = jax.ShapeDtypeStruct
    sums = [shape(p.shape[1:], F32) for p in parts]
    sums[1] = shape((128, 1024), F32)
    sums[6] = shape((16, 256), F32)
    moved = [shape(a.shape, a.dtype) for a in (hidden, embed, grad)]
    dma = pltpu.SemaphoreType.DMA
    return pl.pallas_call(
        finish_kernel,
        out_shape=sums + moved,
        in_specs=[pl.BlockSpec(memory_space=pltpu.HBM)] * 11,
        out_specs=[pl.BlockSpec(memory_space=pltpu.HBM)] * 11,
        scratch_shapes=[pltpu.VMEM(p.shape, p.dtype) for p in parts]
        + [pltpu.VMEM(s.shape, F32) for s in sums]
        + [pltpu.VMEM(a.shape, a.dtype) for a in moved]
        + [dma((8,)), dma((8,)), dma((3, 2))],
        compiler_params=pltpu.CompilerParams(vmem_limit_bytes=60 * 2**20),
        name="finish",
    )(*parts, hidden, embed, grad)


def shards(
    tokens, cot_hidden, cot_embed, lengths, offsets, pack_order,
    w_query, b_query, w_key, b_key, w_value, b_value, w_out, b_out, gain_attn, shift_attn,
    w_up, b_up, w_down, b_down, gain_ffn, shift_ffn, w_proj,
):
    done = forward_pass(
        tokens, cot_hidden, cot_embed,
        (b_query, b_key, b_value, b_out, gain_attn, shift_attn, b_down, gain_ffn, shift_ffn, b_up),
        lengths, offsets, pack_order,
        (w_query, w_key, w_value, w_out, w_up, w_proj, w_down),
    )
    weights = [w.reshape(-1, w.shape[-1]) for w in list(done[:5]) + list(done[6:7])]
    kept = list(done[7 : 7 + 14]) + list(done[7 + 16 :])
    back = backward_pass(cot_embed, lengths, offsets, pack_order, weights, kept)
    *totals, hidden, embed, grad = finish(back[1:], done[7 + 14], done[7 + 15], back[0])
    proj, down, up, out, query, key, vec, val = totals
    own = vec[:9, :32]
    return (
        hidden, embed, grad,
        query, own[V_BQ], key, own[V_BK], val, own[V_BV], out, own[V_BO],
        own[V_GA], own[V_SA], up, vec[9, 128:], down, own[V_BD], own[V_GF], own[V_SF],
        proj, vec[10:13, 0],
    )


def shards_any(
    tokens,
    cot_hidden,
    cot_embed,
    lengths,
    offsets,
    pack_order,
    w_query,
    b_query,
    w_key,
    b_key,
    w_value,
    b_value,
    w_out,
    b_out,
    gain_attn,
    shift_attn,
    w_up,
    b_up,
    w_down,
    b_down,
    gain_ffn,
    shift_ffn,
    w_proj,
):
    gathered = (
        lax.all_gather(w_query, "dp", axis=0, tiled=True),
        lax.all_gather(w_key, "dp", axis=0, tiled=True),
        lax.all_gather(w_value, "dp", axis=0, tiled=True),
        lax.all_gather(w_out, "dp", axis=0, tiled=True),
        lax.all_gather(w_up, "dp", axis=0, tiled=True),
        lax.all_gather(w_down, "dp", axis=0, tiled=True),
        lax.all_gather(w_proj, "dp", axis=0, tiled=True),
        lax.all_gather(b_query, "dp", axis=0, tiled=True),
        lax.all_gather(b_key, "dp", axis=0, tiled=True),
        lax.all_gather(b_value, "dp", axis=0, tiled=True),
        lax.all_gather(b_out, "dp", axis=0, tiled=True),
        lax.all_gather(gain_attn, "dp", axis=0, tiled=True),
        lax.all_gather(shift_attn, "dp", axis=0, tiled=True),
        lax.all_gather(b_up, "dp", axis=0, tiled=True),
        lax.all_gather(b_down, "dp", axis=0, tiled=True),
        lax.all_gather(gain_ffn, "dp", axis=0, tiled=True),
        lax.all_gather(shift_ffn, "dp", axis=0, tiled=True),
    )
    wt_query, wt_key, wt_value, wt_out, wt_up, wt_down, wt_proj = gathered[:7]
    vectors = [piece.astype(jnp.float32) for piece in gathered[7:]]
    (
        bias_query,
        bias_key,
        bias_value,
        bias_out,
        norm_gain_a,
        norm_shift_a,
        bias_up,
        bias_down,
        norm_gain_f,
        norm_shift_f,
    ) = vectors
    row_count = tokens.shape[0]
    model_width = tokens.shape[1]
    head_count = H
    head_dim = model_width // head_count
    device = lax.axis_index("dp")
    slots = jnp.arange(pack_order.shape[0], dtype=jnp.int32)
    pack_id = jnp.sum(jnp.where(slots == device, pack_order, 0))
    length = jnp.sum(jnp.where(slots == pack_id, lengths, 0))
    offset = jnp.sum(jnp.where(slots == pack_id, offsets, 0))
    row_index = jnp.arange(row_count, dtype=jnp.int32)
    is_valid = (row_index >= offset) & (row_index < offset + length)
    keep_rows = is_valid.astype(jnp.float32)[:, None]
    cosine, sine_part = rope_tables((row_index - offset).astype(jnp.float32), head_dim)
    query_pre = matmul(tokens, wt_query) + bias_query
    key_pre = matmul(tokens, wt_key) + bias_key
    value_low = (
        (matmul(tokens, wt_value) + bias_value)
        .astype(jnp.bfloat16)
        .reshape(row_count, head_count, head_dim)
    )
    query_rot = rotate(
        query_pre.reshape(row_count, head_count, head_dim), cosine, sine_part
    ).astype(jnp.bfloat16)
    key_rot = rotate(key_pre.reshape(row_count, head_count, head_dim), cosine, sine_part).astype(
        jnp.bfloat16
    )
    score_scale = 1.0 / math.sqrt(head_dim)
    key_valid = is_valid[None, None, :]
    allowed = is_valid[None, :, None] & key_valid
    masked = masked_scores(query_rot, key_rot, allowed, score_scale)
    row_top = jnp.max(masked, axis=-1, keepdims=True)
    exponent = jnp.exp(masked - row_top)
    row_total = jnp.sum(exponent, axis=-1, keepdims=True)
    prob_low = (exponent / row_total).astype(jnp.bfloat16)
    contexts = jnp.einsum("hqk,khd->qhd", prob_low, value_low, preferred_element_type=jnp.float32)
    log_totals = row_top + jnp.log(row_total)
    context = contexts.astype(jnp.bfloat16).reshape(row_count, model_width)
    tokens_wide = tokens.astype(jnp.float32)
    attn_branch = matmul(context, wt_out) + bias_out
    first, normed_one, inverse_one = norm_forward(
        tokens_wide + attn_branch, norm_gain_a, norm_shift_a
    )
    first_low = first.astype(jnp.bfloat16)
    up_pre = matmul(first_low, wt_up) + bias_up
    act_full, gelu_pull = jax.vjp(exact_gelu, up_pre)
    act_low = act_full.astype(jnp.bfloat16)
    down_branch = matmul(act_low, wt_down) + bias_down
    out, normed_two, inverse_two = norm_forward(first + down_branch, norm_gain_f, norm_shift_f)
    out_low = out.astype(jnp.bfloat16)
    hidden = (out * keep_rows).astype(jnp.bfloat16)
    embedding = (matmul(out_low, wt_proj) * keep_rows).astype(jnp.bfloat16)
    stat_sums = lax.psum(
        (
            jnp.sum(keep_rows * tokens_wide * tokens_wide),
            jnp.sum(keep_rows * attn_branch * attn_branch),
            jnp.sum(keep_rows * down_branch * down_branch),
            jnp.sum(keep_rows),
        ),
        "dp",
    )
    rms_stats = jnp.sqrt(
        jnp.stack([stat_sums[0], stat_sums[1], stat_sums[2]]) / (stat_sums[3] * model_width)
    )
    backward_set = (
        lax.all_gather(w_query, "dp", axis=0, tiled=True),
        lax.all_gather(w_key, "dp", axis=0, tiled=True),
        lax.all_gather(w_value, "dp", axis=0, tiled=True),
        lax.all_gather(w_out, "dp", axis=0, tiled=True),
        lax.all_gather(w_up, "dp", axis=0, tiled=True),
        lax.all_gather(w_down, "dp", axis=0, tiled=True),
        lax.all_gather(w_proj, "dp", axis=0, tiled=True),
        lax.all_gather(b_query, "dp", axis=0, tiled=True),
        lax.all_gather(b_key, "dp", axis=0, tiled=True),
        lax.all_gather(b_value, "dp", axis=0, tiled=True),
        lax.all_gather(b_out, "dp", axis=0, tiled=True),
        lax.all_gather(gain_attn, "dp", axis=0, tiled=True),
        lax.all_gather(shift_attn, "dp", axis=0, tiled=True),
        lax.all_gather(b_up, "dp", axis=0, tiled=True),
        lax.all_gather(b_down, "dp", axis=0, tiled=True),
        lax.all_gather(gain_ffn, "dp", axis=0, tiled=True),
        lax.all_gather(shift_ffn, "dp", axis=0, tiled=True),
    )
    back_query, back_key, back_value, back_out, back_up, back_down, back_proj = backward_set[:7]
    back_gain_a = backward_set[11].astype(jnp.float32)
    back_gain_f = backward_set[15].astype(jnp.float32)
    cot_low = jnp.where(is_valid[:, None], cot_embed, jnp.zeros_like(cot_embed))
    grad_w_proj = matmul_tn(out_low, cot_low)
    grad_out = keep_rows * cot_hidden.astype(jnp.float32) + matmul_nt(cot_low, back_proj)
    grad_resid_two, grad_gain_f, grad_shift_f = norm_backward(
        grad_out, normed_two, inverse_two, back_gain_f
    )
    down_grad = grad_resid_two.astype(jnp.bfloat16)
    grad_w_down = matmul_tn(act_low, down_grad)
    grad_b_down = jnp.sum(down_grad.astype(jnp.float32), axis=0)
    up_grad = gelu_pull(matmul_nt(down_grad, back_down))[0].astype(jnp.bfloat16)
    grad_w_up = matmul_tn(first_low, up_grad)
    grad_b_up = jnp.sum(up_grad.astype(jnp.float32), axis=0)
    grad_first = grad_resid_two + matmul_nt(up_grad, back_up)
    grad_resid_one, grad_gain_a, grad_shift_a = norm_backward(
        grad_first, normed_one, inverse_one, back_gain_a
    )
    attn_grad = grad_resid_one.astype(jnp.bfloat16)
    grad_w_out = matmul_tn(context, attn_grad)
    grad_b_out = jnp.sum(attn_grad.astype(jnp.float32), axis=0)
    ctx_grad = (
        matmul_nt(attn_grad, back_out).astype(jnp.bfloat16).reshape(row_count, head_count, head_dim)
    )
    allowed = is_valid[None, :, None] & key_valid
    masked = masked_scores(query_rot, key_rot, allowed, score_scale)
    prob_full = jnp.exp(masked - log_totals)
    prob_low = prob_full.astype(jnp.bfloat16)
    prob_grad = jnp.einsum("qhd,khd->hqk", ctx_grad, value_low, preferred_element_type=jnp.float32)
    value_sum = jnp.einsum("hqk,qhd->khd", prob_low, ctx_grad, preferred_element_type=jnp.float32)
    row_dot = jnp.sum(prob_full * prob_grad, axis=-1, keepdims=True)
    score_grad = jnp.where(allowed, prob_full * (prob_grad - row_dot), 0.0).astype(jnp.bfloat16)
    query_parts = (
        jnp.einsum("hqk,khd->qhd", score_grad, key_rot, preferred_element_type=jnp.float32)
        * score_scale
    )
    key_sum = (
        jnp.einsum("hqk,qhd->khd", score_grad, query_rot, preferred_element_type=jnp.float32)
        * score_scale
    )
    query_grad = (
        unrotate(query_parts, cosine, sine_part)
        .reshape(row_count, model_width)
        .astype(jnp.bfloat16)
    )
    key_grad = (
        unrotate(key_sum, cosine, sine_part).reshape(row_count, model_width).astype(jnp.bfloat16)
    )
    value_grad = value_sum.reshape(row_count, model_width).astype(jnp.bfloat16)
    grad_w_query = matmul_tn(tokens, query_grad)
    grad_b_query = jnp.sum(query_grad.astype(jnp.float32), axis=0)
    grad_w_key = matmul_tn(tokens, key_grad)
    grad_b_key = jnp.sum(key_grad.astype(jnp.float32), axis=0)
    grad_w_value = matmul_tn(tokens, value_grad)
    grad_b_value = jnp.sum(value_grad.astype(jnp.float32), axis=0)
    grad_tokens = (
        grad_resid_one
        + matmul_nt(query_grad, back_query)
        + matmul_nt(key_grad, back_key)
        + matmul_nt(value_grad, back_value)
    )
    all_parts = (
        lax.psum_scatter(grad_w_query, "dp", scatter_dimension=0, tiled=True),
        lax.psum_scatter(grad_w_key, "dp", scatter_dimension=0, tiled=True),
        lax.psum_scatter(grad_w_value, "dp", scatter_dimension=0, tiled=True),
        lax.psum_scatter(grad_w_out, "dp", scatter_dimension=0, tiled=True),
        lax.psum_scatter(grad_b_query, "dp", scatter_dimension=0, tiled=True),
        lax.psum_scatter(grad_b_key, "dp", scatter_dimension=0, tiled=True),
        lax.psum_scatter(grad_b_value, "dp", scatter_dimension=0, tiled=True),
        lax.psum_scatter(grad_b_out, "dp", scatter_dimension=0, tiled=True),
        lax.psum_scatter(grad_gain_a, "dp", scatter_dimension=0, tiled=True),
        lax.psum_scatter(grad_shift_a, "dp", scatter_dimension=0, tiled=True),
        lax.psum_scatter(grad_w_up, "dp", scatter_dimension=0, tiled=True),
        lax.psum_scatter(grad_w_down, "dp", scatter_dimension=0, tiled=True),
        lax.psum_scatter(grad_w_proj, "dp", scatter_dimension=0, tiled=True),
        lax.psum_scatter(grad_b_up, "dp", scatter_dimension=0, tiled=True),
        lax.psum_scatter(grad_b_down, "dp", scatter_dimension=0, tiled=True),
        lax.psum_scatter(grad_gain_f, "dp", scatter_dimension=0, tiled=True),
        lax.psum_scatter(grad_shift_f, "dp", scatter_dimension=0, tiled=True),
    )
    attn_parts = all_parts[:10]
    ffn_parts = all_parts[10:]
    return (
        hidden,
        embedding,
        grad_tokens,
        attn_parts[0],
        attn_parts[4],
        attn_parts[1],
        attn_parts[5],
        attn_parts[2],
        attn_parts[6],
        attn_parts[3],
        attn_parts[7],
        attn_parts[8],
        attn_parts[9],
        ffn_parts[0],
        ffn_parts[3],
        ffn_parts[1],
        ffn_parts[4],
        ffn_parts[5],
        ffn_parts[6],
        ffn_parts[2],
        rms_stats,
    )


def solution(mesh):
    fast = mesh.shape["dp"] == 32
    placed = (
        P("dp", None),
        P("dp", None),
        P("dp", None),
        P(),
        P(),
        P(),
        P("dp", None),
        P("dp"),
        P("dp", None),
        P("dp"),
        P("dp", None),
        P("dp"),
        P("dp", None),
        P("dp"),
        P("dp"),
        P("dp"),
        P("dp", None),
        P("dp"),
        P("dp", None),
        P("dp"),
        P("dp"),
        P("dp"),
        P("dp", None),
    )
    return jax.shard_map(
        shards if fast else shards_any,
        mesh=mesh,
        in_specs=placed,
        out_specs=(
            P("dp", None),
            P("dp", None),
            P("dp", None),
            P("dp", None),
            P("dp"),
            P("dp", None),
            P("dp"),
            P("dp", None),
            P("dp"),
            P("dp", None),
            P("dp"),
            P("dp"),
            P("dp"),
            P("dp", None),
            P("dp"),
            P("dp", None),
            P("dp"),
            P("dp"),
            P("dp"),
            P("dp", None),
            P(),
        ),
        check_vma=False,
    )
```

```python
import functools
import math

import jax
import jax.numpy as jnp
from jax import lax
from jax.experimental import pallas as pl
from jax.experimental.pallas import tpu as pltpu
from jax.sharding import PartitionSpec as P

MESH = pl.DeviceIdType.MESH

H = 16


eps_norm = 1e-05
neg_large = -1e30


def matmul(left, right):
    return jnp.dot(left, right, preferred_element_type=jnp.float32)


def matmul_nt(left, right):
    return lax.dot_general(
        left, right, (((1,), (1,)), ((), ())), preferred_element_type=jnp.float32
    )


def matmul_tn(left, right):
    return lax.dot_general(
        left, right, (((0,), (0,)), ((), ())), preferred_element_type=jnp.float32
    )


def exact_gelu(values):
    return jax.nn.gelu(values, approximate=False)


def norm_forward(values, gain, shift):
    row_mean = jnp.mean(values, axis=-1, keepdims=True)
    centred = values - row_mean
    inverse = lax.rsqrt(jnp.mean(centred * centred, axis=-1, keepdims=True) + eps_norm)
    normed = centred * inverse
    return (normed * gain + shift, normed, inverse)


def norm_backward(grad_in, normed, inverse, gain):
    scaled = grad_in * gain
    adjusted = (
        scaled
        - jnp.mean(scaled, axis=-1, keepdims=True)
        - normed * jnp.mean(scaled * normed, axis=-1, keepdims=True)
    )
    return (adjusted * inverse, jnp.sum(grad_in * normed, axis=0), jnp.sum(grad_in, axis=0))


def rope_tables(position, head_dim):
    half_dim = head_dim // 2
    freq_index = jnp.arange(half_dim, dtype=jnp.float32)
    frequency = jnp.exp(-math.log(10000.0) * 2.0 * freq_index / head_dim)
    angles = position[:, None] * frequency[None, :]
    return (jnp.cos(angles)[:, None, :], jnp.sin(angles)[:, None, :])


def rotate(values, cosine, sine_part):
    half_dim = values.shape[-1] // 2
    first_half = values[..., :half_dim]
    second = values[..., half_dim:]
    return jnp.concatenate(
        [first_half * cosine - second * sine_part, second * cosine + first_half * sine_part],
        axis=-1,
    )


def unrotate(grad_in, cosine, sine_part):
    half_dim = grad_in.shape[-1] // 2
    first_half = grad_in[..., :half_dim]
    second = grad_in[..., half_dim:]
    return jnp.concatenate(
        [first_half * cosine + second * sine_part, second * cosine - first_half * sine_part],
        axis=-1,
    )


def masked_scores(query_block, key_rot, allowed, score_scale):
    raw_scores = jnp.einsum(
        "qhd,khd->hqk", query_block, key_rot, preferred_element_type=jnp.float32
    )
    return jnp.where(allowed, raw_scores * score_scale, neg_large)


def device_at(z, y, x, c):
    return ((z * 2 + y) * 2 + x) * 2 + c


def wait_bytes(ref, sem):
    pltpu.make_async_copy(ref, ref, sem).wait()


def send(src, dst, sem_out, sem_in, target):
    pltpu.make_async_remote_copy(
        src_ref=src,
        dst_ref=dst,
        send_sem=sem_out,
        recv_sem=sem_in,
        device_id=(target,),
        device_id_type=MESH,
    ).start()


F32, BF16 = jnp.float32, jnp.bfloat16
ANY = pl.BlockSpec(memory_space=pl.ANY)
FWD_TENSORS = (
    (16, 128, F32),
    (32, 1024, BF16),
    (32, 1024, BF16),
    (32, 1024, BF16),
    (32, 1024, BF16),
    (32, 4096, BF16),
    (32, 128, BF16),
    (128, 1024, BF16),
)
FWD_PIECES = (
    ((0, 0, 128), (1, 0, 1024), (2, 0, 1024), (3, 0, 1024), (4, 0, 1024))
    + tuple((5, 1024 * k, 1024) for k in range(4))
    + ((6, 0, 128),)
    + ((7, 0, 256), (7, 256, 256), (7, 512, 256), (7, 768, 128), (7, 896, 128))
)
P_VEC, P_Q, P_K, P_V, P_O, P_UP, P_PROJ, P_DOWN, P_REST = 0, 1, 2, 3, 4, 5, 9, 10, 15
PLANE_FIRST = ()
V_BQ, V_BK, V_BV, V_BO, V_GA, V_SA, V_BD, V_GF, V_SF = range(9)


(
    F_OWN,
    F_PREPARE,
    F_COLUMN,
    F_PLANE,
    F_PAIR,
    F_ARRIVE,
    F_UNPACK,
    F_Q,
    F_K,
    F_V,
    F_ATTEND,
    F_PROJECT,
    F_NORM,
    F_UP,
    F_INCOMING,
    F_DOWN,
    F_TAIL,
) = range(17)
FWD_ORDER = (
    (F_OWN, 0),
    (F_OWN, 1),
    (F_OWN, 2),
    (F_OWN, 3),
    (F_OWN, 4),
    (F_OWN, 5),
    (F_OWN, 6),
    (F_OWN, 7),
    (F_PREPARE, 0),
    (F_OWN, 8),
    (F_COLUMN, 0),
    (F_OWN, 9),
    (F_COLUMN, 1),
    (F_PLANE, 0),
    (F_OWN, 10),
    (F_COLUMN, 2),
    (F_PLANE, 1),
    (F_PAIR, 0),
    (F_OWN, 11),
    (F_COLUMN, 3),
    (F_PLANE, 2),
    (F_PAIR, 1),
    (F_ARRIVE, 0),
    (F_OWN, 12),
    (F_COLUMN, 4),
    (F_UNPACK, 0),
    (F_PLANE, 3),
    (F_PAIR, 2),
    (F_ARRIVE, 1),
    (F_OWN, 13),
    (F_COLUMN, 5),
    (F_Q, 0),
    (F_PLANE, 4),
    (F_PAIR, 3),
    (F_ARRIVE, 2),
    (F_OWN, 14),
    (F_COLUMN, 6),
    (F_K, 0),
    (F_PLANE, 5),
    (F_PAIR, 4),
    (F_ARRIVE, 3),
    (F_COLUMN, 7),
    (F_V, 0),
    (F_PLANE, 6),
    (F_ATTEND, 0),
    (F_PAIR, 5),
    (F_ARRIVE, 4),
    (F_COLUMN, 8),
    (F_ATTEND, 1),
    (F_PLANE, 7),
    (F_ATTEND, 2),
    (F_PAIR, 6),
    (F_ARRIVE, 5),
    (F_COLUMN, 9),
    (F_ATTEND, 3),
    (F_PLANE, 8),
    (F_PROJECT, 0),
    (F_PAIR, 7),
    (F_NORM, 0),
    (F_ARRIVE, 6),
    (F_COLUMN, 10),
    (F_UP, 0),
    (F_PLANE, 9),
    (F_PAIR, 8),
    (F_ARRIVE, 7),
    (F_COLUMN, 11),
    (F_UP, 1),
    (F_PLANE, 10),
    (F_PAIR, 9),
    (F_ARRIVE, 8),
    (F_COLUMN, 12),
    (F_UP, 2),
    (F_PLANE, 11),
    (F_PAIR, 10),
    (F_ARRIVE, 9),
    (F_COLUMN, 13),
    (F_UP, 3),
    (F_PLANE, 12),
    (F_PAIR, 11),
    (F_ARRIVE, 10),
    (F_COLUMN, 14),
    (F_INCOMING, 0),
    (F_PLANE, 13),
    (F_DOWN, 0),
    (F_PAIR, 12),
    (F_ARRIVE, 11),
    (F_PLANE, 14),
    (F_DOWN, 1),
    (F_PAIR, 13),
    (F_ARRIVE, 12),
    (F_PAIR, 14),
    (F_DOWN, 2),
    (F_ARRIVE, 13),
    (F_ARRIVE, 14),
    (F_DOWN, 3),
    (F_DOWN, 4),
    (F_TAIL, 0),
)


def dot(left, right):
    return jnp.dot(left, right, preferred_element_type=F32)


def dot_nt(left, right):
    return lax.dot_general(left, right, (((1,), (1,)), ((), ())), preferred_element_type=F32)


def local_copy(src, dst, sem):
    pltpu.make_async_copy(src, dst, sem).start()


def lanes_at(start, size):
    return pl.ds(pl.multiple_of(start, 128), size)


def rows_at(start, size):
    return pl.ds(pl.multiple_of(start, size), size)


def place():
    me = lax.axis_index("dp")
    return me // 8, (me // 4) % 2, (me // 2) % 2, me % 2


def greet_start(z, y, x, c):
    others = [(z + k) % 4 for k in (1, 2, 3)]
    peers = [device_at(z, y, 1 - x, c), device_at(z, 1 - y, x, c), device_at(z, y, x, 1 - c)]
    peers += [device_at(zz, y, x, c) for zz in others]
    barrier = pltpu.get_barrier_semaphore()
    for peer in peers:
        pl.semaphore_signal(barrier, inc=1, device_id=(peer,), device_id_type=MESH)


def greet_end():
    pl.semaphore_wait(pltpu.get_barrier_semaphore(), 6)


def transpose_blocks(src, dst):
    @pl.loop(0, src.shape[1] // 128)
    def _(j):
        block = src[:, lanes_at(j * 128, 128)].T
        for b in range(4):
            dst[b % 2, rows_at((2 * j + b // 2) * 32, 32), :] = block[32 * b : 32 * b + 32]


def forward_kernel(
    tokens_h, cot_h, cote_h, lengths_s, offsets_s, order_s, *refs
):
    vectors = refs[:10]
    refs = refs[10:]
    src = (None,) + refs[:7]
    refs = refs[7:]
    full = (None,) + refs[:7]
    (
        q_h, kt_h, v_h, prob_h, ctxp_h, n1_h, inv1_h, firstp_h, tokp_h, act_h, slope_h,
        back_h, dg_h, low_h, hidden_h, vecs_h, stats_h, cos_h, sin_h, sums_h,
    ) = refs[7:27]
    refs = refs[27:]
    (
        tok, packed, table, vecs, bias_up, cosine, sine, mask, stats,
        q, k, v, kt, vt, prob, ctx, ctxp, tokp, resid, n1, inv1, low, lowp, act, slope, back, sums,
        hidden, embed,
    ) = refs[:29]
    refs = refs[29:]
    count = len(FWD_PIECES)
    wbuf = (None,) + refs[: count - 1]
    mybuf = (None,) + refs[count - 1 : 2 * count - 2]
    ss, rs, ls, ld, os, ps, ins, ms = refs[2 * count - 2 :]
    z, y, x, c = place()
    me = device_at(z, y, x, c)
    near_x, near_y = device_at(z, y, 1 - x, c), device_at(z, 1 - y, x, c)
    sibling = device_at(z, y, x, 1 - c)
    others = [(z + kk) % 4 for kk in (1, 2, 3)]

    greet_start(z, y, x, c)
    for t in range(1, count):
        tensor, first, width = FWD_PIECES[t]
        local_copy(src[tensor].at[:, pl.ds(first, width)], mybuf[t], ms.at[t])
    local_copy(tokens_h, tok, ins.at[1])
    local_copy(cot_h, hidden, ins.at[0])
    local_copy(cote_h, embed, ins.at[2])

    def home(t, *lead):
        tensor, first, width = FWD_PIECES[t]
        if t == P_VEC:
            return table.at[lead]
        return full[tensor].at[lead + (slice(None), pl.ds(first, width))]

    def part(t, lead, rows):
        tensor, first, width = FWD_PIECES[t]
        if t == P_VEC:
            return table.at[lead + (rows,)]
        return full[tensor].at[lead + (rows, pl.ds(first, width))]

    every = slice(None)

    def cast(t, block, mine):
        for zz in others:
            send(block, mine, ss.at[t, 0], rs.at[t, 0], device_at(zz, y, x, c))

    def wait_cast(t, sem):
        lead = (every, every, 0) if t in PLANE_FIRST else (0, 0, 0)
        wait_bytes(home(t, pl.ds(0, 3), *lead), sem)

    def own(t):
        tensor, first, width = FWD_PIECES[t]
        piece = packed if t == P_VEC else src[tensor].at[:, pl.ds(first, width)]
        mine = home(t, z, y, x, c)
        if t not in PLANE_FIRST:
            cast(t, piece, mine)
        send(piece, mine, ss.at[t, 1], rs.at[t, 1], near_x)
        send(piece, mine, ss.at[t, 2], rs.at[t, 2], near_y)
        if t == P_VEC:
            local_copy(packed, mine, ls.at[t])
        else:
            wait_bytes(mybuf[t], ms.at[t])
            local_copy(mybuf[t], mine, ls.at[t])

    def column(t):
        wait_cast(t, rs.at[t, 0])
        for zz in others:
            block = home(t, zz, y, x, c)
            send(block, block, ss.at[t, 3], rs.at[t, 3], near_x)
            send(block, block, ss.at[t, 4], rs.at[t, 4], near_y)

    def plane(t):
        half = FWD_TENSORS[FWD_PIECES[t][0]][0] // 2
        flat = t in PLANE_FIRST
        layers = z if flat else every
        wait_bytes(home(t, 0, 0, 0, 0), rs.at[t, 1])
        if not flat:
            wait_bytes(home(t, pl.ds(0, 3), 0, 0, 0), rs.at[t, 3])
        block = part(t, (layers, y, 1 - x, c), pl.ds(0, half))
        send(block, block, ss.at[t, 5], rs.at[t, 5], near_y)
        wait_bytes(home(t, 0, 0, 0, 0), rs.at[t, 2])
        if not flat:
            wait_bytes(home(t, pl.ds(0, 3), 0, 0, 0), rs.at[t, 4])
        block = part(t, (layers, 1 - y, x, c), pl.ds(half, half))
        send(block, block, ss.at[t, 6], rs.at[t, 6], near_x)
        wait_bytes(home(t, 0, 0, 0, 0), ls.at[t])
        if not flat:
            for block in (home(t, every, y, every, c), home(t, every, 1 - y, x, c)):
                send(block, block, ss.at[t, 8], rs.at[t, 8], sibling)

    def gathered(t):
        half = FWD_TENSORS[FWD_PIECES[t][0]][0] // 2
        layers = 0 if t in PLANE_FIRST else every
        for kind in (5, 6):
            wait_bytes(part(t, (layers, 0, 0, 0), pl.ds(0, half)), rs.at[t, kind])

    def plane_cast(t):
        gathered(t)
        cast(t, home(t, z, every, every, c), home(t, z, every, every, c))

    def load(t, parity):
        if t != P_VEC:
            tensor, first, width = FWD_PIECES[t]
            local_copy(
                full[tensor].at[:, :, :, parity, :, pl.ds(first, width)],
                wbuf[t].at[:, :, :, parity],
                ld.at[t],
            )

    def pair(t):
        if t in PLANE_FIRST:
            wait_cast(t, rs.at[t, 0])
            block = home(t, every, every, every, c)
        else:
            gathered(t)
            block = home(t, every, 1 - y, 1 - x, c)
        send(block, block, ss.at[t, 7], rs.at[t, 7], sibling)
        load(t, c)

    def last_part(t):
        if t in PLANE_FIRST:
            return home(t, every, every, every, 0)
        return home(t, every, 0, 0, 0)

    def arrive(t):
        wait_bytes(last_part(t), rs.at[t, 7])
        if t not in PLANE_FIRST:
            wait_bytes(home(t, pl.ds(0, 3), every, every, 0), rs.at[t, 8])
        load(t, 1 - c)

    def loaded(t):
        wait_bytes(wbuf[t], ld.at[t])

    def sent(t):
        half = FWD_TENSORS[FWD_PIECES[t][0]][0] // 2
        flat = t in PLANE_FIRST
        wait_cast(t, ss.at[t, 0])
        for kind in (1, 2):
            wait_bytes(home(t, 0, 0, 0, 0), ss.at[t, kind])
        if not flat:
            for kind in (3, 4):
                wait_bytes(home(t, pl.ds(0, 3), 0, 0, 0), ss.at[t, kind])
            wait_bytes(home(t, pl.ds(0, 3), every, every, 0), ss.at[t, 8])
        for kind in (5, 6):
            wait_bytes(part(t, (0 if flat else every, 0, 0, 0), pl.ds(0, half)), ss.at[t, kind])
        wait_bytes(last_part(t), ss.at[t, 7])

    pack = order_s[me]
    length, offset = lengths_s[pack], offsets_s[pack]
    saved = []

    def save(value, out):
        n = len(saved)
        local_copy(value, out, os.at[n])
        saved.append((out, os.at[n]))

    def row_valid(rows, start):
        r = lax.broadcasted_iota(jnp.int32, (rows, 1), 0) + start
        return ((r >= offset) & (r < offset + length)).astype(F32)

    def pack_vectors():
        lane = lax.broadcasted_iota(jnp.int32, (1, 128), 1)
        for i in range(9):
            val = vectors[i][...].astype(F32).reshape(1, 32)
            wide = jnp.concatenate([val] * 4, axis=1)
            packed[i : i + 1, :] = jnp.where(lane // 32 == me % 4, wide, 0.0)
        packed[9:10, :] = vectors[9][...].astype(F32).reshape(1, 128)
        packed[10:16, :] = jnp.zeros((6, 128), F32)

    def prepare():
        lane = lax.broadcasted_iota(jnp.int32, (1, 128), 1)
        freq = jnp.exp((lane % 32).astype(F32) * (-math.log(10000.0) * 2.0 / 64))

        @pl.loop(0, 8)
        def _(i):
            r = lax.broadcasted_iota(jnp.int32, (64, 1), 0) + i * 64
            angle = (r - offset).astype(F32) * freq
            cosine[rows_at(i * 64, 64), :] = jnp.cos(angle)
            sine[rows_at(i * 64, 64), :] = jnp.where(lane % 64 < 32, -1.0, 1.0) * jnp.sin(angle)

        s = lax.broadcasted_iota(jnp.int32, (1, 512), 1)
        col_valid = ((s >= offset) & (s < offset + length)).astype(F32)
        stats[...] = jnp.zeros_like(stats)

        @pl.loop(0, 8)
        def _(i):
            mask[rows_at(i * 64, 64), :] = row_valid(64, i * 64) * col_valid

        stats[3:4, :] = jnp.broadcast_to(
            jnp.sum(col_valid, axis=1, keepdims=True), (1, 128)
        )
        wait_bytes(tok, ins.at[1])

        @pl.loop(0, 8)
        def _(i):
            t32 = tok[rows_at(i * 64, 64), :].astype(F32)
            add_stat(0, jnp.sum(row_valid(64, i * 64) * t32 * t32, axis=0, keepdims=True))

        transpose_blocks(tok, tokp)
        save(tokp, tokp_h)
        save(cosine, cos_h)
        save(sine, sin_h)

    def add_stat(row, wide):
        total = wide[:, 0:128]
        for i in range(1, wide.shape[1] // 128):
            total = total + wide[:, 128 * i : 128 * i + 128]
        stats[row : row + 1, :] = stats[row : row + 1, :] + total

    def unpack_vectors():
        grouped = table[...].reshape(8, 4, 16, 128).sum(axis=1)
        for b in range(8):
            vecs[:, 128 * b : 128 * b + 128] = grouped[b]
        for d in range(32):
            bias_up[0:1, 128 * d : 128 * d + 128] = table[
                d // 8, (d // 4) % 2, (d // 2) % 2, d % 2, 9:10, :
            ]
        save(vecs, vecs_h)

    def weight(t, first, width):
        w = wbuf[t]
        return w[:, :, :, :, :, lanes_at(first, width)].reshape(-1, width)

    lane128 = lambda: lax.broadcasted_iota(jnp.int32, (1, 128), 1)

    def rotary(t, bias, dst, scale, transposed, j0, j1):
        @pl.loop(j0, j1)
        def _(j):
            pre = dot(tok[...], weight(t, j * 256, 256)) + vecs[bias : bias + 1, lanes_at(j * 256, 256)]
            for b in range(2):
                part_in = pre[:, 128 * b : 128 * b + 128]
                swapped = jnp.where(
                    lane128() % 64 < 32, pltpu.roll(part_in, 96, 1), pltpu.roll(part_in, 32, 1)
                )
                turned = (part_in * cosine[...] + swapped * sine[...]).astype(BF16)
                if transposed is not None:
                    transposed[rows_at(j * 256 + 128 * b, 128), :] = turned.T
                dst[:, lanes_at(j * 256 + 128 * b, 128)] = turned * jnp.asarray(scale, BF16)

    def value(j0, j1):
        @pl.loop(j0, j1)
        def _(j):
            pre = dot(tok[...], weight(P_V, j * 256, 256)) + vecs[V_BV : V_BV + 1, lanes_at(j * 256, 256)]
            val = pre.astype(BF16)
            v[:, lanes_at(j * 256, 256)] = val
            vt[rows_at(j * 256, 256), :] = val.T

    def attend(p0, p1):
        @pl.loop(p0, p1)
        def _(p):
            cols = lanes_at(p * 128, 128)
            qp, kp = q[:, cols], k[:, cols]
            pieces = []
            for j in range(2):
                keep = lane128() < 64 if j == 0 else lane128() >= 64
                scores = dot_nt(jnp.where(keep, kp, jnp.zeros((), BF16)), qp)
                scores = jnp.where(mask[...] > 0.0, scores, -1e30)
                top = jnp.max(scores, axis=0, keepdims=True)
                expo = jnp.exp(scores - top)
                total = jnp.sum(expo, axis=0, keepdims=True)
                weights = (expo * (1.0 / total)).astype(BF16)

                @pl.when(p > 0)
                def _():
                    wait_bytes(prob.at[j], ps.at[j])

                prob[j] = weights
                local_copy(prob.at[j], prob_h.at[p, j], ps.at[j])
                mixed = dot(vt[rows_at(p * 128 + 64 * j, 64), :], weights).astype(BF16)
                for b in range(2):
                    ctxp[b, rows_at((2 * p + j) * 32, 32), :] = mixed[32 * b : 32 * b + 32]
                pieces.append(mixed)
            ctx[:, cols] = jnp.concatenate(pieces, axis=0).T

    def attended():
        for j in range(2):
            wait_bytes(prob.at[j], ps.at[j])
        save(ctxp, ctxp_h)

    def project():
        loaded(P_O)

        @pl.loop(0, 4)
        def _(j):
            cols = lanes_at(j * 256, 256)
            branch = dot(ctx[...], weight(P_O, j * 256, 256)) + vecs[V_BO : V_BO + 1, cols]
            add_stat(1, jnp.sum(row_valid(512, 0) * branch * branch, axis=0, keepdims=True))
            resid[:, cols] = branch + tok[:, cols].astype(F32)

    def normalise(i):
        rows = rows_at(i * 32, 32)
        val = resid[rows, :]
        mean = jnp.sum(val, axis=1, keepdims=True) * (1.0 / 1024)
        centred = val - mean
        scale = lax.rsqrt(jnp.sum(centred * centred, axis=1, keepdims=True) * (1.0 / 1024) + eps_norm)
        return rows, centred * scale, scale

    def norm_first():
        @pl.loop(0, 16, unroll=4)
        def _(i):
            rows, normed, scale = normalise(i)
            n1[rows, :] = normed
            inv1[rows, :] = jnp.broadcast_to(scale, (32, 128))
            low[rows, :] = (normed * vecs[V_GA : V_GA + 1, :] + vecs[V_SA : V_SA + 1, :]).astype(BF16)

        save(n1, n1_h)
        save(inv1, inv1_h)
        transpose_blocks(low, lowp)
        save(lowp, firstp_h)

    def incoming():
        loaded(P_PROJ)
        wait_bytes(hidden, ins.at[0])
        wait_bytes(embed, ins.at[2])
        cot = jnp.where(row_valid(512, 0) > 0.0, embed[...].astype(F32), 0.0).astype(BF16)
        w = weight(P_PROJ, 0, 128)
        for j in range(4):
            cols = pl.ds(256 * j, 256)
            back[:, cols] = row_valid(512, 0) * hidden[:, cols].astype(F32) + dot_nt(
                cot, w[256 * j : 256 * j + 256]
            )
        sums[...] = jnp.zeros_like(sums)

    def expand(k0):
        def tile(j, w):
            cols = lanes_at(k0 * 1024 + j * 256, 256)
            pre = dot(low[...], w) + bias_up[0:1, cols]
            cdf = 0.5 * (1.0 + lax.erf(pre * math.sqrt(0.5)))
            val = (pre * cdf).astype(BF16)
            pdf = jnp.exp(pre * pre * -0.5) * (1.0 / math.sqrt(2 * math.pi))
            slope[:, cols] = (cdf + pre * pdf).astype(BF16)
            half = lanes_at(k0 * 512 + j * 128, 128)
            act[0, :, half] = val[:, :128]
            act[1, :, half] = val[:, 128:]

        wide = FWD_PIECES[P_UP + k0][2] // 256

        @pl.loop(0, wide)
        def _(j):
            tile(j, weight(P_UP + k0, j * 256, 256))

        if wide < 4:
            tile(3, weight(P_REST + k0, 0, 256))

    def contract(k0):
        _, first_col, width = FWD_PIECES[P_DOWN + k0]
        cols = pl.ds(first_col, width)
        w = wbuf[P_DOWN + k0]
        branch = dot(act[0], w[:, :, :, 0].reshape(2048, width))
        branch = branch + dot(act[1], w[:, :, :, 1].reshape(2048, width)) + vecs[V_BD : V_BD + 1, cols]
        add_stat(2, jnp.sum(row_valid(512, 0) * branch * branch, axis=0, keepdims=True))
        first = n1[:, cols] * vecs[V_GA : V_GA + 1, cols] + vecs[V_SA : V_SA + 1, cols]
        resid[:, cols] = first + branch

    def norm_second():
        @pl.loop(0, 16, unroll=4)
        def _(i):
            rows, normed, scale = normalise(i)
            gain = vecs[V_GF : V_GF + 1, :]
            out = normed * gain + vecs[V_SF : V_SF + 1, :]
            low[rows, :] = out.astype(BF16)
            hidden[rows, :] = (out * row_valid(32, i * 32)).astype(BF16)
            grad = back[rows, :]
            scaled = grad * gain
            mean = jnp.sum(scaled, axis=1, keepdims=True) * (1.0 / 1024)
            cross = jnp.sum(scaled * normed, axis=1, keepdims=True) * (1.0 / 1024)
            res = (scaled - mean - normed * cross) * scale
            back[rows, :] = res
            ctx[rows, :] = res.astype(BF16)
            sums[0:1, :] = sums[0:1, :] + jnp.sum(grad * normed, axis=0, keepdims=True)
            sums[1:2, :] = sums[1:2, :] + jnp.sum(grad, axis=0, keepdims=True)

        save(ctx, dg_h)
        save(low, low_h)
        save(back, back_h)
        save(hidden, hidden_h)
        save(sums, sums_h)
        save(stats, stats_h)

    pack_vectors()
    greet_end()
    moves = {
        F_OWN: own, F_COLUMN: column, F_PLANE: plane, F_PAIR: pair, F_ARRIVE: arrive,
    }
    work = {
        F_PREPARE: prepare,
        F_UNPACK: unpack_vectors,
        F_Q: lambda: (loaded(P_Q), rotary(P_Q, V_BQ, q, 0.125, None, 0, 4), save(q, q_h)),
        F_K: lambda: (loaded(P_K), rotary(P_K, V_BK, k, 1.0, kt, 0, 4), save(kt, kt_h)),
        F_V: lambda: (loaded(P_V), value(0, 4), save(v, v_h)),
        F_PROJECT: project,
        F_NORM: norm_first,
        F_INCOMING: incoming,
        F_TAIL: norm_second,
    }
    for name, t in FWD_ORDER:
        if name in moves:
            moves[name](t)
        elif name == F_ATTEND:
            attend(2 * t, 2 * t + 2)
            if t == 3:
                attended()
        elif name == F_UP:
            loaded(P_UP + t)
            if P_REST + t < count:
                loaded(P_REST + t)
            expand(t)
            if t == 3:
                save(act, act_h)
                save(slope, slope_h)
        elif name == F_DOWN:
            loaded(P_DOWN + t)
            contract(t)
        else:
            work[name]()
    for t in range(count):
        sent(t)
    for out, sem in saved:
        wait_bytes(out, sem)


FWD_SAVED = (
    ((512, 1024), BF16),
    ((1024, 512), BF16),
    ((512, 1024), BF16),
    ((8, 2, 512, 512), BF16),
    ((2, 512, 512), BF16),
    ((512, 1024), F32),
    ((512, 128), F32),
    ((2, 512, 512), BF16),
    ((2, 512, 512), BF16),
    ((2, 512, 2048), BF16),
    ((512, 4096), BF16),
    ((512, 1024), F32),
    ((512, 1024), BF16),
    ((512, 1024), BF16),
    ((512, 1024), BF16),
    ((16, 1024), F32),
    ((8, 128), F32),
    ((512, 128), F32),
    ((512, 128), F32),
    ((8, 1024), F32),
)


def forward_pass(tokens, cot_hidden, cot_embed, vectors, lengths, offsets, order, weights):
    count = len(FWD_PIECES)
    shape = jax.ShapeDtypeStruct
    outs = [shape((4, 2, 2, 2, r, k), dt) for r, k, dt in FWD_TENSORS[1:]]
    outs += [shape(s, dt) for s, dt in FWD_SAVED]
    big = lambda *s: pltpu.VMEM(s, BF16)
    scratch = [
        big(512, 1024),
        pltpu.VMEM((16, 128), F32),
        pltpu.VMEM((4, 2, 2, 2, 16, 128), F32),
        pltpu.VMEM((16, 1024), F32),
        pltpu.VMEM((1, 4096), F32),
        pltpu.VMEM((512, 128), F32),
        pltpu.VMEM((512, 128), F32),
        pltpu.VMEM((512, 512), F32),
        pltpu.VMEM((8, 128), F32),
        big(512, 1024),
        big(512, 1024),
        big(512, 1024),
        big(1024, 512),
        big(1024, 512),
        big(2, 512, 512),
        big(512, 1024),
        big(2, 512, 512),
        big(2, 512, 512),
        pltpu.VMEM((512, 1024), F32),
        pltpu.VMEM((512, 1024), F32),
        pltpu.VMEM((512, 128), F32),
        big(512, 1024),
        big(2, 512, 512),
        big(2, 512, 2048),
        big(512, 4096),
        pltpu.VMEM((512, 1024), F32),
        pltpu.VMEM((8, 1024), F32),
        big(512, 1024),
        big(512, 128),
    ]
    for tensor, _, width in FWD_PIECES[1:]:
        scratch.append(big(4, 2, 2, 2, FWD_TENSORS[tensor][0], width))
    for tensor, _, width in FWD_PIECES[1:]:
        scratch.append(big(FWD_TENSORS[tensor][0], width))
    dma = pltpu.SemaphoreType.DMA
    scratch += [
        dma((count, 9)), dma((count, 9)), dma((count,)), dma((count,)), dma((24,)), dma((2,)), dma((3,)),
        dma((count,)),
    ]
    smem = pl.BlockSpec(memory_space=pltpu.SMEM)
    return pl.pallas_call(
        forward_kernel,
        out_shape=outs,
        in_specs=[ANY, ANY, ANY, smem, smem, smem]
        + [pl.BlockSpec(memory_space=pltpu.VMEM)] * 10
        + [ANY] * 7,
        out_specs=[ANY] * len(outs),
        scratch_shapes=scratch,
        compiler_params=pltpu.CompilerParams(
            collective_id=0, has_side_effects=True, vmem_limit_bytes=62 * 2**20
        ),
        name="forward_pass",
    )(tokens, cot_hidden, cot_embed, lengths, offsets, order, *vectors, *weights)


R_PROJ, R_DOWN, R_UP, R_OUT, R_Q, R_K, R_VEC, R_V = 0, 1, 5, 9, 10, 11, 12, 13
BWD_OUTS = (
    (32, 128, BF16),
    (1024, 128, BF16),
    (32, 4096, BF16),
    (32, 1024, BF16),
    (32, 1024, BF16),
    (32, 1024, BF16),
    (16, 128, F32),
    (32, 1024, BF16),
)
BWD_PIECES = (
    ((0, 0, 32, 128, BF16),)
    + tuple((1, 256 * k, 256, 128, BF16) for k in range(4))
    + tuple((2, 1024 * k, 32, 1024, BF16) for k in range(4))
    + (
        (3, 0, 32, 1024, BF16),
        (4, 0, 32, 1024, BF16),
        (5, 0, 32, 1024, BF16),
        (6, 0, 16, 128, F32),
        (7, 0, 32, 1024, BF16),
    )
)


(
    B_TURN,
    B_ACTS,
    B_DOWNSIB,
    B_DOWNOWN,
    B_NET,
    B_BEGIN,
    B_DIAGONAL,
    B_SIB,
    B_UP,
    B_FIRST,
    B_OWN,
    B_PLANE,
    B_NORM,
    B_BACK,
    B_ATTEND,
    B_BIAS,
    B_COLUMN,
    B_TOKENS,
) = range(18)
BWD_ORDER = (
    (B_TURN, 0),
    (B_ACTS, 0),
    (B_DOWNSIB, 0),
    (B_DOWNSIB, 1),
    (B_DOWNOWN, 0),
    (B_NET, 1),
    (B_DOWNOWN, 1),
    (B_NET, 2),
    (B_DOWNSIB, 2),
    (B_BEGIN, 0),
    (B_DIAGONAL, 1),
    (B_SIB, 0),
    (B_UP, 0),
    (B_SIB, 5),
    (B_FIRST, 0),
    (B_DIAGONAL, 2),
    (B_OWN, 0),
    (B_DOWNOWN, 2),
    (B_NET, 0),
    (B_NET, 3),
    (B_UP, 1),
    (B_SIB, 6),
    (B_PLANE, 1),
    (B_FIRST, 1),
    (B_OWN, 5),
    (B_DIAGONAL, 0),
    (B_PLANE, 2),
    (B_NET, 4),
    (B_UP, 2),
    (B_NET, 5),
    (B_DIAGONAL, 3),
    (B_SIB, 7),
    (B_OWN, 6),
    (B_FIRST, 2),
    (B_PLANE, 0),
    (B_UP, 3),
    (B_DIAGONAL, 4),
    (B_SIB, 8),
    (B_FIRST, 3),
    (B_NET, 6),
    (B_OWN, 7),
    (B_NORM, 0),
    (B_PLANE, 3),
    (B_OWN, 8),
    (B_BACK, 0),
    (B_PLANE, 4),
    (B_NET, 7),
    (B_SIB, 9),
    (B_ATTEND, 0),
    (B_DIAGONAL, 6),
    (B_ATTEND, 1),
    (B_DIAGONAL, 7),
    (B_OWN, 9),
    (B_ATTEND, 2),
    (B_NET, 8),
    (B_ATTEND, 3),
    (B_PLANE, 6),
    (B_NET, 9),
    (B_PLANE, 7),
    (B_BIAS, 0),
    (B_SIB, 10),
    (B_SIB, 11),
    (B_DIAGONAL, 8),
    (B_SIB, 13),
    (B_SIB, 12),
    (B_OWN, 10),
    (B_COLUMN, 5),
    (B_DIAGONAL, 9),
    (B_OWN, 11),
    (B_TOKENS, 0),
    (B_OWN, 13),
    (B_NET, 10),
    (B_OWN, 12),
    (B_TOKENS, 1),
    (B_PLANE, 8),
    (B_DIAGONAL, 5),
    (B_TOKENS, 2),
    (B_PLANE, 9),
    (B_NET, 11),
    (B_DIAGONAL, 10),
    (B_PLANE, 5),
    (B_DIAGONAL, 11),
    (B_PLANE, 10),
    (B_NET, 12),
    (B_NET, 13),
    (B_PLANE, 11),
    (B_DIAGONAL, 12),
    (B_DIAGONAL, 13),
    (B_PLANE, 12),
    (B_PLANE, 13),
)
Z_FIRST = (R_UP,)


def backward_kernel(cote_h, lengths_s, offsets_s, order_s, *refs):
    wq_h, wk_h, wv_h, wo_h, wup_h, wproj_h, wdown_h = refs[:7]
    (
        q_h, kt_h, v_h, prob_h, ctxp_h, n1_h, inv1_h, firstp_h, tokp_h, act_h, slope_h,
        back_h, dg_h, low_h, vecs_h, stats_h, cos_h, sin_h, sumf_h,
    ) = refs[7:26]
    refs = refs[26:]
    grad_h, embed_h = refs[:2]
    outs = refs[2:10]
    refs = refs[10:]
    (
        ring, resid, nbuf, sumf, inv1, dg, dgt, upg, four, slopes, blocks, kt, mask,
        cosine, sine, cot, vecs, stats, sums, sum_up, table, stage_d, stage_u, stage_p, wproj, embed,
    ) = refs[:26]
    refs = refs[26:]
    count = len(BWD_PIECES)
    acc, diag, from_x, from_y = (refs[i * count : (i + 1) * count] for i in range(4))
    refs = refs[4 * count :]
    from_z = dict(zip(Z_FIRST, refs))
    ss, rs, ls, ins, rsem, psem, gsem, esem = refs[len(Z_FIRST) :]
    z, y, x, c = place()
    me = device_at(z, y, x, c)
    near_x, near_y = device_at(z, y, 1 - x, c), device_at(z, 1 - y, x, c)
    sibling = device_at(z, y, x, 1 - c)
    others = [(z + kk) % 4 for kk in (1, 2, 3)]
    pack = order_s[me]
    length, offset = lengths_s[pack], offsets_s[pack]

    ring_src = []
    for j in range(4):
        ring_src.append(wdown_h.at[pl.ds(1024 * j, 1024), :])
        ring_src.append(wup_h.at[:, pl.ds(1024 * j, 1024)])
    ring_src += [wo_h, wq_h, wk_h, wv_h]

    def ring_start(n):
        local_copy(ring_src[n], ring.at[n % 3], rsem.at[n])

    def ring_wait(n):
        wait_bytes(ring.at[n % 3], rsem.at[n])
        return ring.at[n % 3]

    def ring_next(n):
        if n + 3 < len(ring_src):
            ring_start(n + 3)

    loads = {}

    def load(name, src, dst):
        n = len(loads)
        loads[name] = (dst, ins.at[n])
        local_copy(src, dst, ins.at[n])

    def ready(name):
        dst, sem = loads[name]
        wait_bytes(dst, sem)

    load("dg", dg_h, dg)
    for p in range(2):
        for h in range(2):
            load("act%d%d" % (p, h), act_h.at[p, :, pl.ds(1024 * h, 1024)], four.at[2 * p + h])
    load("cote", cote_h, cot)
    load("low", low_h, slopes.at[1])
    load("wproj", wproj_h, wproj)
    ring_start(0)
    load("slope0", slope_h.at[:, pl.ds(0, 1024)], slopes.at[0])
    load("firstp", firstp_h, blocks.at[1])
    load("back", back_h, resid)
    ring_start(1)
    ring_start(2)
    load("n1", n1_h, nbuf)
    load("inv1", inv1_h, inv1)
    load("vecs", vecs_h, vecs)
    load("sumf", sumf_h, sumf)
    load("stats", stats_h, stats)
    load("cos", cos_h, cosine)
    load("sin", sin_h, sine)
    load("kt", kt_h, kt)
    greet_start(z, y, x, c)

    def out_view(t, *lead):
        out, first, rows, width, _ = BWD_PIECES[t]
        if R_DOWN <= t < R_UP:
            return outs[out].at[lead + (pl.ds(first, rows), slice(None))]
        return outs[out].at[lead + (slice(None), pl.ds(first, width))]

    def give(t, stage):
        send(stage, acc[t], ss.at[t, 0], rs.at[t, 0], sibling)

    def layers(t):
        return z if t in Z_FIRST else slice(None)

    def side(ref, t, rows):
        return ref.at[rows] if t in Z_FIRST else ref.at[:, rows]

    def net(t):
        if t in Z_FIRST:
            for kk, zz in zip((1, 2, 3), others):
                send(acc[t].at[zz], from_z[t].at[3 - kk], ss.at[t, 7], rs.at[t, 7], device_at(zz, y, x, c))
        else:
            spread(t)

    def add_column(t):
        h = acc[t]
        wait_bytes(from_z[t], rs.at[t, 7])

        @pl.loop(0, 4)
        def _(i):
            total = h[z, i // 2, i % 2].astype(F32)
            for k in range(3):
                total = total + from_z[t][k, i // 2, i % 2].astype(F32)
            h[z, i // 2, i % 2] = total.astype(BF16)

        spread(t)

    def spread(t):
        half = BWD_PIECES[t][2] // 2
        h, a = acc[t], layers(t)
        first, second = pl.ds(0, half), pl.ds(half, half)
        send(h.at[a, 1 - y, 1 - x, first], diag[t].at[0], ss.at[t, 1], rs.at[t, 1], near_x)
        send(h.at[a, 1 - y, 1 - x, second], diag[t].at[1], ss.at[t, 2], rs.at[t, 2], near_y)
        send(h.at[a, y, 1 - x, first], side(from_x[t], t, first), ss.at[t, 3], rs.at[t, 3], near_x)
        send(h.at[a, 1 - y, x, second], side(from_y[t], t, second), ss.at[t, 4], rs.at[t, 4], near_y)

    def add_diagonal(t):
        rows = BWD_PIECES[t][2]
        half = rows // 2
        h, a = acc[t], layers(t)
        first, second = pl.ds(0, half), pl.ds(half, half)

        def add(k, yy, xx, lo):
            wait_bytes(diag[t].at[k], rs.at[t, 1 + k])
            if t in Z_FIRST:
                h[z, yy, xx, lo : lo + half, :] = h[z, yy, xx, lo : lo + half, :] + diag[t][k]
                return

            @pl.loop(0, 4)
            def _(i):
                h[i, yy, xx, lo : lo + half, :] = h[i, yy, xx, lo : lo + half, :] + diag[t][k, i]

        add(0, 1 - y, x, 0)
        send(h.at[a, 1 - y, x, first], side(from_y[t], t, first), ss.at[t, 6], rs.at[t, 6], near_y)
        add(1, y, 1 - x, half)
        send(h.at[a, y, 1 - x, second], side(from_x[t], t, second), ss.at[t, 5], rs.at[t, 5], near_x)

    def add_plane(t):
        half = BWD_PIECES[t][2] // 2
        h = acc[t]
        first, second = pl.ds(0, half), pl.ds(half, half)
        wait_bytes(side(from_x[t], t, first), rs.at[t, 3])
        wait_bytes(side(from_x[t], t, second), rs.at[t, 5])
        wait_bytes(side(from_y[t], t, second), rs.at[t, 4])
        wait_bytes(side(from_y[t], t, first), rs.at[t, 6])
        slot = out_view(t, z)
        if t in Z_FIRST:
            h[z, y, x] = h[z, y, x] + from_x[t][...] + from_y[t][...]
        else:

            @pl.loop(0, 4)
            def _(i):
                h[i, y, x] = h[i, y, x] + from_x[t][i] + from_y[t][i]

            for zz in others:
                send(h.at[zz, y, x], slot, ss.at[t, 7], rs.at[t, 7], device_at(zz, y, x, c))
        local_copy(h.at[z, y, x], slot, ls.at[t])

    def finish(t):
        half = BWD_PIECES[t][2] // 2
        three = out_view(t, pl.ds(0, 3))
        if t in Z_FIRST:
            wait_bytes(from_z[t], ss.at[t, 7])
        else:
            wait_bytes(three, rs.at[t, 7])
            wait_bytes(three, ss.at[t, 7])
        wait_bytes(out_view(t, 0), ls.at[t])
        wait_bytes(diag[t].at[0], ss.at[t, 1])
        wait_bytes(diag[t].at[1], ss.at[t, 2])
        for kind in (3, 4, 5, 6):
            wait_bytes(side(from_x[t], t, pl.ds(0, half)), ss.at[t, kind])

    given = {}

    def take_stage(key, t):
        if key in given:
            wait_bytes(acc[given[key]], ss.at[given[key], 0])
        given[key] = t

    def rows_sib(t, lhs, rhs, stage, key):
        take_stage(key, t)
        width = BWD_PIECES[t][3]
        tile = min(width, 1024)

        @pl.loop(0, width // tile)
        def _(j):
            cols = lanes_at(j * tile, tile)
            val = dot(lhs[1 - c], rhs[:, cols]).astype(BF16)
            stage[:, :, :, :, cols] = val.reshape(4, 2, 2, 32, tile)

        give(t, stage)

    def rows_own(t, lhs, rhs):
        width = BWD_PIECES[t][3]
        tile = min(width, 1024)
        wait_bytes(acc[t], rs.at[t, 0])

        @pl.loop(0, width // tile)
        def _(j):
            cols = lanes_at(j * tile, tile)
            val = dot(lhs[c], rhs[:, cols]) + acc[t][:, :, :, :, cols].reshape(512, tile).astype(F32)
            acc[t][:, :, :, :, cols] = val.astype(BF16).reshape(4, 2, 2, 32, tile)

    def down_tile(h, parity, j):
        per = 1024 // DOWN_TILE
        rhs = four[2 * parity + j // per, :, lanes_at((j % per) * DOWN_TILE, DOWN_TILE)]
        return dot(dgt[512 * h : 512 * h + 512, :], rhs)

    def down_blocks(j):
        for b in range(DOWN_TILE // 128):
            s = j * (DOWN_TILE // 128) + b
            yield b, s // 4, (s // 2) % 2, s % 2

    def down_sib(*ks):
        rows = 256 * len(ks)
        for k0 in ks:
            take_stage(k0 % 2, R_DOWN + k0)

        @pl.loop(0, 2)
        def _(j):
            val = dot(dgt[256 * ks[0] : 256 * ks[0] + rows, :], four[2 * (1 - c) + j]).astype(BF16)
            for b in range(8):
                for i, k0 in enumerate(ks):
                    stage_d[k0 % 2, 2 * j + b // 4, (b // 2) % 2, b % 2] = val[
                        256 * i : 256 * i + 256, 128 * b : 128 * b + 128
                    ]

        for k0 in ks:
            give(R_DOWN + k0, stage_d.at[k0 % 2])

    def down_own(*ks):
        rows = 256 * len(ks)
        for k0 in ks:
            wait_bytes(acc[R_DOWN + k0], rs.at[R_DOWN + k0, 0])

        @pl.loop(0, 2)
        def _(j):
            val = dot(dgt[256 * ks[0] : 256 * ks[0] + rows, :], four[2 * c + j])
            for b in range(8):
                for i, k0 in enumerate(ks):
                    h = acc[R_DOWN + k0]
                    old = h[2 * j + b // 4, (b // 2) % 2, b % 2].astype(F32)
                    h[2 * j + b // 4, (b // 2) % 2, b % 2] = (
                        val[256 * i : 256 * i + 256, 128 * b : 128 * b + 128] + old
                    ).astype(BF16)

    def column_sum(ref):
        return dot(jnp.ones((16, 512), BF16), ref)[0:1]

    def row_valid(rows, start):
        r = lax.broadcasted_iota(jnp.int32, (rows, 1), 0) + start
        return ((r >= offset) & (r < offset + length)).astype(F32)

    def norm_back(inv, gain, to_gain, to_shift):
        sums[to_gain : to_gain + 1, :] = jnp.zeros((1, 1024), F32)
        sums[to_shift : to_shift + 1, :] = jnp.zeros((1, 1024), F32)

        @pl.loop(0, 16, unroll=4)
        def _(i):
            rows = rows_at(i * 32, 32)
            grad, normed = resid[rows, :], nbuf[rows, :]
            scaled = grad * vecs[gain : gain + 1, :]
            mean = jnp.sum(scaled, axis=1, keepdims=True) * (1.0 / 1024)
            cross = jnp.sum(scaled * normed, axis=1, keepdims=True) * (1.0 / 1024)
            out = (scaled - mean - normed * cross) * inv[rows, 0:1]
            resid[rows, :] = out
            dg[rows, :] = out.astype(BF16)
            sums[to_gain : to_gain + 1, :] = sums[to_gain : to_gain + 1, :] + jnp.sum(
                grad * normed, axis=0, keepdims=True
            )
            sums[to_shift : to_shift + 1, :] = sums[to_shift : to_shift + 1, :] + jnp.sum(
                grad, axis=0, keepdims=True
            )

    def begin():
        ready("cote")
        cot[...] = jnp.where(row_valid(512, 0) > 0.0, cot[...].astype(F32), 0.0).astype(BF16)
        sums[V_BD : V_BD + 1, :] = column_sum(dg[...])
        ready("low")
        ready("wproj")
        transpose_blocks(slopes.at[1], blocks.at[0])
        embed[...] = (dot(slopes[1], wproj[...]) * row_valid(512, 0)).astype(BF16)
        local_copy(embed, embed_h, esem)
        load("slope1", slope_h.at[:, pl.ds(1024, 1024)], slopes.at[1])

    def turn():
        @pl.loop(0, 8)
        def _(j):
            dgt[rows_at(j * 128, 128), :] = dg[:, lanes_at(j * 128, 128)].T

    def acts():
        for p in range(2):
            for h in range(2):
                ready("act%d%d" % (p, h))

    def up_grad(k0):
        w = ring_wait(2 * k0)
        ready("slope%d" % k0)

        @pl.loop(0, 1)
        def _(j):
            cols = lanes_at(j * 1024, 1024)
            back = dot_nt(dg[...], w[rows_at(j * 1024, 1024), :]) * slopes[k0 % 2, :, cols].astype(F32)
            upg[k0, :, cols] = back.astype(BF16)

        ring_next(2 * k0)
        if k0 + 2 < 4:
            load("slope%d" % (k0 + 2), slope_h.at[:, pl.ds(1024 * (k0 + 2), 1024)], slopes.at[k0 % 2])
        sum_up[0:1, 1024 * k0 : 1024 * k0 + 1024] = column_sum(upg[k0])

    def first_grad(k0):
        if k0 == 0:
            ready("back")
        w = ring_wait(2 * k0 + 1)

        @pl.loop(0, 1)
        def _(j):
            cols = lanes_at(j * 1024, 1024)
            resid[:, cols] = resid[:, cols] + dot_nt(upg[k0], w[rows_at(j * 1024, 1024), :])

        ring_next(2 * k0 + 1)

    def up_sib(k0):
        if k0 == 0:
            ready("firstp")
        rows_sib(R_UP + k0, blocks.at[1], upg.at[k0], stage_u.at[k0 % 2], 2 + k0 % 2)

    def up_own(k0):
        rows_own(R_UP + k0, blocks.at[1], upg.at[k0])

    def norm_one():
        ready("n1")
        ready("inv1")
        ready("vecs")
        norm_back(inv1, V_GA, V_GA, V_SA)
        sums[V_BO : V_BO + 1, :] = column_sum(dg[...])
        load("ctxp", ctxp_h, blocks.at[0])

    def start_attention():
        load("q", q_h, upg.at[0])
        load("v", v_h, upg.at[1])
        load("tokp", tokp_h, blocks.at[1])
        prob_start(0)

    def prob_start(p):
        for j in range(2):
            local_copy(
                prob_h.at[p, j],
                upg.at[2 + p % 2, :, pl.ds(512 * j, 512)],
                psem.at[p % 2, j],
            )

    def ctx_back():
        w = ring_wait(8)

        @pl.loop(0, 1)
        def _(j):
            four[3, :, lanes_at(j * 1024, 1024)] = dot_nt(dg[...], w[rows_at(j * 1024, 1024), :]).astype(BF16)

        ring_next(8)

    def make_mask():
        s = lax.broadcasted_iota(jnp.int32, (1, 512), 1)
        col_valid = ((s >= offset) & (s < offset + length)).astype(F32)

        @pl.loop(0, 8)
        def _(i):
            mask[rows_at(i * 64, 64), :] = row_valid(64, i * 64) * col_valid

    def lane128():
        return lax.broadcasted_iota(jnp.int32, (1, 128), 1)

    def unturn(val):
        swapped = jnp.where(lane128() % 64 < 32, pltpu.roll(val, 96, 1), pltpu.roll(val, 32, 1))
        return (val * cosine[...] - swapped * sine[...]).astype(BF16)

    def attend_back(p0, p1):
        @pl.loop(p0, p1)
        def _(p):
            cols = lanes_at(p * 128, 128)
            for j in range(2):
                wait_bytes(upg.at[2 + p % 2, :, pl.ds(512 * j, 512)], psem.at[p % 2, j])

            @pl.when(p + 1 < 8)
            def _():
                prob_start(p + 1)

            qp, vp, grad = upg[0, :, cols], upg[1, :, cols], four[3, :, cols]
            dv, dk, dqt = [], [], []
            for j in range(2):
                keep = lane128() < 64 if j == 0 else lane128() >= 64
                low = upg[2 + p % 2, :, 512 * j : 512 * j + 512]
                wide = low.astype(F32)
                back = dot_nt(jnp.where(keep, vp, jnp.zeros((), BF16)), grad)
                row_dot = jnp.sum(wide * back, axis=0, keepdims=True)
                sgrad = jnp.where(mask[...] > 0.0, wide * (back - row_dot), 0.0).astype(BF16)
                dv.append(dot(low, grad))
                dk.append(dot(sgrad, qp))
                dqt.append(dot(kt[rows_at(p * 128 + 64 * j, 64), :], sgrad))
            four[2, :, cols] = jnp.where(lane128() < 64, dv[0], dv[1]).astype(BF16)
            four[1, :, cols] = unturn(jnp.where(lane128() < 64, dk[0], dk[1]))
            four[0, :, cols] = unturn(jnp.concatenate(dqt, axis=0).T * 0.125)

    def bias_sums():
        sums[V_BQ : V_BQ + 1, :] = column_sum(four[0])
        sums[V_BK : V_BK + 1, :] = column_sum(four[1])
        sums[V_BV : V_BV + 1, :] = column_sum(four[2])

    def vector_table():
        ready("stats")
        ready("sumf")
        for b in range(8):
            val = jnp.concatenate(
                [sums[0:7, 128 * b : 128 * b + 128], sumf[0:2, 128 * b : 128 * b + 128], jnp.zeros((1, 128), F32), stats[0:4, :], jnp.zeros((2, 128), F32)],
                axis=0,
            )
            for i in range(4):
                table[b // 2, b % 2, i // 2, i % 2] = val
        for d in range(32):
            table[d // 8, (d // 4) % 2, (d // 2) % 2, d % 2, 9:10, :] = sum_up[
                0:1, 128 * d : 128 * d + 128
            ]
        give(R_VEC, table.at[:, :, :, 1 - c])

    def vector_own():
        wait_bytes(acc[R_VEC], rs.at[R_VEC, 0])
        acc[R_VEC][...] = acc[R_VEC][...] + table[:, :, :, c]

    def token_grad(i):
        w = ring_wait(9 + i)

        @pl.loop(0, 1)
        def _(j):
            cols = lanes_at(j * 1024, 1024)
            resid[:, cols] = resid[:, cols] + dot_nt(four[i], w[rows_at(j * 1024, 1024), :])

    def token_out():
        local_copy(resid, grad_h, gsem)

    moves = {B_NET: net, B_COLUMN: add_column, B_DIAGONAL: add_diagonal, B_PLANE: add_plane}
    pieces = {
        B_TURN: turn,
        B_ACTS: lambda: (acts(), greet_end()),
        B_BEGIN: begin,
        B_NORM: lambda: (norm_one(), make_mask()),
        B_BACK: lambda: (start_attention(), ctx_back()),
        B_BIAS: bias_sums,
    }

    def sib(t):
        if t == R_PROJ:
            rows_sib(t, blocks.at[0], cot, stage_p, 4)
        elif t < R_OUT:
            up_sib(t - R_UP)
        elif t == R_OUT:
            ready("ctxp")
            rows_sib(t, blocks.at[0], dg, stage_u.at[0], 2)
        elif t == R_VEC:
            vector_table()
        else:
            if t == R_Q:
                ready("tokp")
            n, stage = {R_Q: (0, 1), R_K: (1, 0), R_V: (2, 1)}[t]
            rows_sib(t, blocks.at[1], four.at[n], stage_u.at[stage], 2 + stage)

    def mine(t):
        if t == R_PROJ:
            rows_own(t, blocks.at[0], cot)
        elif t < R_OUT:
            up_own(t - R_UP)
        elif t == R_OUT:
            rows_own(t, blocks.at[0], dg)
        elif t == R_VEC:
            vector_own()
        else:
            rows_own(t, blocks.at[1], four.at[{R_Q: 0, R_K: 1, R_V: 2}[t]])

    def attend_pairs(n):
        if n == 0:
            for name in ("kt", "q", "v", "cos", "sin"):
                ready(name)
        attend_back(2 * n, 2 * n + 2)

    def tokens(n):
        token_grad(n)
        if n == 2:
            token_out()

    moves.update({
        B_SIB: sib,
        B_OWN: mine,
        B_ATTEND: attend_pairs,
        B_TOKENS: tokens,
        B_UP: up_grad,
        B_FIRST: first_grad,
        B_DOWNSIB: lambda k0: down_sib(2, 3) if k0 == 2 else down_sib(k0),
        B_DOWNOWN: lambda k0: down_own(2, 3) if k0 == 2 else down_own(k0),
    })
    ready("dg")
    for name, t in BWD_ORDER:
        if name in moves:
            moves[name](t)
        else:
            pieces[name]()
    for t in range(count):
        finish(t)
    for t in given.values():
        wait_bytes(acc[t], ss.at[t, 0])
    wait_bytes(acc[R_VEC], ss.at[R_VEC, 0])
    wait_bytes(resid, gsem)
    wait_bytes(embed, esem)


def backward_pass(cot_embed, lengths, offsets, order, weights, kept):
    count = len(BWD_PIECES)
    outs = [jax.ShapeDtypeStruct((512, 1024), F32), jax.ShapeDtypeStruct((512, 128), BF16)]
    outs += [jax.ShapeDtypeStruct((4, r, k), dt) for r, k, dt in BWD_OUTS]
    big = lambda *s: pltpu.VMEM(s, BF16)
    wide = lambda *s: pltpu.VMEM(s, F32)
    scratch = [
        big(3, 1024, 1024),
        wide(512, 1024),
        wide(512, 1024),
        wide(8, 1024),
        wide(512, 128),
        big(512, 1024),
        big(1024, 512),
        big(4, 512, 1024),
        big(4, 512, 1024),
        big(2, 512, 1024),
        big(2, 2, 512, 512),
        big(1024, 512),
        wide(512, 512),
        wide(512, 128),
        wide(512, 128),
        big(512, 128),
        wide(16, 1024),
        wide(8, 128),
        wide(16, 1024),
        wide(1, 4096),
        wide(4, 2, 2, 2, 16, 128),
        big(2, 4, 2, 2, 256, 128),
        big(2, 4, 2, 2, 32, 1024),
        big(4, 2, 2, 32, 128),
        big(1024, 128),
        big(512, 128),
    ]
    for lead, flat in (((4, 2, 2), (4, 2, 2)), ((2, 4), (2,)), ((4,), ()), ((4,), ())):
        for t, (_, _, rows, width, dtype) in enumerate(BWD_PIECES):
            shape = flat if t in Z_FIRST else lead
            scratch.append(pltpu.VMEM(shape + (rows // 2 if lead == (2, 4) else rows, width), dtype))
    for t in Z_FIRST:
        scratch.append(big(3, 2, 2, *BWD_PIECES[t][2:4]))
    dma = pltpu.SemaphoreType.DMA
    scratch += [dma((count, 8)), dma((count, 8)), dma((count,)), dma((32,)), dma((12,)), dma((2, 2)), dma, dma]
    smem = pl.BlockSpec(memory_space=pltpu.SMEM)
    return pl.pallas_call(
        backward_kernel,
        out_shape=outs,
        in_specs=[ANY, smem, smem, smem] + [ANY] * (7 + 19),
        out_specs=[ANY] * len(outs),
        scratch_shapes=scratch,
        compiler_params=pltpu.CompilerParams(
            collective_id=1, has_side_effects=True, vmem_limit_bytes=62 * 2**20
        ),
        name="backward_pass",
    )(cot_embed, lengths, offsets, order, *weights, *kept)


def finish_kernel(*refs):
    parts, (hidden_h, embed_h, tokens_h) = refs[:8], refs[8:11]
    outs, hidden_o, embed_o, tokens_o = refs[11:19], *refs[19:22]
    vec_outs, refs = refs[22:32], refs[32:]
    bufs, results, carry, vectors = refs[:8], refs[8:16], refs[16:19], refs[19:29]
    ins, done, moved, vsem = refs[29:]
    order = (6, 1, 2, 3, 4, 5, 7, 0)
    for i in order:
        local_copy(parts[i], bufs[i], ins.at[i])
    moves = ((hidden_h, hidden_o), (embed_h, embed_o), (tokens_h, tokens_o))
    for i, (src, _) in enumerate(moves):
        local_copy(src, carry[i], moved.at[i, 0])
    me = lax.axis_index("dp")
    z = me // 8
    for i in order:
        wait_bytes(bufs[i], ins.at[i])
        buf = bufs[i]
        total = buf[0].astype(F32) + buf[1].astype(F32) + buf[2].astype(F32) + buf[3].astype(F32)
        if i == 1:
            total = total.T
        if i == 6:
            own = jnp.where(me % 4 == 0, total[:, 0:32], 0.0)
            for j in range(1, 4):
                own = own + jnp.where(me % 4 == j, total[:, 32 * j : 32 * j + 32], 0.0)
            stat = jnp.sum(total, axis=1, keepdims=True)
            root = jnp.sqrt(stat[10:13] / (stat[13:14] * (1024 / 128)))
            results[6][...] = jnp.zeros((8, 128), F32)
            for k in range(3):
                results[6][0:1, k : k + 1] = root[k : k + 1]
            for k in range(9):
                vectors[k][...] = own[k : k + 1].reshape(32)
            vectors[9][...] = total[9:10].reshape(128)
            for k in range(10):
                local_copy(vectors[k], vec_outs[k], vsem.at[k])
        else:
            results[i][...] = total
            for t in Z_FIRST:
                if BWD_PIECES[t][0] == i:
                    cols = slice(BWD_PIECES[t][1], BWD_PIECES[t][1] + BWD_PIECES[t][3])
                    results[i][:, cols] = buf[z, :, cols].astype(F32)
        local_copy(results[i], outs[i], done.at[i])
        if i == 2:
            for k, (src, dst) in enumerate(moves):
                wait_bytes(carry[k], moved.at[k, 0])
                local_copy(carry[k], dst, moved.at[k, 1])
    for i in order:
        wait_bytes(results[i], done.at[i])
    for i in range(3):
        wait_bytes(carry[i], moved.at[i, 1])
    for k in range(10):
        wait_bytes(vectors[k], vsem.at[k])


def finish(parts, hidden, embed, grad):
    shape = jax.ShapeDtypeStruct
    sums = [shape(p.shape[1:], F32) for p in parts]
    sums[1] = shape((128, 1024), F32)
    sums[6] = shape((8, 128), F32)
    vectors = [shape((32,), F32)] * 9 + [shape((128,), F32)]
    moved = [shape(a.shape, a.dtype) for a in (hidden, embed, grad)]
    dma = pltpu.SemaphoreType.DMA
    return pl.pallas_call(
        finish_kernel,
        out_shape=sums + moved + vectors,
        in_specs=[pl.BlockSpec(memory_space=pltpu.HBM)] * 11,
        out_specs=[pl.BlockSpec(memory_space=pltpu.HBM)] * 21,
        scratch_shapes=[pltpu.VMEM(p.shape, p.dtype) for p in parts]
        + [pltpu.VMEM(s.shape, F32) for s in sums]
        + [pltpu.VMEM(a.shape, a.dtype) for a in moved]
        + [pltpu.VMEM(a.shape, F32) for a in vectors]
        + [dma((8,)), dma((8,)), dma((3, 2)), dma((10,))],
        compiler_params=pltpu.CompilerParams(vmem_limit_bytes=60 * 2**20),
        name="finish",
    )(*parts, hidden, embed, grad)


def shards(
    tokens, cot_hidden, cot_embed, lengths, offsets, pack_order,
    w_query, b_query, w_key, b_key, w_value, b_value, w_out, b_out, gain_attn, shift_attn,
    w_up, b_up, w_down, b_down, gain_ffn, shift_ffn, w_proj,
):
    done = forward_pass(
        tokens, cot_hidden, cot_embed,
        (b_query, b_key, b_value, b_out, gain_attn, shift_attn, b_down, gain_ffn, shift_ffn, b_up),
        lengths, offsets, pack_order,
        (w_query, w_key, w_value, w_out, w_up, w_proj, w_down),
    )
    weights = [w.reshape(-1, w.shape[-1]) for w in done[:7]]
    kept = list(done[7 : 7 + 14]) + list(done[7 + 15 :])
    back = backward_pass(cot_embed, lengths, offsets, pack_order, weights, kept)
    results = finish(back[2:], done[7 + 14], back[1], back[0])
    proj, down, up, out, query, key, vec, val, hidden, embed, grad, *own = results
    return (
        hidden, embed, grad,
        query, own[V_BQ], key, own[V_BK], val, own[V_BV], out, own[V_BO],
        own[V_GA], own[V_SA], up, own[9], down, own[V_BD], own[V_GF], own[V_SF],
        proj, vec[0, :3],
    )


def shards_any(
    tokens,
    cot_hidden,
    cot_embed,
    lengths,
    offsets,
    pack_order,
    w_query,
    b_query,
    w_key,
    b_key,
    w_value,
    b_value,
    w_out,
    b_out,
    gain_attn,
    shift_attn,
    w_up,
    b_up,
    w_down,
    b_down,
    gain_ffn,
    shift_ffn,
    w_proj,
):
    gathered = (
        lax.all_gather(w_query, "dp", axis=0, tiled=True),
        lax.all_gather(w_key, "dp", axis=0, tiled=True),
        lax.all_gather(w_value, "dp", axis=0, tiled=True),
        lax.all_gather(w_out, "dp", axis=0, tiled=True),
        lax.all_gather(w_up, "dp", axis=0, tiled=True),
        lax.all_gather(w_down, "dp", axis=0, tiled=True),
        lax.all_gather(w_proj, "dp", axis=0, tiled=True),
        lax.all_gather(b_query, "dp", axis=0, tiled=True),
        lax.all_gather(b_key, "dp", axis=0, tiled=True),
        lax.all_gather(b_value, "dp", axis=0, tiled=True),
        lax.all_gather(b_out, "dp", axis=0, tiled=True),
        lax.all_gather(gain_attn, "dp", axis=0, tiled=True),
        lax.all_gather(shift_attn, "dp", axis=0, tiled=True),
        lax.all_gather(b_up, "dp", axis=0, tiled=True),
        lax.all_gather(b_down, "dp", axis=0, tiled=True),
        lax.all_gather(gain_ffn, "dp", axis=0, tiled=True),
        lax.all_gather(shift_ffn, "dp", axis=0, tiled=True),
    )
    wt_query, wt_key, wt_value, wt_out, wt_up, wt_down, wt_proj = gathered[:7]
    vectors = [piece.astype(jnp.float32) for piece in gathered[7:]]
    (
        bias_query,
        bias_key,
        bias_value,
        bias_out,
        norm_gain_a,
        norm_shift_a,
        bias_up,
        bias_down,
        norm_gain_f,
        norm_shift_f,
    ) = vectors
    row_count = tokens.shape[0]
    model_width = tokens.shape[1]
    head_count = H
    head_dim = model_width // head_count
    device = lax.axis_index("dp")
    slots = jnp.arange(pack_order.shape[0], dtype=jnp.int32)
    pack_id = jnp.sum(jnp.where(slots == device, pack_order, 0))
    length = jnp.sum(jnp.where(slots == pack_id, lengths, 0))
    offset = jnp.sum(jnp.where(slots == pack_id, offsets, 0))
    row_index = jnp.arange(row_count, dtype=jnp.int32)
    is_valid = (row_index >= offset) & (row_index < offset + length)
    keep_rows = is_valid.astype(jnp.float32)[:, None]
    cosine, sine_part = rope_tables((row_index - offset).astype(jnp.float32), head_dim)
    query_pre = matmul(tokens, wt_query) + bias_query
    key_pre = matmul(tokens, wt_key) + bias_key
    value_low = (
        (matmul(tokens, wt_value) + bias_value)
        .astype(jnp.bfloat16)
        .reshape(row_count, head_count, head_dim)
    )
    query_rot = rotate(
        query_pre.reshape(row_count, head_count, head_dim), cosine, sine_part
    ).astype(jnp.bfloat16)
    key_rot = rotate(key_pre.reshape(row_count, head_count, head_dim), cosine, sine_part).astype(
        jnp.bfloat16
    )
    score_scale = 1.0 / math.sqrt(head_dim)
    key_valid = is_valid[None, None, :]
    allowed = is_valid[None, :, None] & key_valid
    masked = masked_scores(query_rot, key_rot, allowed, score_scale)
    row_top = jnp.max(masked, axis=-1, keepdims=True)
    exponent = jnp.exp(masked - row_top)
    row_total = jnp.sum(exponent, axis=-1, keepdims=True)
    prob_low = (exponent / row_total).astype(jnp.bfloat16)
    contexts = jnp.einsum("hqk,khd->qhd", prob_low, value_low, preferred_element_type=jnp.float32)
    log_totals = row_top + jnp.log(row_total)
    context = contexts.astype(jnp.bfloat16).reshape(row_count, model_width)
    tokens_wide = tokens.astype(jnp.float32)
    attn_branch = matmul(context, wt_out) + bias_out
    first, normed_one, inverse_one = norm_forward(
        tokens_wide + attn_branch, norm_gain_a, norm_shift_a
    )
    first_low = first.astype(jnp.bfloat16)
    up_pre = matmul(first_low, wt_up) + bias_up
    act_full, gelu_pull = jax.vjp(exact_gelu, up_pre)
    act_low = act_full.astype(jnp.bfloat16)
    down_branch = matmul(act_low, wt_down) + bias_down
    out, normed_two, inverse_two = norm_forward(first + down_branch, norm_gain_f, norm_shift_f)
    out_low = out.astype(jnp.bfloat16)
    hidden = (out * keep_rows).astype(jnp.bfloat16)
    embedding = (matmul(out_low, wt_proj) * keep_rows).astype(jnp.bfloat16)
    stat_sums = lax.psum(
        (
            jnp.sum(keep_rows * tokens_wide * tokens_wide),
            jnp.sum(keep_rows * attn_branch * attn_branch),
            jnp.sum(keep_rows * down_branch * down_branch),
            jnp.sum(keep_rows),
        ),
        "dp",
    )
    rms_stats = jnp.sqrt(
        jnp.stack([stat_sums[0], stat_sums[1], stat_sums[2]]) / (stat_sums[3] * model_width)
    )
    backward_set = (
        lax.all_gather(w_query, "dp", axis=0, tiled=True),
        lax.all_gather(w_key, "dp", axis=0, tiled=True),
        lax.all_gather(w_value, "dp", axis=0, tiled=True),
        lax.all_gather(w_out, "dp", axis=0, tiled=True),
        lax.all_gather(w_up, "dp", axis=0, tiled=True),
        lax.all_gather(w_down, "dp", axis=0, tiled=True),
        lax.all_gather(w_proj, "dp", axis=0, tiled=True),
        lax.all_gather(b_query, "dp", axis=0, tiled=True),
        lax.all_gather(b_key, "dp", axis=0, tiled=True),
        lax.all_gather(b_value, "dp", axis=0, tiled=True),
        lax.all_gather(b_out, "dp", axis=0, tiled=True),
        lax.all_gather(gain_attn, "dp", axis=0, tiled=True),
        lax.all_gather(shift_attn, "dp", axis=0, tiled=True),
        lax.all_gather(b_up, "dp", axis=0, tiled=True),
        lax.all_gather(b_down, "dp", axis=0, tiled=True),
        lax.all_gather(gain_ffn, "dp", axis=0, tiled=True),
        lax.all_gather(shift_ffn, "dp", axis=0, tiled=True),
    )
    back_query, back_key, back_value, back_out, back_up, back_down, back_proj = backward_set[:7]
    back_gain_a = backward_set[11].astype(jnp.float32)
    back_gain_f = backward_set[15].astype(jnp.float32)
    cot_low = jnp.where(is_valid[:, None], cot_embed, jnp.zeros_like(cot_embed))
    grad_w_proj = matmul_tn(out_low, cot_low)
    grad_out = keep_rows * cot_hidden.astype(jnp.float32) + matmul_nt(cot_low, back_proj)
    grad_resid_two, grad_gain_f, grad_shift_f = norm_backward(
        grad_out, normed_two, inverse_two, back_gain_f
    )
    down_grad = grad_resid_two.astype(jnp.bfloat16)
    grad_w_down = matmul_tn(act_low, down_grad)
    grad_b_down = jnp.sum(down_grad.astype(jnp.float32), axis=0)
    up_grad = gelu_pull(matmul_nt(down_grad, back_down))[0].astype(jnp.bfloat16)
    grad_w_up = matmul_tn(first_low, up_grad)
    grad_b_up = jnp.sum(up_grad.astype(jnp.float32), axis=0)
    grad_first = grad_resid_two + matmul_nt(up_grad, back_up)
    grad_resid_one, grad_gain_a, grad_shift_a = norm_backward(
        grad_first, normed_one, inverse_one, back_gain_a
    )
    attn_grad = grad_resid_one.astype(jnp.bfloat16)
    grad_w_out = matmul_tn(context, attn_grad)
    grad_b_out = jnp.sum(attn_grad.astype(jnp.float32), axis=0)
    ctx_grad = (
        matmul_nt(attn_grad, back_out).astype(jnp.bfloat16).reshape(row_count, head_count, head_dim)
    )
    allowed = is_valid[None, :, None] & key_valid
    masked = masked_scores(query_rot, key_rot, allowed, score_scale)
    prob_full = jnp.exp(masked - log_totals)
    prob_low = prob_full.astype(jnp.bfloat16)
    prob_grad = jnp.einsum("qhd,khd->hqk", ctx_grad, value_low, preferred_element_type=jnp.float32)
    value_sum = jnp.einsum("hqk,qhd->khd", prob_low, ctx_grad, preferred_element_type=jnp.float32)
    row_dot = jnp.sum(prob_full * prob_grad, axis=-1, keepdims=True)
    score_grad = jnp.where(allowed, prob_full * (prob_grad - row_dot), 0.0).astype(jnp.bfloat16)
    query_parts = (
        jnp.einsum("hqk,khd->qhd", score_grad, key_rot, preferred_element_type=jnp.float32)
        * score_scale
    )
    key_sum = (
        jnp.einsum("hqk,qhd->khd", score_grad, query_rot, preferred_element_type=jnp.float32)
        * score_scale
    )
    query_grad = (
        unrotate(query_parts, cosine, sine_part)
        .reshape(row_count, model_width)
        .astype(jnp.bfloat16)
    )
    key_grad = (
        unrotate(key_sum, cosine, sine_part).reshape(row_count, model_width).astype(jnp.bfloat16)
    )
    value_grad = value_sum.reshape(row_count, model_width).astype(jnp.bfloat16)
    grad_w_query = matmul_tn(tokens, query_grad)
    grad_b_query = jnp.sum(query_grad.astype(jnp.float32), axis=0)
    grad_w_key = matmul_tn(tokens, key_grad)
    grad_b_key = jnp.sum(key_grad.astype(jnp.float32), axis=0)
    grad_w_value = matmul_tn(tokens, value_grad)
    grad_b_value = jnp.sum(value_grad.astype(jnp.float32), axis=0)
    grad_tokens = (
        grad_resid_one
        + matmul_nt(query_grad, back_query)
        + matmul_nt(key_grad, back_key)
        + matmul_nt(value_grad, back_value)
    )
    all_parts = (
        lax.psum_scatter(grad_w_query, "dp", scatter_dimension=0, tiled=True),
        lax.psum_scatter(grad_w_key, "dp", scatter_dimension=0, tiled=True),
        lax.psum_scatter(grad_w_value, "dp", scatter_dimension=0, tiled=True),
        lax.psum_scatter(grad_w_out, "dp", scatter_dimension=0, tiled=True),
        lax.psum_scatter(grad_b_query, "dp", scatter_dimension=0, tiled=True),
        lax.psum_scatter(grad_b_key, "dp", scatter_dimension=0, tiled=True),
        lax.psum_scatter(grad_b_value, "dp", scatter_dimension=0, tiled=True),
        lax.psum_scatter(grad_b_out, "dp", scatter_dimension=0, tiled=True),
        lax.psum_scatter(grad_gain_a, "dp", scatter_dimension=0, tiled=True),
        lax.psum_scatter(grad_shift_a, "dp", scatter_dimension=0, tiled=True),
        lax.psum_scatter(grad_w_up, "dp", scatter_dimension=0, tiled=True),
        lax.psum_scatter(grad_w_down, "dp", scatter_dimension=0, tiled=True),
        lax.psum_scatter(grad_w_proj, "dp", scatter_dimension=0, tiled=True),
        lax.psum_scatter(grad_b_up, "dp", scatter_dimension=0, tiled=True),
        lax.psum_scatter(grad_b_down, "dp", scatter_dimension=0, tiled=True),
        lax.psum_scatter(grad_gain_f, "dp", scatter_dimension=0, tiled=True),
        lax.psum_scatter(grad_shift_f, "dp", scatter_dimension=0, tiled=True),
    )
    attn_parts = all_parts[:10]
    ffn_parts = all_parts[10:]
    return (
        hidden,
        embedding,
        grad_tokens,
        attn_parts[0],
        attn_parts[4],
        attn_parts[1],
        attn_parts[5],
        attn_parts[2],
        attn_parts[6],
        attn_parts[3],
        attn_parts[7],
        attn_parts[8],
        attn_parts[9],
        ffn_parts[0],
        ffn_parts[3],
        ffn_parts[1],
        ffn_parts[4],
        ffn_parts[5],
        ffn_parts[6],
        ffn_parts[2],
        rms_stats,
    )


def solution(mesh):
    fast = mesh.shape["dp"] == 32
    placed = (
        P("dp", None),
        P("dp", None),
        P("dp", None),
        P(),
        P(),
        P(),
        P("dp", None),
        P("dp"),
        P("dp", None),
        P("dp"),
        P("dp", None),
        P("dp"),
        P("dp", None),
        P("dp"),
        P("dp"),
        P("dp"),
        P("dp", None),
        P("dp"),
        P("dp", None),
        P("dp"),
        P("dp"),
        P("dp"),
        P("dp", None),
    )
    return jax.shard_map(
        shards if fast else shards_any,
        mesh=mesh,
        in_specs=placed,
        out_specs=(
            P("dp", None),
            P("dp", None),
            P("dp", None),
            P("dp", None),
            P("dp"),
            P("dp", None),
            P("dp"),
            P("dp", None),
            P("dp"),
            P("dp", None),
            P("dp"),
            P("dp"),
            P("dp"),
            P("dp", None),
            P("dp"),
            P("dp", None),
            P("dp"),
            P("dp"),
            P("dp"),
            P("dp", None),
            P(),
        ),
        check_vma=False,
    )
```

```python
import functools
import math

import jax
import jax.numpy as jnp
from jax import lax
from jax.experimental import pallas as pl
from jax.experimental.pallas import tpu as pltpu
from jax.sharding import PartitionSpec as P

MESH = pl.DeviceIdType.MESH

H = 16


eps_norm = 1e-05
neg_large = -1e30


def matmul(left, right):
    return jnp.dot(left, right, preferred_element_type=jnp.float32)


def matmul_nt(left, right):
    return lax.dot_general(
        left, right, (((1,), (1,)), ((), ())), preferred_element_type=jnp.float32
    )


def matmul_tn(left, right):
    return lax.dot_general(
        left, right, (((0,), (0,)), ((), ())), preferred_element_type=jnp.float32
    )


def exact_gelu(values):
    return jax.nn.gelu(values, approximate=False)


def norm_forward(values, gain, shift):
    row_mean = jnp.mean(values, axis=-1, keepdims=True)
    centred = values - row_mean
    inverse = lax.rsqrt(jnp.mean(centred * centred, axis=-1, keepdims=True) + eps_norm)
    normed = centred * inverse
    return (normed * gain + shift, normed, inverse)


def norm_backward(grad_in, normed, inverse, gain):
    scaled = grad_in * gain
    adjusted = (
        scaled
        - jnp.mean(scaled, axis=-1, keepdims=True)
        - normed * jnp.mean(scaled * normed, axis=-1, keepdims=True)
    )
    return (adjusted * inverse, jnp.sum(grad_in * normed, axis=0), jnp.sum(grad_in, axis=0))


def rope_tables(position, head_dim):
    half_dim = head_dim // 2
    freq_index = jnp.arange(half_dim, dtype=jnp.float32)
    frequency = jnp.exp(-math.log(10000.0) * 2.0 * freq_index / head_dim)
    angles = position[:, None] * frequency[None, :]
    return (jnp.cos(angles)[:, None, :], jnp.sin(angles)[:, None, :])


def rotate(values, cosine, sine_part):
    half_dim = values.shape[-1] // 2
    first_half = values[..., :half_dim]
    second = values[..., half_dim:]
    return jnp.concatenate(
        [first_half * cosine - second * sine_part, second * cosine + first_half * sine_part],
        axis=-1,
    )


def unrotate(grad_in, cosine, sine_part):
    half_dim = grad_in.shape[-1] // 2
    first_half = grad_in[..., :half_dim]
    second = grad_in[..., half_dim:]
    return jnp.concatenate(
        [first_half * cosine + second * sine_part, second * cosine - first_half * sine_part],
        axis=-1,
    )


def masked_scores(query_block, key_rot, allowed, score_scale):
    raw_scores = jnp.einsum(
        "qhd,khd->hqk", query_block, key_rot, preferred_element_type=jnp.float32
    )
    return jnp.where(allowed, raw_scores * score_scale, neg_large)


def device_at(z, y, x, c):
    return ((z * 2 + y) * 2 + x) * 2 + c


def wait_bytes(ref, sem):
    pltpu.make_async_copy(ref, ref, sem).wait()


def send(src, dst, sem_out, sem_in, target):
    pltpu.make_async_remote_copy(
        src_ref=src,
        dst_ref=dst,
        send_sem=sem_out,
        recv_sem=sem_in,
        device_id=(target,),
        device_id_type=MESH,
    ).start()


F32, BF16 = jnp.float32, jnp.bfloat16
ANY = pl.BlockSpec(memory_space=pl.ANY)
FWD_TENSORS = (
    (16, 128, F32),
    (32, 1024, BF16),
    (32, 1024, BF16),
    (32, 1024, BF16),
    (32, 1024, BF16),
    (32, 4096, BF16),
    (32, 128, BF16),
    (128, 1024, BF16),
)
FWD_PIECES = (
    ((0, 0, 128), (1, 0, 1024), (2, 0, 1024), (3, 0, 1024), (4, 0, 1024))
    + tuple((5, 1024 * k, 1024) for k in range(4))
    + ((6, 0, 128),)
    + ((7, 0, 256), (7, 256, 256), (7, 512, 256), (7, 768, 128), (7, 896, 128))
)
P_VEC, P_Q, P_K, P_V, P_O, P_UP, P_PROJ, P_DOWN, P_REST = 0, 1, 2, 3, 4, 5, 9, 10, 15
PLANE_FIRST = ()
V_BQ, V_BK, V_BV, V_BO, V_GA, V_SA, V_BD, V_GF, V_SF = range(9)


(
    F_OWN,
    F_PREPARE,
    F_COLUMN,
    F_PLANE,
    F_PAIR,
    F_ARRIVE,
    F_UNPACK,
    F_Q,
    F_K,
    F_V,
    F_ATTEND,
    F_PROJECT,
    F_NORM,
    F_UP,
    F_INCOMING,
    F_DOWN,
    F_TAIL,
) = range(17)
FWD_ORDER = (
    (F_OWN, 0),
    (F_OWN, 1),
    (F_OWN, 2),
    (F_OWN, 3),
    (F_OWN, 4),
    (F_OWN, 5),
    (F_OWN, 6),
    (F_OWN, 7),
    (F_PREPARE, 0),
    (F_OWN, 8),
    (F_COLUMN, 0),
    (F_OWN, 9),
    (F_COLUMN, 1),
    (F_PLANE, 0),
    (F_OWN, 10),
    (F_COLUMN, 2),
    (F_PLANE, 1),
    (F_PAIR, 0),
    (F_OWN, 11),
    (F_COLUMN, 3),
    (F_PLANE, 2),
    (F_PAIR, 1),
    (F_ARRIVE, 0),
    (F_OWN, 12),
    (F_COLUMN, 4),
    (F_UNPACK, 0),
    (F_PLANE, 3),
    (F_PAIR, 2),
    (F_ARRIVE, 1),
    (F_OWN, 13),
    (F_COLUMN, 5),
    (F_Q, 0),
    (F_PLANE, 4),
    (F_PAIR, 3),
    (F_ARRIVE, 2),
    (F_OWN, 14),
    (F_COLUMN, 6),
    (F_K, 0),
    (F_PLANE, 5),
    (F_PAIR, 4),
    (F_ARRIVE, 3),
    (F_COLUMN, 7),
    (F_V, 0),
    (F_PLANE, 6),
    (F_ATTEND, 0),
    (F_PAIR, 5),
    (F_ARRIVE, 4),
    (F_COLUMN, 8),
    (F_ATTEND, 1),
    (F_PLANE, 7),
    (F_ATTEND, 2),
    (F_PAIR, 6),
    (F_ARRIVE, 5),
    (F_COLUMN, 9),
    (F_ATTEND, 3),
    (F_PLANE, 8),
    (F_PROJECT, 0),
    (F_PAIR, 7),
    (F_NORM, 0),
    (F_ARRIVE, 6),
    (F_COLUMN, 10),
    (F_UP, 0),
    (F_PLANE, 9),
    (F_PAIR, 8),
    (F_ARRIVE, 7),
    (F_COLUMN, 11),
    (F_UP, 1),
    (F_PLANE, 10),
    (F_PAIR, 9),
    (F_ARRIVE, 8),
    (F_COLUMN, 12),
    (F_UP, 2),
    (F_PLANE, 11),
    (F_PAIR, 10),
    (F_ARRIVE, 9),
    (F_COLUMN, 13),
    (F_UP, 3),
    (F_PLANE, 12),
    (F_PAIR, 11),
    (F_ARRIVE, 10),
    (F_COLUMN, 14),
    (F_INCOMING, 0),
    (F_PLANE, 13),
    (F_DOWN, 0),
    (F_PAIR, 12),
    (F_ARRIVE, 11),
    (F_PLANE, 14),
    (F_DOWN, 1),
    (F_PAIR, 13),
    (F_ARRIVE, 12),
    (F_PAIR, 14),
    (F_DOWN, 2),
    (F_ARRIVE, 13),
    (F_ARRIVE, 14),
    (F_DOWN, 3),
    (F_DOWN, 4),
    (F_TAIL, 0),
)


def dot(left, right):
    return jnp.dot(left, right, preferred_element_type=F32)


def dot_nt(left, right):
    return lax.dot_general(left, right, (((1,), (1,)), ((), ())), preferred_element_type=F32)


def local_copy(src, dst, sem):
    pltpu.make_async_copy(src, dst, sem).start()


def lanes_at(start, size):
    return pl.ds(pl.multiple_of(start, 128), size)


def rows_at(start, size):
    return pl.ds(pl.multiple_of(start, size), size)


def place():
    me = lax.axis_index("dp")
    return me // 8, (me // 4) % 2, (me // 2) % 2, me % 2


def greet_start(z, y, x, c):
    others = [(z + k) % 4 for k in (1, 2, 3)]
    peers = [device_at(z, y, 1 - x, c), device_at(z, 1 - y, x, c), device_at(z, y, x, 1 - c)]
    peers += [device_at(zz, y, x, c) for zz in others]
    barrier = pltpu.get_barrier_semaphore()
    for peer in peers:
        pl.semaphore_signal(barrier, inc=1, device_id=(peer,), device_id_type=MESH)


def greet_end():
    pl.semaphore_wait(pltpu.get_barrier_semaphore(), 6)


def transpose_blocks(src, dst):
    @pl.loop(0, src.shape[1] // 128)
    def _(j):
        block = src[:, lanes_at(j * 128, 128)].T
        for b in range(4):
            dst[b % 2, rows_at((2 * j + b // 2) * 32, 32), :] = block[32 * b : 32 * b + 32]


def forward_kernel(
    tokens_h, cot_h, cote_h, lengths_s, offsets_s, order_s, *refs
):
    vectors = refs[:10]
    refs = refs[10:]
    src = (None,) + refs[:7]
    refs = refs[7:]
    full = (None,) + refs[:7]
    (
        q_h, kt_h, v_h, prob_h, ctxp_h, n1_h, inv1_h, firstp_h, tokp_h, act_h, slope_h,
        back_h, dg_h, low_h, hidden_h, vecs_h, stats_h, cos_h, sin_h, sums_h,
    ) = refs[7:27]
    refs = refs[27:]
    (
        tok, packed, table, vecs, bias_up, cosine, sine, mask, stats,
        q, k, v, kt, vt, prob, ctx, ctxp, tokp, resid, n1, inv1, low, lowp, act, slope, back, sums,
        hidden, embed,
    ) = refs[:29]
    refs = refs[29:]
    count = len(FWD_PIECES)
    wbuf = (None,) + refs[: count - 1]
    mybuf = (None,) + refs[count - 1 : 2 * count - 2]
    ss, rs, ls, ld, os, ps, ins, ms = refs[2 * count - 2 :]
    z, y, x, c = place()
    me = device_at(z, y, x, c)
    near_x, near_y = device_at(z, y, 1 - x, c), device_at(z, 1 - y, x, c)
    sibling = device_at(z, y, x, 1 - c)
    others = [(z + kk) % 4 for kk in (1, 2, 3)]

    greet_start(z, y, x, c)
    for t in range(1, count):
        tensor, first, width = FWD_PIECES[t]
        local_copy(src[tensor].at[:, pl.ds(first, width)], mybuf[t], ms.at[t])
    local_copy(tokens_h, tok, ins.at[1])
    local_copy(cot_h, hidden, ins.at[0])
    local_copy(cote_h, embed, ins.at[2])

    def home(t, *lead):
        tensor, first, width = FWD_PIECES[t]
        if t == P_VEC:
            return table.at[lead]
        return full[tensor].at[lead + (slice(None), pl.ds(first, width))]

    def part(t, lead, rows):
        tensor, first, width = FWD_PIECES[t]
        if t == P_VEC:
            return table.at[lead + (rows,)]
        return full[tensor].at[lead + (rows, pl.ds(first, width))]

    every = slice(None)

    def cast(t, block, mine):
        for zz in others:
            send(block, mine, ss.at[t, 0], rs.at[t, 0], device_at(zz, y, x, c))

    def wait_cast(t, sem):
        lead = (every, every, 0) if t in PLANE_FIRST else (0, 0, 0)
        wait_bytes(home(t, pl.ds(0, 3), *lead), sem)

    def own(t):
        tensor, first, width = FWD_PIECES[t]
        piece = packed if t == P_VEC else src[tensor].at[:, pl.ds(first, width)]
        mine = home(t, z, y, x, c)
        if t not in PLANE_FIRST:
            cast(t, piece, mine)
        send(piece, mine, ss.at[t, 1], rs.at[t, 1], near_x)
        send(piece, mine, ss.at[t, 2], rs.at[t, 2], near_y)
        if t == P_VEC:
            local_copy(packed, mine, ls.at[t])
        else:
            wait_bytes(mybuf[t], ms.at[t])
            local_copy(mybuf[t], mine, ls.at[t])

    def column(t):
        wait_cast(t, rs.at[t, 0])
        for zz in others:
            block = home(t, zz, y, x, c)
            send(block, block, ss.at[t, 3], rs.at[t, 3], near_x)
            send(block, block, ss.at[t, 4], rs.at[t, 4], near_y)

    def plane(t):
        half = FWD_TENSORS[FWD_PIECES[t][0]][0] // 2
        flat = t in PLANE_FIRST
        layers = z if flat else every
        wait_bytes(home(t, 0, 0, 0, 0), rs.at[t, 1])
        if not flat:
            wait_bytes(home(t, pl.ds(0, 3), 0, 0, 0), rs.at[t, 3])
        block = part(t, (layers, y, 1 - x, c), pl.ds(0, half))
        send(block, block, ss.at[t, 5], rs.at[t, 5], near_y)
        wait_bytes(home(t, 0, 0, 0, 0), rs.at[t, 2])
        if not flat:
            wait_bytes(home(t, pl.ds(0, 3), 0, 0, 0), rs.at[t, 4])
        block = part(t, (layers, 1 - y, x, c), pl.ds(half, half))
        send(block, block, ss.at[t, 6], rs.at[t, 6], near_x)
        wait_bytes(home(t, 0, 0, 0, 0), ls.at[t])
        if not flat:
            for block in (home(t, every, y, every, c), home(t, every, 1 - y, x, c)):
                send(block, block, ss.at[t, 8], rs.at[t, 8], sibling)

    def gathered(t):
        half = FWD_TENSORS[FWD_PIECES[t][0]][0] // 2
        layers = 0 if t in PLANE_FIRST else every
        for kind in (5, 6):
            wait_bytes(part(t, (layers, 0, 0, 0), pl.ds(0, half)), rs.at[t, kind])

    def plane_cast(t):
        gathered(t)
        cast(t, home(t, z, every, every, c), home(t, z, every, every, c))

    def load(t, parity):
        if t != P_VEC:
            tensor, first, width = FWD_PIECES[t]
            local_copy(
                full[tensor].at[:, :, :, parity, :, pl.ds(first, width)],
                wbuf[t].at[:, :, :, parity],
                ld.at[t],
            )

    def pair(t):
        if t in PLANE_FIRST:
            wait_cast(t, rs.at[t, 0])
            block = home(t, every, every, every, c)
        else:
            gathered(t)
            block = home(t, every, 1 - y, 1 - x, c)
        send(block, block, ss.at[t, 7], rs.at[t, 7], sibling)
        load(t, c)

    def last_part(t):
        if t in PLANE_FIRST:
            return home(t, every, every, every, 0)
        return home(t, every, 0, 0, 0)

    def arrive(t):
        wait_bytes(last_part(t), rs.at[t, 7])
        if t not in PLANE_FIRST:
            wait_bytes(home(t, pl.ds(0, 3), every, every, 0), rs.at[t, 8])
        load(t, 1 - c)

    def loaded(t):
        wait_bytes(wbuf[t], ld.at[t])

    def sent(t):
        half = FWD_TENSORS[FWD_PIECES[t][0]][0] // 2
        flat = t in PLANE_FIRST
        wait_cast(t, ss.at[t, 0])
        for kind in (1, 2):
            wait_bytes(home(t, 0, 0, 0, 0), ss.at[t, kind])
        if not flat:
            for kind in (3, 4):
                wait_bytes(home(t, pl.ds(0, 3), 0, 0, 0), ss.at[t, kind])
            wait_bytes(home(t, pl.ds(0, 3), every, every, 0), ss.at[t, 8])
        for kind in (5, 6):
            wait_bytes(part(t, (0 if flat else every, 0, 0, 0), pl.ds(0, half)), ss.at[t, kind])
        wait_bytes(last_part(t), ss.at[t, 7])

    pack = order_s[me]
    length, offset = lengths_s[pack], offsets_s[pack]
    saved = []

    def save(value, out):
        n = len(saved)
        local_copy(value, out, os.at[n])
        saved.append((out, os.at[n]))

    def row_valid(rows, start):
        r = lax.broadcasted_iota(jnp.int32, (rows, 1), 0) + start
        return ((r >= offset) & (r < offset + length)).astype(F32)

    def pack_vectors():
        lane = lax.broadcasted_iota(jnp.int32, (1, 128), 1)
        for i in range(9):
            val = vectors[i][...].astype(F32).reshape(1, 32)
            wide = jnp.concatenate([val] * 4, axis=1)
            packed[i : i + 1, :] = jnp.where(lane // 32 == me % 4, wide, 0.0)
        packed[9:10, :] = vectors[9][...].astype(F32).reshape(1, 128)
        packed[10:16, :] = jnp.zeros((6, 128), F32)

    def prepare():
        lane = lax.broadcasted_iota(jnp.int32, (1, 128), 1)
        freq = jnp.exp((lane % 32).astype(F32) * (-math.log(10000.0) * 2.0 / 64))

        @pl.loop(0, 8)
        def _(i):
            r = lax.broadcasted_iota(jnp.int32, (64, 1), 0) + i * 64
            angle = (r - offset).astype(F32) * freq
            cosine[rows_at(i * 64, 64), :] = jnp.cos(angle)
            sine[rows_at(i * 64, 64), :] = jnp.where(lane % 64 < 32, -1.0, 1.0) * jnp.sin(angle)

        s = lax.broadcasted_iota(jnp.int32, (1, 512), 1)
        col_valid = ((s >= offset) & (s < offset + length)).astype(F32)
        stats[...] = jnp.zeros_like(stats)

        @pl.loop(0, 8)
        def _(i):
            mask[rows_at(i * 64, 64), :] = row_valid(64, i * 64) * col_valid

        stats[3:4, :] = jnp.broadcast_to(
            jnp.sum(col_valid, axis=1, keepdims=True), (1, 128)
        )
        wait_bytes(tok, ins.at[1])

        @pl.loop(0, 8)
        def _(i):
            t32 = tok[rows_at(i * 64, 64), :].astype(F32)
            add_stat(0, jnp.sum(row_valid(64, i * 64) * t32 * t32, axis=0, keepdims=True))

        transpose_blocks(tok, tokp)
        save(tokp, tokp_h)
        save(cosine, cos_h)
        save(sine, sin_h)

    def add_stat(row, wide):
        total = wide[:, 0:128]
        for i in range(1, wide.shape[1] // 128):
            total = total + wide[:, 128 * i : 128 * i + 128]
        stats[row : row + 1, :] = stats[row : row + 1, :] + total

    def unpack_vectors():
        grouped = table[...].reshape(8, 4, 16, 128).sum(axis=1)
        for b in range(8):
            vecs[:, 128 * b : 128 * b + 128] = grouped[b]
        for d in range(32):
            bias_up[0:1, 128 * d : 128 * d + 128] = table[
                d // 8, (d // 4) % 2, (d // 2) % 2, d % 2, 9:10, :
            ]
        save(vecs, vecs_h)

    def weight(t, first, width):
        w = wbuf[t]
        return w[:, :, :, :, :, lanes_at(first, width)].reshape(-1, width)

    lane128 = lambda: lax.broadcasted_iota(jnp.int32, (1, 128), 1)

    def rotary(t, bias, dst, scale, transposed, j0, j1):
        @pl.loop(j0, j1)
        def _(j):
            pre = dot(tok[...], weight(t, j * 256, 256)) + vecs[bias : bias + 1, lanes_at(j * 256, 256)]
            for b in range(2):
                part_in = pre[:, 128 * b : 128 * b + 128]
                swapped = jnp.where(
                    lane128() % 64 < 32, pltpu.roll(part_in, 96, 1), pltpu.roll(part_in, 32, 1)
                )
                turned = (part_in * cosine[...] + swapped * sine[...]).astype(BF16)
                if transposed is not None:
                    transposed[rows_at(j * 256 + 128 * b, 128), :] = turned.T
                dst[:, lanes_at(j * 256 + 128 * b, 128)] = turned * jnp.asarray(scale, BF16)

    def value(j0, j1):
        @pl.loop(j0, j1)
        def _(j):
            pre = dot(tok[...], weight(P_V, j * 256, 256)) + vecs[V_BV : V_BV + 1, lanes_at(j * 256, 256)]
            val = pre.astype(BF16)
            v[:, lanes_at(j * 256, 256)] = val
            vt[rows_at(j * 256, 256), :] = val.T

    def attend(p0, p1):
        @pl.loop(p0, p1)
        def _(p):
            cols = lanes_at(p * 128, 128)
            qp, kp = q[:, cols], k[:, cols]
            pieces = []
            for j in range(2):
                keep = lane128() < 64 if j == 0 else lane128() >= 64
                scores = dot_nt(jnp.where(keep, kp, jnp.zeros((), BF16)), qp)
                scores = jnp.where(mask[...] > 0.0, scores, -1e30)
                top = jnp.max(scores, axis=0, keepdims=True)
                expo = jnp.exp(scores - top)
                total = jnp.sum(expo, axis=0, keepdims=True)
                weights = (expo * (1.0 / total)).astype(BF16)

                @pl.when(p > 0)
                def _():
                    wait_bytes(prob.at[j], ps.at[j])

                prob[j] = weights
                local_copy(prob.at[j], prob_h.at[p, j], ps.at[j])
                mixed = dot(vt[rows_at(p * 128 + 64 * j, 64), :], weights).astype(BF16)
                for b in range(2):
                    ctxp[b, rows_at((2 * p + j) * 32, 32), :] = mixed[32 * b : 32 * b + 32]
                pieces.append(mixed)
            ctx[:, cols] = jnp.concatenate(pieces, axis=0).T

    def attended():
        for j in range(2):
            wait_bytes(prob.at[j], ps.at[j])
        save(ctxp, ctxp_h)

    def project():
        loaded(P_O)

        @pl.loop(0, 4)
        def _(j):
            cols = lanes_at(j * 256, 256)
            branch = dot(ctx[...], weight(P_O, j * 256, 256)) + vecs[V_BO : V_BO + 1, cols]
            add_stat(1, jnp.sum(row_valid(512, 0) * branch * branch, axis=0, keepdims=True))
            resid[:, cols] = branch + tok[:, cols].astype(F32)

    def normalise(i):
        rows = rows_at(i * 32, 32)
        val = resid[rows, :]
        mean = jnp.sum(val, axis=1, keepdims=True) * (1.0 / 1024)
        centred = val - mean
        scale = lax.rsqrt(jnp.sum(centred * centred, axis=1, keepdims=True) * (1.0 / 1024) + eps_norm)
        return rows, centred * scale, scale

    def norm_first():
        @pl.loop(0, 16, unroll=4)
        def _(i):
            rows, normed, scale = normalise(i)
            n1[rows, :] = normed
            inv1[rows, :] = jnp.broadcast_to(scale, (32, 128))
            low[rows, :] = (normed * vecs[V_GA : V_GA + 1, :] + vecs[V_SA : V_SA + 1, :]).astype(BF16)

        save(n1, n1_h)
        save(inv1, inv1_h)
        transpose_blocks(low, lowp)
        save(lowp, firstp_h)

    def incoming():
        loaded(P_PROJ)
        wait_bytes(hidden, ins.at[0])
        wait_bytes(embed, ins.at[2])
        cot = jnp.where(row_valid(512, 0) > 0.0, embed[...].astype(F32), 0.0).astype(BF16)
        w = weight(P_PROJ, 0, 128)
        for j in range(4):
            cols = pl.ds(256 * j, 256)
            back[:, cols] = row_valid(512, 0) * hidden[:, cols].astype(F32) + dot_nt(
                cot, w[256 * j : 256 * j + 256]
            )
        sums[...] = jnp.zeros_like(sums)

    def expand(k0):
        def tile(j, w):
            cols = lanes_at(k0 * 1024 + j * 256, 256)
            pre = dot(low[...], w) + bias_up[0:1, cols]
            cdf = 0.5 * (1.0 + lax.erf(pre * math.sqrt(0.5)))
            val = (pre * cdf).astype(BF16)
            pdf = jnp.exp(pre * pre * -0.5) * (1.0 / math.sqrt(2 * math.pi))
            slope[:, cols] = (cdf + pre * pdf).astype(BF16)
            half = lanes_at(k0 * 512 + j * 128, 128)
            act[0, :, half] = val[:, :128]
            act[1, :, half] = val[:, 128:]

        wide = FWD_PIECES[P_UP + k0][2] // 256

        @pl.loop(0, wide)
        def _(j):
            tile(j, weight(P_UP + k0, j * 256, 256))

        if wide < 4:
            tile(3, weight(P_REST + k0, 0, 256))

    def contract(k0):
        _, first_col, width = FWD_PIECES[P_DOWN + k0]
        cols = pl.ds(first_col, width)
        w = wbuf[P_DOWN + k0]
        branch = dot(act[0], w[:, :, :, 0].reshape(2048, width))
        branch = branch + dot(act[1], w[:, :, :, 1].reshape(2048, width)) + vecs[V_BD : V_BD + 1, cols]
        add_stat(2, jnp.sum(row_valid(512, 0) * branch * branch, axis=0, keepdims=True))
        first = n1[:, cols] * vecs[V_GA : V_GA + 1, cols] + vecs[V_SA : V_SA + 1, cols]
        resid[:, cols] = first + branch

    def norm_second():
        def block(i):
            rows, normed, scale = normalise(i)
            gain = vecs[V_GF : V_GF + 1, :]
            out = normed * gain + vecs[V_SF : V_SF + 1, :]
            low[rows, :] = out.astype(BF16)
            hidden[rows, :] = (out * row_valid(32, i * 32)).astype(BF16)
            grad = back[rows, :]
            scaled = grad * gain
            mean = jnp.sum(scaled, axis=1, keepdims=True) * (1.0 / 1024)
            cross = jnp.sum(scaled * normed, axis=1, keepdims=True) * (1.0 / 1024)
            res = (scaled - mean - normed * cross) * scale
            back[rows, :] = res
            ctx[rows, :] = res.astype(BF16)
            sums[0:1, :] = sums[0:1, :] + jnp.sum(grad * normed, axis=0, keepdims=True)
            sums[1:2, :] = sums[1:2, :] + jnp.sum(grad, axis=0, keepdims=True)

        for part_of in (0, 1):
            pl.loop(8 * part_of, 8 * part_of + 8, unroll=4)(block)
            rows = pl.ds(256 * part_of, 256)
            for value, out in ((ctx, dg_h), (low, low_h), (back, back_h), (hidden, hidden_h)):
                save(value.at[rows], out.at[rows])
        save(sums, sums_h)
        save(stats, stats_h)

    pack_vectors()
    greet_end()
    moves = {
        F_OWN: own, F_COLUMN: column, F_PLANE: plane, F_PAIR: pair, F_ARRIVE: arrive,
    }
    work = {
        F_PREPARE: prepare,
        F_UNPACK: unpack_vectors,
        F_Q: lambda: (loaded(P_Q), rotary(P_Q, V_BQ, q, 0.125, None, 0, 4), save(q, q_h)),
        F_K: lambda: (loaded(P_K), rotary(P_K, V_BK, k, 1.0, kt, 0, 4), save(kt, kt_h)),
        F_V: lambda: (loaded(P_V), value(0, 4), save(v, v_h)),
        F_PROJECT: project,
        F_NORM: norm_first,
        F_INCOMING: incoming,
        F_TAIL: norm_second,
    }
    for name, t in FWD_ORDER:
        if name in moves:
            moves[name](t)
        elif name == F_ATTEND:
            attend(2 * t, 2 * t + 2)
            if t == 3:
                attended()
        elif name == F_UP:
            loaded(P_UP + t)
            if P_REST + t < count:
                loaded(P_REST + t)
            expand(t)
            cols = pl.ds(512 * t, 512)
            save(act.at[:, :, cols], act_h.at[:, :, cols])
            cols = pl.ds(1024 * t, 1024)
            save(slope.at[:, cols], slope_h.at[:, cols])
        elif name == F_DOWN:
            loaded(P_DOWN + t)
            contract(t)
        else:
            work[name]()
    for t in range(count):
        sent(t)
    for out, sem in saved:
        wait_bytes(out, sem)


FWD_SAVED = (
    ((512, 1024), BF16),
    ((1024, 512), BF16),
    ((512, 1024), BF16),
    ((8, 2, 512, 512), BF16),
    ((2, 512, 512), BF16),
    ((512, 1024), F32),
    ((512, 128), F32),
    ((2, 512, 512), BF16),
    ((2, 512, 512), BF16),
    ((2, 512, 2048), BF16),
    ((512, 4096), BF16),
    ((512, 1024), F32),
    ((512, 1024), BF16),
    ((512, 1024), BF16),
    ((512, 1024), BF16),
    ((16, 1024), F32),
    ((8, 128), F32),
    ((512, 128), F32),
    ((512, 128), F32),
    ((8, 1024), F32),
)


def forward_pass(tokens, cot_hidden, cot_embed, vectors, lengths, offsets, order, weights):
    count = len(FWD_PIECES)
    shape = jax.ShapeDtypeStruct
    outs = [shape((4, 2, 2, 2, r, k), dt) for r, k, dt in FWD_TENSORS[1:]]
    outs += [shape(s, dt) for s, dt in FWD_SAVED]
    big = lambda *s: pltpu.VMEM(s, BF16)
    scratch = [
        big(512, 1024),
        pltpu.VMEM((16, 128), F32),
        pltpu.VMEM((4, 2, 2, 2, 16, 128), F32),
        pltpu.VMEM((16, 1024), F32),
        pltpu.VMEM((1, 4096), F32),
        pltpu.VMEM((512, 128), F32),
        pltpu.VMEM((512, 128), F32),
        pltpu.VMEM((512, 512), F32),
        pltpu.VMEM((8, 128), F32),
        big(512, 1024),
        big(512, 1024),
        big(512, 1024),
        big(1024, 512),
        big(1024, 512),
        big(2, 512, 512),
        big(512, 1024),
        big(2, 512, 512),
        big(2, 512, 512),
        pltpu.VMEM((512, 1024), F32),
        pltpu.VMEM((512, 1024), F32),
        pltpu.VMEM((512, 128), F32),
        big(512, 1024),
        big(2, 512, 512),
        big(2, 512, 2048),
        big(512, 4096),
        pltpu.VMEM((512, 1024), F32),
        pltpu.VMEM((8, 1024), F32),
        big(512, 1024),
        big(512, 128),
    ]
    for tensor, _, width in FWD_PIECES[1:]:
        scratch.append(big(4, 2, 2, 2, FWD_TENSORS[tensor][0], width))
    for tensor, _, width in FWD_PIECES[1:]:
        scratch.append(big(FWD_TENSORS[tensor][0], width))
    dma = pltpu.SemaphoreType.DMA
    scratch += [
        dma((count, 9)), dma((count, 9)), dma((count,)), dma((count,)), dma((32,)), dma((2,)), dma((3,)),
        dma((count,)),
    ]
    smem = pl.BlockSpec(memory_space=pltpu.SMEM)
    return pl.pallas_call(
        forward_kernel,
        out_shape=outs,
        in_specs=[ANY, ANY, ANY, smem, smem, smem]
        + [pl.BlockSpec(memory_space=pltpu.VMEM)] * 10
        + [ANY] * 7,
        out_specs=[ANY] * len(outs),
        scratch_shapes=scratch,
        compiler_params=pltpu.CompilerParams(
            collective_id=0, has_side_effects=True, vmem_limit_bytes=62 * 2**20
        ),
        name="forward_pass",
    )(tokens, cot_hidden, cot_embed, lengths, offsets, order, *vectors, *weights)


R_PROJ, R_DOWN, R_UP, R_OUT, R_Q, R_K, R_VEC, R_V, R_K_END, R_V_END = 0, 1, 5, 9, 10, 11, 12, 13, 14, 15
BWD_OUTS = (
    (32, 128, BF16),
    (1024, 128, BF16),
    (32, 4096, BF16),
    (32, 1024, BF16),
    (32, 1024, BF16),
    (32, 1024, BF16),
    (16, 128, F32),
    (32, 1024, BF16),
)
BWD_PIECES = (
    ((0, 0, 32, 128, BF16),)
    + tuple((1, 256 * k, 256, 128, BF16) for k in range(4))
    + tuple((2, 1024 * k, 32, 1024, BF16) for k in range(4))
    + (
        (3, 0, 32, 1024, BF16),
        (4, 0, 32, 1024, BF16),
        (5, 0, 32, 512, BF16),
        (6, 0, 16, 128, F32),
        (7, 0, 32, 512, BF16),
        (5, 512, 32, 512, BF16),
        (7, 512, 32, 512, BF16),
    )
)


(
    B_TURN,
    B_ACTS,
    B_DOWNSIB,
    B_DOWNOWN,
    B_NET,
    B_BEGIN,
    B_DIAGONAL,
    B_SIB,
    B_UP,
    B_FIRST,
    B_OWN,
    B_PLANE,
    B_NORM,
    B_BACK,
    B_ATTEND,
    B_BIAS,
    B_COLUMN,
    B_TOKENS,
) = range(18)
BWD_ORDER = (
    (B_TURN, 0),
    (B_ACTS, 0),
    (B_DOWNSIB, 0),
    (B_DOWNSIB, 1),
    (B_DOWNOWN, 0),
    (B_NET, 1),
    (B_DOWNOWN, 1),
    (B_DOWNSIB, 2),
    (B_NET, 2),
    (B_BEGIN, 0),
    (B_DIAGONAL, 1),
    (B_SIB, 0),
    (B_UP, 0),
    (B_SIB, 5),
    (B_FIRST, 0),
    (B_DIAGONAL, 2),
    (B_OWN, 0),
    (B_DOWNOWN, 2),
    (B_UP, 1),
    (B_NET, 0),
    (B_SIB, 6),
    (B_PLANE, 1),
    (B_NET, 3),
    (B_FIRST, 1),
    (B_OWN, 5),
    (B_DIAGONAL, 0),
    (B_PLANE, 2),
    (B_NET, 5),
    (B_UP, 2),
    (B_DIAGONAL, 3),
    (B_SIB, 7),
    (B_OWN, 6),
    (B_NET, 4),
    (B_FIRST, 2),
    (B_PLANE, 0),
    (B_UP, 3),
    (B_PLANE, 3),
    (B_SIB, 8),
    (B_NET, 6),
    (B_FIRST, 3),
    (B_DIAGONAL, 4),
    (B_OWN, 7),
    (B_NORM, 0),
    (B_OWN, 8),
    (B_BACK, 0),
    (B_DIAGONAL, 6),
    (B_SIB, 9),
    (B_ATTEND, 0),
    (B_NET, 7),
    (B_ATTEND, 1),
    (B_PLANE, 4),
    (B_PLANE, 6),
    (B_OWN, 9),
    (B_NET, 8),
    (B_ATTEND, 2),
    (B_DIAGONAL, 7),
    (B_ATTEND, 3),
    (B_BIAS, 0),
    (B_DIAGONAL, 8),
    (B_SIB, 10),
    (B_SIB, 11),
    (B_SIB, 14),
    (B_SIB, 13),
    (B_SIB, 15),
    (B_SIB, 12),
    (B_PLANE, 7),
    (B_NET, 9),
    (B_OWN, 10),
    (B_COLUMN, 5),
    (B_OWN, 11),
    (B_PLANE, 8),
    (B_OWN, 14),
    (B_OWN, 13),
    (B_OWN, 15),
    (B_OWN, 12),
    (B_TOKENS, 0),
    (B_DIAGONAL, 9),
    (B_TOKENS, 1),
    (B_NET, 10),
    (B_DIAGONAL, 5),
    (B_TOKENS, 2),
    (B_PLANE, 9),
    (B_DIAGONAL, 10),
    (B_PLANE, 5),
    (B_NET, 11),
    (B_PLANE, 10),
    (B_NET, 14),
    (B_DIAGONAL, 11),
    (B_DIAGONAL, 14),
    (B_NET, 12),
    (B_NET, 13),
    (B_PLANE, 11),
    (B_NET, 15),
    (B_PLANE, 14),
    (B_DIAGONAL, 12),
    (B_DIAGONAL, 13),
    (B_DIAGONAL, 15),
    (B_PLANE, 12),
    (B_PLANE, 13),
    (B_PLANE, 15),
)
Z_FIRST = (R_UP,)


def backward_kernel(cote_h, lengths_s, offsets_s, order_s, *refs):
    wq_h, wk_h, wv_h, wo_h, wup_h, wproj_h, wdown_h = refs[:7]
    (
        q_h, kt_h, v_h, prob_h, ctxp_h, n1_h, inv1_h, firstp_h, tokp_h, act_h, slope_h,
        back_h, dg_h, low_h, vecs_h, stats_h, cos_h, sin_h, sumf_h,
    ) = refs[7:26]
    refs = refs[26:]
    grad_h, embed_h = refs[:2]
    outs = refs[2:10]
    refs = refs[10:]
    (
        ring, resid, nbuf, sumf, inv1, dg, dgt, upg, four, slopes, blocks, kt, mask,
        cosine, sine, cot, vecs, stats, sums, sum_up, table, stage_d, stage_u, stage_p, wproj, embed,
    ) = refs[:26]
    refs = refs[26:]
    count = len(BWD_PIECES)
    acc, diag, from_x, from_y = (refs[i * count : (i + 1) * count] for i in range(4))
    refs = refs[4 * count :]
    from_z = dict(zip(Z_FIRST, refs))
    ss, rs, ls, ins, rsem, psem, gsem, esem = refs[len(Z_FIRST) :]
    z, y, x, c = place()
    me = device_at(z, y, x, c)
    near_x, near_y = device_at(z, y, 1 - x, c), device_at(z, 1 - y, x, c)
    sibling = device_at(z, y, x, 1 - c)
    others = [(z + kk) % 4 for kk in (1, 2, 3)]
    pack = order_s[me]
    length, offset = lengths_s[pack], offsets_s[pack]

    ring_src = []
    for j in range(4):
        ring_src.append(wdown_h.at[pl.ds(1024 * j, 1024), :])
        ring_src.append(wup_h.at[:, pl.ds(1024 * j, 1024)])
    ring_src += [wo_h, wq_h, wk_h, wv_h]

    def ring_start(n):
        local_copy(ring_src[n], ring.at[n % 3], rsem.at[n])

    def ring_wait(n):
        wait_bytes(ring.at[n % 3], rsem.at[n])
        return ring.at[n % 3]

    def ring_next(n):
        if n + 3 < len(ring_src):
            ring_start(n + 3)

    loads = {}

    def load(name, src, dst):
        n = len(loads)
        loads[name] = (dst, ins.at[n])
        local_copy(src, dst, ins.at[n])

    def ready(name):
        dst, sem = loads[name]
        wait_bytes(dst, sem)

    load("dg", dg_h, dg)
    for p in range(2):
        for h in range(2):
            load("act%d%d" % (p, h), act_h.at[p, :, pl.ds(1024 * h, 1024)], four.at[2 * p + h])
    load("cote", cote_h, cot)
    load("low", low_h, slopes.at[1])
    load("wproj", wproj_h, wproj)
    ring_start(0)
    load("slope0", slope_h.at[:, pl.ds(0, 1024)], slopes.at[0])
    load("firstp", firstp_h, blocks.at[1])
    load("back", back_h, resid)
    ring_start(1)
    ring_start(2)
    load("n1", n1_h, nbuf)
    load("inv1", inv1_h, inv1)
    load("vecs", vecs_h, vecs)
    load("sumf", sumf_h, sumf)
    load("stats", stats_h, stats)
    load("cos", cos_h, cosine)
    load("sin", sin_h, sine)
    load("kt", kt_h, kt)
    greet_start(z, y, x, c)

    def out_view(t, *lead):
        out, first, rows, width, _ = BWD_PIECES[t]
        if R_DOWN <= t < R_UP:
            return outs[out].at[lead + (pl.ds(first, rows), slice(None))]
        return outs[out].at[lead + (slice(None), pl.ds(first, width))]

    def give(t, stage):
        send(stage, acc[t], ss.at[t, 0], rs.at[t, 0], sibling)

    def layers(t):
        return z if t in Z_FIRST else slice(None)

    def side(ref, t, rows):
        return ref.at[rows] if t in Z_FIRST else ref.at[:, rows]

    def net(t):
        if t in Z_FIRST:
            for kk, zz in zip((1, 2, 3), others):
                send(acc[t].at[zz], from_z[t].at[3 - kk], ss.at[t, 7], rs.at[t, 7], device_at(zz, y, x, c))
        else:
            spread(t)

    def add_column(t):
        h = acc[t]
        wait_bytes(from_z[t], rs.at[t, 7])

        @pl.loop(0, 4)
        def _(i):
            total = h[z, i // 2, i % 2].astype(F32)
            for k in range(3):
                total = total + from_z[t][k, i // 2, i % 2].astype(F32)
            h[z, i // 2, i % 2] = total.astype(BF16)

        spread(t)

    def spread(t):
        half = BWD_PIECES[t][2] // 2
        h, a = acc[t], layers(t)
        first, second = pl.ds(0, half), pl.ds(half, half)
        send(h.at[a, 1 - y, 1 - x, first], diag[t].at[0], ss.at[t, 1], rs.at[t, 1], near_x)
        send(h.at[a, 1 - y, 1 - x, second], diag[t].at[1], ss.at[t, 2], rs.at[t, 2], near_y)
        send(h.at[a, y, 1 - x, first], side(from_x[t], t, first), ss.at[t, 3], rs.at[t, 3], near_x)
        send(h.at[a, 1 - y, x, second], side(from_y[t], t, second), ss.at[t, 4], rs.at[t, 4], near_y)

    def add_diagonal(t):
        rows = BWD_PIECES[t][2]
        half = rows // 2
        h, a = acc[t], layers(t)
        first, second = pl.ds(0, half), pl.ds(half, half)

        def add(k, yy, xx, lo):
            wait_bytes(diag[t].at[k], rs.at[t, 1 + k])
            if t in Z_FIRST:
                h[z, yy, xx, lo : lo + half, :] = h[z, yy, xx, lo : lo + half, :] + diag[t][k]
                return

            @pl.loop(0, 4)
            def _(i):
                h[i, yy, xx, lo : lo + half, :] = h[i, yy, xx, lo : lo + half, :] + diag[t][k, i]

        add(0, 1 - y, x, 0)
        send(h.at[a, 1 - y, x, first], side(from_y[t], t, first), ss.at[t, 6], rs.at[t, 6], near_y)
        add(1, y, 1 - x, half)
        send(h.at[a, y, 1 - x, second], side(from_x[t], t, second), ss.at[t, 5], rs.at[t, 5], near_x)

    def add_plane(t):
        half = BWD_PIECES[t][2] // 2
        h = acc[t]
        first, second = pl.ds(0, half), pl.ds(half, half)
        wait_bytes(side(from_x[t], t, first), rs.at[t, 3])
        wait_bytes(side(from_x[t], t, second), rs.at[t, 5])
        wait_bytes(side(from_y[t], t, second), rs.at[t, 4])
        wait_bytes(side(from_y[t], t, first), rs.at[t, 6])
        slot = out_view(t, z)
        if t in Z_FIRST:
            h[z, y, x] = h[z, y, x] + from_x[t][...] + from_y[t][...]
        else:

            @pl.loop(0, 4)
            def _(i):
                h[i, y, x] = h[i, y, x] + from_x[t][i] + from_y[t][i]

            for zz in others:
                send(h.at[zz, y, x], slot, ss.at[t, 7], rs.at[t, 7], device_at(zz, y, x, c))
        local_copy(h.at[z, y, x], slot, ls.at[t])

    def finish(t):
        half = BWD_PIECES[t][2] // 2
        three = out_view(t, pl.ds(0, 3))
        if t in Z_FIRST:
            wait_bytes(from_z[t], ss.at[t, 7])
        else:
            wait_bytes(three, rs.at[t, 7])
            wait_bytes(three, ss.at[t, 7])
        wait_bytes(out_view(t, 0), ls.at[t])
        wait_bytes(diag[t].at[0], ss.at[t, 1])
        wait_bytes(diag[t].at[1], ss.at[t, 2])
        for kind in (3, 4, 5, 6):
            wait_bytes(side(from_x[t], t, pl.ds(0, half)), ss.at[t, kind])

    given = {}

    def take_stage(key, t):
        if key in given:
            wait_bytes(acc[given[key]], ss.at[given[key], 0])
        given[key] = t

    def rows_sib(t, lhs, rhs, stage, key):
        take_stage(key, t)
        width = BWD_PIECES[t][3]
        tile = min(width, 1024)

        @pl.loop(0, width // tile)
        def _(j):
            cols = lanes_at(j * tile, tile)
            val = dot(lhs[1 - c], rhs[:, cols]).astype(BF16)
            stage[:, :, :, :, cols] = val.reshape(4, 2, 2, 32, tile)

        give(t, stage)

    def rows_own(t, lhs, rhs):
        width = BWD_PIECES[t][3]
        tile = min(width, 1024)
        wait_bytes(acc[t], rs.at[t, 0])

        @pl.loop(0, width // tile)
        def _(j):
            cols = lanes_at(j * tile, tile)
            val = dot(lhs[c], rhs[:, cols]) + acc[t][:, :, :, :, cols].reshape(512, tile).astype(F32)
            acc[t][:, :, :, :, cols] = val.astype(BF16).reshape(4, 2, 2, 32, tile)

    def down_tile(h, parity, j):
        per = 1024 // DOWN_TILE
        rhs = four[2 * parity + j // per, :, lanes_at((j % per) * DOWN_TILE, DOWN_TILE)]
        return dot(dgt[512 * h : 512 * h + 512, :], rhs)

    def down_blocks(j):
        for b in range(DOWN_TILE // 128):
            s = j * (DOWN_TILE // 128) + b
            yield b, s // 4, (s // 2) % 2, s % 2

    def down_sib(*ks):
        rows = 256 * len(ks)
        for k0 in ks:
            take_stage(k0 % 2, R_DOWN + k0)

        @pl.loop(0, 2)
        def _(j):
            val = dot(dgt[256 * ks[0] : 256 * ks[0] + rows, :], four[2 * (1 - c) + j]).astype(BF16)
            for b in range(8):
                for i, k0 in enumerate(ks):
                    stage_d[k0 % 2, 2 * j + b // 4, (b // 2) % 2, b % 2] = val[
                        256 * i : 256 * i + 256, 128 * b : 128 * b + 128
                    ]

        for k0 in ks:
            give(R_DOWN + k0, stage_d.at[k0 % 2])

    def down_own(*ks):
        rows = 256 * len(ks)
        for k0 in ks:
            wait_bytes(acc[R_DOWN + k0], rs.at[R_DOWN + k0, 0])

        @pl.loop(0, 2)
        def _(j):
            val = dot(dgt[256 * ks[0] : 256 * ks[0] + rows, :], four[2 * c + j])
            for b in range(8):
                for i, k0 in enumerate(ks):
                    h = acc[R_DOWN + k0]
                    old = h[2 * j + b // 4, (b // 2) % 2, b % 2].astype(F32)
                    h[2 * j + b // 4, (b // 2) % 2, b % 2] = (
                        val[256 * i : 256 * i + 256, 128 * b : 128 * b + 128] + old
                    ).astype(BF16)

    def column_sum(ref):
        return dot(jnp.ones((16, 512), BF16), ref)[0:1]

    def row_valid(rows, start):
        r = lax.broadcasted_iota(jnp.int32, (rows, 1), 0) + start
        return ((r >= offset) & (r < offset + length)).astype(F32)

    def norm_back(inv, gain, to_gain, to_shift):
        sums[to_gain : to_gain + 1, :] = jnp.zeros((1, 1024), F32)
        sums[to_shift : to_shift + 1, :] = jnp.zeros((1, 1024), F32)

        @pl.loop(0, 16, unroll=4)
        def _(i):
            rows = rows_at(i * 32, 32)
            grad, normed = resid[rows, :], nbuf[rows, :]
            scaled = grad * vecs[gain : gain + 1, :]
            mean = jnp.sum(scaled, axis=1, keepdims=True) * (1.0 / 1024)
            cross = jnp.sum(scaled * normed, axis=1, keepdims=True) * (1.0 / 1024)
            out = (scaled - mean - normed * cross) * inv[rows, 0:1]
            resid[rows, :] = out
            dg[rows, :] = out.astype(BF16)
            sums[to_gain : to_gain + 1, :] = sums[to_gain : to_gain + 1, :] + jnp.sum(
                grad * normed, axis=0, keepdims=True
            )
            sums[to_shift : to_shift + 1, :] = sums[to_shift : to_shift + 1, :] + jnp.sum(
                grad, axis=0, keepdims=True
            )

    def begin():
        ready("cote")
        cot[...] = jnp.where(row_valid(512, 0) > 0.0, cot[...].astype(F32), 0.0).astype(BF16)
        sums[V_BD : V_BD + 1, :] = column_sum(dg[...])
        ready("low")
        ready("wproj")
        transpose_blocks(slopes.at[1], blocks.at[0])
        embed[...] = (dot(slopes[1], wproj[...]) * row_valid(512, 0)).astype(BF16)
        local_copy(embed, embed_h, esem)
        load("slope1", slope_h.at[:, pl.ds(1024, 1024)], slopes.at[1])

    def turn():
        @pl.loop(0, 8)
        def _(j):
            dgt[rows_at(j * 128, 128), :] = dg[:, lanes_at(j * 128, 128)].T

    def acts():
        for p in range(2):
            for h in range(2):
                ready("act%d%d" % (p, h))

    def up_grad(k0):
        w = ring_wait(2 * k0)
        ready("slope%d" % k0)

        @pl.loop(0, 1)
        def _(j):
            cols = lanes_at(j * 1024, 1024)
            back = dot_nt(dg[...], w[rows_at(j * 1024, 1024), :]) * slopes[k0 % 2, :, cols].astype(F32)
            upg[k0, :, cols] = back.astype(BF16)

        ring_next(2 * k0)
        if k0 + 2 < 4:
            load("slope%d" % (k0 + 2), slope_h.at[:, pl.ds(1024 * (k0 + 2), 1024)], slopes.at[k0 % 2])
        sum_up[0:1, 1024 * k0 : 1024 * k0 + 1024] = column_sum(upg[k0])

    def first_grad(k0):
        if k0 == 0:
            ready("back")
        w = ring_wait(2 * k0 + 1)

        @pl.loop(0, 1)
        def _(j):
            cols = lanes_at(j * 1024, 1024)
            resid[:, cols] = resid[:, cols] + dot_nt(upg[k0], w[rows_at(j * 1024, 1024), :])

        ring_next(2 * k0 + 1)

    def up_sib(k0):
        if k0 == 0:
            ready("firstp")
        rows_sib(R_UP + k0, blocks.at[1], upg.at[k0], stage_u.at[k0 % 2], 2 + k0 % 2)

    def up_own(k0):
        rows_own(R_UP + k0, blocks.at[1], upg.at[k0])

    def norm_one():
        ready("n1")
        ready("inv1")
        ready("vecs")
        norm_back(inv1, V_GA, V_GA, V_SA)
        sums[V_BO : V_BO + 1, :] = column_sum(dg[...])
        load("ctxp", ctxp_h, blocks.at[0])

    def start_attention():
        load("q", q_h, upg.at[0])
        load("v", v_h, upg.at[1])
        load("tokp", tokp_h, blocks.at[1])
        prob_start(0)

    def prob_start(p):
        for j in range(2):
            local_copy(
                prob_h.at[p, j],
                upg.at[2 + p % 2, :, pl.ds(512 * j, 512)],
                psem.at[p % 2, j],
            )

    def ctx_back():
        w = ring_wait(8)

        @pl.loop(0, 1)
        def _(j):
            four[3, :, lanes_at(j * 1024, 1024)] = dot_nt(dg[...], w[rows_at(j * 1024, 1024), :]).astype(BF16)

        ring_next(8)

    def make_mask():
        s = lax.broadcasted_iota(jnp.int32, (1, 512), 1)
        col_valid = ((s >= offset) & (s < offset + length)).astype(F32)

        @pl.loop(0, 8)
        def _(i):
            mask[rows_at(i * 64, 64), :] = row_valid(64, i * 64) * col_valid

    def lane128():
        return lax.broadcasted_iota(jnp.int32, (1, 128), 1)

    def unturn(val):
        swapped = jnp.where(lane128() % 64 < 32, pltpu.roll(val, 96, 1), pltpu.roll(val, 32, 1))
        return (val * cosine[...] - swapped * sine[...]).astype(BF16)

    def attend_back(p0, p1):
        @pl.loop(p0, p1)
        def _(p):
            cols = lanes_at(p * 128, 128)
            for j in range(2):
                wait_bytes(upg.at[2 + p % 2, :, pl.ds(512 * j, 512)], psem.at[p % 2, j])

            @pl.when(p + 1 < 8)
            def _():
                prob_start(p + 1)

            qp, vp, grad = upg[0, :, cols], upg[1, :, cols], four[3, :, cols]
            dv, dk, dqt = [], [], []
            for j in range(2):
                keep = lane128() < 64 if j == 0 else lane128() >= 64
                low = upg[2 + p % 2, :, 512 * j : 512 * j + 512]
                wide = low.astype(F32)
                back = dot_nt(jnp.where(keep, vp, jnp.zeros((), BF16)), grad)
                row_dot = jnp.sum(wide * back, axis=0, keepdims=True)
                sgrad = jnp.where(mask[...] > 0.0, wide * (back - row_dot), 0.0).astype(BF16)
                dv.append(dot(low, grad))
                dk.append(dot(sgrad, qp))
                dqt.append(dot(kt[rows_at(p * 128 + 64 * j, 64), :], sgrad))
            four[2, :, cols] = jnp.where(lane128() < 64, dv[0], dv[1]).astype(BF16)
            four[1, :, cols] = unturn(jnp.where(lane128() < 64, dk[0], dk[1]))
            four[0, :, cols] = unturn(jnp.concatenate(dqt, axis=0).T * 0.125)

    def bias_sums():
        sums[V_BQ : V_BQ + 1, :] = column_sum(four[0])
        sums[V_BK : V_BK + 1, :] = column_sum(four[1])
        sums[V_BV : V_BV + 1, :] = column_sum(four[2])

    def vector_table():
        ready("stats")
        ready("sumf")
        for b in range(8):
            val = jnp.concatenate(
                [sums[0:7, 128 * b : 128 * b + 128], sumf[0:2, 128 * b : 128 * b + 128], jnp.zeros((1, 128), F32), stats[0:4, :], jnp.zeros((2, 128), F32)],
                axis=0,
            )
            for i in range(4):
                table[b // 2, b % 2, i // 2, i % 2] = val
        for d in range(32):
            table[d // 8, (d // 4) % 2, (d // 2) % 2, d % 2, 9:10, :] = sum_up[
                0:1, 128 * d : 128 * d + 128
            ]
        give(R_VEC, table.at[:, :, :, 1 - c])

    def vector_own():
        wait_bytes(acc[R_VEC], rs.at[R_VEC, 0])
        acc[R_VEC][...] = acc[R_VEC][...] + table[:, :, :, c]

    def token_grad(i):
        w = ring_wait(9 + i)

        @pl.loop(0, 1)
        def _(j):
            cols = lanes_at(j * 1024, 1024)
            resid[:, cols] = resid[:, cols] + dot_nt(four[i], w[rows_at(j * 1024, 1024), :])

    def token_out():
        local_copy(resid, grad_h, gsem)

    moves = {B_NET: net, B_COLUMN: add_column, B_DIAGONAL: add_diagonal, B_PLANE: add_plane}
    pieces = {
        B_TURN: turn,
        B_ACTS: lambda: (acts(), greet_end()),
        B_BEGIN: begin,
        B_NORM: lambda: (norm_one(), make_mask()),
        B_BACK: lambda: (start_attention(), ctx_back()),
        B_BIAS: bias_sums,
    }

    def source(t):
        n = {R_Q: 0, R_K: 1, R_V: 2, R_K_END: 1, R_V_END: 2}[t]
        return four.at[n, :, pl.ds(BWD_PIECES[t][1], BWD_PIECES[t][3])]

    def sib(t):
        if t == R_PROJ:
            rows_sib(t, blocks.at[0], cot, stage_p, 4)
        elif t < R_OUT:
            up_sib(t - R_UP)
        elif t == R_OUT:
            ready("ctxp")
            rows_sib(t, blocks.at[0], dg, stage_u.at[0], 2)
        elif t == R_VEC:
            vector_table()
        else:
            if t == R_Q:
                ready("tokp")
            first, width = BWD_PIECES[t][1], BWD_PIECES[t][3]
            stage, key = {R_Q: (1, 3), R_K: (0, 2), R_V: (1, 3), R_K_END: (0, 5), R_V_END: (1, 6)}[t]
            room = stage_u.at[stage, :, :, :, :, pl.ds(first, width)]
            rows_sib(t, blocks.at[1], source(t), room, key)

    def mine(t):
        if t == R_PROJ:
            rows_own(t, blocks.at[0], cot)
        elif t < R_OUT:
            up_own(t - R_UP)
        elif t == R_OUT:
            rows_own(t, blocks.at[0], dg)
        elif t == R_VEC:
            vector_own()
        else:
            rows_own(t, blocks.at[1], source(t))

    def attend_pairs(n):
        if n == 0:
            for name in ("kt", "q", "v", "cos", "sin"):
                ready(name)
        attend_back(2 * n, 2 * n + 2)

    def tokens(n):
        token_grad(n)
        if n == 2:
            token_out()

    moves.update({
        B_SIB: sib,
        B_OWN: mine,
        B_ATTEND: attend_pairs,
        B_TOKENS: tokens,
        B_UP: up_grad,
        B_FIRST: first_grad,
        B_DOWNSIB: lambda k0: down_sib(2, 3) if k0 == 2 else down_sib(k0),
        B_DOWNOWN: lambda k0: down_own(2, 3) if k0 == 2 else down_own(k0),
    })
    ready("dg")
    for name, t in BWD_ORDER:
        if name in moves:
            moves[name](t)
        else:
            pieces[name]()
    for t in range(count):
        finish(t)
    for t in given.values():
        wait_bytes(acc[t], ss.at[t, 0])
    wait_bytes(acc[R_VEC], ss.at[R_VEC, 0])
    wait_bytes(resid, gsem)
    wait_bytes(embed, esem)


def backward_pass(cot_embed, lengths, offsets, order, weights, kept):
    count = len(BWD_PIECES)
    outs = [jax.ShapeDtypeStruct((512, 1024), F32), jax.ShapeDtypeStruct((512, 128), BF16)]
    outs += [jax.ShapeDtypeStruct((4, r, k), dt) for r, k, dt in BWD_OUTS]
    big = lambda *s: pltpu.VMEM(s, BF16)
    wide = lambda *s: pltpu.VMEM(s, F32)
    scratch = [
        big(3, 1024, 1024),
        wide(512, 1024),
        wide(512, 1024),
        wide(8, 1024),
        wide(512, 128),
        big(512, 1024),
        big(1024, 512),
        big(4, 512, 1024),
        big(4, 512, 1024),
        big(2, 512, 1024),
        big(2, 2, 512, 512),
        big(1024, 512),
        wide(512, 512),
        wide(512, 128),
        wide(512, 128),
        big(512, 128),
        wide(16, 1024),
        wide(8, 128),
        wide(16, 1024),
        wide(1, 4096),
        wide(4, 2, 2, 2, 16, 128),
        big(2, 4, 2, 2, 256, 128),
        big(2, 4, 2, 2, 32, 1024),
        big(4, 2, 2, 32, 128),
        big(1024, 128),
        big(512, 128),
    ]
    for lead, flat in (((4, 2, 2), (4, 2, 2)), ((2, 4), (2,)), ((4,), ()), ((4,), ())):
        for t, (_, _, rows, width, dtype) in enumerate(BWD_PIECES):
            shape = flat if t in Z_FIRST else lead
            scratch.append(pltpu.VMEM(shape + (rows // 2 if lead == (2, 4) else rows, width), dtype))
    for t in Z_FIRST:
        scratch.append(big(3, 2, 2, *BWD_PIECES[t][2:4]))
    dma = pltpu.SemaphoreType.DMA
    scratch += [dma((count, 8)), dma((count, 8)), dma((count,)), dma((32,)), dma((12,)), dma((2, 2)), dma, dma]
    smem = pl.BlockSpec(memory_space=pltpu.SMEM)
    return pl.pallas_call(
        backward_kernel,
        out_shape=outs,
        in_specs=[ANY, smem, smem, smem] + [ANY] * (7 + 19),
        out_specs=[ANY] * len(outs),
        scratch_shapes=scratch,
        compiler_params=pltpu.CompilerParams(
            collective_id=1, has_side_effects=True, vmem_limit_bytes=62 * 2**20
        ),
        name="backward_pass",
    )(cot_embed, lengths, offsets, order, *weights, *kept)


def finish_kernel(*refs):
    parts, (hidden_h, embed_h, tokens_h) = refs[:8], refs[8:11]
    outs, hidden_o, embed_o, tokens_o = refs[11:19], *refs[19:22]
    vec_outs, refs = refs[22:32], refs[32:]
    bufs, results, carry, vectors = refs[:8], refs[8:16], refs[16:19], refs[19:29]
    ins, done, moved, vsem = refs[29:]
    order = (6, 1, 2, 3, 4, 5, 7, 0)
    for i in order:
        local_copy(parts[i], bufs[i], ins.at[i])
    moves = ((hidden_h, hidden_o), (embed_h, embed_o), (tokens_h, tokens_o))
    for i, (src, _) in enumerate(moves):
        local_copy(src, carry[i], moved.at[i, 0])
    me = lax.axis_index("dp")
    z = me // 8
    for i in order:
        wait_bytes(bufs[i], ins.at[i])
        buf = bufs[i]
        total = buf[0].astype(F32) + buf[1].astype(F32) + buf[2].astype(F32) + buf[3].astype(F32)
        if i == 1:
            total = total.T
        if i == 6:
            own = jnp.where(me % 4 == 0, total[:, 0:32], 0.0)
            for j in range(1, 4):
                own = own + jnp.where(me % 4 == j, total[:, 32 * j : 32 * j + 32], 0.0)
            stat = jnp.sum(total, axis=1, keepdims=True)
            root = jnp.sqrt(stat[10:13] / (stat[13:14] * (1024 / 128)))
            results[6][...] = jnp.zeros((8, 128), F32)
            for k in range(3):
                results[6][0:1, k : k + 1] = root[k : k + 1]
            for k in range(9):
                vectors[k][...] = own[k : k + 1].reshape(32)
            vectors[9][...] = total[9:10].reshape(128)
            for k in range(10):
                local_copy(vectors[k], vec_outs[k], vsem.at[k])
        else:
            results[i][...] = total
            for t in Z_FIRST:
                if BWD_PIECES[t][0] == i:
                    cols = slice(BWD_PIECES[t][1], BWD_PIECES[t][1] + BWD_PIECES[t][3])
                    results[i][:, cols] = buf[z, :, cols].astype(F32)
        local_copy(results[i], outs[i], done.at[i])
        if i == 2:
            for k, (src, dst) in enumerate(moves):
                wait_bytes(carry[k], moved.at[k, 0])
                local_copy(carry[k], dst, moved.at[k, 1])
    for i in order:
        wait_bytes(results[i], done.at[i])
    for i in range(3):
        wait_bytes(carry[i], moved.at[i, 1])
    for k in range(10):
        wait_bytes(vectors[k], vsem.at[k])


def finish(parts, hidden, embed, grad):
    shape = jax.ShapeDtypeStruct
    sums = [shape(p.shape[1:], F32) for p in parts]
    sums[1] = shape((128, 1024), F32)
    sums[6] = shape((8, 128), F32)
    vectors = [shape((32,), F32)] * 9 + [shape((128,), F32)]
    moved = [shape(a.shape, a.dtype) for a in (hidden, embed, grad)]
    dma = pltpu.SemaphoreType.DMA
    return pl.pallas_call(
        finish_kernel,
        out_shape=sums + moved + vectors,
        in_specs=[pl.BlockSpec(memory_space=pltpu.HBM)] * 11,
        out_specs=[pl.BlockSpec(memory_space=pltpu.HBM)] * 21,
        scratch_shapes=[pltpu.VMEM(p.shape, p.dtype) for p in parts]
        + [pltpu.VMEM(s.shape, F32) for s in sums]
        + [pltpu.VMEM(a.shape, a.dtype) for a in moved]
        + [pltpu.VMEM(a.shape, F32) for a in vectors]
        + [dma((8,)), dma((8,)), dma((3, 2)), dma((10,))],
        compiler_params=pltpu.CompilerParams(vmem_limit_bytes=60 * 2**20),
        name="finish",
    )(*parts, hidden, embed, grad)


def shards(
    tokens, cot_hidden, cot_embed, lengths, offsets, pack_order,
    w_query, b_query, w_key, b_key, w_value, b_value, w_out, b_out, gain_attn, shift_attn,
    w_up, b_up, w_down, b_down, gain_ffn, shift_ffn, w_proj,
):
    done = forward_pass(
        tokens, cot_hidden, cot_embed,
        (b_query, b_key, b_value, b_out, gain_attn, shift_attn, b_down, gain_ffn, shift_ffn, b_up),
        lengths, offsets, pack_order,
        (w_query, w_key, w_value, w_out, w_up, w_proj, w_down),
    )
    weights = [w.reshape(-1, w.shape[-1]) for w in done[:7]]
    kept = list(done[7 : 7 + 14]) + list(done[7 + 15 :])
    back = backward_pass(cot_embed, lengths, offsets, pack_order, weights, kept)
    results = finish(back[2:], done[7 + 14], back[1], back[0])
    proj, down, up, out, query, key, vec, val, hidden, embed, grad, *own = results
    return (
        hidden, embed, grad,
        query, own[V_BQ], key, own[V_BK], val, own[V_BV], out, own[V_BO],
        own[V_GA], own[V_SA], up, own[9], down, own[V_BD], own[V_GF], own[V_SF],
        proj, vec[0, :3],
    )


def shards_any(
    tokens,
    cot_hidden,
    cot_embed,
    lengths,
    offsets,
    pack_order,
    w_query,
    b_query,
    w_key,
    b_key,
    w_value,
    b_value,
    w_out,
    b_out,
    gain_attn,
    shift_attn,
    w_up,
    b_up,
    w_down,
    b_down,
    gain_ffn,
    shift_ffn,
    w_proj,
):
    gathered = (
        lax.all_gather(w_query, "dp", axis=0, tiled=True),
        lax.all_gather(w_key, "dp", axis=0, tiled=True),
        lax.all_gather(w_value, "dp", axis=0, tiled=True),
        lax.all_gather(w_out, "dp", axis=0, tiled=True),
        lax.all_gather(w_up, "dp", axis=0, tiled=True),
        lax.all_gather(w_down, "dp", axis=0, tiled=True),
        lax.all_gather(w_proj, "dp", axis=0, tiled=True),
        lax.all_gather(b_query, "dp", axis=0, tiled=True),
        lax.all_gather(b_key, "dp", axis=0, tiled=True),
        lax.all_gather(b_value, "dp", axis=0, tiled=True),
        lax.all_gather(b_out, "dp", axis=0, tiled=True),
        lax.all_gather(gain_attn, "dp", axis=0, tiled=True),
        lax.all_gather(shift_attn, "dp", axis=0, tiled=True),
        lax.all_gather(b_up, "dp", axis=0, tiled=True),
        lax.all_gather(b_down, "dp", axis=0, tiled=True),
        lax.all_gather(gain_ffn, "dp", axis=0, tiled=True),
        lax.all_gather(shift_ffn, "dp", axis=0, tiled=True),
    )
    wt_query, wt_key, wt_value, wt_out, wt_up, wt_down, wt_proj = gathered[:7]
    vectors = [piece.astype(jnp.float32) for piece in gathered[7:]]
    (
        bias_query,
        bias_key,
        bias_value,
        bias_out,
        norm_gain_a,
        norm_shift_a,
        bias_up,
        bias_down,
        norm_gain_f,
        norm_shift_f,
    ) = vectors
    row_count = tokens.shape[0]
    model_width = tokens.shape[1]
    head_count = H
    head_dim = model_width // head_count
    device = lax.axis_index("dp")
    slots = jnp.arange(pack_order.shape[0], dtype=jnp.int32)
    pack_id = jnp.sum(jnp.where(slots == device, pack_order, 0))
    length = jnp.sum(jnp.where(slots == pack_id, lengths, 0))
    offset = jnp.sum(jnp.where(slots == pack_id, offsets, 0))
    row_index = jnp.arange(row_count, dtype=jnp.int32)
    is_valid = (row_index >= offset) & (row_index < offset + length)
    keep_rows = is_valid.astype(jnp.float32)[:, None]
    cosine, sine_part = rope_tables((row_index - offset).astype(jnp.float32), head_dim)
    query_pre = matmul(tokens, wt_query) + bias_query
    key_pre = matmul(tokens, wt_key) + bias_key
    value_low = (
        (matmul(tokens, wt_value) + bias_value)
        .astype(jnp.bfloat16)
        .reshape(row_count, head_count, head_dim)
    )
    query_rot = rotate(
        query_pre.reshape(row_count, head_count, head_dim), cosine, sine_part
    ).astype(jnp.bfloat16)
    key_rot = rotate(key_pre.reshape(row_count, head_count, head_dim), cosine, sine_part).astype(
        jnp.bfloat16
    )
    score_scale = 1.0 / math.sqrt(head_dim)
    key_valid = is_valid[None, None, :]
    allowed = is_valid[None, :, None] & key_valid
    masked = masked_scores(query_rot, key_rot, allowed, score_scale)
    row_top = jnp.max(masked, axis=-1, keepdims=True)
    exponent = jnp.exp(masked - row_top)
    row_total = jnp.sum(exponent, axis=-1, keepdims=True)
    prob_low = (exponent / row_total).astype(jnp.bfloat16)
    contexts = jnp.einsum("hqk,khd->qhd", prob_low, value_low, preferred_element_type=jnp.float32)
    log_totals = row_top + jnp.log(row_total)
    context = contexts.astype(jnp.bfloat16).reshape(row_count, model_width)
    tokens_wide = tokens.astype(jnp.float32)
    attn_branch = matmul(context, wt_out) + bias_out
    first, normed_one, inverse_one = norm_forward(
        tokens_wide + attn_branch, norm_gain_a, norm_shift_a
    )
    first_low = first.astype(jnp.bfloat16)
    up_pre = matmul(first_low, wt_up) + bias_up
    act_full, gelu_pull = jax.vjp(exact_gelu, up_pre)
    act_low = act_full.astype(jnp.bfloat16)
    down_branch = matmul(act_low, wt_down) + bias_down
    out, normed_two, inverse_two = norm_forward(first + down_branch, norm_gain_f, norm_shift_f)
    out_low = out.astype(jnp.bfloat16)
    hidden = (out * keep_rows).astype(jnp.bfloat16)
    embedding = (matmul(out_low, wt_proj) * keep_rows).astype(jnp.bfloat16)
    stat_sums = lax.psum(
        (
            jnp.sum(keep_rows * tokens_wide * tokens_wide),
            jnp.sum(keep_rows * attn_branch * attn_branch),
            jnp.sum(keep_rows * down_branch * down_branch),
            jnp.sum(keep_rows),
        ),
        "dp",
    )
    rms_stats = jnp.sqrt(
        jnp.stack([stat_sums[0], stat_sums[1], stat_sums[2]]) / (stat_sums[3] * model_width)
    )
    backward_set = (
        lax.all_gather(w_query, "dp", axis=0, tiled=True),
        lax.all_gather(w_key, "dp", axis=0, tiled=True),
        lax.all_gather(w_value, "dp", axis=0, tiled=True),
        lax.all_gather(w_out, "dp", axis=0, tiled=True),
        lax.all_gather(w_up, "dp", axis=0, tiled=True),
        lax.all_gather(w_down, "dp", axis=0, tiled=True),
        lax.all_gather(w_proj, "dp", axis=0, tiled=True),
        lax.all_gather(b_query, "dp", axis=0, tiled=True),
        lax.all_gather(b_key, "dp", axis=0, tiled=True),
        lax.all_gather(b_value, "dp", axis=0, tiled=True),
        lax.all_gather(b_out, "dp", axis=0, tiled=True),
        lax.all_gather(gain_attn, "dp", axis=0, tiled=True),
        lax.all_gather(shift_attn, "dp", axis=0, tiled=True),
        lax.all_gather(b_up, "dp", axis=0, tiled=True),
        lax.all_gather(b_down, "dp", axis=0, tiled=True),
        lax.all_gather(gain_ffn, "dp", axis=0, tiled=True),
        lax.all_gather(shift_ffn, "dp", axis=0, tiled=True),
    )
    back_query, back_key, back_value, back_out, back_up, back_down, back_proj = backward_set[:7]
    back_gain_a = backward_set[11].astype(jnp.float32)
    back_gain_f = backward_set[15].astype(jnp.float32)
    cot_low = jnp.where(is_valid[:, None], cot_embed, jnp.zeros_like(cot_embed))
    grad_w_proj = matmul_tn(out_low, cot_low)
    grad_out = keep_rows * cot_hidden.astype(jnp.float32) + matmul_nt(cot_low, back_proj)
    grad_resid_two, grad_gain_f, grad_shift_f = norm_backward(
        grad_out, normed_two, inverse_two, back_gain_f
    )
    down_grad = grad_resid_two.astype(jnp.bfloat16)
    grad_w_down = matmul_tn(act_low, down_grad)
    grad_b_down = jnp.sum(down_grad.astype(jnp.float32), axis=0)
    up_grad = gelu_pull(matmul_nt(down_grad, back_down))[0].astype(jnp.bfloat16)
    grad_w_up = matmul_tn(first_low, up_grad)
    grad_b_up = jnp.sum(up_grad.astype(jnp.float32), axis=0)
    grad_first = grad_resid_two + matmul_nt(up_grad, back_up)
    grad_resid_one, grad_gain_a, grad_shift_a = norm_backward(
        grad_first, normed_one, inverse_one, back_gain_a
    )
    attn_grad = grad_resid_one.astype(jnp.bfloat16)
    grad_w_out = matmul_tn(context, attn_grad)
    grad_b_out = jnp.sum(attn_grad.astype(jnp.float32), axis=0)
    ctx_grad = (
        matmul_nt(attn_grad, back_out).astype(jnp.bfloat16).reshape(row_count, head_count, head_dim)
    )
    allowed = is_valid[None, :, None] & key_valid
    masked = masked_scores(query_rot, key_rot, allowed, score_scale)
    prob_full = jnp.exp(masked - log_totals)
    prob_low = prob_full.astype(jnp.bfloat16)
    prob_grad = jnp.einsum("qhd,khd->hqk", ctx_grad, value_low, preferred_element_type=jnp.float32)
    value_sum = jnp.einsum("hqk,qhd->khd", prob_low, ctx_grad, preferred_element_type=jnp.float32)
    row_dot = jnp.sum(prob_full * prob_grad, axis=-1, keepdims=True)
    score_grad = jnp.where(allowed, prob_full * (prob_grad - row_dot), 0.0).astype(jnp.bfloat16)
    query_parts = (
        jnp.einsum("hqk,khd->qhd", score_grad, key_rot, preferred_element_type=jnp.float32)
        * score_scale
    )
    key_sum = (
        jnp.einsum("hqk,qhd->khd", score_grad, query_rot, preferred_element_type=jnp.float32)
        * score_scale
    )
    query_grad = (
        unrotate(query_parts, cosine, sine_part)
        .reshape(row_count, model_width)
        .astype(jnp.bfloat16)
    )
    key_grad = (
        unrotate(key_sum, cosine, sine_part).reshape(row_count, model_width).astype(jnp.bfloat16)
    )
    value_grad = value_sum.reshape(row_count, model_width).astype(jnp.bfloat16)
    grad_w_query = matmul_tn(tokens, query_grad)
    grad_b_query = jnp.sum(query_grad.astype(jnp.float32), axis=0)
    grad_w_key = matmul_tn(tokens, key_grad)
    grad_b_key = jnp.sum(key_grad.astype(jnp.float32), axis=0)
    grad_w_value = matmul_tn(tokens, value_grad)
    grad_b_value = jnp.sum(value_grad.astype(jnp.float32), axis=0)
    grad_tokens = (
        grad_resid_one
        + matmul_nt(query_grad, back_query)
        + matmul_nt(key_grad, back_key)
        + matmul_nt(value_grad, back_value)
    )
    all_parts = (
        lax.psum_scatter(grad_w_query, "dp", scatter_dimension=0, tiled=True),
        lax.psum_scatter(grad_w_key, "dp", scatter_dimension=0, tiled=True),
        lax.psum_scatter(grad_w_value, "dp", scatter_dimension=0, tiled=True),
        lax.psum_scatter(grad_w_out, "dp", scatter_dimension=0, tiled=True),
        lax.psum_scatter(grad_b_query, "dp", scatter_dimension=0, tiled=True),
        lax.psum_scatter(grad_b_key, "dp", scatter_dimension=0, tiled=True),
        lax.psum_scatter(grad_b_value, "dp", scatter_dimension=0, tiled=True),
        lax.psum_scatter(grad_b_out, "dp", scatter_dimension=0, tiled=True),
        lax.psum_scatter(grad_gain_a, "dp", scatter_dimension=0, tiled=True),
        lax.psum_scatter(grad_shift_a, "dp", scatter_dimension=0, tiled=True),
        lax.psum_scatter(grad_w_up, "dp", scatter_dimension=0, tiled=True),
        lax.psum_scatter(grad_w_down, "dp", scatter_dimension=0, tiled=True),
        lax.psum_scatter(grad_w_proj, "dp", scatter_dimension=0, tiled=True),
        lax.psum_scatter(grad_b_up, "dp", scatter_dimension=0, tiled=True),
        lax.psum_scatter(grad_b_down, "dp", scatter_dimension=0, tiled=True),
        lax.psum_scatter(grad_gain_f, "dp", scatter_dimension=0, tiled=True),
        lax.psum_scatter(grad_shift_f, "dp", scatter_dimension=0, tiled=True),
    )
    attn_parts = all_parts[:10]
    ffn_parts = all_parts[10:]
    return (
        hidden,
        embedding,
        grad_tokens,
        attn_parts[0],
        attn_parts[4],
        attn_parts[1],
        attn_parts[5],
        attn_parts[2],
        attn_parts[6],
        attn_parts[3],
        attn_parts[7],
        attn_parts[8],
        attn_parts[9],
        ffn_parts[0],
        ffn_parts[3],
        ffn_parts[1],
        ffn_parts[4],
        ffn_parts[5],
        ffn_parts[6],
        ffn_parts[2],
        rms_stats,
    )


def solution(mesh):
    fast = mesh.shape["dp"] == 32
    placed = (
        P("dp", None),
        P("dp", None),
        P("dp", None),
        P(),
        P(),
        P(),
        P("dp", None),
        P("dp"),
        P("dp", None),
        P("dp"),
        P("dp", None),
        P("dp"),
        P("dp", None),
        P("dp"),
        P("dp"),
        P("dp"),
        P("dp", None),
        P("dp"),
        P("dp", None),
        P("dp"),
        P("dp"),
        P("dp"),
        P("dp", None),
    )
    return jax.shard_map(
        shards if fast else shards_any,
        mesh=mesh,
        in_specs=placed,
        out_specs=(
            P("dp", None),
            P("dp", None),
            P("dp", None),
            P("dp", None),
            P("dp"),
            P("dp", None),
            P("dp"),
            P("dp", None),
            P("dp"),
            P("dp", None),
            P("dp"),
            P("dp"),
            P("dp"),
            P("dp", None),
            P("dp"),
            P("dp", None),
            P("dp"),
            P("dp"),
            P("dp"),
            P("dp", None),
            P(),
        ),
        check_vma=False,
    )
```
